32 devices in a mesh: dp: 8 (over z, x), expert: 4 (over y, core).
Axes of the slice: x: 2, y: 2, z: 4, core: 2. Of those that a mesh axis runs over, the one named last changes fastest.
Arguments:
- tokens: bfloat16 [6144, 768], P(('dp', 'expert')), may hold values from -6 to 6
- seq_lengths: int32 [8, 4, 4], P('dp'), may hold values from 1 to 96, 192 in all within a row
- block_perm: int32 [8, 4], P('dp'), may hold values from 0 to 3, each once within a row
- routes: int32 [2, 6144, 2], P(None, ('dp', 'expert')), may hold values from 0 to 11, all different within a row; in each aligned block of 192 rows (0 to 191, 192 to 383, ..., all dimensions but the last counted through in order) at most 48 rows name the same one
- norm_gains: float32 [2, 2, 768], P(None, None, 'dp'), may hold values from 0.5 to 1.5
- w_qkv: float32 [2, 768, 2304], P(None, None, 'dp'), may hold values from -0.21875 to 0.21875
- w_out: float32 [2, 768, 768], P(None, 'dp'), may hold values from -1.25 to 1.25
- w_router: float32 [2, 768, 12], P(None, 'dp'), may hold values from -0.15625 to 0.15625
- w_residual: float32 [12, 12], replicated, may hold values from -1.25 to 1.25
- w_const: float32 [2, 2, 768, 2], P(None, None, 'dp'), may hold values from -0.21875 to 0.21875
- v_const: float32 [2, 2, 768], P(None, None, 'dp'), may hold values from -6 to 6
- w_gate: float32 [2, 8, 768, 2048], P(None, 'expert', None, 'dp'), may hold values from -0.21875 to 0.21875
- w_up: float32 [2, 8, 768, 2048], P(None, 'expert', None, 'dp'), may hold values from -0.21875 to 0.21875
- w_down: float32 [2, 8, 2048, 768], P(None, 'expert', 'dp'), may hold values from -0.125 to 0.125
- cotangent: bfloat16 [6144, 768], P(('dp', 'expert')), may hold values from -6 to 6
Outputs:
- output: bfloat16 [6144, 768], P(('dp', 'expert'))
- tokens_grad: float32 [6144, 768], P(('dp', 'expert'))
- gains_grad: float32 [2, 2, 768], P(None, None, 'dp')
- qkv_grad: float32 [2, 768, 2304], P(None, None, 'dp')
- out_grad: float32 [2, 768, 768], P(None, 'dp')
- router_grad: float32 [2, 768, 12], P(None, 'dp')
- residual_grad: float32 [12, 12], replicated
- const_grad: float32 [2, 2, 768, 2], P(None, None, 'dp')
- vector_grad: float32 [2, 2, 768], P(None, None, 'dp')
- gate_grad: float32 [2, 8, 768, 2048], P(None, 'expert', None, 'dp')
- up_grad: float32 [2, 8, 768, 2048], P(None, 'expert', None, 'dp')
- down_grad: float32 [2, 8, 2048, 768], P(None, 'expert', 'dp')
The draws below stay inside these ranges and needn't reach their ends.
Inputs may be any that keep to these rules, and one draw needn't show every extreme that they name: `seq_lengths`: entry [g, i] holds the lengths of the 4 sequences of initial device block g * 4 + i, in order; they sum to 192, and the longest is exactly 96. `block_perm`: each row is a permutation of 0 to 3. `routes`: each token names two different targets in each layer: under 8 a feed-forward expert, 8 the zero expert, 9 the copy expert, 10 and 11 the constant experts. In one layer the rows of one device name no target more than 48 times, a bound that some block reaches.
All inputs are finite; a program needn't handle non-finite values.
Results may differ from the reference program's by a relative error of at most 0.017.
The reference program's roundings to bfloat16 on the way count: a program that leaves them out, or rounds other values in their place, can miss the bound.
Values may be sent and summed in bfloat16 or wider, within the bound.
A program may use at most 320 MiB of HBM per device.

```python
import math
import jax
import jax.numpy as jnp
import numpy as np
from jax import lax

D = 768
HEADS = 12
HEAD_DIM = 64
FF = 2048
LAYERS = 2
DOCS = 4
TOK_DEV = 192
EXPERTS = 8
NROUTE = 12
CAP = 48
SEQ_MAX = 96
TOKENS = 6144
N_DP = 8
N_EXPERT = 4


def shard_levels(own_key, extent, cuts, low, top_value):
    factor_of, own = 1.0, jax.random.fold_in(own_key, 6)
    for position, parts in cuts:
        steps = jnp.exp(jax.random.uniform(jax.random.fold_in(own, position), (parts,), jnp.float32, low / len(cuts), top_value / len(cuts)))
        factor_of = factor_of * jnp.repeat(steps, extent[position] // parts).reshape([-1 if axis == position else 1 for axis in range(len(extent))])
    return factor_of


def length_profile(amount, total, reach, skew):
    loads = [(1 << 20) // math.isqrt(grade ** skew) + 1 for grade in range(2, amount + 1)]
    spare, counts = total - reach - (amount - 1), [1] * (amount - 1)
    while spare > 0:
        free = [i for i in range(amount - 1) if counts[i] < reach]
        whole, remaining = sum([loads[i] for i in free]), spare
        for i in free:
            extra = min(reach - counts[i], max(1, remaining * loads[i] // whole), spare)
            counts[i] = counts[i] + extra
            spare = spare - extra
    return np.array([reach] + counts)


def ragged_sizes(stream_key, count, total, reach, lean):
    if count == 2:
        one = jax.random.randint(stream_key, (), max(1, total - reach), min(reach, total - 1) + 1)
        return jnp.stack([one, total - one])
    sizes = jnp.asarray(length_profile(count, total, reach, lean), jnp.int32)
    twos = (count - 1) // 2
    giver, taker = sizes[1:1 + 2 * twos:2], sizes[2:2 + 2 * twos:2]
    room = jnp.minimum(giver - 1, reach - taker)
    moved = jax.random.randint(jax.random.fold_in(stream_key, 1), (twos,), 0, 1 << 20) % (room + 1)
    sizes = sizes.at[1:1 + 2 * twos:2].set(giver - moved).at[2:2 + 2 * twos:2].set(taker + moved)
    return sizes[jax.random.permutation(jax.random.fold_in(stream_key, 2), count)]


def assign_block(own_key, own, number, rows, amount, top, most, lean):
    order = jax.random.permutation(own_key, amount)
    heavy_load, ordinary = shares(amount, rows * top, most, lean, True), shares(amount, rows * top, most, lean, False)
    places = jnp.arange(amount)

    def named(tallies, turn):
        used = int((tallies > 0).sum())
        fixed = max(1, used // 4)
        moved = fixed + (places - fixed + turn * (used - fixed)) % max(1, amount - fixed)
        return jnp.zeros((amount,), jnp.int32).at[order[jnp.where(places < fixed, places, moved)]].set(jnp.asarray(tallies, jnp.int32))

    tallies = jnp.where(number % 4 == 0, named(heavy_load, number // 4), named(ordinary, number - number // 4 - 1))
    mixed = jax.random.permutation(jax.random.fold_in(own, 3), amount)
    donor, receiver = mixed[0:amount // 2 * 2:2], mixed[1:amount // 2 * 2:2]
    slack = jnp.minimum(tallies[donor] - 1, most - tallies[receiver]) // 2
    slack = jnp.where((donor == order[0]) | (receiver == order[0]) | (tallies[receiver] == 0), 0, jnp.maximum(slack, 0))
    moved = jax.random.randint(jax.random.fold_in(own, 4), (amount // 2,), 0, 1 << 20) % (slack + 1)
    tallies = tallies.at[donor].add(-moved).at[receiver].add(moved)
    items = jnp.searchsorted(jnp.cumsum(tallies), jnp.arange(rows * top), side="right").astype(jnp.int32)
    listing = items.reshape(top, rows).T
    listing = listing[jax.random.permutation(jax.random.fold_in(own, 1), rows)]
    turn = jax.random.randint(jax.random.fold_in(own, 2), (rows, 1), 0, top)
    return jnp.take_along_axis(listing, (jnp.arange(top)[None, :] + turn) % top, axis=1)


def shares(number_of, total, bound, skew, full):
    weights = [(1 << 20) // math.isqrt(standing ** skew) + 1 for standing in range(1, number_of + 1)]
    largest = bound if full else min(bound, max(-(-total // number_of), total * weights[0] // sum(weights)))
    least = 1 if total - largest >= number_of - 1 else 0
    given, rest = [largest] + [least] * (number_of - 1), total - largest - least * (number_of - 1)
    while rest > 0:
        movable = [i for i in range(1, number_of) if given[i] < largest] or [i for i in range(1, number_of) if given[i] < bound]
        whole, remaining = sum([weights[i] for i in movable]), rest
        for i in movable:
            extra = min(bound - given[i], max(1, remaining * weights[i] // whole), rest)
            given[i] = given[i] + extra
            rest = rest - extra
    return np.array(given)


def noise(own_key, dims, width, reach, split=(), kind=jnp.bfloat16):
    loudness = shard_levels(own_key, dims, split, -0.22, 0.18) if split else 1.0
    array = jax.random.normal(own_key, dims, jnp.float32) * width * loudness
    return jnp.minimum(jnp.maximum(array, -reach), reach).astype(kind)


def setup_inputs(seed: int = 0) -> dict:
    streams_of = jax.random.split(jax.random.key(seed), 16)
    tokens = noise(streams_of[0], (TOKENS, D), 1.0, 6.0, ((0, 32),))
    seq_lengths = jax.vmap(lambda own: ragged_sizes(own, DOCS, TOK_DEV, SEQ_MAX, 2))(jax.random.split(streams_of[1], N_DP * N_EXPERT)).reshape((N_DP, N_EXPERT, DOCS)).astype(jnp.int32)
    block_perm = jax.vmap(lambda own: jax.random.permutation(own, N_EXPERT))(jax.random.split(streams_of[2], N_DP)).reshape((N_DP, N_EXPERT)).astype(jnp.int32)
    routes_keys = jax.random.split(jax.random.fold_in(streams_of[3], 1), LAYERS * TOKENS // TOK_DEV)
    routes_turns = jax.random.permutation(jax.random.fold_in(streams_of[3], 3), LAYERS * TOKENS // TOK_DEV)
    routes = jax.vmap(lambda own, number: assign_block(jax.random.fold_in(streams_of[3], 2), own, number, TOK_DEV, NROUTE, 2, CAP, 1))(routes_keys, routes_turns).reshape((LAYERS, TOKENS, 2))
    norm_gains = jnp.clip(1.0 + 0.1 * jax.random.normal(streams_of[4], (LAYERS, 2, D), jnp.float32), 0.5, 1.5)
    w_qkv = noise(streams_of[5], (LAYERS, D, 3 * D), D ** -0.5, 0.21875, ((2, 8),), jnp.float32)
    w_out = noise(streams_of[6], (LAYERS, D, D), (D // 32) ** -0.5, 1.25, ((1, 8),), jnp.float32)
    w_router = noise(streams_of[7], (LAYERS, D, NROUTE), (2 * D) ** -0.5, 0.15625, ((1, 8),), jnp.float32)
    w_residual = noise(streams_of[8], (NROUTE, NROUTE), (2 * NROUTE) ** -0.5, 1.25, (), jnp.float32)
    w_const = noise(streams_of[9], (LAYERS, 2, D, 2), D ** -0.5, 0.21875, ((2, 8),), jnp.float32)
    v_const = noise(streams_of[10], (LAYERS, 2, D), 1.0, 6.0, ((2, 8),), jnp.float32)
    w_gate = noise(streams_of[11], (LAYERS, EXPERTS, D, FF), D ** -0.5, 0.21875, ((1, 4), (3, 8)), jnp.float32)
    w_up = noise(streams_of[12], (LAYERS, EXPERTS, D, FF), D ** -0.5, 0.21875, ((1, 4), (3, 8)), jnp.float32)
    w_down = noise(streams_of[13], (LAYERS, EXPERTS, FF, D), FF ** -0.5, 0.125, ((1, 4), (2, 8)), jnp.float32)
    cotangent = noise(streams_of[14], (TOKENS, D), 1.0, 6.0, ((0, 32),))
    return {"tokens": tokens, "seq_lengths": seq_lengths, "block_perm": block_perm, "routes": routes, "norm_gains": norm_gains, "w_qkv": w_qkv, "w_out": w_out, "w_router": w_router, "w_residual": w_residual, "w_const": w_const, "v_const": v_const, "w_gate": w_gate, "w_up": w_up, "w_down": w_down, "cotangent": cotangent}


EPSILON = 1e-05
MASKED = -1e+30
HIGH = lax.Precision.HIGHEST

@jax.custom_vjp
def low(v):
    return lax.optimization_barrier(v.astype(jnp.bfloat16)).astype(jnp.float32)

@jax.custom_vjp
def low_back(v):
    return v

def low_keep(v):
    return (low(v), None)

def low_pass(kept, grad):
    return (grad,)

def back_keep(v):
    return (v, None)

def back_low(kept, grad):
    return (low(grad),)
low.defvjp(low_keep, low_pass)
low_back.defvjp(back_keep, back_low)

def rms_scale(values):
    return lax.rsqrt(lax.optimization_barrier(jnp.mean(values * values, axis=-1, keepdims=True)) + EPSILON)

def attention_mask(lengths, row_count):
    doc_ends = jnp.cumsum(lengths).astype(jnp.int32)
    places = jnp.arange(row_count, dtype=jnp.int32)
    doc_owner = lax.optimization_barrier(jnp.sum((places[:, None] >= doc_ends[None, :]).astype(jnp.int32), axis=1)).astype(jnp.int32)
    same_doc = doc_owner[:, None] == doc_owner[None, :]
    return jnp.logical_and(same_doc, places[:, None] >= places[None, :])

def slot_plan(route_rows, experts, capacity):
    flat_routes = route_rows.reshape(-1).astype(jnp.int32)
    labels = jnp.arange(experts, dtype=jnp.int32)
    onehot = (flat_routes[:, None] == labels[None, :]).astype(jnp.int32)
    before = (jnp.cumsum(onehot, axis=0) - 1).astype(jnp.int32)
    slot_place = lax.optimization_barrier(jnp.sum(before * onehot, axis=1)).astype(jnp.int32)
    is_valid = flat_routes < experts
    slot_ids = jnp.where(is_valid, flat_routes * capacity + slot_place, experts * capacity).astype(jnp.int32)
    pair_ids = jnp.arange(flat_routes.shape[0], dtype=jnp.int32)
    owner_pair = jnp.zeros((experts * capacity,), jnp.int32).at[slot_ids].set(pair_ids, mode='drop')
    filled = jnp.zeros((experts * capacity,), jnp.float32).at[slot_ids].set(1.0, mode='drop')
    return (slot_ids, is_valid, owner_pair, filled)

def block_forward(params, tokens_block, lengths_block, routes_block):
    gains, w_qkv, w_out, w_router, w_residual, w_const, v_const, w_gate, w_up, w_down = params
    row_count, model_width = tokens_block.shape
    experts = w_gate.shape[1]
    attend_mask = attention_mask(lengths_block, row_count)
    factor = 1.0 / math.sqrt(HEAD_DIM)
    const_ids = experts + 2 + jnp.arange(2, dtype=jnp.int32)
    stream = tokens_block
    prev_logits = None
    for layer_index in range(LAYERS):
        scale_attn = rms_scale(stream)
        attn_in = low(stream * scale_attn * low(gains[layer_index, 0]))
        qkv_rows = low_back(low(jnp.dot(attn_in, low(w_qkv[layer_index]), precision=HIGH)))
        pieces = qkv_rows.reshape(row_count, 3, HEADS, HEAD_DIM)
        query_rows, key_rows, value_rows = (pieces[:, 0], pieces[:, 1], pieces[:, 2])
        scores = low_back(jnp.einsum('qhd,khd->hqk', query_rows, key_rows, precision=HIGH) * factor)
        scores = jnp.where(attend_mask[None], scores, MASKED)
        row_peak = lax.optimization_barrier(jnp.max(scores, axis=-1, keepdims=True))
        exponent = jnp.exp(scores - row_peak)
        softmaxed = exponent / lax.optimization_barrier(jnp.sum(exponent, axis=-1, keepdims=True))
        mixed_heads = jnp.einsum('hqk,khd->qhd', low(softmaxed), value_rows, precision=HIGH)
        attn_out = low_back(low(mixed_heads.reshape(row_count, model_width)))
        branch = low_back(jnp.dot(attn_out, low(w_out[layer_index]), precision=HIGH))
        stream_mid = stream + branch
        scale_ffn = rms_scale(stream_mid)
        hidden_full = stream_mid * scale_ffn * low(gains[layer_index, 1])
        hidden = low(hidden_full)
        logits = jnp.dot(hidden, low(w_router[layer_index]), precision=HIGH)
        if prev_logits is not None:
            logits = logits + jnp.dot(prev_logits, w_residual, precision=HIGH)
        route_rows = routes_block[layer_index]
        chosen = jnp.take_along_axis(logits, route_rows, axis=1)
        gate_share = jax.nn.softmax(chosen, axis=-1)
        slot_ids, is_valid, owner_pair, filled = slot_plan(route_rows, experts, CAP)
        expert_in = low_back(hidden[owner_pair // 2] * filled[:, None]).reshape(experts, CAP, model_width)
        gate_proj = low_back(jnp.einsum('ecd,edf->ecf', expert_in, low(w_gate[layer_index]), precision=HIGH))
        up_proj = low_back(jnp.einsum('ecd,edf->ecf', expert_in, low(w_up[layer_index]), precision=HIGH))
        activated = low(jax.nn.silu(gate_proj) * up_proj)
        expert_out = low_back(low(jnp.einsum('ecf,efd->ecd', activated, low(w_down[layer_index]), precision=HIGH)))
        flat_out = expert_out.reshape(experts * CAP, model_width)
        valid_f = is_valid.astype(jnp.float32)
        pair_out = (flat_out[jnp.minimum(slot_ids, experts * CAP - 1)] * valid_f[:, None]).reshape(row_count, 2, model_width)
        ffn_term = lax.optimization_barrier(jnp.sum(gate_share[:, :, None] * pair_out, axis=1))
        copy_weight = lax.optimization_barrier(jnp.sum(gate_share * (route_rows == experts + 1).astype(jnp.float32), axis=1))
        const_pick = (route_rows[:, :, None] == const_ids[None, None, :]).astype(jnp.float32)
        const_weight = lax.optimization_barrier(jnp.sum(gate_share[:, :, None] * const_pick, axis=1))
        const_logits = jnp.einsum('td,jdc->tjc', hidden, low(w_const[layer_index]), precision=HIGH)
        const_probs = jax.nn.softmax(const_logits, axis=-1)
        const_vec = low(v_const[layer_index])
        local_weight = copy_weight + lax.optimization_barrier(jnp.sum(const_weight * const_probs[:, :, 0], axis=1))
        local_term = local_weight[:, None] * hidden_full + jnp.dot(const_weight * const_probs[:, :, 1], const_vec, precision=HIGH)
        stream = stream_mid + ffn_term + local_term
        prev_logits = logits
    return stream

def reference(tokens, seq_lengths, block_perm, routes, norm_gains, w_qkv, w_out, w_router, w_residual, w_const, v_const, w_gate, w_up, w_down, cotangent):
    params = (norm_gains.astype(jnp.float32), w_qkv.astype(jnp.float32), w_out.astype(jnp.float32), w_router.astype(jnp.float32), w_residual.astype(jnp.float32), w_const.astype(jnp.float32), v_const.astype(jnp.float32), w_gate.astype(jnp.float32), w_up.astype(jnp.float32), w_down.astype(jnp.float32))
    owners = seq_lengths.shape[1]
    blocks = seq_lengths.shape[0] * owners
    lengths_flat = seq_lengths.reshape(blocks, DOCS).astype(jnp.int32)
    block_ids = jnp.arange(blocks, dtype=jnp.int32)
    places = (block_ids // owners * owners + block_perm.reshape(-1)).astype(jnp.int32)
    tokens_blocks = tokens.astype(jnp.float32).reshape(blocks, TOK_DEV, D)
    cot_blocks = cotangent.astype(jnp.float32).reshape(blocks, TOK_DEV, D)
    routes_places = jnp.transpose(routes.reshape(LAYERS, blocks, TOK_DEV, 2), (1, 0, 2, 3))
    routes_blocks = jnp.take(routes_places, places, axis=0)

    def step(carry, inputs):
        tokens_block, lengths_block, routes_block, cot_block = inputs

        def forward(params_in, tokens_in):
            return block_forward(params_in, tokens_in, lengths_block, routes_block)
        result, pullback = jax.vjp(forward, params, tokens_block)
        grad_params, grad_tokens = pullback(cot_block)
        carry = jax.tree.map(jnp.add, carry, grad_params)
        return (carry, (result.astype(jnp.bfloat16), grad_tokens))
    zero_grads = jax.tree.map(jnp.zeros_like, params)
    totals, stacked = lax.scan(step, zero_grads, (tokens_blocks, lengths_flat, routes_blocks, cot_blocks))
    outputs, grads_in = stacked
    return (outputs.reshape(TOKENS, D), grads_in.reshape(TOKENS, D), totals[0], totals[1], totals[2], totals[3], totals[4], totals[5], totals[6], totals[7], totals[8], totals[9])
```

```python
import functools

import jax
import jax.numpy as jnp
from jax import lax
from jax.experimental import pallas as pl
from jax.experimental.pallas import tpu as pltpu
from jax.sharding import PartitionSpec as P

HEADS = 12
CAP = 48
LINE = 4
EPSILON = 1e-05
MASKED = -1e30
HIGH = lax.Precision.HIGHEST
F32 = jnp.float32
BF16 = jnp.bfloat16
MESH = pl.DeviceIdType.MESH
VMEM = pl.BlockSpec(memory_space=pltpu.VMEM)
ANY = pl.BlockSpec(memory_space=pl.ANY)

CONST0, GAIN0, VECTOR0 = 12, 16, 18
STAT = {
    name: i
    for i, name in enumerate(
        ("r0", "r1", "share0", "share1", "slot0", "slot1", "p00", "p01", "p10", "p11")
    )
}


def dot_nn(a, b, **kw):
    return lax.dot_general(a, b, (((1,), (0,)), ((), ())), preferred_element_type=F32, **kw)


def dot_nt(a, b, **kw):
    return lax.dot_general(a, b, (((1,), (1,)), ((), ())), preferred_element_type=F32, **kw)


def dot_tn(a, b, **kw):
    return lax.dot_general(a, b, (((0,), (0,)), ((), ())), preferred_element_type=F32, **kw)


def lanes(rows, width=128):
    return lax.broadcasted_iota(jnp.int32, (rows, width), 1)


def rms_scale(values):
    return lax.rsqrt(jnp.mean(values * values, axis=-1, keepdims=True) + EPSILON)


def row_vectors(small):
    pick = lax.broadcasted_iota(jnp.int32, (8, 128), 0) + GAIN0 == lanes(8)
    rows = dot_nt(pick.astype(BF16), small)
    return rows[0:1], rows[1:2], rows[2:3], rows[3:4]


def stat_columns(stat):
    return {name: stat[:, i : i + 1] for name, i in STAT.items()}


def slot_picks(stat, slots):
    place = lanes(stat["slot0"].shape[0], slots).astype(F32)
    first = (place == stat["slot0"]).astype(BF16)
    second = (place == stat["slot1"]).astype(BF16)
    return first, second


def const_weights(stat, experts):
    out = []
    for kind in (experts + 1, experts + 2, experts + 3):
        out.append(
            stat["share0"] * (stat["r0"] == kind).astype(F32)
            + stat["share1"] * (stat["r1"] == kind).astype(F32)
        )
    return out


def attend_part(stream, small, w_qkv_t, w_out, doc_col, doc_row, attn_in_ref, qkv_ref, probs_ref, attn_ref):
    rows, width = stream.shape
    gain, _, _, _ = row_vectors(small)
    attn_in_ref[...] = (stream * rms_scale(stream) * gain).astype(BF16)

    def project(i, carry):
        at = pl.multiple_of(i * width, width)
        qkv_ref[:, pl.ds(at, width)] = dot_nt(
            attn_in_ref[...], w_qkv_t[pl.ds(at, width), :]
        ).astype(BF16)
        return carry

    lax.fori_loop(0, 3, project, 0)
    head_dim = width // HEADS
    factor = 1.0 / head_dim**0.5
    allowed = jnp.logical_and(
        doc_col[...] == doc_row[...],
        lax.broadcasted_iota(jnp.int32, (rows, rows), 0)
        >= lax.broadcasted_iota(jnp.int32, (rows, rows), 1),
    )

    def heads(i, carry):
        at = pl.multiple_of(i * 2 * head_dim, 2 * head_dim)
        query = qkv_ref[:, pl.ds(at, 2 * head_dim)]
        key = qkv_ref[:, pl.ds(pl.multiple_of(at + width, 128), 2 * head_dim)]
        value = qkv_ref[:, pl.ds(pl.multiple_of(at + 2 * width, 128), 2 * head_dim)]
        second = lanes(rows, 2 * head_dim) >= head_dim
        mixed = []
        for sub in (0, 1):
            mine = second if sub else jnp.logical_not(second)
            scores = dot_nt(jnp.where(mine, query, jnp.zeros_like(query)), key) * factor
            scores = jnp.where(allowed, scores, MASKED)
            exponent = jnp.exp(scores - jnp.max(scores, axis=-1, keepdims=True))
            probs = exponent / jnp.sum(exponent, axis=-1, keepdims=True)
            probs_ref[2 * i + sub] = probs
            mixed.append(dot_nn(probs.astype(BF16), value))
        attn_ref[:, pl.ds(at, 2 * head_dim)] = jnp.where(second, mixed[1], mixed[0]).astype(BF16)
        return carry

    lax.fori_loop(0, HEADS // 2, heads, 0, unroll=2)
    return stream + dot_nn(attn_ref[...], w_out[...])


def route_part(mid, small, routes, prev_logits, w_res, experts):
    rows = mid.shape[0]
    _, gain, _, _ = row_vectors(small)
    hidden = (mid * rms_scale(mid) * gain).astype(BF16)
    lane = lanes(rows)
    raw = dot_nn(hidden, small)
    logits = jnp.where(lane < CONST0, raw, 0.0)
    if prev_logits is not None:
        logits = logits + dot_nn(prev_logits, w_res, precision=HIGH)
    r0, r1 = routes[:, 0:1], routes[:, 1:2]
    hot0, hot1 = (lane == r0).astype(F32), (lane == r1).astype(F32)
    c0 = jnp.sum(hot0 * logits, axis=-1, keepdims=True)
    c1 = jnp.sum(hot1 * logits, axis=-1, keepdims=True)
    peak = jnp.maximum(c0, c1)
    e0, e1 = jnp.exp(c0 - peak), jnp.exp(c1 - peak)
    total = e0 + e1
    share0, share1 = e0 / total, e1 / total
    probs = []
    for j in (0, 1):
        a = raw[:, CONST0 + 2 * j : CONST0 + 2 * j + 1]
        b = raw[:, CONST0 + 2 * j + 1 : CONST0 + 2 * j + 2]
        top = jnp.maximum(a, b)
        ea, eb = jnp.exp(a - top), jnp.exp(b - top)
        probs += [ea / (ea + eb), eb / (ea + eb)]
    earlier = lax.broadcasted_iota(jnp.int32, (rows, rows), 0) > lax.broadcasted_iota(
        jnp.int32, (rows, rows), 1
    )
    before = dot_nn(earlier.astype(BF16), (hot0 + hot1).astype(BF16))
    f0, f1 = r0.astype(F32), r1.astype(F32)
    slot0 = jnp.where(
        r0 < experts, f0 * CAP + jnp.sum(before * hot0, axis=-1, keepdims=True), -1.0
    )
    slot1 = jnp.where(
        r1 < experts, f1 * CAP + jnp.sum(before * hot1, axis=-1, keepdims=True), -1.0
    )
    stat = jnp.zeros((rows, 128), F32)
    for i, column in enumerate([f0, f1, share0, share1, slot0, slot1] + probs):
        stat = jnp.where(lane == i, column, stat)
    first, second = slot_picks({"slot0": slot0, "slot1": slot1}, experts * CAP)
    outgoing = dot_tn(first + second, hidden).astype(BF16)
    return logits, stat, outgoing


def combine_part(mid, small, stat, returned, experts):
    _, gain, vec0, vec1 = row_vectors(small)
    hidden_full = mid * rms_scale(mid) * gain
    first, second = slot_picks(stat, experts * CAP)
    pair0, pair1 = dot_nn(first, returned), dot_nn(second, returned)
    copy, const0, const1 = const_weights(stat, experts)
    local = copy + const0 * stat["p00"] + const1 * stat["p10"]
    moe = stat["share0"] * pair0 + stat["share1"] * pair1 + local * hidden_full
    moe = moe + (const0 * stat["p01"]) * vec0 + (const1 * stat["p11"]) * vec1
    return mid + moe, hidden_full, pair0, pair1


def share_backward(grad, small, stat, hidden_full, pair0, pair1, extra, experts):
    rows = grad.shape[0]
    _, _, vec0, vec1 = row_vectors(small)
    first, second = slot_picks(stat, experts * CAP)
    lane = lanes(rows).astype(F32)
    rowsum = functools.partial(jnp.sum, axis=-1, keepdims=True)
    dot_hidden = rowsum(grad * hidden_full)
    dot_vec = (rowsum(grad * vec0), rowsum(grad * vec1))
    _, const0, const1 = const_weights(stat, experts)
    probs = ((stat["p00"], stat["p01"]), (stat["p10"], stat["p11"]))
    value = [probs[j][0] * dot_hidden + probs[j][1] * dot_vec[j] for j in (0, 1)]
    shares = []
    for r, pair in ((stat["r0"], pair0), (stat["r1"], pair1)):
        shares.append(
            rowsum(grad * pair)
            + (r == experts + 1).astype(F32) * dot_hidden
            + (r == experts + 2).astype(F32) * value[0]
            + (r == experts + 3).astype(F32) * value[1]
        )
    inner = stat["share0"] * shares[0] + stat["share1"] * shares[1]
    g_small = (lane == stat["r0"]).astype(F32) * (stat["share0"] * (shares[0] - inner))
    g_small = g_small + (lane == stat["r1"]).astype(F32) * (stat["share1"] * (shares[1] - inner))
    if extra is not None:
        g_small = g_small + extra
    g_logits = g_small
    for j, weight in ((0, const0), (1, const1)):
        q = (weight * dot_hidden, weight * dot_vec[j])
        mean = probs[j][0] * q[0] + probs[j][1] * q[1]
        for c in (0, 1):
            g_small = jnp.where(lane == CONST0 + 2 * j + c, probs[j][c] * (q[c] - mean), g_small)
    sent0 = (jnp.where(stat["r0"] < experts, stat["share0"], 0.0) * grad).astype(BF16)
    sent1 = (jnp.where(stat["r1"] < experts, stat["share1"], 0.0) * grad).astype(BF16)
    outgoing = (dot_tn(first, sent0) + dot_tn(second, sent1)).astype(BF16)
    hidden = hidden_full.astype(BF16).astype(F32)
    projections = dot_tn(g_small, hidden, precision=HIGH)
    vector0 = jnp.sum((const0 * stat["p01"]) * grad, axis=0, keepdims=True)
    vector1 = jnp.sum((const1 * stat["p11"]) * grad, axis=0, keepdims=True)
    return g_small, g_logits, outgoing, projections, vector0, vector1


def store_small(ref, projections, vector0, vector1):
    ref[0:16, :] = projections[0:16]
    ref[16:24, :] = jnp.zeros((8, ref.shape[1]), F32)
    ref[VECTOR0 : VECTOR0 + 1, :] = vector0
    ref[VECTOR0 + 1 : VECTOR0 + 2, :] = vector1


def first_kernel(experts, tokens, small, w_qkv_t, w_out, doc_col, doc_row, routes,
                 attn_in, qkv, probs, attn, mid_ref, logits_ref, stat_ref, out_ref):
    mid = attend_part(tokens[...].astype(F32), small[...], w_qkv_t, w_out, doc_col, doc_row, attn_in, qkv, probs, attn)
    mid_ref[...] = mid
    logits, stat, out = route_part(mid, small[...], routes[...], None, None, experts)
    logits_ref[...], stat_ref[...], out_ref[...] = logits, stat, out


def middle_kernel(experts, mid_in, small_in, stat_in, returned, small, w_qkv_t, w_out, doc_col, doc_row, routes, logits_in, w_res,
                  stream_ref, attn_in, qkv, probs, attn, mid_ref, stat_ref, out_ref):
    stream, _, _, _ = combine_part(mid_in[...], small_in[...], stat_columns(stat_in[...]), returned[...], experts)
    stream_ref[...] = stream
    mid = attend_part(stream, small[...], w_qkv_t, w_out, doc_col, doc_row, attn_in, qkv, probs, attn)
    mid_ref[...] = mid
    _, stat, out = route_part(mid, small[...], routes[...], logits_in[...], w_res[...], experts)
    stat_ref[...], out_ref[...] = stat, out


def turn_kernel(experts, mid, small, stat_in, returned, cotangent, logits_in, w_res,
                output, g_small_ref, extra_ref, out_ref, small_grad, res_grad):
    stat = stat_columns(stat_in[...])
    stream, hidden_full, pair0, pair1 = combine_part(mid[...], small[...], stat, returned[...], experts)
    output[...] = stream.astype(BF16)
    grad = cotangent[...].astype(F32)
    g_small, g_logits, out, projections, v0, v1 = share_backward(grad, small[...], stat, hidden_full, pair0, pair1, None, experts)
    g_small_ref[...] = g_small
    out_ref[...] = out
    store_small(small_grad, projections, v0, v1)
    res_grad[...] = dot_tn(logits_in[...], g_logits, precision=HIGH)
    extra_ref[...] = dot_nt(g_logits, w_res[...], precision=HIGH)


def layer_backward(experts, grad, back, g_small, stat, mid, small, stream, w_qkv_t, w_out, attn_in, qkv, probs, attn,
                   qkv_grad, out_grad, small_grad, g_qkv, g_attn):
    rows, width = mid.shape
    gain1, gain2, _, _ = row_vectors(small)
    first, second = slot_picks(stat, experts * CAP)
    copy, const0, const1 = const_weights(stat, experts)
    local = copy + const0 * stat["p00"] + const1 * stat["p10"]
    g_full = dot_nt(g_small, small.astype(F32), precision=HIGH) + dot_nn(first + second, back)
    g_full = g_full + grad * local
    s2 = rms_scale(mid)
    small_grad[GAIN0 + 1 : GAIN0 + 2, :] = jnp.sum(g_full * mid * s2, axis=0, keepdims=True)
    m = g_full * gain2
    g_mid = grad + s2 * m - mid * (s2 * s2 * s2 * jnp.mean(m * mid, axis=-1, keepdims=True))
    branch = g_mid.astype(BF16)
    out_grad[...] = dot_tn(attn[...], branch).astype(out_grad.dtype)
    g_attn[...] = dot_nt(branch, w_out[...]).astype(BF16)
    head_dim = width // HEADS
    factor = 1.0 / head_dim**0.5

    def heads(i, carry):
        at = pl.multiple_of(i * 2 * head_dim, 2 * head_dim)
        at_k = pl.multiple_of(at + width, 128)
        at_v = pl.multiple_of(at + 2 * width, 128)
        query = qkv[:, pl.ds(at, 2 * head_dim)]
        key = qkv[:, pl.ds(at_k, 2 * head_dim)]
        value = qkv[:, pl.ds(at_v, 2 * head_dim)]
        ga = g_attn[:, pl.ds(at, 2 * head_dim)]
        second_half = lanes(rows, 2 * head_dim) >= head_dim
        gq, gk, gv = [], [], []
        for sub in (0, 1):
            mine = second_half if sub else jnp.logical_not(second_half)
            p = probs[2 * i + sub]
            gp = dot_nt(jnp.where(mine, ga, jnp.zeros_like(ga)), value)
            gs = (p * (gp - jnp.sum(p * gp, axis=-1, keepdims=True))).astype(BF16)
            gq.append(dot_nn(gs, key))
            gk.append(dot_tn(gs, query))
            gv.append(dot_tn(p.astype(BF16), ga))
        g_qkv[:, pl.ds(at, 2 * head_dim)] = (jnp.where(second_half, gq[1], gq[0]) * factor).astype(BF16)
        g_qkv[:, pl.ds(at_k, 2 * head_dim)] = (jnp.where(second_half, gk[1], gk[0]) * factor).astype(BF16)
        g_qkv[:, pl.ds(at_v, 2 * head_dim)] = jnp.where(second_half, gv[1], gv[0]).astype(BF16)
        return carry

    lax.fori_loop(0, HEADS // 2, heads, 0, unroll=2)

    def weights(i, carry):
        at = pl.multiple_of(i * width, width)
        qkv_grad[pl.ds(at, width), :] = dot_tn(g_qkv[:, pl.ds(at, width)], attn_in[...]).astype(qkv_grad.dtype)
        return carry + dot_nn(g_qkv[:, pl.ds(at, width)], w_qkv_t[pl.ds(at, width), :])

    g_in = lax.fori_loop(0, 3, weights, jnp.zeros((rows, width), F32))
    s1 = rms_scale(stream)
    small_grad[GAIN0 : GAIN0 + 1, :] = jnp.sum(g_in * stream * s1, axis=0, keepdims=True)
    n = g_in * gain1
    return g_mid + s1 * n - stream * (s1 * s1 * s1 * jnp.mean(n * stream, axis=-1, keepdims=True))


def between_kernel(experts, cotangent, back, g_small, stat_in, mid, small, stream, w_qkv_t, w_out, attn_in, qkv, probs, attn, small_grad_in,
                   mid0, small0, stat0_in, returned0, extra,
                   qkv_grad, out_grad, small_grad, grad_ref, g_small0_ref, out_ref, small_grad0, g_qkv, g_attn):
    small_grad[...] = small_grad_in[...]
    grad = layer_backward(experts, cotangent[...].astype(F32), back[...], g_small[...], stat_columns(stat_in[...]), mid[...],
                          small[...], stream[...], w_qkv_t, w_out, attn_in, qkv, probs, attn, qkv_grad, out_grad, small_grad, g_qkv, g_attn)
    grad_ref[...] = grad
    stat0 = stat_columns(stat0_in[...])
    _, hidden_full, pair0, pair1 = combine_part(mid0[...], small0[...], stat0, returned0[...], experts)
    g_small0, _, out, projections, v0, v1 = share_backward(grad, small0[...], stat0, hidden_full, pair0, pair1, extra[...], experts)
    g_small0_ref[...] = g_small0
    out_ref[...] = out
    store_small(small_grad0, projections, v0, v1)


def last_kernel(experts, grad_in, back, g_small, stat_in, mid, small, tokens, w_qkv_t, w_out, attn_in, qkv, probs, attn, small_grad_in,
                qkv_grad, out_grad, small_grad, grad_ref, g_qkv, g_attn):
    small_grad[...] = small_grad_in[...]
    grad_ref[...] = layer_backward(experts, grad_in[...], back[...], g_small[...], stat_columns(stat_in[...]), mid[...], small[...],
                                   tokens[...].astype(F32), w_qkv_t, w_out, attn_in, qkv, probs, attn, qkv_grad, out_grad, small_grad,
                                   g_qkv, g_attn)


def local_call(kernel, experts, args, outs, scratch=()):
    return pl.pallas_call(
        functools.partial(kernel, experts),
        out_shape=[jax.ShapeDtypeStruct(shape, dtype) for shape, dtype in outs],
        in_specs=[VMEM] * len(args),
        out_specs=[VMEM] * len(outs),
        scratch_shapes=[pltpu.VMEM(shape, dtype) for shape, dtype in scratch],
        compiler_params=pltpu.CompilerParams(vmem_limit_bytes=60 * 2**20),
    )(*args)


def mate(place, step, owners):
    if owners != 4 or step == 0:
        return lax.rem(place + step, owners)
    if step == 1:
        return place + 1 - 2 * lax.rem(place, 2)
    return lax.rem(place + 2, 4) if step == 2 else 3 - place


class Line:
    def __init__(self, spread, owners, x, part, stage, arrived, final, returned, sems):
        self.owners, self.spread = owners, spread
        self.d, self.e = lax.axis_index("dp"), lax.axis_index("expert")
        self.t = self.d // spread
        self.x, self.part, self.stage, self.arrived = x, part, stage, arrived
        self.final, self.returned = final, returned
        (self.out_send, self.x_recv, self.x_send, self.sum_send, self.sum_recv, self.ret_send, self.ret_recv) = sems
        self.above, self.below = self.t < LINE - 1, self.t > 0

    def greet(self):
        barrier = pltpu.get_barrier_semaphore()
        for i in range(1, self.owners):
            pl.semaphore_signal(barrier, inc=1, device_id=(self.d, mate(self.e, i, self.owners)), device_id_type=MESH)

        @pl.when(self.above)
        def _():
            pl.semaphore_signal(barrier, inc=1, device_id=(self.d + self.spread, self.e), device_id_type=MESH)

        @pl.when(self.below)
        def _():
            pl.semaphore_signal(barrier, inc=1, device_id=(self.d - self.spread, self.e), device_id_type=MESH)

        ends = self.above.astype(jnp.int32) + self.below.astype(jnp.int32)
        pl.semaphore_wait(barrier, self.owners - 1 + ends)

    def slot_copy(self, out, i):
        to = mate(self.e, i, self.owners)
        return pltpu.make_async_remote_copy(
            src_ref=out.at[to], dst_ref=self.x.at[:, self.t, self.e], send_sem=self.out_send.at[i],
            recv_sem=self.x_recv.at[self.t, self.e], device_id=(self.d, to), device_id_type=MESH)

    def x_copy(self, up, s, b):
        to = self.d + self.spread if up else self.d - self.spread
        return pltpu.make_async_remote_copy(
            src_ref=self.x.at[:, s, b], dst_ref=self.x.at[:, s, b], send_sem=self.x_send.at[up, s, b],
            recv_sem=self.x_recv.at[s, b], device_id=(to, self.e), device_id_type=MESH)

    def sum_copy(self, up, s, b):
        to = self.d + self.spread if up else self.d - self.spread
        return pltpu.make_async_remote_copy(
            src_ref=self.stage.at[s, :, b], dst_ref=self.arrived.at[up, s, :, b], send_sem=self.sum_send.at[s, b],
            recv_sem=self.sum_recv.at[up, s, b], device_id=(to, self.e), device_id_type=MESH)

    def ret_copy(self, i):
        to = mate(self.e, i, self.owners)
        return pltpu.make_async_remote_copy(
            src_ref=self.final.at[to], dst_ref=self.returned.at[self.e], send_sem=self.ret_send.at[i],
            recv_sem=self.ret_recv.at[self.e], device_id=(self.d, to), device_id_type=MESH)

    def run(self, out, compute, meanwhile, keep):
        t, e, owners = self.t, self.e, self.owners
        self.greet()
        for i in list(range(2, owners)) + [1]:
            self.slot_copy(out, i).start()
        self.x[:, t, e] = out[e]
        for i in range(owners):
            b = mate(e, i, owners)
            if i:
                self.x_copy(0, t, b).wait_recv()
            for up, there in ((0, self.below), (1, self.above)):

                @pl.when(there)
                def _(up=up, b=b):
                    self.x_copy(up, t, b).start()

        keep(t)
        compute(t)

        def step(k, carry):
            for i in range(owners):
                b = mate(e, i, owners)

                @pl.when(t + k < LINE)
                def _(b=b):
                    self.x_copy(0, t + k, b).wait_recv()

                    @pl.when(self.below)
                    def _():
                        self.x_copy(0, t + k, b).start()

                @pl.when(t - k >= 0)
                def _(b=b):
                    self.x_copy(1, t - k, b).wait_recv()

                    @pl.when(self.above)
                    def _():
                        self.x_copy(1, t - k, b).start()

            def side(up, carry):
                s = t + k - 2 * k * up

                @pl.when(jnp.logical_and(s >= 0, s < LINE))
                def _():
                    keep(s)
                    compute(s)

                return carry

            lax.fori_loop(0, 2, side, 0)
            for up, first, s in ((1, t == 0, k), (0, t == LINE - 1, LINE - 1 - k)):

                @pl.when(first)
                def _(up=up, s=s):
                    for i in (list(range(2, owners)) + [0, 1])[:owners]:
                        b = mate(e, i, owners)
                        self.stage[s, :, b] = self.part[s, :, b].astype(BF16)
                        self.sum_copy(up, s, b).start()

            return carry

        lax.fori_loop(1, LINE, step, 0)
        meanwhile()

        def relay(k, carry):
            for i in (list(range(2, owners)) + [0, 1])[:owners]:
                b = mate(e, i, owners)
                for up, s, inside in (
                    (1, k, jnp.logical_and(t > 0, t < k)),
                    (0, LINE - 1 - k, jnp.logical_and(t > LINE - 1 - k, t < LINE - 1)),
                ):

                    @pl.when(inside)
                    def _(up=up, s=s, b=b):
                        self.sum_copy(up, s, b).wait_recv()
                        total = self.part[s, :, b] + self.arrived[up, s, :, b].astype(F32)
                        self.stage[s, :, b] = total.astype(BF16)
                        self.sum_copy(up, s, b).start()

            return carry

        lax.fori_loop(2, LINE, relay, 0)
        for i in (list(range(2, owners)) + [0, 1])[:owners]:
            b = mate(e, i, owners)
            for up, there in ((1, self.below), (0, self.above)):

                @pl.when(there)
                def _(up=up, b=b):
                    self.sum_copy(up, t, b).wait_recv()
                    self.part[t, :, b] = self.part[t, :, b] + self.arrived[up, t, :, b].astype(F32)

            if i:
                self.final[b] = self.part[t, :, b].astype(BF16)
                self.ret_copy(i).start()
            else:
                self.returned[e] = self.part[t, :, e].astype(BF16)

        def sent(s, carry):
            for i in range(owners):
                for up, mine in ((0, jnp.logical_and(self.below, s >= t)), (1, jnp.logical_and(self.above, s <= t))):

                    @pl.when(mine)
                    def _(up=up, i=i):
                        self.x_copy(up, s, i).wait_send()

                @pl.when(s != t)
                def _(i=i):
                    self.sum_copy(0, s, i).wait_send()

            return carry

        for i in range(1, owners):
            self.slot_copy(out, i).wait_send()
        lax.fori_loop(0, LINE, sent, 0)
        for i in range(1, owners):
            self.ret_copy(i).wait_send()
            pltpu.make_async_remote_copy(
                src_ref=self.final.at[e], dst_ref=self.returned.at[mate(e, i, owners)], send_sem=self.ret_send.at[i],
                recv_sem=self.ret_recv.at[mate(e, i, owners)], device_id=(self.d, mate(e, i, owners)), device_id_type=MESH).wait_recv()


def line_scratch(local, owners, width):
    shape = (local, owners, CAP, width)
    dma = pltpu.SemaphoreType.DMA
    return [
        pltpu.VMEM((local, LINE, owners, CAP, width), BF16),
        pltpu.VMEM((LINE,) + shape, F32),
        pltpu.VMEM((LINE,) + shape, BF16),
        pltpu.VMEM((2, LINE) + shape, BF16),
        pltpu.VMEM((owners, local, CAP, width), BF16),
        dma((owners,)), dma((LINE, owners)), dma((2, LINE, owners)), dma((LINE, owners)), dma((2, LINE, owners)),
        dma((owners,)), dma((owners,)),
    ]


def expert_forward_kernel(spread, parts, out, *refs):
    gate, up, down = refs[:parts], refs[parts : 2 * parts], refs[2 * parts : 3 * parts]
    returned, x_keep, g_keep, u_keep, x, part, stage, arrived, final = refs[3 * parts : 3 * parts + 9]
    sems, (g_all, u_all, keep_sem) = refs[3 * parts + 9 : 3 * parts + 16], refs[3 * parts + 16 :]
    local, _, owners, _, width = x.shape
    rows = owners * CAP
    line = Line(spread, owners, x, part, stage, arrived, final, returned, sems)

    def kept(s):
        yield pltpu.make_async_copy(x.at[:, s], x_keep.at[:, s], keep_sem.at[0, s])
        yield pltpu.make_async_copy(g_all.at[s], g_keep.at[s], keep_sem.at[1, s])
        yield pltpu.make_async_copy(u_all.at[s], u_keep.at[s], keep_sem.at[2, s])

    def compute(s):
        def one(l, carry):
            rows_in = x[l, s].reshape(rows, width)
            total = jnp.zeros((rows, width), F32)
            for p in range(parts):
                cols = gate[p].shape[2]
                g = dot_nn(rows_in, gate[p][l])
                u = dot_nn(rows_in, up[p][l])
                g_all[s, l, :, p * cols : (p + 1) * cols] = g
                u_all[s, l, :, p * cols : (p + 1) * cols] = u
                act = (g * jax.nn.sigmoid(g) * u).astype(BF16)
                total = total + dot_nn(act, down[p][l])
            part[s, l] = total.reshape(owners, CAP, width)
            return carry

        lax.fori_loop(0, local, one, 0)
        for copy in list(kept(s))[1:]:
            copy.start()

    line.run(out, compute, lambda: None, lambda s: next(kept(s)).start())
    for s in range(LINE):
        for copy in kept(s):
            copy.wait()


def expert_backward_kernel(spread, parts, out, x_in, g_all, u_all, *refs):
    gate, up, down = refs[:parts], refs[parts : 2 * parts], refs[2 * parts : 3 * parts]
    returned = refs[3 * parts]
    grads = refs[3 * parts + 1 : 6 * parts + 1]
    x, part, stage, arrived, final = refs[6 * parts + 1 : 6 * parts + 6]
    sems, (act_all, gg_all, gu_all) = refs[6 * parts + 6 : 6 * parts + 13], refs[6 * parts + 13 :]
    local, _, owners, _, width = x.shape
    rows = owners * CAP
    line = Line(spread, owners, x, part, stage, arrived, final, returned, sems)

    def compute(s):
        at = pl.multiple_of(s * rows, rows)

        def one(l, carry):
            rows_in = x[l, s].reshape(rows, width)
            total = jnp.zeros((rows, width), F32)
            for p in range(parts):
                cols = gate[p].shape[2]
                here = slice(p * cols, (p + 1) * cols)
                g, u = g_all[s, l, :, here], u_all[s, l, :, here]
                g_act = dot_nt(rows_in, down[p][l])
                sigma = jax.nn.sigmoid(g)
                swish = g * sigma
                gg = (g_act * u * sigma * (1.0 + g * (1.0 - sigma))).astype(BF16)
                gu = (g_act * swish).astype(BF16)
                act_all[l, pl.ds(at, rows), here] = (swish * u).astype(BF16)
                gg_all[l, pl.ds(at, rows), here] = gg
                gu_all[l, pl.ds(at, rows), here] = gu
                total = total + dot_nt(gg, gate[p][l]) + dot_nt(gu, up[p][l])
            part[s, l] = total.reshape(owners, CAP, width)
            return carry

        lax.fori_loop(0, local, one, 0)

    def weights():
        def one(l, carry):
            x_rows = x_in[l].reshape(LINE * rows, width)
            g_rows = x[l].reshape(LINE * rows, width)
            for p in range(parts):
                cols = gate[p].shape[2]
                here = slice(p * cols, (p + 1) * cols)
                for grad, value in (
                    (grads[p], dot_tn(x_rows, gg_all[l, :, here])),
                    (grads[parts + p], dot_tn(x_rows, gu_all[l, :, here])),
                    (grads[2 * parts + p], dot_tn(act_all[l, :, here], g_rows)),
                ):
                    grad[l] = value.astype(grad.dtype)
            return carry

        lax.fori_loop(0, local, one, 0)

    line.run(out, compute, weights, lambda s: None)


def expert_forward(spread, call_id, out, weights):
    parts = len(weights) // 3
    owners, local, cap, width = out.shape
    columns = sum(w.shape[2] for w in weights[:parts])
    kept = (LINE, local, owners * cap, columns)
    return pl.pallas_call(
        functools.partial(expert_forward_kernel, spread, parts),
        out_shape=[
            jax.ShapeDtypeStruct(out.shape, BF16),
            jax.ShapeDtypeStruct((local, LINE, owners, cap, width), BF16),
            jax.ShapeDtypeStruct(kept, F32),
            jax.ShapeDtypeStruct(kept, F32),
        ],
        in_specs=[VMEM] * (1 + len(weights)),
        out_specs=[VMEM, ANY, ANY, ANY],
        scratch_shapes=line_scratch(local, owners, width)
        + [pltpu.VMEM(kept, F32), pltpu.VMEM(kept, F32), pltpu.SemaphoreType.DMA((3, LINE))],
        compiler_params=pltpu.CompilerParams(
            collective_id=call_id, has_side_effects=True, vmem_limit_bytes=60 * 2**20
        ),
    )(out, *weights)


def expert_backward(spread, call_id, out, kept, weights):
    parts = len(weights) // 3
    owners, local, cap, width = out.shape
    columns = sum(w.shape[2] for w in weights[:parts])
    shapes = [
        jax.ShapeDtypeStruct(w.shape, F32 if i % parts == 0 else BF16) for i, w in enumerate(weights)
    ]
    wide = pltpu.VMEM((local, LINE * owners * cap, columns), BF16)
    return pl.pallas_call(
        functools.partial(expert_backward_kernel, spread, parts),
        out_shape=[jax.ShapeDtypeStruct(out.shape, BF16)] + shapes,
        in_specs=[VMEM] * (4 + len(weights)),
        out_specs=[VMEM] * (1 + len(weights)),
        scratch_shapes=line_scratch(local, owners, width) + [wide] * 3,
        compiler_params=pltpu.CompilerParams(
            collective_id=call_id, has_side_effects=True, vmem_limit_bytes=60 * 2**20
        ),
    )(out, *kept, *weights)


def from_partner(array, shift, spread, groups):
    pairs = [
        (t * spread + (f + shift) % spread, t * spread + f) for t in range(groups) for f in range(spread)
    ]
    return lax.ppermute(array, "dp", pairs)


def to_partner(array, shift, spread, groups):
    pairs = [
        (t * spread + f, t * spread + (f + shift) % spread) for t in range(groups) for f in range(spread)
    ]
    return lax.ppermute(array, "dp", pairs)


def pair_weights(shard, axis, spread):
    shard = shard.astype(BF16)
    parts = [shard] + [from_partner(shard, i, spread, LINE) for i in range(1, spread)]
    if shard.shape[axis] % 128:
        return [jnp.concatenate(parts, axis=axis)]
    return parts


def pair_sum(parts, axis, spread):
    if len(parts) == 1 and spread > 1:
        parts = jnp.split(parts[0], spread, axis=axis)
    total = parts[0]
    for i in range(1, spread):
        total = total + to_partner(parts[i].astype(BF16), i, spread, LINE).astype(F32)
    return total


def per_device(
    tokens, seq_lengths, block_perm, routes, norm_gains, w_qkv, w_out, w_router, w_residual, w_const, v_const,
    w_gate, w_up, w_down, cotangent,
):
    rows, width = tokens.shape
    owners = lax.axis_size("expert")
    shards = lax.axis_size("dp")
    spread = shards // LINE
    local = w_gate.shape[1]
    experts = local * owners
    layers = routes.shape[0]
    slots = experts * CAP
    place = lax.axis_index("expert")

    my_place = jnp.sum(jnp.where(jnp.arange(owners) == place, block_perm[0], 0))
    all_routes = lax.all_gather(routes, "expert", axis=0)
    my_routes = lax.dynamic_index_in_dim(all_routes, my_place, 0, keepdims=False)
    lengths = lax.dynamic_index_in_dim(seq_lengths[0], place, 0, keepdims=False)
    order = jnp.arange(lengths.shape[0])
    ends = jnp.sum(jnp.where(order[:, None] <= order[None, :], lengths[:, None], 0), axis=0)
    doc = jnp.sum((jnp.arange(rows)[:, None] >= ends[None, :]).astype(jnp.int32), axis=1)
    doc_col, doc_row = doc[:, None], doc[None, :]

    weights = []
    for l in range(layers):
        weights.append(
            pair_weights(w_gate[l], 2, spread) + pair_weights(w_up[l], 2, spread) + pair_weights(w_down[l], 1, spread)
        )

    depth = w_out.shape[1]
    small = jnp.concatenate(
        [
            w_router, w_const[:, 0], w_const[:, 1], jnp.swapaxes(norm_gains, 1, 2), jnp.swapaxes(v_const, 1, 2),
            jnp.zeros((layers, depth, 108), F32),
        ],
        axis=2,
    ).astype(BF16)
    qkv_t = jnp.swapaxes(w_qkv, 1, 2).astype(BF16)
    qkv_all = lax.all_gather(qkv_t, "dp", axis=1, tiled=True)
    out_all = lax.all_gather(w_out.astype(BF16), "dp", axis=1, tiled=True)
    small_all = lax.all_gather(small, "dp", axis=1, tiled=True)
    dense = [(small_all[l], qkv_all[l], out_all[l]) for l in range(layers)]
    w_res = jnp.zeros((128, 128), F32).at[: w_residual.shape[0], : w_residual.shape[1]].set(w_residual)

    cols = ((rows, width), F32)
    attention = [((rows, width), BF16), ((rows, 3 * width), BF16), ((HEADS, rows, rows), F32), ((rows, width), BF16)]
    per_token, sent = ((rows, 128), F32), ((slots, width), BF16)

    def group(array):
        return array.reshape(owners, local, CAP, width)

    attn_in0, qkv0, probs0, attn0, mid0, logits0, stat0, out = local_call(
        first_kernel, experts, (tokens, *dense[0], doc_col, doc_row, my_routes[0]),
        attention + [cols, per_token, per_token, sent])
    ret0, *kept0 = expert_forward(spread, 0, group(out), weights[0])
    ret0 = ret0.reshape(slots, width)
    stream1, attn_in1, qkv1, probs1, attn1, mid1, stat1, out = local_call(
        middle_kernel, experts,
        (mid0, dense[0][0], stat0, ret0, *dense[1], doc_col, doc_row, my_routes[1], logits0, w_res),
        [cols] + attention + [cols, per_token, sent])
    ret1, *kept1 = expert_forward(spread, 1, group(out), weights[1])
    ret1 = ret1.reshape(slots, width)

    small_grads = ((24, width), F32)
    output, g_small1, extra, out, small_grad1, res_grad = local_call(
        turn_kernel, experts, (mid1, dense[1][0], stat1, ret1, cotangent, logits0, w_res),
        [((rows, width), BF16), per_token, per_token, sent, small_grads, ((128, 128), F32)])
    back, *expert_grads1 = expert_backward(spread, 2, group(out), kept1, weights[1])
    dense_grads = [((3 * width, width), F32), ((width, width), F32), small_grads]
    attention_scratch = [((rows, 3 * width), BF16), ((rows, width), BF16)]
    qkv_grad1, out_grad1, small_grad1, grad, g_small0, out, small_grad0 = local_call(
        between_kernel, experts,
        (cotangent, back.reshape(slots, width), g_small1, stat1, mid1, dense[1][0], stream1, dense[1][1], dense[1][2],
         attn_in1, qkv1, probs1, attn1, small_grad1, mid0, dense[0][0], stat0, ret0, extra),
        dense_grads + [cols, per_token, sent, small_grads], attention_scratch)
    back, *expert_grads0 = expert_backward(spread, 3, group(out), kept0, weights[0])
    qkv_grad0, out_grad0, small_grad0, tokens_grad = local_call(
        last_kernel, experts,
        (grad, back.reshape(slots, width), g_small0, stat0, mid0, dense[0][0], tokens, dense[0][1], dense[0][2],
         attn_in0, qkv0, probs0, attn0, small_grad0),
        dense_grads + [cols], attention_scratch)

    expert_out = []
    for axis, at in ((2, 0), (2, 1), (1, 2)):
        per_layer = []
        for grads in (expert_grads0, expert_grads1):
            n = len(grads) // 3
            per_layer.append(pair_sum(grads[at * n : (at + 1) * n], axis, spread))
        expert_out.append(jnp.stack(per_layer))
    gate_grad, up_grad, down_grad = expert_out
    qkv_grad = lax.psum(
        lax.psum_scatter(jnp.stack([qkv_grad0, qkv_grad1]), "dp", scatter_dimension=1, tiled=True), "expert")
    out_grad = lax.psum(
        lax.psum_scatter(jnp.stack([out_grad0, out_grad1]), "dp", scatter_dimension=1, tiled=True), "expert")
    packed = jnp.concatenate([small_grad0, small_grad1, jnp.pad(res_grad[:16], ((0, 0), (0, width - 128)))])
    packed = lax.psum(packed, ("dp", "expert"))
    mine = lax.dynamic_slice_in_dim(packed, lax.axis_index("dp") * depth, depth, axis=1)
    mine = jnp.stack([mine[:24], mine[24:48]])
    router_grad = jnp.swapaxes(mine[:, :CONST0], 1, 2)
    const_grad = jnp.swapaxes(mine[:, CONST0:GAIN0].reshape(layers, 2, 2, depth), 2, 3)
    residual_grad = packed[48 : 48 + CONST0, :CONST0]
    return (
        output, tokens_grad, mine[:, GAIN0 : GAIN0 + 2], jnp.swapaxes(qkv_grad, 1, 2), out_grad, router_grad,
        residual_grad, const_grad, mine[:, VECTOR0 : VECTOR0 + 2], gate_grad, up_grad, down_grad,
    )


def solution(mesh):
    in_specs = (
        P(("dp", "expert"), None), P("dp", None, None), P("dp", None), P(None, ("dp", "expert"), None),
        P(None, None, "dp"), P(None, None, "dp"), P(None, "dp", None), P(None, "dp", None), P(),
        P(None, None, "dp", None), P(None, None, "dp"), P(None, "expert", None, "dp"), P(None, "expert", None, "dp"),
        P(None, "expert", "dp", None), P(("dp", "expert"), None),
    )
    out_specs = (
        P(("dp", "expert"), None), P(("dp", "expert"), None), P(None, None, "dp"), P(None, None, "dp"),
        P(None, "dp", None), P(None, "dp", None), P(), P(None, None, "dp", None), P(None, None, "dp"),
        P(None, "expert", None, "dp"), P(None, "expert", None, "dp"), P(None, "expert", "dp", None),
    )
    return jax.shard_map(per_device, mesh=mesh, in_specs=in_specs, out_specs=out_specs, check_vma=False)
```

```python
import functools

import jax
import jax.numpy as jnp
from jax import lax
from jax.experimental import pallas as pl
from jax.experimental.pallas import tpu as pltpu
from jax.sharding import PartitionSpec as P

HEADS = 12
CAP = 48
LINE = 4
EPSILON = 1e-05
MASKED = -1e30
HIGH = lax.Precision.HIGHEST
F32 = jnp.float32
BF16 = jnp.bfloat16
MESH = pl.DeviceIdType.MESH
VMEM = pl.BlockSpec(memory_space=pltpu.VMEM)
ANY = pl.BlockSpec(memory_space=pl.ANY)

CONST0, GAIN0, VECTOR0 = 12, 16, 18
STAT = {
    name: i
    for i, name in enumerate(
        ("r0", "r1", "share0", "share1", "slot0", "slot1", "p00", "p01", "p10", "p11")
    )
}


def dot_nn(a, b, **kw):
    return lax.dot_general(a, b, (((1,), (0,)), ((), ())), preferred_element_type=F32, **kw)


def dot_nt(a, b, **kw):
    return lax.dot_general(a, b, (((1,), (1,)), ((), ())), preferred_element_type=F32, **kw)


def dot_tn(a, b, **kw):
    return lax.dot_general(a, b, (((0,), (0,)), ((), ())), preferred_element_type=F32, **kw)


def lanes(rows, width=128):
    return lax.broadcasted_iota(jnp.int32, (rows, width), 1)


def rms_scale(values):
    return lax.rsqrt(jnp.mean(values * values, axis=-1, keepdims=True) + EPSILON)


def row_vectors(small):
    pick = lax.broadcasted_iota(jnp.int32, (8, 128), 0) + GAIN0 == lanes(8)
    rows = dot_nt(pick.astype(BF16), small)
    return rows[0:1], rows[1:2], rows[2:3], rows[3:4]


def stat_columns(stat):
    return {name: stat[:, i : i + 1] for name, i in STAT.items()}


def slot_picks(stat, slots):
    place = lanes(stat["slot0"].shape[0], slots).astype(F32)
    first = (place == stat["slot0"]).astype(BF16)
    second = (place == stat["slot1"]).astype(BF16)
    return first, second


def const_weights(stat, experts):
    out = []
    for kind in (experts + 1, experts + 2, experts + 3):
        out.append(
            stat["share0"] * (stat["r0"] == kind).astype(F32)
            + stat["share1"] * (stat["r1"] == kind).astype(F32)
        )
    return out


def attend_part(stream, small, w_qkv_t, w_out, doc_col, doc_row, attn_in_ref, qkv_ref, probs_ref, attn_ref):
    rows, width = stream.shape
    gain, _, _, _ = row_vectors(small)
    attn_in_ref[...] = (stream * rms_scale(stream) * gain).astype(BF16)

    def project(i, carry):
        at = pl.multiple_of(i * width, width)
        qkv_ref[:, pl.ds(at, width)] = dot_nt(
            attn_in_ref[...], w_qkv_t[pl.ds(at, width), :]
        ).astype(BF16)
        return carry

    lax.fori_loop(0, 3, project, 0)
    head_dim = width // HEADS
    factor = 1.0 / head_dim**0.5
    allowed = jnp.logical_and(
        doc_col[...] == doc_row[...],
        lax.broadcasted_iota(jnp.int32, (rows, rows), 0)
        >= lax.broadcasted_iota(jnp.int32, (rows, rows), 1),
    )

    def heads(i, carry):
        at = pl.multiple_of(i * 2 * head_dim, 2 * head_dim)
        query = qkv_ref[:, pl.ds(at, 2 * head_dim)]
        key = qkv_ref[:, pl.ds(pl.multiple_of(at + width, 128), 2 * head_dim)]
        value = qkv_ref[:, pl.ds(pl.multiple_of(at + 2 * width, 128), 2 * head_dim)]
        second = lanes(rows, 2 * head_dim) >= head_dim
        mixed = []
        for sub in (0, 1):
            mine = second if sub else jnp.logical_not(second)
            scores = dot_nt(jnp.where(mine, query, jnp.zeros_like(query)), key) * factor
            scores = jnp.where(allowed, scores, MASKED)
            exponent = jnp.exp(scores - jnp.max(scores, axis=-1, keepdims=True))
            probs = exponent / jnp.sum(exponent, axis=-1, keepdims=True)
            probs_ref[2 * i + sub] = probs
            mixed.append(dot_nn(probs.astype(BF16), value))
        attn_ref[:, pl.ds(at, 2 * head_dim)] = jnp.where(second, mixed[1], mixed[0]).astype(BF16)
        return carry

    lax.fori_loop(0, HEADS // 2, heads, 0, unroll=2)
    return stream + dot_nn(attn_ref[...], w_out[...])


def route_part(mid, small, routes, prev_logits, w_res, experts):
    rows = mid.shape[0]
    _, gain, _, _ = row_vectors(small)
    hidden = (mid * rms_scale(mid) * gain).astype(BF16)
    lane = lanes(rows)
    raw = dot_nn(hidden, small)
    logits = jnp.where(lane < CONST0, raw, 0.0)
    if prev_logits is not None:
        logits = logits + dot_nn(prev_logits, w_res, precision=HIGH)
    r0, r1 = routes[:, 0:1], routes[:, 1:2]
    hot0, hot1 = (lane == r0).astype(F32), (lane == r1).astype(F32)
    c0 = jnp.sum(hot0 * logits, axis=-1, keepdims=True)
    c1 = jnp.sum(hot1 * logits, axis=-1, keepdims=True)
    peak = jnp.maximum(c0, c1)
    e0, e1 = jnp.exp(c0 - peak), jnp.exp(c1 - peak)
    total = e0 + e1
    share0, share1 = e0 / total, e1 / total
    probs = []
    for j in (0, 1):
        a = raw[:, CONST0 + 2 * j : CONST0 + 2 * j + 1]
        b = raw[:, CONST0 + 2 * j + 1 : CONST0 + 2 * j + 2]
        top = jnp.maximum(a, b)
        ea, eb = jnp.exp(a - top), jnp.exp(b - top)
        probs += [ea / (ea + eb), eb / (ea + eb)]
    earlier = lax.broadcasted_iota(jnp.int32, (rows, rows), 0) > lax.broadcasted_iota(
        jnp.int32, (rows, rows), 1
    )
    before = dot_nn(earlier.astype(BF16), (hot0 + hot1).astype(BF16))
    f0, f1 = r0.astype(F32), r1.astype(F32)
    slot0 = jnp.where(
        r0 < experts, f0 * CAP + jnp.sum(before * hot0, axis=-1, keepdims=True), -1.0
    )
    slot1 = jnp.where(
        r1 < experts, f1 * CAP + jnp.sum(before * hot1, axis=-1, keepdims=True), -1.0
    )
    stat = jnp.zeros((rows, 128), F32)
    for i, column in enumerate([f0, f1, share0, share1, slot0, slot1] + probs):
        stat = jnp.where(lane == i, column, stat)
    first, second = slot_picks({"slot0": slot0, "slot1": slot1}, experts * CAP)
    outgoing = dot_tn(first + second, hidden).astype(BF16)
    return logits, stat, outgoing


def combine_part(mid, small, stat, returned, experts):
    _, gain, vec0, vec1 = row_vectors(small)
    hidden_full = mid * rms_scale(mid) * gain
    first, second = slot_picks(stat, experts * CAP)
    pair0, pair1 = dot_nn(first, returned), dot_nn(second, returned)
    copy, const0, const1 = const_weights(stat, experts)
    local = copy + const0 * stat["p00"] + const1 * stat["p10"]
    moe = stat["share0"] * pair0 + stat["share1"] * pair1 + local * hidden_full
    moe = moe + (const0 * stat["p01"]) * vec0 + (const1 * stat["p11"]) * vec1
    return mid + moe, hidden_full, pair0, pair1


def share_backward(grad, small, stat, hidden_full, pair0, pair1, extra, experts):
    rows = grad.shape[0]
    _, _, vec0, vec1 = row_vectors(small)
    first, second = slot_picks(stat, experts * CAP)
    lane = lanes(rows).astype(F32)
    rowsum = functools.partial(jnp.sum, axis=-1, keepdims=True)
    dot_hidden = rowsum(grad * hidden_full)
    dot_vec = (rowsum(grad * vec0), rowsum(grad * vec1))
    _, const0, const1 = const_weights(stat, experts)
    probs = ((stat["p00"], stat["p01"]), (stat["p10"], stat["p11"]))
    value = [probs[j][0] * dot_hidden + probs[j][1] * dot_vec[j] for j in (0, 1)]
    shares = []
    for r, pair in ((stat["r0"], pair0), (stat["r1"], pair1)):
        shares.append(
            rowsum(grad * pair)
            + (r == experts + 1).astype(F32) * dot_hidden
            + (r == experts + 2).astype(F32) * value[0]
            + (r == experts + 3).astype(F32) * value[1]
        )
    inner = stat["share0"] * shares[0] + stat["share1"] * shares[1]
    g_small = (lane == stat["r0"]).astype(F32) * (stat["share0"] * (shares[0] - inner))
    g_small = g_small + (lane == stat["r1"]).astype(F32) * (stat["share1"] * (shares[1] - inner))
    if extra is not None:
        g_small = g_small + extra
    g_logits = g_small
    for j, weight in ((0, const0), (1, const1)):
        q = (weight * dot_hidden, weight * dot_vec[j])
        mean = probs[j][0] * q[0] + probs[j][1] * q[1]
        for c in (0, 1):
            g_small = jnp.where(lane == CONST0 + 2 * j + c, probs[j][c] * (q[c] - mean), g_small)
    sent0 = (jnp.where(stat["r0"] < experts, stat["share0"], 0.0) * grad).astype(BF16)
    sent1 = (jnp.where(stat["r1"] < experts, stat["share1"], 0.0) * grad).astype(BF16)
    outgoing = (dot_tn(first, sent0) + dot_tn(second, sent1)).astype(BF16)
    hidden = hidden_full.astype(BF16).astype(F32)
    projections = dot_tn(g_small, hidden, precision=HIGH)
    vector0 = jnp.sum((const0 * stat["p01"]) * grad, axis=0, keepdims=True)
    vector1 = jnp.sum((const1 * stat["p11"]) * grad, axis=0, keepdims=True)
    return g_small, g_logits, outgoing, projections, vector0, vector1


def store_small(ref, projections, vector0, vector1):
    ref[0:16, :] = projections[0:16]
    ref[16:24, :] = jnp.zeros((8, ref.shape[1]), F32)
    ref[VECTOR0 : VECTOR0 + 1, :] = vector0
    ref[VECTOR0 + 1 : VECTOR0 + 2, :] = vector1


def first_kernel(experts, tokens, small, w_qkv_t, w_out, doc_col, doc_row, routes,
                 attn_in, qkv, probs, attn, mid_ref, logits_ref, stat_ref, out_ref):
    mid = attend_part(tokens[...].astype(F32), small[...], w_qkv_t, w_out, doc_col, doc_row, attn_in, qkv, probs, attn)
    mid_ref[...] = mid
    logits, stat, out = route_part(mid, small[...], routes[...], None, None, experts)
    logits_ref[...], stat_ref[...], out_ref[...] = logits, stat, out


def middle_kernel(experts, mid_in, small_in, stat_in, returned, small, w_qkv_t, w_out, doc_col, doc_row, routes, logits_in, w_res,
                  stream_ref, attn_in, qkv, probs, attn, mid_ref, stat_ref, out_ref):
    stream, _, _, _ = combine_part(mid_in[...], small_in[...], stat_columns(stat_in[...]), returned[...], experts)
    stream_ref[...] = stream
    mid = attend_part(stream, small[...], w_qkv_t, w_out, doc_col, doc_row, attn_in, qkv, probs, attn)
    mid_ref[...] = mid
    _, stat, out = route_part(mid, small[...], routes[...], logits_in[...], w_res[...], experts)
    stat_ref[...], out_ref[...] = stat, out


def turn_kernel(experts, mid, small, stat_in, returned, cotangent, logits_in, w_res,
                output, g_small_ref, extra_ref, out_ref, small_grad, res_grad):
    stat = stat_columns(stat_in[...])
    stream, hidden_full, pair0, pair1 = combine_part(mid[...], small[...], stat, returned[...], experts)
    output[...] = stream.astype(BF16)
    grad = cotangent[...].astype(F32)
    g_small, g_logits, out, projections, v0, v1 = share_backward(grad, small[...], stat, hidden_full, pair0, pair1, None, experts)
    g_small_ref[...] = g_small
    out_ref[...] = out
    store_small(small_grad, projections, v0, v1)
    res_grad[...] = dot_tn(logits_in[...], g_logits, precision=HIGH)
    extra_ref[...] = dot_nt(g_logits, w_res[...], precision=HIGH)


def layer_backward(experts, grad, back, g_small, stat, mid, small, stream, w_qkv_t, w_out, attn_in, qkv, probs, attn,
                   qkv_grad, out_grad, small_grad, g_qkv, g_attn):
    rows, width = mid.shape
    gain1, gain2, _, _ = row_vectors(small)
    first, second = slot_picks(stat, experts * CAP)
    copy, const0, const1 = const_weights(stat, experts)
    local = copy + const0 * stat["p00"] + const1 * stat["p10"]
    g_full = dot_nt(g_small, small.astype(F32), precision=HIGH) + dot_nn(first + second, back)
    g_full = g_full + grad * local
    s2 = rms_scale(mid)
    small_grad[GAIN0 + 1 : GAIN0 + 2, :] = jnp.sum(g_full * mid * s2, axis=0, keepdims=True)
    m = g_full * gain2
    g_mid = grad + s2 * m - mid * (s2 * s2 * s2 * jnp.mean(m * mid, axis=-1, keepdims=True))
    branch = g_mid.astype(BF16)
    out_grad[...] = dot_tn(attn[...], branch).astype(out_grad.dtype)
    g_attn[...] = dot_nt(branch, w_out[...]).astype(BF16)
    head_dim = width // HEADS
    factor = 1.0 / head_dim**0.5

    def heads(i, carry):
        at = pl.multiple_of(i * 2 * head_dim, 2 * head_dim)
        at_k = pl.multiple_of(at + width, 128)
        at_v = pl.multiple_of(at + 2 * width, 128)
        query = qkv[:, pl.ds(at, 2 * head_dim)]
        key = qkv[:, pl.ds(at_k, 2 * head_dim)]
        value = qkv[:, pl.ds(at_v, 2 * head_dim)]
        ga = g_attn[:, pl.ds(at, 2 * head_dim)]
        second_half = lanes(rows, 2 * head_dim) >= head_dim
        gq, gk, gv = [], [], []
        for sub in (0, 1):
            mine = second_half if sub else jnp.logical_not(second_half)
            p = probs[2 * i + sub]
            gp = dot_nt(jnp.where(mine, ga, jnp.zeros_like(ga)), value)
            gs = (p * (gp - jnp.sum(p * gp, axis=-1, keepdims=True))).astype(BF16)
            gq.append(dot_nn(gs, key))
            gk.append(dot_tn(gs, query))
            gv.append(dot_tn(p.astype(BF16), ga))
        g_qkv[:, pl.ds(at, 2 * head_dim)] = (jnp.where(second_half, gq[1], gq[0]) * factor).astype(BF16)
        g_qkv[:, pl.ds(at_k, 2 * head_dim)] = (jnp.where(second_half, gk[1], gk[0]) * factor).astype(BF16)
        g_qkv[:, pl.ds(at_v, 2 * head_dim)] = jnp.where(second_half, gv[1], gv[0]).astype(BF16)
        return carry

    lax.fori_loop(0, HEADS // 2, heads, 0, unroll=2)

    def weights(i, carry):
        at = pl.multiple_of(i * width, width)
        qkv_grad[pl.ds(at, width), :] = dot_tn(g_qkv[:, pl.ds(at, width)], attn_in[...]).astype(qkv_grad.dtype)
        return carry + dot_nn(g_qkv[:, pl.ds(at, width)], w_qkv_t[pl.ds(at, width), :])

    g_in = lax.fori_loop(0, 3, weights, jnp.zeros((rows, width), F32))
    s1 = rms_scale(stream)
    small_grad[GAIN0 : GAIN0 + 1, :] = jnp.sum(g_in * stream * s1, axis=0, keepdims=True)
    n = g_in * gain1
    return g_mid + s1 * n - stream * (s1 * s1 * s1 * jnp.mean(n * stream, axis=-1, keepdims=True))


def between_kernel(experts, cotangent, back, g_small, stat_in, mid, small, stream, w_qkv_t, w_out, attn_in, qkv, probs, attn, small_grad_in,
                   mid0, small0, stat0_in, returned0, extra,
                   qkv_grad, out_grad, small_grad, grad_ref, g_small0_ref, out_ref, small_grad0, g_qkv, g_attn):
    small_grad[...] = small_grad_in[...]
    grad = layer_backward(experts, cotangent[...].astype(F32), back[...], g_small[...], stat_columns(stat_in[...]), mid[...],
                          small[...], stream[...], w_qkv_t, w_out, attn_in, qkv, probs, attn, qkv_grad, out_grad, small_grad, g_qkv, g_attn)
    grad_ref[...] = grad
    stat0 = stat_columns(stat0_in[...])
    _, hidden_full, pair0, pair1 = combine_part(mid0[...], small0[...], stat0, returned0[...], experts)
    g_small0, _, out, projections, v0, v1 = share_backward(grad, small0[...], stat0, hidden_full, pair0, pair1, extra[...], experts)
    g_small0_ref[...] = g_small0
    out_ref[...] = out
    store_small(small_grad0, projections, v0, v1)


def last_kernel(experts, grad_in, back, g_small, stat_in, mid, small, tokens, w_qkv_t, w_out, attn_in, qkv, probs, attn, small_grad_in,
                qkv_grad, out_grad, small_grad, grad_ref, g_qkv, g_attn):
    small_grad[...] = small_grad_in[...]
    grad_ref[...] = layer_backward(experts, grad_in[...], back[...], g_small[...], stat_columns(stat_in[...]), mid[...], small[...],
                                   tokens[...].astype(F32), w_qkv_t, w_out, attn_in, qkv, probs, attn, qkv_grad, out_grad, small_grad,
                                   g_qkv, g_attn)


def local_call(kernel, experts, args, outs, scratch=()):
    return pl.pallas_call(
        functools.partial(kernel, experts),
        out_shape=[jax.ShapeDtypeStruct(shape, dtype) for shape, dtype in outs],
        in_specs=[VMEM] * len(args),
        out_specs=[VMEM] * len(outs),
        scratch_shapes=[pltpu.VMEM(shape, dtype) for shape, dtype in scratch],
        compiler_params=pltpu.CompilerParams(vmem_limit_bytes=60 * 2**20),
    )(*args)


def mate(place, step, owners):
    if owners != 4 or step == 0:
        return lax.rem(place + step, owners)
    if step == 1:
        return place + 1 - 2 * lax.rem(place, 2)
    return lax.rem(place + 2, 4) if step == 2 else 3 - place


class Line:
    def __init__(self, spread, owners, x, part, stage, arrived, final, returned, sems):
        self.owners, self.spread = owners, spread
        self.d, self.e = lax.axis_index("dp"), lax.axis_index("expert")
        self.t = self.d // spread
        self.x, self.part, self.stage, self.arrived = x, part, stage, arrived
        self.final, self.returned = final, returned
        (self.out_send, self.x_recv, self.x_send, self.sum_send, self.sum_recv, self.ret_send, self.ret_recv) = sems
        self.above, self.below = self.t < LINE - 1, self.t > 0

    def greet(self):
        barrier = pltpu.get_barrier_semaphore()
        for i in range(1, self.owners):
            pl.semaphore_signal(barrier, inc=1, device_id=(self.d, mate(self.e, i, self.owners)), device_id_type=MESH)

        @pl.when(self.above)
        def _():
            pl.semaphore_signal(barrier, inc=1, device_id=(self.d + self.spread, self.e), device_id_type=MESH)

        @pl.when(self.below)
        def _():
            pl.semaphore_signal(barrier, inc=1, device_id=(self.d - self.spread, self.e), device_id_type=MESH)

        ends = self.above.astype(jnp.int32) + self.below.astype(jnp.int32)
        pl.semaphore_wait(barrier, self.owners - 1 + ends)

    def slot_copy(self, out, i):
        to = mate(self.e, i, self.owners)
        return pltpu.make_async_remote_copy(
            src_ref=out.at[to], dst_ref=self.x.at[:, self.t, self.e], send_sem=self.out_send.at[i],
            recv_sem=self.x_recv.at[self.t, self.e], device_id=(self.d, to), device_id_type=MESH)

    def x_copy(self, up, s, b):
        to = self.d + self.spread if up else self.d - self.spread
        return pltpu.make_async_remote_copy(
            src_ref=self.x.at[:, s, b], dst_ref=self.x.at[:, s, b], send_sem=self.x_send.at[up, s, b],
            recv_sem=self.x_recv.at[s, b], device_id=(to, self.e), device_id_type=MESH)

    def sum_copy(self, up, s, b):
        to = self.d + self.spread if up else self.d - self.spread
        return pltpu.make_async_remote_copy(
            src_ref=self.stage.at[s, :, b], dst_ref=self.arrived.at[up, s, :, b], send_sem=self.sum_send.at[s, b],
            recv_sem=self.sum_recv.at[up, s, b], device_id=(to, self.e), device_id_type=MESH)

    def ret_copy(self, i):
        to = mate(self.e, i, self.owners)
        return pltpu.make_async_remote_copy(
            src_ref=self.final.at[to], dst_ref=self.returned.at[self.e], send_sem=self.ret_send.at[i],
            recv_sem=self.ret_recv.at[self.e], device_id=(self.d, to), device_id_type=MESH)

    def run(self, out, compute, meanwhile, keep):
        t, e, owners = self.t, self.e, self.owners
        self.greet()
        for i in list(range(2, owners)) + [1]:
            self.slot_copy(out, i).start()
        self.x[:, t, e] = out[e]
        for i in range(owners):
            b = mate(e, i, owners)
            if i:
                self.x_copy(0, t, b).wait_recv()
            for up, there in ((0, self.below), (1, self.above)):

                @pl.when(there)
                def _(up=up, b=b):
                    self.x_copy(up, t, b).start()

        keep(t)
        compute(t)

        def step(k, carry):
            for i in range(owners):
                b = mate(e, i, owners)

                @pl.when(t + k < LINE)
                def _(b=b):
                    self.x_copy(0, t + k, b).wait_recv()

                    @pl.when(self.below)
                    def _():
                        self.x_copy(0, t + k, b).start()

                @pl.when(t - k >= 0)
                def _(b=b):
                    self.x_copy(1, t - k, b).wait_recv()

                    @pl.when(self.above)
                    def _():
                        self.x_copy(1, t - k, b).start()

            def side(up, carry):
                s = t + k - 2 * k * up

                @pl.when(jnp.logical_and(s >= 0, s < LINE))
                def _():
                    keep(s)
                    compute(s)

                return carry

            lax.fori_loop(0, 2, side, 0)
            for up, first, s in ((1, t == 0, k), (0, t == LINE - 1, LINE - 1 - k)):

                @pl.when(first)
                def _(up=up, s=s):
                    for i in (list(range(2, owners)) + [0, 1])[:owners]:
                        b = mate(e, i, owners)
                        self.stage[s, :, b] = self.part[s, :, b].astype(BF16)
                        self.sum_copy(up, s, b).start()

            return carry

        lax.fori_loop(1, LINE, step, 0)
        meanwhile()

        def relay(k, carry):
            for i in (list(range(2, owners)) + [0, 1])[:owners]:
                b = mate(e, i, owners)
                for up, s, inside in (
                    (1, k, jnp.logical_and(t > 0, t < k)),
                    (0, LINE - 1 - k, jnp.logical_and(t > LINE - 1 - k, t < LINE - 1)),
                ):

                    @pl.when(inside)
                    def _(up=up, s=s, b=b):
                        self.sum_copy(up, s, b).wait_recv()
                        total = self.part[s, :, b] + self.arrived[up, s, :, b].astype(F32)
                        self.stage[s, :, b] = total.astype(BF16)
                        self.sum_copy(up, s, b).start()

            return carry

        lax.fori_loop(2, LINE, relay, 0)
        for i in (list(range(2, owners)) + [0, 1])[:owners]:
            b = mate(e, i, owners)
            for up, there in ((1, self.below), (0, self.above)):

                @pl.when(there)
                def _(up=up, b=b):
                    self.sum_copy(up, t, b).wait_recv()
                    self.part[t, :, b] = self.part[t, :, b] + self.arrived[up, t, :, b].astype(F32)

            if i:
                self.final[b] = self.part[t, :, b].astype(BF16)
                self.ret_copy(i).start()
            else:
                self.returned[e] = self.part[t, :, e].astype(BF16)

        def sent(s, carry):
            for i in range(owners):
                for up, mine in ((0, jnp.logical_and(self.below, s >= t)), (1, jnp.logical_and(self.above, s <= t))):

                    @pl.when(mine)
                    def _(up=up, i=i):
                        self.x_copy(up, s, i).wait_send()

                @pl.when(s != t)
                def _(i=i):
                    self.sum_copy(0, s, i).wait_send()

            return carry

        for i in range(1, owners):
            self.slot_copy(out, i).wait_send()
        lax.fori_loop(0, LINE, sent, 0)
        for i in range(1, owners):
            self.ret_copy(i).wait_send()
            pltpu.make_async_remote_copy(
                src_ref=self.final.at[e], dst_ref=self.returned.at[mate(e, i, owners)], send_sem=self.ret_send.at[i],
                recv_sem=self.ret_recv.at[mate(e, i, owners)], device_id=(self.d, mate(e, i, owners)), device_id_type=MESH).wait_recv()


def line_scratch(local, owners, width):
    shape = (local, owners, CAP, width)
    dma = pltpu.SemaphoreType.DMA
    return [
        pltpu.VMEM((local, LINE, owners, CAP, width), BF16),
        pltpu.VMEM((LINE,) + shape, F32),
        pltpu.VMEM((LINE,) + shape, BF16),
        pltpu.VMEM((2, LINE) + shape, BF16),
        pltpu.VMEM((owners, local, CAP, width), BF16),
        dma((owners,)), dma((LINE, owners)), dma((2, LINE, owners)), dma((LINE, owners)), dma((2, LINE, owners)),
        dma((owners,)), dma((owners,)),
    ]


def expert_forward_kernel(spread, parts, out, *refs):
    gate, up, down = refs[:parts], refs[parts : 2 * parts], refs[2 * parts : 3 * parts]
    returned, x_keep, g_keep, u_keep, x, part, stage, arrived, final = refs[3 * parts : 3 * parts + 9]
    sems, (g_all, u_all, keep_sem) = refs[3 * parts + 9 : 3 * parts + 16], refs[3 * parts + 16 :]
    local, _, owners, _, width = x.shape
    rows = owners * CAP
    line = Line(spread, owners, x, part, stage, arrived, final, returned, sems)

    def keep_x(s):
        return pltpu.make_async_copy(x.at[:, s], x_keep.at[:, s], keep_sem.at[0, s])

    def keep_g(s):
        return pltpu.make_async_copy(g_all.at[s], g_keep.at[s], keep_sem.at[1, s])

    def keep_u(s):
        return pltpu.make_async_copy(u_all.at[s], u_keep.at[s], keep_sem.at[2, s])

    def compute(s):
        def one(l, carry):
            rows_in = x[l, s].reshape(rows, width)
            total = jnp.zeros((rows, width), F32)
            for p in range(parts):
                cols = gate[p].shape[2]
                g = dot_nn(rows_in, gate[p][l])
                u = dot_nn(rows_in, up[p][l])
                g_all[s, l, :, p * cols : (p + 1) * cols] = g
                u_all[s, l, :, p * cols : (p + 1) * cols] = u
                act = (g * jax.nn.sigmoid(g) * u).astype(BF16)
                total = total + dot_nn(act, down[p][l])
            part[s, l] = total.reshape(owners, CAP, width)
            return carry

        lax.fori_loop(0, local, one, 0)
        keep_g(s).start()
        keep_u(s).start()

    line.run(out, compute, lambda: None, lambda s: keep_x(s).start())
    for s in range(LINE):
        keep_x(s).wait()
        keep_g(s).wait()
        keep_u(s).wait()


def expert_backward_kernel(spread, parts, out, x_in, g_all, u_all, *refs):
    gate, up, down = refs[:parts], refs[parts : 2 * parts], refs[2 * parts : 3 * parts]
    returned = refs[3 * parts]
    grads = refs[3 * parts + 1 : 6 * parts + 1]
    x, part, stage, arrived, final = refs[6 * parts + 1 : 6 * parts + 6]
    sems, (act_all, gg_all, gu_all) = refs[6 * parts + 6 : 6 * parts + 13], refs[6 * parts + 13 :]
    local, _, owners, _, width = x.shape
    rows = owners * CAP
    line = Line(spread, owners, x, part, stage, arrived, final, returned, sems)

    def compute(s):
        at = pl.multiple_of(s * rows, rows)

        def one(l, carry):
            rows_in = x[l, s].reshape(rows, width)
            total = jnp.zeros((rows, width), F32)
            for p in range(parts):
                cols = gate[p].shape[2]
                here = slice(p * cols, (p + 1) * cols)
                g, u = g_all[s, l, :, here], u_all[s, l, :, here]
                g_act = dot_nt(rows_in, down[p][l])
                sigma = jax.nn.sigmoid(g)
                swish = g * sigma
                gg = (g_act * u * sigma * (1.0 + g * (1.0 - sigma))).astype(BF16)
                gu = (g_act * swish).astype(BF16)
                act_all[l, pl.ds(at, rows), here] = (swish * u).astype(BF16)
                gg_all[l, pl.ds(at, rows), here] = gg
                gu_all[l, pl.ds(at, rows), here] = gu
                total = total + dot_nt(gg, gate[p][l]) + dot_nt(gu, up[p][l])
            part[s, l] = total.reshape(owners, CAP, width)
            return carry

        lax.fori_loop(0, local, one, 0)

    def weights():
        def one(l, carry):
            x_rows = x_in[l].reshape(LINE * rows, width)
            g_rows = x[l].reshape(LINE * rows, width)
            for p in range(parts):
                cols = gate[p].shape[2]
                here = slice(p * cols, (p + 1) * cols)
                for grad, value in (
                    (grads[p], dot_tn(x_rows, gg_all[l, :, here])),
                    (grads[parts + p], dot_tn(x_rows, gu_all[l, :, here])),
                    (grads[2 * parts + p], dot_tn(act_all[l, :, here], g_rows)),
                ):
                    grad[l] = value.astype(grad.dtype)
            return carry

        lax.fori_loop(0, local, one, 0)

    line.run(out, compute, weights, lambda s: None)


def expert_forward(spread, call_id, out, weights):
    parts = len(weights) // 3
    owners, local, cap, width = out.shape
    columns = sum(w.shape[2] for w in weights[:parts])
    kept = (LINE, local, owners * cap, columns)
    return pl.pallas_call(
        functools.partial(expert_forward_kernel, spread, parts),
        out_shape=[
            jax.ShapeDtypeStruct(out.shape, BF16),
            jax.ShapeDtypeStruct((local, LINE, owners, cap, width), BF16),
            jax.ShapeDtypeStruct(kept, F32),
            jax.ShapeDtypeStruct(kept, F32),
        ],
        in_specs=[VMEM] * (1 + len(weights)),
        out_specs=[VMEM, ANY, ANY, ANY],
        scratch_shapes=line_scratch(local, owners, width)
        + [pltpu.VMEM(kept, F32), pltpu.VMEM(kept, F32), pltpu.SemaphoreType.DMA((3, LINE))],
        compiler_params=pltpu.CompilerParams(
            collective_id=call_id, has_side_effects=True, vmem_limit_bytes=60 * 2**20
        ),
    )(out, *weights)


def expert_backward(spread, call_id, out, kept, weights):
    parts = len(weights) // 3
    owners, local, cap, width = out.shape
    columns = sum(w.shape[2] for w in weights[:parts])
    shapes = [
        jax.ShapeDtypeStruct(w.shape, F32 if i % parts == 0 else BF16) for i, w in enumerate(weights)
    ]
    wide = pltpu.VMEM((local, LINE * owners * cap, columns), BF16)
    return pl.pallas_call(
        functools.partial(expert_backward_kernel, spread, parts),
        out_shape=[jax.ShapeDtypeStruct(out.shape, BF16)] + shapes,
        in_specs=[VMEM] * (4 + len(weights)),
        out_specs=[VMEM] * (1 + len(weights)),
        scratch_shapes=line_scratch(local, owners, width) + [wide] * 3,
        compiler_params=pltpu.CompilerParams(
            collective_id=call_id, has_side_effects=True, vmem_limit_bytes=60 * 2**20
        ),
    )(out, *kept, *weights)


def from_partner(array, shift, spread, groups):
    pairs = [
        (t * spread + (f + shift) % spread, t * spread + f) for t in range(groups) for f in range(spread)
    ]
    return lax.ppermute(array, "dp", pairs)


def to_partner(array, shift, spread, groups):
    pairs = [
        (t * spread + f, t * spread + (f + shift) % spread) for t in range(groups) for f in range(spread)
    ]
    return lax.ppermute(array, "dp", pairs)


def pair_weights(shard, axis, spread):
    shard = shard.astype(BF16)
    parts = [shard] + [from_partner(shard, i, spread, LINE) for i in range(1, spread)]
    if shard.shape[axis] % 128:
        return [jnp.concatenate(parts, axis=axis)]
    return parts


def pair_sum(parts, axis, spread):
    if len(parts) == 1 and spread > 1:
        parts = jnp.split(parts[0], spread, axis=axis)
    total = parts[0]
    for i in range(1, spread):
        total = total + to_partner(parts[i].astype(BF16), i, spread, LINE).astype(F32)
    return total


class Place:
    def __init__(self, spread):
        self.spread = spread
        self.d, self.e = lax.axis_index("dp"), lax.axis_index("expert")
        self.t, self.f = self.d // spread, lax.rem(self.d, spread)
        self.y, self.c = self.e // 2, lax.rem(self.e, 2)
        self.above, self.below = self.t < LINE - 1, self.t > 0
        self.sibling = (self.d, self.e + 1 - 2 * self.c)
        self.across = (self.d, lax.rem(self.e + 2, 4))
        self.corner = (self.d, 3 - self.e)
        self.beside = (self.t * spread + 1 - self.f, self.e)

    def on_line(self, up):
        return (self.d + self.spread if up else self.d - self.spread, self.e)


def greet(always, place):
    barrier = pltpu.get_barrier_semaphore()
    for device in always:
        pl.semaphore_signal(barrier, inc=1, device_id=device, device_id_type=MESH)
    for up, there in ((1, place.above), (0, place.below)):

        @pl.when(there)
        def _(up=up):
            pl.semaphore_signal(barrier, inc=1, device_id=place.on_line(up), device_id_type=MESH)

    ends = place.above.astype(jnp.int32) + place.below.astype(jnp.int32)
    pl.semaphore_wait(barrier, len(always) + ends)


def remote(src, dst, send, recv, device):
    return pltpu.make_async_remote_copy(
        src_ref=src, dst_ref=dst, send_sem=send, recv_sem=recv, device_id=device, device_id_type=MESH)


class DenseGather:
    def __init__(self, place, shards, whole, sems):
        self.p, self.shards, self.whole = place, shards, whole
        self.z_send, self.z_recv, self.x_send, self.x_recv, self.y_send, self.y_recv, self.c_send, self.c_recv = sems

    @staticmethod
    def scratch(count):
        dma = pltpu.SemaphoreType.DMA
        return [dma((2, LINE, 3)), dma((LINE, 3)), dma((LINE, 3)), dma((LINE, 3)),
                dma((count, 2)), dma((count, 2)), dma((count, 2, 2)), dma((count, 2, 2))]

    def region(self, kind, s, y, c):
        depth = self.shards[kind].shape[0]
        if kind == 2:
            return self.whole[2].at[pl.ds(pl.multiple_of(s * depth, 16), depth)]
        half, wide = depth // 2, self.shards[kind].shape[1] // 2
        return self.whole[kind].at[
            pl.ds(pl.multiple_of(s * depth + y * half, 16), half), pl.ds(pl.multiple_of(c * wide, 128), wide)]

    def z_copy(self, kind, up, t):
        at = self.region(kind, t * self.p.spread + self.p.f, self.p.y, self.p.c)
        return remote(at, at, self.z_send.at[up, t, kind], self.z_recv.at[t, kind], self.p.on_line(up))

    def x_copy(self, kind, t, f):
        at = self.region(kind, t * self.p.spread + f, self.p.y, self.p.c)
        return remote(at, at, self.x_send.at[t, kind], self.x_recv.at[t, kind], self.p.beside)

    def y_copy(self, kind, s, y):
        at = self.region(kind, s, y, self.p.c)
        return remote(at, at, self.y_send.at[s, kind], self.y_recv.at[s, kind], self.p.across)

    def c_copy(self, kind, s, y, c):
        at = self.region(kind, s, y, c)
        return remote(at, at, self.c_send.at[s, y, kind], self.c_recv.at[s, y, kind], self.p.sibling)

    def spread_out(self, t, f):
        for kind in (0, 1):
            self.y_copy(kind, t * self.p.spread + f, self.p.y).start()
            self.c_copy(kind, t * self.p.spread + f, self.p.y, self.p.c).start()

    def begin(self):
        p = self.p
        for kind in range(3):
            depth = self.shards[kind].shape[0]
            self.whole[kind][pl.ds(pl.multiple_of(p.d * depth, 16), depth), :] = self.shards[kind][...]
        for up, there in ((0, p.below), (1, p.above)):

            @pl.when(there)
            def _(up=up):
                for kind in range(3):
                    self.z_copy(kind, up, p.t).start()

        for kind in range(3):
            self.x_copy(kind, p.t, p.f).start()

    def step(self, k):
        p = self.p
        for up, there, onward in ((0, p.t + k < LINE, p.below), (1, p.t - k >= 0, p.above)):
            t = p.t - k if up else p.t + k

            @pl.when(there)
            def _(up=up, onward=onward, t=t):
                for kind in range(3):
                    self.z_copy(kind, up, t).wait_recv()

                @pl.when(onward)
                def _():
                    for kind in range(3):
                        self.z_copy(kind, up, t).start()

                for kind in range(3):
                    self.x_copy(kind, t, p.f).start()
                self.spread_out(t, p.f)

    def in_order(self, body):
        body(self.p.t)

        def step(k, carry):
            for t in (self.p.t + k, self.p.t - k):

                @pl.when(jnp.logical_and(t >= 0, t < LINE))
                def _(t=t):
                    body(t)

            return carry

        lax.fori_loop(1, LINE, step, 0)

    def after_x(self):
        def body(t):
            for kind in range(3):
                self.x_copy(kind, t, 1 - self.p.f).wait_recv()
            self.spread_out(t, 1 - self.p.f)

        self.in_order(body)

    def after_y(self):
        p = self.p

        def body(t, f):
            for kind in (0, 1):
                self.y_copy(kind, t * p.spread + f, 1 - p.y).wait_recv()
                self.c_copy(kind, t * p.spread + f, 1 - p.y, p.c).start()

        def came_on_line(t):
            @pl.when(t != p.t)
            def _():
                body(t, p.f)

        self.in_order(came_on_line)
        self.in_order(lambda t: body(t, 1 - p.f))

    def finish(self):
        p = self.p

        def line(t, carry):
            for up, mine in ((0, jnp.logical_and(p.below, t >= p.t)), (1, jnp.logical_and(p.above, t <= p.t))):

                @pl.when(mine)
                def _(up=up):
                    for kind in range(3):
                        self.z_copy(kind, up, t).wait_send()

            for kind in range(3):
                self.x_copy(kind, t, p.f).wait_send()
            for f in range(p.spread):
                s = t * p.spread + f

                @pl.when(s != p.d)
                def _(s=s):
                    for kind in (0, 1):
                        self.y_copy(kind, s, p.y).wait_send()
                        for y in (0, 1):
                            self.c_copy(kind, s, y, p.c).wait_send()
                            self.c_copy(kind, s, y, 1 - p.c).wait_recv()

            return carry

        lax.fori_loop(0, LINE, line, 0)


def dense_gather_kernel(spread, qkv, out, small, routes, qkv_all, out_all, small_all, routes_all, *sems):
    p = Place(spread)
    r_send, r_recv = sems[-2:]
    gather = DenseGather(p, (qkv, out, small), (qkv_all, out_all, small_all), sems[:-2])
    mates = [p.sibling, p.across, p.corner]
    greet(mates + [p.beside], p)
    routes_all[p.e] = routes[...]
    for i, mate_id in enumerate(mates):
        remote(routes, routes_all.at[p.e], r_send.at[i], r_recv.at[p.e], mate_id).start()
    gather.begin()
    lax.fori_loop(1, LINE, lambda k, carry: (gather.step(k), carry)[1], 0)
    gather.after_x()
    gather.after_y()
    gather.finish()
    for i, mate_id in enumerate(mates):
        remote(routes, routes_all.at[p.e], r_send.at[i], r_recv.at[p.e], mate_id).wait_send()
        remote(routes, routes_all.at[mate_id[1]], r_send.at[i], r_recv.at[mate_id[1]], mate_id).wait_recv()


def dense_gather(spread, call_id, shards, routes):
    count = spread * LINE
    shapes = [jax.ShapeDtypeStruct((count * s.shape[0], s.shape[1]), s.dtype) for s in shards]
    dma = pltpu.SemaphoreType.DMA
    return pl.pallas_call(
        functools.partial(dense_gather_kernel, spread),
        out_shape=shapes + [jax.ShapeDtypeStruct((4,) + routes.shape, routes.dtype)],
        in_specs=[VMEM] * 4,
        out_specs=[VMEM] * 4,
        scratch_shapes=DenseGather.scratch(count) + [dma((3,)), dma((4,))],
        compiler_params=pltpu.CompilerParams(
            collective_id=call_id, has_side_effects=True, vmem_limit_bytes=60 * 2**20),
    )(*shards, routes)


class DenseReduce:
    def __init__(self, place, grads, sums, scratch):
        self.p, self.grads, self.sums = place, grads, sums
        (self.core, self.stage_y, self.came_y, self.quarter, self.stage_z, self.came_z, self.stage_x, self.came_x,
         self.a_send, self.a_recv, self.y_send, self.y_recv, self.z_send, self.z_recv, self.x_send, self.x_recv,
         self.e_send, self.e_recv) = scratch
        self.depths = [g.shape[0] // (LINE * place.spread) for g in grads]
        self.wide = grads[0].shape[1] // 2
        self.rows = sum(self.depths) // 2

    @staticmethod
    def scratch(spread, depths, width):
        count, rows, wide = LINE * spread, sum(depths) // 2, width // 2
        dma = pltpu.SemaphoreType.DMA
        return [
            pltpu.VMEM((count * sum(depths), wide), BF16),
            pltpu.VMEM((LINE, spread, rows, wide), BF16),
            pltpu.VMEM((LINE, spread, rows, wide), BF16),
            pltpu.VMEM((LINE, spread, rows, wide), F32),
            pltpu.VMEM((LINE, spread, rows, wide), BF16),
            pltpu.VMEM((2, LINE, spread, rows, wide), BF16),
            pltpu.VMEM((rows, wide), BF16),
            pltpu.VMEM((rows, wide), BF16),
            dma((2,)), dma((2,)), dma((LINE,)), dma((LINE,)), dma((LINE,)), dma((2, LINE)), dma(()), dma(()),
            dma((3, 2)), dma((3, 2)),
        ]

    def lanes(self, c):
        return pl.ds(pl.multiple_of(c * self.wide, 128), self.wide)

    def a_copy(self, kind):
        first = 0 if kind == 0 else self.grads[0].shape[0]
        count = self.grads[kind].shape[0]
        return remote(self.grads[kind].at[:, self.lanes(1 - self.p.c)], self.core.at[first : first + count],
                      self.a_send.at[kind], self.a_recv.at[kind], self.p.sibling)

    def y_copy(self, t):
        return remote(self.stage_y.at[t], self.came_y.at[t], self.y_send.at[t], self.y_recv.at[t], self.p.across)

    def z_copy(self, up, t):
        return remote(self.stage_z.at[t], self.came_z.at[up, t], self.z_send.at[t], self.z_recv.at[up, t], self.p.on_line(up))

    def x_copy(self):
        return remote(self.stage_x, self.came_x, self.x_send, self.x_recv, self.p.beside)

    def e_copy(self, i, kind, y, c):
        half = self.depths[kind] // 2
        at = self.sums[kind].at[pl.ds(pl.multiple_of(y * half, 8), half), self.lanes(c)]
        return remote(at, at, self.e_send.at[i, kind], self.e_recv.at[i, kind], self.p.across if i == 0 else self.p.sibling)

    def pieces(self, t, f, y):
        s, first, row = t * self.p.spread + f, 0, 0
        for grad, depth in zip(self.grads, self.depths):
            at = s * depth + y * (depth // 2)
            mine = grad[pl.ds(pl.multiple_of(at, 16), depth // 2), self.lanes(self.p.c)]
            other = self.core[pl.ds(pl.multiple_of(first + at, 16), depth // 2), :]
            yield slice(row, row + depth // 2), mine.astype(F32) + other.astype(F32)
            first, row = first + grad.shape[0], row + depth // 2

    def order(self, i):
        return jnp.where(self.p.t >= LINE // 2, i, LINE - 1 - i)

    def begin(self):
        for kind in (0, 1):
            self.a_copy(kind).start()

    def after_core(self):
        for kind in (0, 1):
            self.a_copy(kind).wait_recv()

        def body(i, carry):
            t = self.order(i)
            for f in range(self.p.spread):
                for where, value in self.pieces(t, f, 1 - self.p.y):
                    self.stage_y[t, f, where] = value.astype(BF16)
            self.y_copy(t).start()
            for f in range(self.p.spread):
                for where, value in self.pieces(t, f, self.p.y):
                    self.quarter[t, f, where] = value
            return carry

        lax.fori_loop(0, LINE, body, 0)

    def after_y(self):
        p = self.p

        def body(i, carry):
            t = self.order(i)
            self.y_copy(t).wait_recv()
            self.quarter[t] = self.quarter[t] + self.came_y[t].astype(F32)
            for up, mine, first in ((1, p.t < t, p.t == 0), (0, p.t > t, p.t == LINE - 1)):

                @pl.when(jnp.logical_and(mine, jnp.logical_not(first)))
                def _(up=up):
                    self.z_copy(up, t).wait_recv()
                    self.quarter[t] = self.quarter[t] + self.came_z[up, t].astype(F32)

                @pl.when(mine)
                def _(up=up):
                    self.stage_z[t] = self.quarter[t].astype(BF16)
                    self.z_copy(up, t).start()

            return carry

        lax.fori_loop(0, LINE, body, 0)

    def after_z(self):
        p = self.p
        for up, there in ((1, p.below), (0, p.above)):

            @pl.when(there)
            def _(up=up):
                self.z_copy(up, p.t).wait_recv()
                self.quarter[p.t] = self.quarter[p.t] + self.came_z[up, p.t].astype(F32)

        self.stage_x[...] = self.quarter[p.t, 1 - p.f].astype(BF16)
        self.x_copy().start()

    def after_x(self):
        p = self.p
        self.x_copy().wait_recv()
        row = 0
        for kind, depth in enumerate(self.depths):
            half = depth // 2
            value = self.quarter[p.t, p.f, row : row + half] + self.came_x[row : row + half].astype(F32)
            self.sums[kind][pl.ds(pl.multiple_of(p.y * half, 8), half), self.lanes(p.c)] = value
            row += half
        for kind in (0, 1):
            self.e_copy(0, kind, p.y, p.c).start()
        for kind in (0, 1):
            self.e_copy(1, kind, p.y, p.c).start()

    def finish(self):
        p = self.p
        for kind in (0, 1):
            self.e_copy(0, kind, 1 - p.y, p.c).wait_recv()
            self.e_copy(2, kind, 1 - p.y, p.c).start()
        for kind in (0, 1):
            self.a_copy(kind).wait_send()
            self.e_copy(0, kind, p.y, p.c).wait_send()
            self.e_copy(1, kind, p.y, p.c).wait_send()
            self.e_copy(1, kind, p.y, 1 - p.c).wait_recv()
            self.e_copy(2, kind, 1 - p.y, p.c).wait_send()
            self.e_copy(2, kind, 1 - p.y, 1 - p.c).wait_recv()
        self.x_copy().wait_send()

        def body(t, carry):
            self.y_copy(t).wait_send()

            @pl.when(t != p.t)
            def _():
                self.z_copy(0, t).wait_send()

            return carry

        lax.fori_loop(0, LINE, body, 0)


class SmallSum:
    def __init__(self, place, grads, total, scratch):
        self.p, self.grads, self.total = place, grads, total
        self.stage, self.came, self.send, self.recv = scratch
        p = place
        near = (p.d + p.spread - 2 * p.spread * lax.rem(p.t, 2), p.e)
        far = (lax.rem(p.d + 2 * p.spread, LINE * p.spread), p.e)
        self.partners = [p.sibling, p.across, p.beside, near, far]

    @staticmethod
    def scratch(rows, width):
        dma = pltpu.SemaphoreType.DMA
        return [pltpu.VMEM((5, rows, width // 2), F32), pltpu.VMEM((5, rows, width // 2), F32), dma((6,)), dma((6,))]

    def lanes(self, c):
        wide = self.grads.shape[1] // 2
        return pl.ds(pl.multiple_of(c * wide, 128), wide)

    def copy(self, i):
        src = self.grads.at[:, self.lanes(1 - self.p.c)] if i == 0 else self.stage.at[i]
        return remote(src, self.came.at[i], self.send.at[i], self.recv.at[i], self.partners[i])

    def last(self, c):
        at = self.total.at[:, self.lanes(c)]
        return remote(at, at, self.send.at[5], self.recv.at[5], self.p.sibling)

    def step(self, i):
        if i == 0:
            self.copy(0).start()
            return
        self.copy(i - 1).wait_recv()
        mine = self.grads[:, self.lanes(self.p.c)] if i == 1 else self.stage[i - 1]
        value = mine + self.came[i - 1]
        if i < 5:
            self.stage[i] = value
            self.copy(i).start()
        else:
            self.total[:, self.lanes(self.p.c)] = value
            self.last(self.p.c).start()

    def finish(self):
        for i in range(5):
            self.copy(i).wait_send()
        self.last(self.p.c).wait_send()
        self.last(1 - self.p.c).wait_recv()


REDUCE_REFS = 18


def dense_reduce_kernel(spread, layers, small, *refs):
    p = Place(spread)
    n = 2 * layers
    grads, small_sum, sums, scratch = refs[:n], refs[n], refs[n + 1 : 2 * n + 1], refs[2 * n + 1 :]
    both = [
        DenseReduce(p, grads[2 * l : 2 * l + 2], sums[2 * l : 2 * l + 2], scratch[REDUCE_REFS * l : REDUCE_REFS * (l + 1)])
        for l in range(layers)
    ]
    little = SmallSum(p, small, small_sum, scratch[REDUCE_REFS * layers :])
    greet(little.partners[:3] + little.partners[4:], p)
    for one in both:
        one.begin()
    little.step(0)
    for one in both:
        one.after_core()
    little.step(1)
    both[0].after_y()
    little.step(2)
    for one in both[1:]:
        one.after_y()
    little.step(3)
    for one in both:
        one.after_z()
    little.step(4)
    for one in both:
        one.after_x()
    little.step(5)
    for one in both:
        one.finish()
    little.finish()


def dense_reduce(spread, call_id, grads, small):
    layers = len(grads)
    count = LINE * spread
    flat = [g for layer in grads for g in layer]
    depths = [g.shape[0] // count for g in grads[0]]
    width = flat[0].shape[1]
    scratch = []
    for _ in range(layers):
        scratch += DenseReduce.scratch(spread, depths, width)
    return pl.pallas_call(
        functools.partial(dense_reduce_kernel, spread, layers),
        out_shape=[jax.ShapeDtypeStruct(small.shape, F32)]
        + [jax.ShapeDtypeStruct((g.shape[0] // count, width), F32) for g in flat],
        in_specs=[VMEM] * (1 + len(flat)),
        out_specs=[VMEM] * (1 + len(flat)),
        scratch_shapes=scratch + SmallSum.scratch(*small.shape),
        compiler_params=pltpu.CompilerParams(
            collective_id=call_id, has_side_effects=True, vmem_limit_bytes=60 * 2**20),
    )(small, *flat)


def per_device(
    tokens, seq_lengths, block_perm, routes, norm_gains, w_qkv, w_out, w_router, w_residual, w_const, v_const,
    w_gate, w_up, w_down, cotangent,
):
    rows, width = tokens.shape
    owners = lax.axis_size("expert")
    shards = lax.axis_size("dp")
    spread = shards // LINE
    local = w_gate.shape[1]
    experts = local * owners
    layers = routes.shape[0]
    slots = experts * CAP
    place = lax.axis_index("expert")

    my_place = jnp.sum(jnp.where(jnp.arange(owners) == place, block_perm[0], 0))
    lengths = lax.dynamic_index_in_dim(seq_lengths[0], place, 0, keepdims=False)
    order = jnp.arange(lengths.shape[0])
    ends = jnp.sum(jnp.where(order[:, None] <= order[None, :], lengths[:, None], 0), axis=0)
    doc = jnp.sum((jnp.arange(rows)[:, None] >= ends[None, :]).astype(jnp.int32), axis=1)
    doc_col, doc_row = doc[:, None], doc[None, :]

    weights = []
    for l in range(layers):
        weights.append(
            pair_weights(w_gate[l], 2, spread) + pair_weights(w_up[l], 2, spread) + pair_weights(w_down[l], 1, spread)
        )

    depth = w_out.shape[1]
    small = jnp.concatenate(
        [
            w_router, w_const[:, 0], w_const[:, 1], jnp.swapaxes(norm_gains, 1, 2), jnp.swapaxes(v_const, 1, 2),
            jnp.zeros((layers, depth, 108), F32),
        ],
        axis=2,
    ).astype(BF16)
    qkv_t = jnp.swapaxes(w_qkv, 1, 2).astype(BF16)
    out_rows = w_out.astype(BF16)
    in_kernels = spread == 2 and owners == 4 and qkv_t.shape[1] % 32 == 0 and depth % 32 == 0
    if in_kernels:
        packed_routes = jnp.zeros((8, 256), jnp.int32).at[: 2 * layers, :rows].set(
            jnp.swapaxes(routes, 1, 2).reshape(2 * layers, rows))
        dense = []
        for l in range(layers):
            qkv_all, out_all, small_all, routes_all = dense_gather(
                spread, 4 + l, (qkv_t[l], out_rows[l], small[l]), packed_routes)
            dense.append((small_all, qkv_all, out_all))
        picked = lax.dynamic_index_in_dim(routes_all, my_place, 0, keepdims=False)
        my_routes = jnp.swapaxes(picked[: 2 * layers, :rows].reshape(layers, 2, rows), 1, 2)
    else:
        all_routes = lax.all_gather(routes, "expert", axis=0)
        my_routes = lax.dynamic_index_in_dim(all_routes, my_place, 0, keepdims=False)
        qkv_all = lax.all_gather(qkv_t, "dp", axis=1, tiled=True)
        out_all = lax.all_gather(out_rows, "dp", axis=1, tiled=True)
        small_all = lax.all_gather(small, "dp", axis=1, tiled=True)
        dense = [(small_all[l], qkv_all[l], out_all[l]) for l in range(layers)]
    w_res = jnp.zeros((128, 128), F32).at[: w_residual.shape[0], : w_residual.shape[1]].set(w_residual)

    cols = ((rows, width), F32)
    attention = [((rows, width), BF16), ((rows, 3 * width), BF16), ((HEADS, rows, rows), F32), ((rows, width), BF16)]
    per_token, sent = ((rows, 128), F32), ((slots, width), BF16)

    def group(array):
        return array.reshape(owners, local, CAP, width)

    attn_in0, qkv0, probs0, attn0, mid0, logits0, stat0, out = local_call(
        first_kernel, experts, (tokens, *dense[0], doc_col, doc_row, my_routes[0]),
        attention + [cols, per_token, per_token, sent])
    ret0, *kept0 = expert_forward(spread, 0, group(out), weights[0])
    ret0 = ret0.reshape(slots, width)
    stream1, attn_in1, qkv1, probs1, attn1, mid1, stat1, out = local_call(
        middle_kernel, experts,
        (mid0, dense[0][0], stat0, ret0, *dense[1], doc_col, doc_row, my_routes[1], logits0, w_res),
        [cols] + attention + [cols, per_token, sent])
    ret1, *kept1 = expert_forward(spread, 1, group(out), weights[1])
    ret1 = ret1.reshape(slots, width)

    small_grads = ((24, width), F32)
    output, g_small1, extra, out, small_grad1, res_grad = local_call(
        turn_kernel, experts, (mid1, dense[1][0], stat1, ret1, cotangent, logits0, w_res),
        [((rows, width), BF16), per_token, per_token, sent, small_grads, ((128, 128), F32)])
    back, *expert_grads1 = expert_backward(spread, 2, group(out), kept1, weights[1])
    grad_type = BF16 if in_kernels else F32
    dense_grads = [((3 * width, width), grad_type), ((width, width), grad_type), small_grads]
    attention_scratch = [((rows, 3 * width), BF16), ((rows, width), BF16)]
    qkv_grad1, out_grad1, small_grad1, grad, g_small0, out, small_grad0 = local_call(
        between_kernel, experts,
        (cotangent, back.reshape(slots, width), g_small1, stat1, mid1, dense[1][0], stream1, dense[1][1], dense[1][2],
         attn_in1, qkv1, probs1, attn1, small_grad1, mid0, dense[0][0], stat0, ret0, extra),
        dense_grads + [cols, per_token, sent, small_grads], attention_scratch)
    back, *expert_grads0 = expert_backward(spread, 3, group(out), kept0, weights[0])
    qkv_grad0, out_grad0, small_grad0, tokens_grad = local_call(
        last_kernel, experts,
        (grad, back.reshape(slots, width), g_small0, stat0, mid0, dense[0][0], tokens, dense[0][1], dense[0][2],
         attn_in0, qkv0, probs0, attn0, small_grad0),
        dense_grads + [cols], attention_scratch)

    expert_out = []
    for axis, at in ((2, 0), (2, 1), (1, 2)):
        per_layer = []
        for grads in (expert_grads0, expert_grads1):
            n = len(grads) // 3
            per_layer.append(pair_sum(grads[at * n : (at + 1) * n], axis, spread))
        expert_out.append(jnp.stack(per_layer))
    gate_grad, up_grad, down_grad = expert_out
    packed = jnp.concatenate([small_grad0, small_grad1, jnp.pad(res_grad[:16], ((0, 0), (0, width - 128)))])
    if in_kernels:
        packed, qkv_sum0, out_sum0, qkv_sum1, out_sum1 = dense_reduce(
            spread, 6, [(qkv_grad0, out_grad0), (qkv_grad1, out_grad1)], packed)
        qkv_grad = jnp.stack([qkv_sum0, qkv_sum1])
        out_grad = jnp.stack([out_sum0, out_sum1])
    else:
        packed = lax.psum(packed, ("dp", "expert"))
        qkv_grad, out_grad = (
            lax.psum(lax.psum_scatter(jnp.stack(pair), "dp", scatter_dimension=1, tiled=True), "expert")
            for pair in ((qkv_grad0, qkv_grad1), (out_grad0, out_grad1)))
    mine = lax.dynamic_slice_in_dim(packed, lax.axis_index("dp") * depth, depth, axis=1)
    mine = jnp.stack([mine[:24], mine[24:48]])
    router_grad = jnp.swapaxes(mine[:, :CONST0], 1, 2)
    const_grad = jnp.swapaxes(mine[:, CONST0:GAIN0].reshape(layers, 2, 2, depth), 2, 3)
    residual_grad = packed[48 : 48 + CONST0, :CONST0]
    return (
        output, tokens_grad, mine[:, GAIN0 : GAIN0 + 2], jnp.swapaxes(qkv_grad, 1, 2), out_grad, router_grad,
        residual_grad, const_grad, mine[:, VECTOR0 : VECTOR0 + 2], gate_grad, up_grad, down_grad,
    )


def solution(mesh):
    in_specs = (
        P(("dp", "expert"), None), P("dp", None, None), P("dp", None), P(None, ("dp", "expert"), None),
        P(None, None, "dp"), P(None, None, "dp"), P(None, "dp", None), P(None, "dp", None), P(),
        P(None, None, "dp", None), P(None, None, "dp"), P(None, "expert", None, "dp"), P(None, "expert", None, "dp"),
        P(None, "expert", "dp", None), P(("dp", "expert"), None),
    )
    out_specs = (
        P(("dp", "expert"), None), P(("dp", "expert"), None), P(None, None, "dp"), P(None, None, "dp"),
        P(None, "dp", None), P(None, "dp", None), P(), P(None, None, "dp", None), P(None, None, "dp"),
        P(None, "expert", None, "dp"), P(None, "expert", None, "dp"), P(None, "expert", "dp", None),
    )
    return jax.shard_map(per_device, mesh=mesh, in_specs=in_specs, out_specs=out_specs, check_vma=False)
```

```python
import functools

import jax
import jax.numpy as jnp
from jax import lax
from jax.experimental import pallas as pl
from jax.experimental.pallas import tpu as pltpu
from jax.sharding import PartitionSpec as P

HEADS = 12
CAP = 48
LINE = 4
EPSILON = 1e-05
MASKED = -1e30
HIGH = lax.Precision.HIGHEST
F32 = jnp.float32
BF16 = jnp.bfloat16
MESH = pl.DeviceIdType.MESH
VMEM = pl.BlockSpec(memory_space=pltpu.VMEM)
ANY = pl.BlockSpec(memory_space=pl.ANY)

CONST0, GAIN0, VECTOR0 = 12, 16, 18
STAT = {
    name: i
    for i, name in enumerate(
        ("r0", "r1", "share0", "share1", "slot0", "slot1", "p00", "p01", "p10", "p11")
    )
}


def dot_nn(a, b, **kw):
    return lax.dot_general(a, b, (((1,), (0,)), ((), ())), preferred_element_type=F32, **kw)


def dot_nt(a, b, **kw):
    return lax.dot_general(a, b, (((1,), (1,)), ((), ())), preferred_element_type=F32, **kw)


def dot_tn(a, b, **kw):
    return lax.dot_general(a, b, (((0,), (0,)), ((), ())), preferred_element_type=F32, **kw)


def lanes(rows, width=128):
    return lax.broadcasted_iota(jnp.int32, (rows, width), 1)


def rms_scale(values):
    return lax.rsqrt(jnp.mean(values * values, axis=-1, keepdims=True) + EPSILON)


def row_vectors(small):
    pick = lax.broadcasted_iota(jnp.int32, (8, 128), 0) + GAIN0 == lanes(8)
    rows = dot_nt(pick.astype(BF16), small)
    return rows[0:1], rows[1:2], rows[2:3], rows[3:4]


def stat_columns(stat):
    return {name: stat[:, i : i + 1] for name, i in STAT.items()}


def slot_picks(stat, slots):
    place = lanes(stat["slot0"].shape[0], slots).astype(F32)
    first = (place == stat["slot0"]).astype(BF16)
    second = (place == stat["slot1"]).astype(BF16)
    return first, second


def const_weights(stat, experts):
    out = []
    for kind in (experts + 1, experts + 2, experts + 3):
        out.append(
            stat["share0"] * (stat["r0"] == kind).astype(F32)
            + stat["share1"] * (stat["r1"] == kind).astype(F32)
        )
    return out


def attend_part(stream, small, w_qkv_t, w_out, doc_col, doc_row, attn_in_ref, qkv_ref, probs_ref, attn_ref):
    rows, width = stream.shape
    gain, _, _, _ = row_vectors(small)
    attn_in_ref[...] = (stream * rms_scale(stream) * gain).astype(BF16)

    def project(i, carry):
        at = pl.multiple_of(i * width, width)
        qkv_ref[:, pl.ds(at, width)] = dot_nt(
            attn_in_ref[...], w_qkv_t[pl.ds(at, width), :]
        ).astype(BF16)
        return carry

    lax.fori_loop(0, 3, project, 0)
    head_dim = width // HEADS
    factor = 1.0 / head_dim**0.5
    allowed = jnp.logical_and(
        doc_col[...] == doc_row[...],
        lax.broadcasted_iota(jnp.int32, (rows, rows), 0)
        >= lax.broadcasted_iota(jnp.int32, (rows, rows), 1),
    )

    def heads(i, carry):
        at = pl.multiple_of(i * 2 * head_dim, 2 * head_dim)
        query = qkv_ref[:, pl.ds(at, 2 * head_dim)]
        key = qkv_ref[:, pl.ds(pl.multiple_of(at + width, 128), 2 * head_dim)]
        value = qkv_ref[:, pl.ds(pl.multiple_of(at + 2 * width, 128), 2 * head_dim)]
        second = lanes(rows, 2 * head_dim) >= head_dim
        mixed = []
        for sub in (0, 1):
            mine = second if sub else jnp.logical_not(second)
            scores = dot_nt(jnp.where(mine, query, jnp.zeros_like(query)), key) * factor
            scores = jnp.where(allowed, scores, MASKED)
            exponent = jnp.exp(scores - jnp.max(scores, axis=-1, keepdims=True))
            probs = exponent / jnp.sum(exponent, axis=-1, keepdims=True)
            probs_ref[2 * i + sub] = probs
            mixed.append(dot_nn(probs.astype(BF16), value))
        attn_ref[:, pl.ds(at, 2 * head_dim)] = jnp.where(second, mixed[1], mixed[0]).astype(BF16)
        return carry

    lax.fori_loop(0, HEADS // 2, heads, 0, unroll=2)
    return stream + dot_nn(attn_ref[...], w_out[...])


def route_part(mid, small, routes, prev_logits, w_res, experts):
    rows = mid.shape[0]
    _, gain, _, _ = row_vectors(small)
    hidden = (mid * rms_scale(mid) * gain).astype(BF16)
    lane = lanes(rows)
    raw = dot_nn(hidden, small)
    logits = jnp.where(lane < CONST0, raw, 0.0)
    if prev_logits is not None:
        logits = logits + dot_nn(prev_logits, w_res, precision=HIGH)
    r0, r1 = routes[:, 0:1], routes[:, 1:2]
    hot0, hot1 = (lane == r0).astype(F32), (lane == r1).astype(F32)
    c0 = jnp.sum(hot0 * logits, axis=-1, keepdims=True)
    c1 = jnp.sum(hot1 * logits, axis=-1, keepdims=True)
    peak = jnp.maximum(c0, c1)
    e0, e1 = jnp.exp(c0 - peak), jnp.exp(c1 - peak)
    total = e0 + e1
    share0, share1 = e0 / total, e1 / total
    probs = []
    for j in (0, 1):
        a = raw[:, CONST0 + 2 * j : CONST0 + 2 * j + 1]
        b = raw[:, CONST0 + 2 * j + 1 : CONST0 + 2 * j + 2]
        top = jnp.maximum(a, b)
        ea, eb = jnp.exp(a - top), jnp.exp(b - top)
        probs += [ea / (ea + eb), eb / (ea + eb)]
    earlier = lax.broadcasted_iota(jnp.int32, (rows, rows), 0) > lax.broadcasted_iota(
        jnp.int32, (rows, rows), 1
    )
    before = dot_nn(earlier.astype(BF16), (hot0 + hot1).astype(BF16))
    f0, f1 = r0.astype(F32), r1.astype(F32)
    slot0 = jnp.where(
        r0 < experts, f0 * CAP + jnp.sum(before * hot0, axis=-1, keepdims=True), -1.0
    )
    slot1 = jnp.where(
        r1 < experts, f1 * CAP + jnp.sum(before * hot1, axis=-1, keepdims=True), -1.0
    )
    stat = jnp.zeros((rows, 128), F32)
    for i, column in enumerate([f0, f1, share0, share1, slot0, slot1] + probs):
        stat = jnp.where(lane == i, column, stat)
    first, second = slot_picks({"slot0": slot0, "slot1": slot1}, experts * CAP)
    outgoing = dot_tn(first + second, hidden).astype(BF16)
    return logits, stat, outgoing


def combine_part(mid, small, stat, returned, experts):
    _, gain, vec0, vec1 = row_vectors(small)
    hidden_full = mid * rms_scale(mid) * gain
    first, second = slot_picks(stat, experts * CAP)
    pair0, pair1 = dot_nn(first, returned), dot_nn(second, returned)
    copy, const0, const1 = const_weights(stat, experts)
    local = copy + const0 * stat["p00"] + const1 * stat["p10"]
    moe = stat["share0"] * pair0 + stat["share1"] * pair1 + local * hidden_full
    moe = moe + (const0 * stat["p01"]) * vec0 + (const1 * stat["p11"]) * vec1
    return mid + moe, hidden_full, pair0, pair1


def share_backward(grad, small, stat, hidden_full, pair0, pair1, extra, experts):
    rows = grad.shape[0]
    _, _, vec0, vec1 = row_vectors(small)
    first, second = slot_picks(stat, experts * CAP)
    lane = lanes(rows).astype(F32)
    rowsum = functools.partial(jnp.sum, axis=-1, keepdims=True)
    dot_hidden = rowsum(grad * hidden_full)
    dot_vec = (rowsum(grad * vec0), rowsum(grad * vec1))
    _, const0, const1 = const_weights(stat, experts)
    probs = ((stat["p00"], stat["p01"]), (stat["p10"], stat["p11"]))
    value = [probs[j][0] * dot_hidden + probs[j][1] * dot_vec[j] for j in (0, 1)]
    shares = []
    for r, pair in ((stat["r0"], pair0), (stat["r1"], pair1)):
        shares.append(
            rowsum(grad * pair)
            + (r == experts + 1).astype(F32) * dot_hidden
            + (r == experts + 2).astype(F32) * value[0]
            + (r == experts + 3).astype(F32) * value[1]
        )
    inner = stat["share0"] * shares[0] + stat["share1"] * shares[1]
    g_small = (lane == stat["r0"]).astype(F32) * (stat["share0"] * (shares[0] - inner))
    g_small = g_small + (lane == stat["r1"]).astype(F32) * (stat["share1"] * (shares[1] - inner))
    if extra is not None:
        g_small = g_small + extra
    g_logits = g_small
    for j, weight in ((0, const0), (1, const1)):
        q = (weight * dot_hidden, weight * dot_vec[j])
        mean = probs[j][0] * q[0] + probs[j][1] * q[1]
        for c in (0, 1):
            g_small = jnp.where(lane == CONST0 + 2 * j + c, probs[j][c] * (q[c] - mean), g_small)
    sent0 = (jnp.where(stat["r0"] < experts, stat["share0"], 0.0) * grad).astype(BF16)
    sent1 = (jnp.where(stat["r1"] < experts, stat["share1"], 0.0) * grad).astype(BF16)
    outgoing = (dot_tn(first, sent0) + dot_tn(second, sent1)).astype(BF16)
    hidden = hidden_full.astype(BF16).astype(F32)
    projections = dot_tn(g_small, hidden, precision=HIGH)
    vector0 = jnp.sum((const0 * stat["p01"]) * grad, axis=0, keepdims=True)
    vector1 = jnp.sum((const1 * stat["p11"]) * grad, axis=0, keepdims=True)
    return g_small, g_logits, outgoing, projections, vector0, vector1


def store_small(ref, projections, vector0, vector1):
    ref[0:16, :] = projections[0:16]
    ref[16:24, :] = jnp.zeros((8, ref.shape[1]), F32)
    ref[VECTOR0 : VECTOR0 + 1, :] = vector0
    ref[VECTOR0 + 1 : VECTOR0 + 2, :] = vector1


def first_kernel(experts, tokens, small, w_qkv_t, w_out, doc_col, doc_row, routes,
                 attn_in, qkv, probs, attn, mid_ref, logits_ref, stat_ref, out_ref):
    mid = attend_part(tokens[...].astype(F32), small[...], w_qkv_t, w_out, doc_col, doc_row, attn_in, qkv, probs, attn)
    mid_ref[...] = mid
    logits, stat, out = route_part(mid, small[...], routes[...], None, None, experts)
    logits_ref[...], stat_ref[...], out_ref[...] = logits, stat, out


def middle_kernel(experts, mid_in, small_in, stat_in, returned, small, w_qkv_t, w_out, doc_col, doc_row, routes, logits_in, w_res,
                  stream_ref, attn_in, qkv, probs, attn, mid_ref, stat_ref, out_ref):
    stream, _, _, _ = combine_part(mid_in[...], small_in[...], stat_columns(stat_in[...]), returned[...], experts)
    stream_ref[...] = stream
    mid = attend_part(stream, small[...], w_qkv_t, w_out, doc_col, doc_row, attn_in, qkv, probs, attn)
    mid_ref[...] = mid
    _, stat, out = route_part(mid, small[...], routes[...], logits_in[...], w_res[...], experts)
    stat_ref[...], out_ref[...] = stat, out


def turn_kernel(experts, mid, small, stat_in, returned, cotangent, logits_in, w_res,
                output, g_small_ref, extra_ref, out_ref, small_grad, res_grad):
    stat = stat_columns(stat_in[...])
    stream, hidden_full, pair0, pair1 = combine_part(mid[...], small[...], stat, returned[...], experts)
    output[...] = stream.astype(BF16)
    grad = cotangent[...].astype(F32)
    g_small, g_logits, out, projections, v0, v1 = share_backward(grad, small[...], stat, hidden_full, pair0, pair1, None, experts)
    g_small_ref[...] = g_small
    out_ref[...] = out
    store_small(small_grad, projections, v0, v1)
    res_grad[...] = dot_tn(logits_in[...], g_logits, precision=HIGH)
    extra_ref[...] = dot_nt(g_logits, w_res[...], precision=HIGH)


def layer_backward(experts, grad, back, g_small, stat, mid, small, stream, w_qkv_t, w_out, attn_in, qkv, probs, attn,
                   qkv_grad, out_grad, small_grad, g_qkv, g_attn):
    rows, width = mid.shape
    gain1, gain2, _, _ = row_vectors(small)
    first, second = slot_picks(stat, experts * CAP)
    copy, const0, const1 = const_weights(stat, experts)
    local = copy + const0 * stat["p00"] + const1 * stat["p10"]
    g_full = dot_nt(g_small, small.astype(F32), precision=HIGH) + dot_nn(first + second, back)
    g_full = g_full + grad * local
    s2 = rms_scale(mid)
    small_grad[GAIN0 + 1 : GAIN0 + 2, :] = jnp.sum(g_full * mid * s2, axis=0, keepdims=True)
    m = g_full * gain2
    g_mid = grad + s2 * m - mid * (s2 * s2 * s2 * jnp.mean(m * mid, axis=-1, keepdims=True))
    branch = g_mid.astype(BF16)
    out_grad[...] = dot_tn(attn[...], branch).astype(out_grad.dtype)
    g_attn[...] = dot_nt(branch, w_out[...]).astype(BF16)
    head_dim = width // HEADS
    factor = 1.0 / head_dim**0.5

    def heads(i, carry):
        at = pl.multiple_of(i * 2 * head_dim, 2 * head_dim)
        at_k = pl.multiple_of(at + width, 128)
        at_v = pl.multiple_of(at + 2 * width, 128)
        query = qkv[:, pl.ds(at, 2 * head_dim)]
        key = qkv[:, pl.ds(at_k, 2 * head_dim)]
        value = qkv[:, pl.ds(at_v, 2 * head_dim)]
        ga = g_attn[:, pl.ds(at, 2 * head_dim)]
        second_half = lanes(rows, 2 * head_dim) >= head_dim
        gq, gk, gv = [], [], []
        for sub in (0, 1):
            mine = second_half if sub else jnp.logical_not(second_half)
            p = probs[2 * i + sub]
            gp = dot_nt(jnp.where(mine, ga, jnp.zeros_like(ga)), value)
            gs = (p * (gp - jnp.sum(p * gp, axis=-1, keepdims=True))).astype(BF16)
            gq.append(dot_nn(gs, key))
            gk.append(dot_tn(gs, query))
            gv.append(dot_tn(p.astype(BF16), ga))
        g_qkv[:, pl.ds(at, 2 * head_dim)] = (jnp.where(second_half, gq[1], gq[0]) * factor).astype(BF16)
        g_qkv[:, pl.ds(at_k, 2 * head_dim)] = (jnp.where(second_half, gk[1], gk[0]) * factor).astype(BF16)
        g_qkv[:, pl.ds(at_v, 2 * head_dim)] = jnp.where(second_half, gv[1], gv[0]).astype(BF16)
        return carry

    lax.fori_loop(0, HEADS // 2, heads, 0, unroll=2)

    def weights(i, carry):
        at = pl.multiple_of(i * width, width)
        qkv_grad[pl.ds(at, width), :] = dot_tn(g_qkv[:, pl.ds(at, width)], attn_in[...]).astype(qkv_grad.dtype)
        return carry + dot_nn(g_qkv[:, pl.ds(at, width)], w_qkv_t[pl.ds(at, width), :])

    g_in = lax.fori_loop(0, 3, weights, jnp.zeros((rows, width), F32))
    s1 = rms_scale(stream)
    small_grad[GAIN0 : GAIN0 + 1, :] = jnp.sum(g_in * stream * s1, axis=0, keepdims=True)
    n = g_in * gain1
    return g_mid + s1 * n - stream * (s1 * s1 * s1 * jnp.mean(n * stream, axis=-1, keepdims=True))


def between_kernel(experts, cotangent, back, g_small, stat_in, mid, small, stream, w_qkv_t, w_out, attn_in, qkv, probs, attn, small_grad_in,
                   mid0, small0, stat0_in, returned0, extra,
                   qkv_grad, out_grad, small_grad, grad_ref, g_small0_ref, out_ref, small_grad0, g_qkv, g_attn):
    small_grad[...] = small_grad_in[...]
    grad = layer_backward(experts, cotangent[...].astype(F32), back[...], g_small[...], stat_columns(stat_in[...]), mid[...],
                          small[...], stream[...], w_qkv_t, w_out, attn_in, qkv, probs, attn, qkv_grad, out_grad, small_grad, g_qkv, g_attn)
    grad_ref[...] = grad
    stat0 = stat_columns(stat0_in[...])
    _, hidden_full, pair0, pair1 = combine_part(mid0[...], small0[...], stat0, returned0[...], experts)
    g_small0, _, out, projections, v0, v1 = share_backward(grad, small0[...], stat0, hidden_full, pair0, pair1, extra[...], experts)
    g_small0_ref[...] = g_small0
    out_ref[...] = out
    store_small(small_grad0, projections, v0, v1)


def last_kernel(experts, grad_in, back, g_small, stat_in, mid, small, tokens, w_qkv_t, w_out, attn_in, qkv, probs, attn, small_grad_in,
                qkv_grad, out_grad, small_grad, grad_ref, g_qkv, g_attn):
    small_grad[...] = small_grad_in[...]
    grad_ref[...] = layer_backward(experts, grad_in[...], back[...], g_small[...], stat_columns(stat_in[...]), mid[...], small[...],
                                   tokens[...].astype(F32), w_qkv_t, w_out, attn_in, qkv, probs, attn, qkv_grad, out_grad, small_grad,
                                   g_qkv, g_attn)


def local_call(kernel, experts, args, outs, scratch=()):
    return pl.pallas_call(
        functools.partial(kernel, experts),
        out_shape=[jax.ShapeDtypeStruct(shape, dtype) for shape, dtype in outs],
        in_specs=[VMEM] * len(args),
        out_specs=[VMEM] * len(outs),
        scratch_shapes=[pltpu.VMEM(shape, dtype) for shape, dtype in scratch],
        compiler_params=pltpu.CompilerParams(vmem_limit_bytes=60 * 2**20),
    )(*args)


class Place:
    def __init__(self, spread):
        self.spread = spread
        self.d, self.e = lax.axis_index("dp"), lax.axis_index("expert")
        self.t, self.f = self.d // spread, lax.rem(self.d, spread)
        self.y, self.c = self.e // 2, lax.rem(self.e, 2)
        self.above, self.below = self.t < LINE - 1, self.t > 0
        self.sibling = (self.d, self.e + 1 - 2 * self.c)
        self.across = (self.d, lax.rem(self.e + 2, 4))
        self.corner = (self.d, 3 - self.e)
        self.beside = (self.t * spread + 1 - self.f, self.e)
        self.mates = [(self.d, self.e), self.sibling, self.across, self.corner]

    def on_line(self, up):
        return (self.d + self.spread if up else self.d - self.spread, self.e)


def greet(always, place):
    barrier = pltpu.get_barrier_semaphore()
    for device in always:
        pl.semaphore_signal(barrier, inc=1, device_id=device, device_id_type=MESH)
    for up, there in ((1, place.above), (0, place.below)):

        @pl.when(there)
        def _(up=up):
            pl.semaphore_signal(barrier, inc=1, device_id=place.on_line(up), device_id_type=MESH)

    ends = place.above.astype(jnp.int32) + place.below.astype(jnp.int32)
    pl.semaphore_wait(barrier, len(always) + ends)


def remote(src, dst, send, recv, device):
    return pltpu.make_async_remote_copy(
        src_ref=src, dst_ref=dst, send_sem=send, recv_sem=recv, device_id=device, device_id_type=MESH)


def dma(*shape):
    return pltpu.SemaphoreType.DMA(shape)


def along(place, body, start=0):
    if start == 0:
        body(place.t)

    def step(k, carry):
        for t in (place.t + k, place.t - k):

            @pl.when(jnp.logical_and(t >= 0, t < LINE))
            def _(t=t):
                body(t)

        return carry

    lax.fori_loop(1, LINE, step, 0)


class Rider:
    partners = ()

    def begin(self):
        pass

    def after_first(self):
        pass

    def after_line(self):
        pass

    def after_relay(self):
        pass

    def finish(self):
        pass


class Line:
    def __init__(self, place, x, part, stage, arrived, final, returned, sems):
        self.p = place
        self.x, self.part, self.stage, self.arrived = x, part, stage, arrived
        self.final, self.returned = final, returned
        (self.out_send, self.x_recv, self.x_send, self.sum_send, self.sum_recv, self.ret_send, self.ret_recv) = sems

    @staticmethod
    def scratch(local, width):
        shape = (local, 4, CAP, width)
        return [
            pltpu.VMEM((local, LINE, 4, CAP, width), BF16),
            pltpu.VMEM((LINE,) + shape, F32),
            pltpu.VMEM((LINE,) + shape, BF16),
            pltpu.VMEM((2, LINE) + shape, BF16),
            pltpu.VMEM((4, local, CAP, width), BF16),
            dma(4), dma(LINE, 4), dma(2, LINE, 4), dma(LINE, 4), dma(2, LINE, 4), dma(4), dma(4),
        ]

    def slot_copy(self, out, i):
        to, p = self.p.mates[i], self.p
        return remote(out.at[to[1]], self.x.at[:, p.t, p.e], self.out_send.at[i], self.x_recv.at[p.t, p.e], to)

    def x_copy(self, up, s, b):
        at = self.x.at[:, s, b]
        return remote(at, at, self.x_send.at[up, s, b], self.x_recv.at[s, b], self.p.on_line(up))

    def sum_copy(self, up, s, b):
        return remote(self.stage.at[s, :, b], self.arrived.at[up, s, :, b], self.sum_send.at[s, b],
                      self.sum_recv.at[up, s, b], self.p.on_line(up))

    def ret_copy(self, i, to_mate=True):
        to = self.p.mates[i]
        row = self.p.e if to_mate else to[1]
        return remote(self.final.at[to[1]], self.returned.at[row], self.ret_send.at[i], self.ret_recv.at[row], to)

    def send_sum(self, up, s, b, total):
        self.stage[s, :, b] = total.astype(BF16)
        self.sum_copy(up, s, b).start()

    def relay(self, stage):
        p = self.p
        for up, mine in ((1, p.t == stage), (0, p.t == LINE - 1 - stage)):

            @pl.when(mine)
            def _(up=up):
                def one(n, carry):
                    s = p.t + 1 + n if up else p.t - 1 - n
                    for _, b in p.mates:
                        self.sum_copy(up, s, b).wait_recv()
                        self.send_sum(up, s, b, self.part[s, :, b] + self.arrived[up, s, :, b].astype(F32))
                    return carry

                lax.fori_loop(0, LINE - 1 - stage, one, 0)

    def run(self, out, compute, kept, meanwhile, rider):
        p = self.p
        t, e = p.t, p.e
        blocks = [b for _, b in p.mates]
        greet(p.mates[1:] + list(rider.partners), p)
        for i in (2, 3, 1):
            self.slot_copy(out, i).start()
        self.x[:, t, e] = out[e]
        rider.begin()
        for half in (0, 1):
            for i in (2 * half, 2 * half + 1):
                if i:
                    self.x_copy(0, t, blocks[i]).wait_recv()
                for up, there in ((0, p.below), (1, p.above)):

                    @pl.when(there)
                    def _(up=up, i=i):
                        self.x_copy(up, t, blocks[i]).start()

            compute(t, p.y + half - 2 * p.y * half)
        kept(t)
        rider.after_first()

        def step(k, carry):
            def part(half, carry):
                pair = p.y + half - 2 * p.y * half
                first = jnp.where(half == 0, blocks[0], blocks[2])
                second = jnp.where(half == 0, blocks[1], blocks[3])
                for b in (first, second):
                    for up, there, onward in ((0, t + k < LINE, p.below), (1, t - k >= 0, p.above)):
                        s = t - k if up else t + k

                        @pl.when(there)
                        def _(up=up, onward=onward, s=s, b=b):
                            self.x_copy(up, s, b).wait_recv()

                            @pl.when(onward)
                            def _():
                                self.x_copy(up, s, b).start()

                def side(up, carry):
                    s = t + k - 2 * k * up

                    @pl.when(jnp.logical_and(s >= 0, s < LINE))
                    def _():
                        compute(s, pair)

                        @pl.when(half == 1)
                        def _():
                            kept(s)

                    return carry

                lax.fori_loop(0, 2, side, 0)
                for up, starts, s in ((1, t == 0, k), (0, t == LINE - 1, LINE - 1 - k)):

                    @pl.when(starts)
                    def _(up=up, s=s):
                        for b in (first, second):
                            self.send_sum(up, s, b, self.part[s, :, b])

                return carry

            lax.fori_loop(0, 2, part, 0)
            return carry

        lax.fori_loop(1, LINE, step, 0)
        rider.after_line()
        meanwhile()
        for stage in range(1, LINE - 1):
            self.relay(stage)
        rider.after_relay()
        for i, b in enumerate(blocks):
            for up, there in ((1, p.below), (0, p.above)):

                @pl.when(there)
                def _(up=up, b=b):
                    self.sum_copy(up, t, b).wait_recv()
                    self.part[t, :, b] = self.part[t, :, b] + self.arrived[up, t, :, b].astype(F32)

            if i:
                self.final[b] = self.part[t, :, b].astype(BF16)
                self.ret_copy(i).start()
            else:
                self.returned[e] = self.part[t, :, e].astype(BF16)

        def sent(s, carry):
            for i in range(4):
                for up, mine in ((0, jnp.logical_and(p.below, s >= t)), (1, jnp.logical_and(p.above, s <= t))):

                    @pl.when(mine)
                    def _(up=up, i=i):
                        self.x_copy(up, s, i).wait_send()

                @pl.when(s != t)
                def _(i=i):
                    self.sum_copy(0, s, i).wait_send()

            return carry

        for i in (1, 2, 3):
            self.slot_copy(out, i).wait_send()
        lax.fori_loop(0, LINE, sent, 0)
        rider.finish()
        for i in (1, 2, 3):
            self.ret_copy(i).wait_send()
            self.ret_copy(i, False).wait_recv()


def split(refs, *counts):
    out, at = [], 0
    for count in counts:
        out.append(refs[at : at + count])
        at += count
    return out + [refs[at:]]


def expert_forward_kernel(spread, parts, ride, out, *refs):
    weights_in, shards, outs, whole, scratch, line_refs, sems, ride_refs = split(
        refs, 3 * parts, 9 if ride else 0, 4, 6 if ride else 0, 3 * parts, 5, 7)
    (g_all, u_all, keep_sem, load_sem), ride_refs = ride_refs[:4], ride_refs[4:]
    returned, x_keep, g_keep, u_keep = outs
    gate, up, down = scratch[:parts], scratch[parts : 2 * parts], scratch[2 * parts :]
    x, part, stage, arrived, final = line_refs
    local, _, _, _, width = x.shape
    rows = 2 * CAP
    p = Place(spread)
    line = Line(p, x, part, stage, arrived, final, returned, sems)
    rider = Spread(p, shards, whole, ride_refs) if ride else Rider()

    def load(i):
        return pltpu.make_async_copy(weights_in[i], scratch[i], load_sem.at[i])

    for i in range(3 * parts):
        load(i).start()

    def keep_x(s):
        return pltpu.make_async_copy(x.at[:, s], x_keep.at[:, s], keep_sem.at[0, s])

    def keep_g(s):
        return pltpu.make_async_copy(g_all.at[s], g_keep.at[s], keep_sem.at[1, s])

    def keep_u(s):
        return pltpu.make_async_copy(u_all.at[s], u_keep.at[s], keep_sem.at[2, s])

    def kept(s):
        keep_x(s).start()
        keep_g(s).start()
        keep_u(s).start()

    def compute(s, pair):
        at = pl.multiple_of(pair * rows, rows)

        def one(l, carry):
            rows_in = x[l, s, pl.ds(2 * pair, 2)].reshape(rows, width)
            total = jnp.zeros((rows, width), F32)
            for q in range(parts):
                cols = gate[q].shape[2]
                here = slice(q * cols, (q + 1) * cols)
                g = dot_nn(rows_in, gate[q][l])
                u = dot_nn(rows_in, up[q][l])
                g_all[s, l, pl.ds(at, rows), here] = g
                u_all[s, l, pl.ds(at, rows), here] = u
                act = (g * jax.nn.sigmoid(g) * u).astype(BF16)
                total = total + dot_nn(act, down[q][l])
            part[s, l, pl.ds(2 * pair, 2)] = total.reshape(2, CAP, width)
            return carry

        lax.fori_loop(0, local, one, 0)

    class Loaded(Rider):
        partners = rider.partners
        after_first, after_line, after_relay, finish = (
            rider.after_first, rider.after_line, rider.after_relay, rider.finish)

        def begin(self):
            rider.begin()
            for i in range(3 * parts):
                load(i).wait()

    line.run(out, compute, kept, lambda: None, Loaded())
    for s in range(LINE):
        keep_x(s).wait()
        keep_g(s).wait()
        keep_u(s).wait()


def expert_backward_kernel(spread, parts, ride, out, *refs):
    loads_in, dense, outs, quarter, loads, line_refs, sems, rest = split(
        refs, 3 + 3 * parts, 2 if ride else 0, 1 + 3 * parts, 1 if ride else 0, 3 + 3 * parts, 5, 7)
    (act_all, gg_all, gu_all), grads, (load_sem, grad_sem), ride_refs = split(rest, 3, 3 * parts, 2)
    returned, grads_out = outs[0], outs[1:]
    x_in, g_all, u_all = loads[:3]
    gate, up, down = loads[3 : 3 + parts], loads[3 + parts : 3 + 2 * parts], loads[3 + 2 * parts :]
    x, part, stage, arrived, final = line_refs
    local, _, _, _, width = x.shape
    rows = 2 * CAP
    p = Place(spread)
    line = Line(p, x, part, stage, arrived, final, returned, sems)
    rider = Halve(p, dense, quarter[0], ride_refs) if ride else Rider()

    def load(i):
        return pltpu.make_async_copy(loads_in[i], loads[i], load_sem.at[i])

    def store(i, l):
        return pltpu.make_async_copy(grads[i].at[l], grads_out[i].at[l], grad_sem.at[i, l])

    for i in range(3 + 3 * parts):
        load(i).start()

    def compute(s, pair):
        at = pl.multiple_of(pair * rows, rows)
        into = pl.ds(pl.multiple_of((2 * s + pair) * rows, rows), rows)

        def one(l, carry):
            rows_in = x[l, s, pl.ds(2 * pair, 2)].reshape(rows, width)
            total = jnp.zeros((rows, width), F32)
            for q in range(parts):
                cols = gate[q].shape[2]
                here = slice(q * cols, (q + 1) * cols)
                g, u = g_all[s, l, pl.ds(at, rows), here], u_all[s, l, pl.ds(at, rows), here]
                g_act = dot_nt(rows_in, down[q][l])
                sigma = jax.nn.sigmoid(g)
                swish = g * sigma
                gg = (g_act * u * sigma * (1.0 + g * (1.0 - sigma))).astype(BF16)
                gu = (g_act * swish).astype(BF16)
                act_all[l, into, here] = (swish * u).astype(BF16)
                gg_all[l, into, here] = gg
                gu_all[l, into, here] = gu
                total = total + dot_nt(gg, gate[q][l]) + dot_nt(gu, up[q][l])
            part[s, l, pl.ds(2 * pair, 2)] = total.reshape(2, CAP, width)
            return carry

        lax.fori_loop(0, local, one, 0)

    def weights():
        def one(l, carry):
            x_rows = x_in[l].reshape(2 * LINE * rows, width)
            g_rows = x[l].reshape(2 * LINE * rows, width)
            for q in range(parts):
                cols = gate[q].shape[2]
                here = slice(q * cols, (q + 1) * cols)
                for i, value in (
                    (q, dot_tn(x_rows, gg_all[l, :, here])),
                    (parts + q, dot_tn(x_rows, gu_all[l, :, here])),
                    (2 * parts + q, dot_tn(act_all[l, :, here], g_rows)),
                ):
                    grads[i][l] = value.astype(grads[i].dtype)
                    store(i, l).start()
            return carry

        lax.fori_loop(0, local, one, 0)

    class Loaded(Rider):
        partners = rider.partners
        after_first, after_line, after_relay, finish = (
            rider.after_first, rider.after_line, rider.after_relay, rider.finish)

        def begin(self):
            rider.begin()
            for i in range(3 + 3 * parts):
                load(i).wait()

    line.run(out, compute, lambda s: None, weights, Loaded())
    for i in range(3 * parts):
        for l in range(local):
            store(i, l).wait()


def remote_params(call_id):
    return pltpu.CompilerParams(collective_id=call_id, has_side_effects=True, vmem_limit_bytes=61 * 2**20)


def struct(shape, dtype):
    return jax.ShapeDtypeStruct(tuple(shape), dtype)


def expert_forward(spread, call_id, out, weights, ride=None):
    parts = len(weights) // 3
    _, local, cap, width = out.shape
    columns = sum(w.shape[2] for w in weights[:parts])
    kept = (LINE, local, 4 * cap, columns)
    outs = [struct(out.shape, BF16), struct((local, LINE, 4, cap, width), BF16), struct(kept, F32), struct(kept, F32)]
    scratch = [pltpu.VMEM(w.shape, BF16) for w in weights] + Line.scratch(local, width)
    scratch += [pltpu.VMEM(kept, F32), pltpu.VMEM(kept, F32), dma(3, LINE), dma(len(weights))]
    more = ()
    if ride:
        more = ride
        count = LINE * spread
        outs += [struct((count * s.shape[0], s.shape[1]), BF16) for s in ride[3:6]]
        outs += [struct(w.shape, BF16) for w in ride[6:]]
        scratch += Spread.scratch(count)
    return pl.pallas_call(
        functools.partial(expert_forward_kernel, spread, parts, ride is not None),
        out_shape=outs,
        in_specs=[VMEM] + [ANY] * (len(weights) + len(more)),
        out_specs=[VMEM] + [ANY] * (len(outs) - 1),
        scratch_shapes=scratch,
        compiler_params=remote_params(call_id),
    )(out, *weights, *more)


def expert_backward(spread, call_id, out, kept, weights, ride=None):
    parts = len(weights) // 3
    _, local, cap, width = out.shape
    columns = sum(w.shape[2] for w in weights[:parts])
    loads = list(kept) + list(weights)
    grads = [(w.shape, F32 if i % parts == 0 else BF16) for i, w in enumerate(weights)]
    wide = pltpu.VMEM((local, LINE * 4 * cap, columns), BF16)
    outs = [struct(out.shape, BF16)] + [struct(*g) for g in grads]
    scratch = [pltpu.VMEM(a.shape, a.dtype) for a in loads] + Line.scratch(local, width)
    scratch += [wide] * 3 + [pltpu.VMEM(*g) for g in grads] + [dma(len(loads)), dma(len(grads), local)]
    more = ()
    if ride:
        more = ride
        depths = [g.shape[0] // (LINE * spread) for g in ride]
        outs.append(struct((LINE, spread, sum(depths) // 2, width // 2), F32))
        scratch += Halve.scratch(spread, depths, width)
    return pl.pallas_call(
        functools.partial(expert_backward_kernel, spread, parts, ride is not None),
        out_shape=outs,
        in_specs=[VMEM] + [ANY] * (len(loads) + len(more)),
        out_specs=[VMEM] + [ANY] * len(grads) + [VMEM] * len(more[:1]),
        scratch_shapes=scratch,
        compiler_params=remote_params(call_id),
    )(out, *loads, *more)


def from_partner(array, shift, spread, groups):
    pairs = [
        (t * spread + (f + shift) % spread, t * spread + f) for t in range(groups) for f in range(spread)
    ]
    return lax.ppermute(array, "dp", pairs)


def to_partner(array, shift, spread, groups):
    pairs = [
        (t * spread + f, t * spread + (f + shift) % spread) for t in range(groups) for f in range(spread)
    ]
    return lax.ppermute(array, "dp", pairs)


def pair_weights(shard, axis, spread):
    parts = [shard] + [from_partner(shard, i, spread, LINE) for i in range(1, spread)]
    if shard.shape[axis] % 128:
        return [jnp.concatenate(parts, axis=axis)]
    return parts


def pair_sum(parts, axis, spread):
    if len(parts) == 1 and spread > 1:
        parts = jnp.split(parts[0], spread, axis=axis)
    total = parts[0]
    for i in range(1, spread):
        total = total + to_partner(parts[i].astype(BF16), i, spread, LINE).astype(F32)
    return total


class LineGather:
    def __init__(self, place, shards, quarters, sems):
        self.p, self.shards, self.quarters = place, shards, quarters
        self.send, self.recv = sems

    @staticmethod
    def shapes(shards):
        (a, wide), (b, _), (c, narrow) = (s.shape for s in shards)
        return [(LINE, a // 2, wide // 2), (LINE, b // 2, wide // 2), (LINE, c, narrow)]

    @staticmethod
    def scratch():
        return [dma(2, LINE, 3), dma(LINE, 3)]

    def copy(self, kind, up, t):
        at = self.quarters[kind].at[t]
        return remote(at, at, self.send.at[up, t, kind], self.recv.at[t, kind], self.p.on_line(up))

    def begin(self):
        p = self.p
        for kind in (0, 1):
            half, wide = self.quarters[kind].shape[1:]
            self.quarters[kind][p.t] = self.shards[kind][
                pl.ds(pl.multiple_of(p.y * half, 16), half), pl.ds(pl.multiple_of(p.c * wide, 128), wide)]
        self.quarters[2][p.t] = self.shards[2][...]
        for up, there in ((0, p.below), (1, p.above)):

            @pl.when(there)
            def _(up=up):
                for kind in range(3):
                    self.copy(kind, up, p.t).start()

    def step(self, k, then):
        p = self.p
        for up, there, onward in ((0, p.t + k < LINE, p.below), (1, p.t - k >= 0, p.above)):
            t = p.t - k if up else p.t + k

            @pl.when(there)
            def _(up=up, onward=onward, t=t):
                for kind in range(3):
                    self.copy(kind, up, t).wait_recv()

                @pl.when(onward)
                def _():
                    for kind in range(3):
                        self.copy(kind, up, t).start()

                then(t)

    def finish(self):
        p = self.p

        def line(t, carry):
            for up, mine in ((0, jnp.logical_and(p.below, t >= p.t)), (1, jnp.logical_and(p.above, t <= p.t))):

                @pl.when(mine)
                def _(up=up):
                    for kind in range(3):
                        self.copy(kind, up, t).wait_send()

            return carry

        lax.fori_loop(0, LINE, line, 0)


class Spread:
    def __init__(self, place, given, whole, sems):
        self.p = place
        self.quarters, self.shards, self.own = given[:3], given[3:6], given[6:]
        self.whole, self.other = whole[:3], whole[3:]
        (self.x_send, self.x_recv, self.y_send, self.y_recv, self.c_send, self.c_recv, self.l_sem, self.s_sem,
         self.w_send, self.w_recv) = sems
        self.partners = [place.beside]

    @staticmethod
    def scratch(count):
        return [dma(LINE, 3), dma(LINE, 3), dma(count, 2), dma(count, 2), dma(count, 2, 2), dma(count, 2, 2),
                dma(LINE, 3), dma(3), dma(3), dma(3)]

    def region(self, kind, s, y, c):
        depth = self.shards[kind].shape[0]
        if kind == 2:
            return self.whole[2].at[pl.ds(pl.multiple_of(s * depth, 16), depth)]
        half, wide = depth // 2, self.shards[kind].shape[1] // 2
        return self.whole[kind].at[
            pl.ds(pl.multiple_of(s * depth + y * half, 16), half), pl.ds(pl.multiple_of(c * wide, 128), wide)]

    def mine(self, kind, s):
        return self.region(kind, s, self.p.y, self.p.c)

    def place_of(self, t):
        return t * self.p.spread + self.p.f

    def beside_of(self, t):
        return t * self.p.spread + 1 - self.p.f

    def x_copy(self, kind, t):
        return remote(self.quarters[kind].at[t], self.mine(kind, self.place_of(t)), self.x_send.at[t, kind],
                      self.x_recv.at[t, kind], self.p.beside)

    def x_came(self, kind, t):
        return remote(self.quarters[kind].at[t], self.mine(kind, self.beside_of(t)), self.x_send.at[t, kind],
                      self.x_recv.at[t, kind], self.p.beside)

    def y_copy(self, kind, src, s):
        return remote(src, self.mine(kind, s), self.y_send.at[s, kind], self.y_recv.at[s, kind], self.p.across)

    def y_came(self, kind, s):
        at = self.region(kind, s, 1 - self.p.y, self.p.c)
        return remote(at, at, self.y_send.at[s, kind], self.y_recv.at[s, kind], self.p.across)

    def c_copy(self, kind, src, s, y):
        return remote(src, self.region(kind, s, y, self.p.c), self.c_send.at[s, y, kind], self.c_recv.at[s, y, kind],
                      self.p.sibling)

    def c_came(self, kind, s, y):
        at = self.region(kind, s, y, 1 - self.p.c)
        return remote(at, at, self.c_send.at[s, y, kind], self.c_recv.at[s, y, kind], self.p.sibling)

    def local(self, kind, t):
        return pltpu.make_async_copy(self.quarters[kind].at[t], self.mine(kind, self.place_of(t)), self.l_sem.at[t, kind])

    def shard(self, kind):
        depth = self.shards[kind].shape[0]
        at = self.whole[kind].at[pl.ds(pl.multiple_of(self.p.d * depth, 16), depth)]
        return pltpu.make_async_copy(self.shards[kind], at, self.s_sem.at[kind])

    def weight(self, i):
        return remote(self.own[i], self.other[i], self.w_send.at[i], self.w_recv.at[i], self.p.beside)

    def own_shard(self):
        for kind in range(3):
            self.shard(kind).start()

    def from_line(self, t):
        for kind in range(3):
            self.x_copy(kind, t).start()

        @pl.when(t != self.p.t)
        def _():
            for kind in range(3):
                self.local(kind, t).start()
            for kind in (0, 1):
                self.y_copy(kind, self.quarters[kind].at[t], self.place_of(t)).start()
                self.c_copy(kind, self.quarters[kind].at[t], self.place_of(t), self.p.y).start()

    def begin(self):
        self.own_shard()
        along(self.p, self.from_line)
        for i in range(len(self.own)):
            self.weight(i).start()

    def after_first(self):
        pass

    def after_line(self):
        def body(t):
            for kind in range(3):
                self.x_came(kind, t).wait_recv()
            for kind in (0, 1):
                s = self.beside_of(t)
                self.y_copy(kind, self.mine(kind, s), s).start()
                self.c_copy(kind, self.mine(kind, s), s, self.p.y).start()

        along(self.p, body)

    def after_relay(self):
        p = self.p

        def across(s):
            for kind in (0, 1):
                at = self.region(kind, s, 1 - p.y, p.c)
                self.y_came(kind, s).wait_recv()
                self.c_copy(kind, at, s, 1 - p.y).start()

        along(p, lambda t: across(self.place_of(t)), start=1)
        along(p, lambda t: across(self.beside_of(t)))

    def finish(self):
        p = self.p
        for kind in range(3):
            self.shard(kind).wait()
        for i in range(len(self.own)):
            self.weight(i).wait()

        def line(t, carry):
            for kind in range(3):
                self.x_copy(kind, t).wait_send()

            @pl.when(t != p.t)
            def _():
                for kind in range(3):
                    self.local(kind, t).wait()

            for f in range(p.spread):
                s = t * p.spread + f

                @pl.when(s != p.d)
                def _(s=s):
                    for kind in (0, 1):
                        self.y_came(kind, s).wait_send()
                        for y in (0, 1):
                            self.c_came(kind, s, y).wait_send()
                            self.c_came(kind, s, y).wait_recv()

            return carry

        lax.fori_loop(0, LINE, line, 0)


def dense_gather_kernel(spread, *refs):
    p = Place(spread)
    shards0, shards1, (routes,), whole, quarters1, (routes_all,), quarters0, rest = split(refs, 3, 3, 1, 3, 3, 1, 3)
    sems0, sems1, (r_send, r_recv), spread_sems = split(rest, 2, 2, 2)
    line0 = LineGather(p, shards0, quarters0, sems0)
    line1 = LineGather(p, shards1, quarters1, sems1)
    spreading = Spread(p, tuple(quarters0) + tuple(shards0), whole, spread_sems)
    greet(p.mates[1:] + [p.beside], p)

    def route_copy(i, row):
        return remote(routes, routes_all.at[row], r_send.at[i], r_recv.at[row], p.mates[i])

    routes_all[p.e] = routes[...]
    line0.begin()
    for i in (1, 2, 3):
        route_copy(i, p.e).start()
    spreading.own_shard()
    spreading.from_line(p.t)
    line1.begin()

    def step(k, carry):
        line0.step(k, spreading.from_line)
        line1.step(k, lambda t: None)
        return carry

    lax.fori_loop(1, LINE, step, 0)
    spreading.after_line()
    spreading.after_relay()
    spreading.finish()
    line0.finish()
    line1.finish()
    for i in (1, 2, 3):
        route_copy(i, p.e).wait_send()
        route_copy(i, p.mates[i][1]).wait_recv()


def dense_gather(spread, call_id, shards0, shards1, routes):
    count = spread * LINE
    quarters = LineGather.shapes(shards0)
    outs = [struct((count * s.shape[0], s.shape[1]), s.dtype) for s in shards0]
    outs += [struct(q, BF16) for q in quarters] + [struct((4,) + routes.shape, routes.dtype)]
    scratch = [pltpu.VMEM(q, BF16) for q in quarters] + LineGather.scratch() * 2 + [dma(4), dma(4)]
    return pl.pallas_call(
        functools.partial(dense_gather_kernel, spread),
        out_shape=outs,
        in_specs=[VMEM] * 7,
        out_specs=[ANY] * 3 + [VMEM] * 4,
        scratch_shapes=scratch + Spread.scratch(count),
        compiler_params=remote_params(call_id),
    )(*shards0, *shards1, routes)


class Halve:
    def __init__(self, place, grads, quarter, scratch):
        self.p, self.grads, self.quarter = place, grads, quarter
        (self.mine, self.core, self.stage, self.came, self.l_sem, self.a_send, self.a_recv, self.y_send,
         self.y_recv) = scratch
        self.depths = [g.shape[0] // (LINE * place.spread) for g in grads]
        self.wide = grads[0].shape[1] // 2
        self.partners = []

    @staticmethod
    def scratch(spread, depths, width):
        count, rows, wide = LINE * spread, sum(depths) // 2, width // 2
        half = pltpu.VMEM((LINE, spread, rows, wide), BF16)
        everything = pltpu.VMEM((count * sum(depths), wide), BF16)
        return [everything, everything, half, half, dma(2), dma(2), dma(2), dma(LINE), dma(LINE)]

    def rows_of(self, kind):
        first = 0 if kind == 0 else self.grads[0].shape[0]
        return slice(first, first + self.grads[kind].shape[0])

    def lanes(self, c):
        return pl.ds(pl.multiple_of(c * self.wide, 128), self.wide)

    def local(self, kind):
        return pltpu.make_async_copy(
            self.grads[kind].at[:, self.lanes(self.p.c)], self.mine.at[self.rows_of(kind)], self.l_sem.at[kind])

    def a_copy(self, kind):
        return remote(self.grads[kind].at[:, self.lanes(1 - self.p.c)], self.core.at[self.rows_of(kind)],
                      self.a_send.at[kind], self.a_recv.at[kind], self.p.sibling)

    def y_copy(self, t):
        return remote(self.stage.at[t], self.came.at[t], self.y_send.at[t], self.y_recv.at[t], self.p.across)

    def pieces(self, t, f, y):
        s, row = t * self.p.spread + f, 0
        for kind, depth in enumerate(self.depths):
            at = self.rows_of(kind).start + s * depth + y * (depth // 2)
            here = pl.ds(pl.multiple_of(at, 16), depth // 2)
            yield slice(row, row + depth // 2), self.mine[here, :].astype(F32) + self.core[here, :].astype(F32)
            row += depth // 2

    def order(self, i):
        return jnp.where(self.p.t >= LINE // 2, i, LINE - 1 - i)

    def begin(self):
        for kind in (0, 1):
            self.a_copy(kind).start()
            self.local(kind).start()

    def after_first(self):
        for kind in (0, 1):
            self.a_copy(kind).wait_recv()
            self.local(kind).wait()

        def body(i, carry):
            t = self.order(i)
            for f in range(self.p.spread):
                for where, value in self.pieces(t, f, 1 - self.p.y):
                    self.stage[t, f, where] = value.astype(BF16)
            self.y_copy(t).start()
            return carry

        lax.fori_loop(0, LINE, body, 0)

        def own(t, carry):
            for f in range(self.p.spread):
                for where, value in self.pieces(t, f, self.p.y):
                    self.quarter[t, f, where] = value
            return carry

        lax.fori_loop(0, LINE, own, 0)

    def add(self, t):
        self.y_copy(t).wait_recv()
        self.quarter[t] = self.quarter[t] + self.came[t].astype(F32)

    def after_line(self):
        pass

    def after_relay(self):
        lax.fori_loop(0, LINE, lambda i, carry: (self.add(self.order(i)), carry)[1], 0)

    def finish(self):
        for kind in (0, 1):
            self.a_copy(kind).wait_send()
        lax.fori_loop(0, LINE, lambda t, carry: (self.y_copy(t).wait_send(), carry)[1], 0)


class LineSum:
    def __init__(self, place, depths, quarter, sums, scratch):
        self.p, self.depths, self.quarter, self.sums = place, depths, quarter, sums
        (self.stage, self.came, self.stage_x, self.came_x, self.z_send, self.z_recv, self.x_send, self.x_recv,
         self.e_send, self.e_recv) = scratch
        self.wide = sums[0].shape[1] // 2

    @staticmethod
    def scratch(spread, depths, width):
        rows, wide = sum(depths) // 2, width // 2
        return [
            pltpu.VMEM((LINE, spread, rows, wide), BF16),
            pltpu.VMEM((2, LINE, spread, rows, wide), BF16),
            pltpu.VMEM((rows, wide), BF16),
            pltpu.VMEM((rows, wide), BF16),
            dma(LINE), dma(2, LINE), dma(1), dma(1), dma(3, 2), dma(3, 2),
        ]

    def lanes(self, c):
        return pl.ds(pl.multiple_of(c * self.wide, 128), self.wide)

    def z_copy(self, up, t):
        return remote(self.stage.at[t], self.came.at[up, t], self.z_send.at[t], self.z_recv.at[up, t], self.p.on_line(up))

    def x_copy(self):
        return remote(self.stage_x, self.came_x, self.x_send.at[0], self.x_recv.at[0], self.p.beside)

    def e_copy(self, i, kind, y, c):
        half = self.depths[kind] // 2
        at = self.sums[kind].at[pl.ds(pl.multiple_of(y * half, 8), half), self.lanes(c)]
        return remote(at, at, self.e_send.at[i, kind], self.e_recv.at[i, kind], self.p.across if i == 0 else self.p.sibling)

    def start(self, t):
        p = self.p
        for up, mine in ((1, jnp.logical_and(p.t == 0, t > 0)), (0, jnp.logical_and(p.t == LINE - 1, t < LINE - 1))):

            @pl.when(mine)
            def _(up=up):
                self.stage[t] = self.quarter[t].astype(BF16)
                self.z_copy(up, t).start()

    def relay(self, stage):
        p = self.p
        for up, mine in ((1, p.t == stage), (0, p.t == LINE - 1 - stage)):

            @pl.when(mine)
            def _(up=up):
                def one(n, carry):
                    t = LINE - 1 - n if up else n
                    self.z_copy(up, t).wait_recv()
                    self.stage[t] = (self.quarter[t] + self.came[up, t].astype(F32)).astype(BF16)
                    self.z_copy(up, t).start()
                    return carry

                lax.fori_loop(0, LINE - 1 - stage, one, 0)

    def after_z(self):
        p = self.p

        for up, there in ((1, p.below), (0, p.above)):

            @pl.when(there)
            def _(up=up):
                self.z_copy(up, p.t).wait_recv()
                self.quarter[p.t] = self.quarter[p.t] + self.came[up, p.t].astype(F32)

        self.stage_x[...] = self.quarter[p.t, 1 - p.f].astype(BF16)
        self.x_copy().start()

    def after_x(self):
        p = self.p
        self.x_copy().wait_recv()
        row = 0
        for kind, depth in enumerate(self.depths):
            half = depth // 2
            value = self.quarter[p.t, p.f, row : row + half] + self.came_x[row : row + half].astype(F32)
            self.sums[kind][pl.ds(pl.multiple_of(p.y * half, 8), half), self.lanes(p.c)] = value
            row += half
        for i in (0, 1):
            for kind in (0, 1):
                self.e_copy(i, kind, p.y, p.c).start()

    def finish(self):
        p = self.p
        for kind in (0, 1):
            self.e_copy(0, kind, 1 - p.y, p.c).wait_recv()
            self.e_copy(2, kind, 1 - p.y, p.c).start()
        for kind in (0, 1):
            self.e_copy(0, kind, p.y, p.c).wait_send()
            self.e_copy(1, kind, p.y, p.c).wait_send()
            self.e_copy(1, kind, p.y, 1 - p.c).wait_recv()
            self.e_copy(2, kind, 1 - p.y, p.c).wait_send()
            self.e_copy(2, kind, 1 - p.y, 1 - p.c).wait_recv()
        self.x_copy().wait_send()

        def body(t, carry):
            @pl.when(t != p.t)
            def _():
                self.z_copy(0, t).wait_send()

            return carry

        lax.fori_loop(0, LINE, body, 0)


class SmallSum:
    def __init__(self, place, grads, total, scratch):
        self.p, self.grads, self.total = place, grads, total
        self.stage, self.came, self.send, self.recv = scratch
        p = place
        near = (p.d + p.spread - 2 * p.spread * lax.rem(p.t, 2), p.e)
        self.far = (lax.rem(p.d + 2 * p.spread, LINE * p.spread), p.e)
        self.partners = [p.sibling, p.across, p.beside, near, self.far]

    @staticmethod
    def scratch(rows, width):
        half = pltpu.VMEM((5, rows, width // 2), F32)
        return [half, half, dma(6), dma(6)]

    def lanes(self, c):
        wide = self.grads.shape[1] // 2
        return pl.ds(pl.multiple_of(c * wide, 128), wide)

    def copy(self, i):
        src = self.grads.at[:, self.lanes(1 - self.p.c)] if i == 0 else self.stage.at[i]
        return remote(src, self.came.at[i], self.send.at[i], self.recv.at[i], self.partners[i])

    def last(self, c):
        at = self.total.at[:, self.lanes(c)]
        return remote(at, at, self.send.at[5], self.recv.at[5], self.p.sibling)

    def step(self, i):
        if i == 0:
            self.copy(0).start()
            return
        self.copy(i - 1).wait_recv()
        mine = self.grads[:, self.lanes(self.p.c)] if i == 1 else self.stage[i - 1]
        value = mine + self.came[i - 1]
        if i < 5:
            self.stage[i] = value
            self.copy(i).start()
        else:
            self.total[:, self.lanes(self.p.c)] = value
            self.last(self.p.c).start()

    def finish(self):
        for i in range(5):
            self.copy(i).wait_send()
        self.last(self.p.c).wait_send()
        self.last(1 - self.p.c).wait_recv()


def dense_reduce_kernel(spread, depths, small, qkv0, out0, quarter1, small_sum, *refs):
    p = Place(spread)
    sums0, sums1, (mine0, mine1), halve_refs, line0, line1, small_refs = split(refs, 2, 2, 2, 9, 10, 10)
    halve = Halve(p, (qkv0, out0), mine0, halve_refs)
    sum0 = LineSum(p, depths, mine0, sums0, line0)
    sum1 = LineSum(p, depths, mine1, sums1, line1)
    little = SmallSum(p, small, small_sum, small_refs)
    greet([p.sibling, p.across, p.beside, little.far], p)
    halve.begin()
    little.step(0)
    mine1[...] = quarter1[...]
    for t in range(LINE):
        sum1.start(t)
    little.step(1)
    halve.after_first()
    little.step(2)
    for stage in range(1, LINE - 1):
        sum1.relay(stage)
    little.step(3)
    sum1.after_z()

    def arrive(i, carry):
        t = halve.order(i)
        halve.add(t)
        sum0.start(t)
        return carry

    lax.fori_loop(0, LINE, arrive, 0)
    little.step(4)
    sum1.after_x()
    for stage in range(1, LINE - 1):
        sum0.relay(stage)
    little.step(5)
    sum0.after_z()
    sum1.finish()
    sum0.after_x()
    halve.finish()
    little.finish()
    sum0.finish()


def dense_reduce(spread, call_id, small, grads0, quarter1):
    count = LINE * spread
    depths = [g.shape[0] // count for g in grads0]
    width = grads0[0].shape[1]
    shards = [struct((depth, width), F32) for depth in depths]
    line = LineSum.scratch(spread, depths, width)
    mine = pltpu.VMEM(quarter1.shape, F32)
    return pl.pallas_call(
        functools.partial(dense_reduce_kernel, spread, depths),
        out_shape=[struct(small.shape, F32)] + shards + shards,
        in_specs=[VMEM, ANY, ANY, VMEM],
        out_specs=[VMEM] * 5,
        scratch_shapes=[mine, mine] + Halve.scratch(spread, depths, width) + line + line + SmallSum.scratch(*small.shape),
        compiler_params=remote_params(call_id),
    )(small, *grads0, quarter1)


def per_device(
    tokens, seq_lengths, block_perm, routes, norm_gains, w_qkv, w_out, w_router, w_residual, w_const, v_const,
    w_gate, w_up, w_down, cotangent,
):
    rows, width = tokens.shape
    owners = lax.axis_size("expert")
    shards = lax.axis_size("dp")
    spread = shards // LINE
    local = w_gate.shape[1]
    experts = local * owners
    layers = routes.shape[0]
    slots = experts * CAP
    place = lax.axis_index("expert")

    my_place = jnp.sum(jnp.where(jnp.arange(owners) == place, block_perm[0], 0))
    lengths = lax.dynamic_index_in_dim(seq_lengths[0], place, 0, keepdims=False)
    order = jnp.arange(lengths.shape[0])
    ends = jnp.sum(jnp.where(order[:, None] <= order[None, :], lengths[:, None], 0), axis=0)
    doc = jnp.sum((jnp.arange(rows)[:, None] >= ends[None, :]).astype(jnp.int32), axis=1)
    doc_col, doc_row = doc[:, None], doc[None, :]

    depth = w_out.shape[1]
    small = jnp.concatenate(
        [
            w_router, w_const[:, 0], w_const[:, 1], jnp.swapaxes(norm_gains, 1, 2), jnp.swapaxes(v_const, 1, 2),
            jnp.zeros((layers, depth, 108), F32),
        ],
        axis=2,
    ).astype(BF16)
    qkv_t = jnp.swapaxes(w_qkv, 1, 2).astype(BF16)
    out_rows = w_out.astype(BF16)
    in_kernels = spread == 2 and owners == 4 and qkv_t.shape[1] % 32 == 0 and depth % 32 == 0
    if in_kernels:
        packed_routes = jnp.zeros((8, 256), jnp.int32).at[: 2 * layers, :rows].set(
            jnp.swapaxes(routes, 1, 2).reshape(2 * layers, rows))
        shards = [(qkv_t[l], out_rows[l], small[l]) for l in range(layers)]
        *gathered, routes_all = dense_gather(spread, 4, *shards, packed_routes)
        dense = [(gathered[2], gathered[0], gathered[1])]
        picked = lax.dynamic_index_in_dim(routes_all, my_place, 0, keepdims=False)
        my_routes = jnp.swapaxes(picked[: 2 * layers, :rows].reshape(layers, 2, rows), 1, 2)
    else:
        all_routes = lax.all_gather(routes, "expert", axis=0)
        my_routes = lax.dynamic_index_in_dim(all_routes, my_place, 0, keepdims=False)
        qkv_all = lax.all_gather(qkv_t, "dp", axis=1, tiled=True)
        out_all = lax.all_gather(out_rows, "dp", axis=1, tiled=True)
        small_all = lax.all_gather(small, "dp", axis=1, tiled=True)
        dense = [(small_all[l], qkv_all[l], out_all[l]) for l in range(layers)]

    own = [[w[l].astype(BF16) for w in (w_gate, w_up, w_down)] for l in range(layers)]
    weights = []
    for l in range(1 if in_kernels else layers):
        weights.append([part for w, axis in zip(own[l], (2, 2, 1)) for part in pair_weights(w, axis, spread)])
    w_res = jnp.zeros((128, 128), F32).at[: w_residual.shape[0], : w_residual.shape[1]].set(w_residual)

    cols = ((rows, width), F32)
    attention = [((rows, width), BF16), ((rows, 3 * width), BF16), ((HEADS, rows, rows), F32), ((rows, width), BF16)]
    per_token, sent = ((rows, 128), F32), ((slots, width), BF16)

    def group(array):
        return array.reshape(owners, local, CAP, width)

    attn_in0, qkv0, probs0, attn0, mid0, logits0, stat0, out = local_call(
        first_kernel, experts, (tokens, *dense[0], doc_col, doc_row, my_routes[0]),
        attention + [cols, per_token, per_token, sent])
    ride = (*gathered[3:], *shards[1], *own[1]) if in_kernels else None
    ret0, *kept0 = expert_forward(spread, 0, group(out), weights[0], ride)
    if in_kernels:
        kept0, (qkv_all, out_all, small_all), partner = kept0[:3], kept0[3:6], kept0[6:]
        dense.append((small_all, qkv_all, out_all))
        weights.append([w for pair in zip(own[1], partner) for w in pair])
    ret0 = ret0.reshape(slots, width)
    stream1, attn_in1, qkv1, probs1, attn1, mid1, stat1, out = local_call(
        middle_kernel, experts,
        (mid0, dense[0][0], stat0, ret0, *dense[1], doc_col, doc_row, my_routes[1], logits0, w_res),
        [cols] + attention + [cols, per_token, sent])
    ret1, *kept1 = expert_forward(spread, 1, group(out), weights[1])
    ret1 = ret1.reshape(slots, width)

    small_grads = ((24, width), F32)
    output, g_small1, extra, out, small_grad1, res_grad = local_call(
        turn_kernel, experts, (mid1, dense[1][0], stat1, ret1, cotangent, logits0, w_res),
        [((rows, width), BF16), per_token, per_token, sent, small_grads, ((128, 128), F32)])
    back, *expert_grads1 = expert_backward(spread, 2, group(out), kept1, weights[1])
    grad_type = BF16 if in_kernels else F32
    dense_grads = [((3 * width, width), grad_type), ((width, width), grad_type), small_grads]
    attention_scratch = [((rows, 3 * width), BF16), ((rows, width), BF16)]
    qkv_grad1, out_grad1, small_grad1, grad, g_small0, out, small_grad0 = local_call(
        between_kernel, experts,
        (cotangent, back.reshape(slots, width), g_small1, stat1, mid1, dense[1][0], stream1, dense[1][1], dense[1][2],
         attn_in1, qkv1, probs1, attn1, small_grad1, mid0, dense[0][0], stat0, ret0, extra),
        dense_grads + [cols, per_token, sent, small_grads], attention_scratch)
    ride = (qkv_grad1, out_grad1) if in_kernels else None
    back, *expert_grads0 = expert_backward(spread, 3, group(out), kept0, weights[0], ride)
    if in_kernels:
        *expert_grads0, quarter1 = expert_grads0
    qkv_grad0, out_grad0, small_grad0, tokens_grad = local_call(
        last_kernel, experts,
        (grad, back.reshape(slots, width), g_small0, stat0, mid0, dense[0][0], tokens, dense[0][1], dense[0][2],
         attn_in0, qkv0, probs0, attn0, small_grad0),
        dense_grads + [cols], attention_scratch)

    expert_out = []
    for axis, at in ((2, 0), (2, 1), (1, 2)):
        per_layer = []
        for grads in (expert_grads0, expert_grads1):
            n = len(grads) // 3
            per_layer.append(pair_sum(grads[at * n : (at + 1) * n], axis, spread))
        expert_out.append(jnp.stack(per_layer))
    gate_grad, up_grad, down_grad = expert_out
    packed = jnp.concatenate([small_grad0, small_grad1, jnp.pad(res_grad[:16], ((0, 0), (0, width - 128)))])
    if in_kernels:
        packed, qkv_sum0, out_sum0, qkv_sum1, out_sum1 = dense_reduce(
            spread, 5, packed, (qkv_grad0, out_grad0), quarter1)
        qkv_grad = jnp.stack([qkv_sum0, qkv_sum1])
        out_grad = jnp.stack([out_sum0, out_sum1])
    else:
        packed = lax.psum(packed, ("dp", "expert"))
        qkv_grad, out_grad = (
            lax.psum(lax.psum_scatter(jnp.stack(pair), "dp", scatter_dimension=1, tiled=True), "expert")
            for pair in ((qkv_grad0, qkv_grad1), (out_grad0, out_grad1)))
    mine = lax.dynamic_slice_in_dim(packed, lax.axis_index("dp") * depth, depth, axis=1)
    mine = jnp.stack([mine[:24], mine[24:48]])
    router_grad = jnp.swapaxes(mine[:, :CONST0], 1, 2)
    const_grad = jnp.swapaxes(mine[:, CONST0:GAIN0].reshape(layers, 2, 2, depth), 2, 3)
    residual_grad = packed[48 : 48 + CONST0, :CONST0]
    return (
        output, tokens_grad, mine[:, GAIN0 : GAIN0 + 2], jnp.swapaxes(qkv_grad, 1, 2), out_grad, router_grad,
        residual_grad, const_grad, mine[:, VECTOR0 : VECTOR0 + 2], gate_grad, up_grad, down_grad,
    )


def solution(mesh):
    in_specs = (
        P(("dp", "expert"), None), P("dp", None, None), P("dp", None), P(None, ("dp", "expert"), None),
        P(None, None, "dp"), P(None, None, "dp"), P(None, "dp", None), P(None, "dp", None), P(),
        P(None, None, "dp", None), P(None, None, "dp"), P(None, "expert", None, "dp"), P(None, "expert", None, "dp"),
        P(None, "expert", "dp", None), P(("dp", "expert"), None),
    )
    out_specs = (
        P(("dp", "expert"), None), P(("dp", "expert"), None), P(None, None, "dp"), P(None, None, "dp"),
        P(None, "dp", None), P(None, "dp", None), P(), P(None, None, "dp", None), P(None, None, "dp"),
        P(None, "expert", None, "dp"), P(None, "expert", None, "dp"), P(None, "expert", "dp", None),
    )
    return jax.shard_map(per_device, mesh=mesh, in_specs=in_specs, out_specs=out_specs, check_vma=False)
```

```python
import functools

import jax
import jax.numpy as jnp
from jax import lax
from jax.experimental import pallas as pl
from jax.experimental.pallas import tpu as pltpu
from jax.sharding import PartitionSpec as P

HEADS = 12
CAP = 48
LINE = 4
EPSILON = 1e-05
MASKED = -1e30
HIGH = lax.Precision.HIGHEST
F32 = jnp.float32
BF16 = jnp.bfloat16
MESH = pl.DeviceIdType.MESH
VMEM = pl.BlockSpec(memory_space=pltpu.VMEM)
ANY = pl.BlockSpec(memory_space=pl.ANY)

CONST0, GAIN0, VECTOR0 = 12, 16, 18
STAT = {
    name: i
    for i, name in enumerate(
        ("r0", "r1", "share0", "share1", "slot0", "slot1", "p00", "p01", "p10", "p11")
    )
}


def dot_nn(a, b, **kw):
    return lax.dot_general(a, b, (((1,), (0,)), ((), ())), preferred_element_type=F32, **kw)


def dot_nt(a, b, **kw):
    return lax.dot_general(a, b, (((1,), (1,)), ((), ())), preferred_element_type=F32, **kw)


def dot_tn(a, b, **kw):
    return lax.dot_general(a, b, (((0,), (0,)), ((), ())), preferred_element_type=F32, **kw)


def lanes(rows, width=128):
    return lax.broadcasted_iota(jnp.int32, (rows, width), 1)


def rms_scale(values):
    return lax.rsqrt(jnp.mean(values * values, axis=-1, keepdims=True) + EPSILON)


def row_vectors(small):
    pick = lax.broadcasted_iota(jnp.int32, (8, 128), 0) + GAIN0 == lanes(8)
    rows = dot_nt(pick.astype(BF16), small)
    return rows[0:1], rows[1:2], rows[2:3], rows[3:4]


def stat_columns(stat):
    return {name: stat[:, i : i + 1] for name, i in STAT.items()}


def slot_picks(stat, slots):
    place = lanes(stat["slot0"].shape[0], slots).astype(F32)
    first = (place == stat["slot0"]).astype(BF16)
    second = (place == stat["slot1"]).astype(BF16)
    return first, second


def const_weights(stat, experts):
    out = []
    for kind in (experts + 1, experts + 2, experts + 3):
        out.append(
            stat["share0"] * (stat["r0"] == kind).astype(F32)
            + stat["share1"] * (stat["r1"] == kind).astype(F32)
        )
    return out


def attend_part(stream, small, w_qkv_t, w_out, doc_col, doc_row, attn_in_ref, qkv_ref, probs_ref, attn_ref):
    rows, width = stream.shape
    gain, _, _, _ = row_vectors(small)
    attn_in_ref[...] = (stream * rms_scale(stream) * gain).astype(BF16)

    def project(i, carry):
        at = pl.multiple_of(i * width, width)
        qkv_ref[:, pl.ds(at, width)] = dot_nt(
            attn_in_ref[...], w_qkv_t[pl.ds(at, width), :]
        ).astype(BF16)
        return carry

    lax.fori_loop(0, 3, project, 0)
    head_dim = width // HEADS
    factor = 1.0 / head_dim**0.5
    allowed = jnp.logical_and(
        doc_col[...] == doc_row[...],
        lax.broadcasted_iota(jnp.int32, (rows, rows), 0)
        >= lax.broadcasted_iota(jnp.int32, (rows, rows), 1),
    )

    def heads(i, carry):
        at = pl.multiple_of(i * 2 * head_dim, 2 * head_dim)
        query = qkv_ref[:, pl.ds(at, 2 * head_dim)]
        key = qkv_ref[:, pl.ds(pl.multiple_of(at + width, 128), 2 * head_dim)]
        value = qkv_ref[:, pl.ds(pl.multiple_of(at + 2 * width, 128), 2 * head_dim)]
        second = lanes(rows, 2 * head_dim) >= head_dim
        mixed = []
        for sub in (0, 1):
            mine = second if sub else jnp.logical_not(second)
            scores = dot_nt(jnp.where(mine, query, jnp.zeros_like(query)), key) * factor
            scores = jnp.where(allowed, scores, MASKED)
            exponent = jnp.exp(scores - jnp.max(scores, axis=-1, keepdims=True))
            probs = exponent / jnp.sum(exponent, axis=-1, keepdims=True)
            probs_ref[2 * i + sub] = probs
            mixed.append(dot_nn(probs.astype(BF16), value))
        attn_ref[:, pl.ds(at, 2 * head_dim)] = jnp.where(second, mixed[1], mixed[0]).astype(BF16)
        return carry

    lax.fori_loop(0, HEADS // 2, heads, 0, unroll=2)
    return stream + dot_nn(attn_ref[...], w_out[...])


def route_part(mid, small, routes, prev_logits, w_res, experts):
    rows = mid.shape[0]
    _, gain, _, _ = row_vectors(small)
    hidden = (mid * rms_scale(mid) * gain).astype(BF16)
    lane = lanes(rows)
    raw = dot_nn(hidden, small)
    logits = jnp.where(lane < CONST0, raw, 0.0)
    if prev_logits is not None:
        logits = logits + dot_nn(prev_logits, w_res, precision=HIGH)
    r0, r1 = routes[:, 0:1], routes[:, 1:2]
    hot0, hot1 = (lane == r0).astype(F32), (lane == r1).astype(F32)
    c0 = jnp.sum(hot0 * logits, axis=-1, keepdims=True)
    c1 = jnp.sum(hot1 * logits, axis=-1, keepdims=True)
    peak = jnp.maximum(c0, c1)
    e0, e1 = jnp.exp(c0 - peak), jnp.exp(c1 - peak)
    total = e0 + e1
    share0, share1 = e0 / total, e1 / total
    probs = []
    for j in (0, 1):
        a = raw[:, CONST0 + 2 * j : CONST0 + 2 * j + 1]
        b = raw[:, CONST0 + 2 * j + 1 : CONST0 + 2 * j + 2]
        top = jnp.maximum(a, b)
        ea, eb = jnp.exp(a - top), jnp.exp(b - top)
        probs += [ea / (ea + eb), eb / (ea + eb)]
    earlier = lax.broadcasted_iota(jnp.int32, (rows, rows), 0) > lax.broadcasted_iota(
        jnp.int32, (rows, rows), 1
    )
    before = dot_nn(earlier.astype(BF16), (hot0 + hot1).astype(BF16))
    f0, f1 = r0.astype(F32), r1.astype(F32)
    slot0 = jnp.where(
        r0 < experts, f0 * CAP + jnp.sum(before * hot0, axis=-1, keepdims=True), -1.0
    )
    slot1 = jnp.where(
        r1 < experts, f1 * CAP + jnp.sum(before * hot1, axis=-1, keepdims=True), -1.0
    )
    stat = jnp.zeros((rows, 128), F32)
    for i, column in enumerate([f0, f1, share0, share1, slot0, slot1] + probs):
        stat = jnp.where(lane == i, column, stat)
    first, second = slot_picks({"slot0": slot0, "slot1": slot1}, experts * CAP)
    outgoing = dot_tn(first + second, hidden).astype(BF16)
    return logits, stat, outgoing


def combine_part(mid, small, stat, returned, experts):
    _, gain, vec0, vec1 = row_vectors(small)
    hidden_full = mid * rms_scale(mid) * gain
    first, second = slot_picks(stat, experts * CAP)
    pair0, pair1 = dot_nn(first, returned), dot_nn(second, returned)
    copy, const0, const1 = const_weights(stat, experts)
    local = copy + const0 * stat["p00"] + const1 * stat["p10"]
    moe = stat["share0"] * pair0 + stat["share1"] * pair1 + local * hidden_full
    moe = moe + (const0 * stat["p01"]) * vec0 + (const1 * stat["p11"]) * vec1
    return mid + moe, hidden_full, pair0, pair1


def share_backward(grad, small, stat, hidden_full, pair0, pair1, extra, experts):
    rows = grad.shape[0]
    _, _, vec0, vec1 = row_vectors(small)
    first, second = slot_picks(stat, experts * CAP)
    lane = lanes(rows).astype(F32)
    rowsum = functools.partial(jnp.sum, axis=-1, keepdims=True)
    dot_hidden = rowsum(grad * hidden_full)
    dot_vec = (rowsum(grad * vec0), rowsum(grad * vec1))
    _, const0, const1 = const_weights(stat, experts)
    probs = ((stat["p00"], stat["p01"]), (stat["p10"], stat["p11"]))
    value = [probs[j][0] * dot_hidden + probs[j][1] * dot_vec[j] for j in (0, 1)]
    shares = []
    for r, pair in ((stat["r0"], pair0), (stat["r1"], pair1)):
        shares.append(
            rowsum(grad * pair)
            + (r == experts + 1).astype(F32) * dot_hidden
            + (r == experts + 2).astype(F32) * value[0]
            + (r == experts + 3).astype(F32) * value[1]
        )
    inner = stat["share0"] * shares[0] + stat["share1"] * shares[1]
    g_small = (lane == stat["r0"]).astype(F32) * (stat["share0"] * (shares[0] - inner))
    g_small = g_small + (lane == stat["r1"]).astype(F32) * (stat["share1"] * (shares[1] - inner))
    if extra is not None:
        g_small = g_small + extra
    g_logits = g_small
    for j, weight in ((0, const0), (1, const1)):
        q = (weight * dot_hidden, weight * dot_vec[j])
        mean = probs[j][0] * q[0] + probs[j][1] * q[1]
        for c in (0, 1):
            g_small = jnp.where(lane == CONST0 + 2 * j + c, probs[j][c] * (q[c] - mean), g_small)
    sent0 = (jnp.where(stat["r0"] < experts, stat["share0"], 0.0) * grad).astype(BF16)
    sent1 = (jnp.where(stat["r1"] < experts, stat["share1"], 0.0) * grad).astype(BF16)
    outgoing = (dot_tn(first, sent0) + dot_tn(second, sent1)).astype(BF16)
    hidden = hidden_full.astype(BF16).astype(F32)
    projections = dot_tn(g_small, hidden, precision=HIGH)
    vector0 = jnp.sum((const0 * stat["p01"]) * grad, axis=0, keepdims=True)
    vector1 = jnp.sum((const1 * stat["p11"]) * grad, axis=0, keepdims=True)
    return g_small, g_logits, outgoing, projections, vector0, vector1


def store_small(ref, projections, vector0, vector1):
    ref[0:16, :] = projections[0:16]
    ref[16:24, :] = jnp.zeros((8, ref.shape[1]), F32)
    ref[VECTOR0 : VECTOR0 + 1, :] = vector0
    ref[VECTOR0 + 1 : VECTOR0 + 2, :] = vector1


def first_kernel(experts, tokens, small, w_qkv_t, w_out, doc_col, doc_row, routes,
                 attn_in, qkv, probs, attn, mid_ref, logits_ref, stat_ref, out_ref):
    mid = attend_part(tokens[...].astype(F32), small[...], w_qkv_t, w_out, doc_col, doc_row, attn_in, qkv, probs, attn)
    mid_ref[...] = mid
    logits, stat, out = route_part(mid, small[...], routes[...], None, None, experts)
    logits_ref[...], stat_ref[...], out_ref[...] = logits, stat, out


def middle_kernel(experts, mid_in, small_in, stat_in, returned, small, w_qkv_t, w_out, doc_col, doc_row, routes, logits_in, w_res,
                  stream_ref, attn_in, qkv, probs, attn, mid_ref, stat_ref, out_ref):
    stream, _, _, _ = combine_part(mid_in[...], small_in[...], stat_columns(stat_in[...]), returned[...], experts)
    stream_ref[...] = stream
    mid = attend_part(stream, small[...], w_qkv_t, w_out, doc_col, doc_row, attn_in, qkv, probs, attn)
    mid_ref[...] = mid
    _, stat, out = route_part(mid, small[...], routes[...], logits_in[...], w_res[...], experts)
    stat_ref[...], out_ref[...] = stat, out


def turn_kernel(experts, mid, small, stat_in, returned, cotangent, logits_in, w_res,
                output, g_small_ref, extra_ref, out_ref, small_grad, res_grad):
    stat = stat_columns(stat_in[...])
    stream, hidden_full, pair0, pair1 = combine_part(mid[...], small[...], stat, returned[...], experts)
    output[...] = stream.astype(BF16)
    grad = cotangent[...].astype(F32)
    g_small, g_logits, out, projections, v0, v1 = share_backward(grad, small[...], stat, hidden_full, pair0, pair1, None, experts)
    g_small_ref[...] = g_small
    out_ref[...] = out
    store_small(small_grad, projections, v0, v1)
    res_grad[...] = dot_tn(logits_in[...], g_logits, precision=HIGH)
    extra_ref[...] = dot_nt(g_logits, w_res[...], precision=HIGH)


def layer_backward(experts, grad, back, g_small, stat, mid, small, stream, w_qkv_t, w_out, attn_in, qkv, probs, attn,
                   qkv_grad, out_grad, small_grad, g_qkv, g_attn):
    rows, width = mid.shape
    gain1, gain2, _, _ = row_vectors(small)
    first, second = slot_picks(stat, experts * CAP)
    copy, const0, const1 = const_weights(stat, experts)
    local = copy + const0 * stat["p00"] + const1 * stat["p10"]
    g_full = dot_nt(g_small, small.astype(F32), precision=HIGH) + dot_nn(first + second, back)
    g_full = g_full + grad * local
    s2 = rms_scale(mid)
    small_grad[GAIN0 + 1 : GAIN0 + 2, :] = jnp.sum(g_full * mid * s2, axis=0, keepdims=True)
    m = g_full * gain2
    g_mid = grad + s2 * m - mid * (s2 * s2 * s2 * jnp.mean(m * mid, axis=-1, keepdims=True))
    branch = g_mid.astype(BF16)
    out_grad[...] = dot_tn(attn[...], branch).astype(out_grad.dtype)
    g_attn[...] = dot_nt(branch, w_out[...]).astype(BF16)
    head_dim = width // HEADS
    factor = 1.0 / head_dim**0.5

    def heads(i, carry):
        at = pl.multiple_of(i * 2 * head_dim, 2 * head_dim)
        at_k = pl.multiple_of(at + width, 128)
        at_v = pl.multiple_of(at + 2 * width, 128)
        query = qkv[:, pl.ds(at, 2 * head_dim)]
        key = qkv[:, pl.ds(at_k, 2 * head_dim)]
        value = qkv[:, pl.ds(at_v, 2 * head_dim)]
        ga = g_attn[:, pl.ds(at, 2 * head_dim)]
        second_half = lanes(rows, 2 * head_dim) >= head_dim
        gq, gk, gv = [], [], []
        for sub in (0, 1):
            mine = second_half if sub else jnp.logical_not(second_half)
            p = probs[2 * i + sub]
            gp = dot_nt(jnp.where(mine, ga, jnp.zeros_like(ga)), value)
            gs = (p * (gp - jnp.sum(p * gp, axis=-1, keepdims=True))).astype(BF16)
            gq.append(dot_nn(gs, key))
            gk.append(dot_tn(gs, query))
            gv.append(dot_tn(p.astype(BF16), ga))
        g_qkv[:, pl.ds(at, 2 * head_dim)] = (jnp.where(second_half, gq[1], gq[0]) * factor).astype(BF16)
        g_qkv[:, pl.ds(at_k, 2 * head_dim)] = (jnp.where(second_half, gk[1], gk[0]) * factor).astype(BF16)
        g_qkv[:, pl.ds(at_v, 2 * head_dim)] = jnp.where(second_half, gv[1], gv[0]).astype(BF16)
        return carry

    lax.fori_loop(0, HEADS // 2, heads, 0, unroll=2)

    def weights(i, carry):
        at = pl.multiple_of(i * width, width)
        qkv_grad[pl.ds(at, width), :] = dot_tn(g_qkv[:, pl.ds(at, width)], attn_in[...]).astype(qkv_grad.dtype)
        return carry + dot_nn(g_qkv[:, pl.ds(at, width)], w_qkv_t[pl.ds(at, width), :])

    g_in = lax.fori_loop(0, 3, weights, jnp.zeros((rows, width), F32))
    s1 = rms_scale(stream)
    small_grad[GAIN0 : GAIN0 + 1, :] = jnp.sum(g_in * stream * s1, axis=0, keepdims=True)
    n = g_in * gain1
    return g_mid + s1 * n - stream * (s1 * s1 * s1 * jnp.mean(n * stream, axis=-1, keepdims=True))


def between_kernel(experts, cotangent, back, g_small, stat_in, mid, small, stream, w_qkv_t, w_out, attn_in, qkv, probs, attn, small_grad_in,
                   mid0, small0, stat0_in, returned0, extra,
                   qkv_grad, out_grad, small_grad, grad_ref, g_small0_ref, out_ref, small_grad0, g_qkv, g_attn):
    small_grad[...] = small_grad_in[...]
    grad = layer_backward(experts, cotangent[...].astype(F32), back[...], g_small[...], stat_columns(stat_in[...]), mid[...],
                          small[...], stream[...], w_qkv_t, w_out, attn_in, qkv, probs, attn, qkv_grad, out_grad, small_grad, g_qkv, g_attn)
    grad_ref[...] = grad
    stat0 = stat_columns(stat0_in[...])
    _, hidden_full, pair0, pair1 = combine_part(mid0[...], small0[...], stat0, returned0[...], experts)
    g_small0, _, out, projections, v0, v1 = share_backward(grad, small0[...], stat0, hidden_full, pair0, pair1, extra[...], experts)
    g_small0_ref[...] = g_small0
    out_ref[...] = out
    store_small(small_grad0, projections, v0, v1)


def last_kernel(experts, grad_in, back, g_small, stat_in, mid, small, tokens, w_qkv_t, w_out, attn_in, qkv, probs, attn, small_grad_in,
                qkv_grad, out_grad, small_grad, grad_ref, g_qkv, g_attn):
    small_grad[...] = small_grad_in[...]
    grad_ref[...] = layer_backward(experts, grad_in[...], back[...], g_small[...], stat_columns(stat_in[...]), mid[...], small[...],
                                   tokens[...].astype(F32), w_qkv_t, w_out, attn_in, qkv, probs, attn, qkv_grad, out_grad, small_grad,
                                   g_qkv, g_attn)


def local_call(kernel, experts, args, outs, scratch=()):
    return pl.pallas_call(
        functools.partial(kernel, experts),
        out_shape=[jax.ShapeDtypeStruct(shape, dtype) for shape, dtype in outs],
        in_specs=[VMEM] * len(args),
        out_specs=[VMEM] * len(outs),
        scratch_shapes=[pltpu.VMEM(shape, dtype) for shape, dtype in scratch],
        compiler_params=pltpu.CompilerParams(vmem_limit_bytes=60 * 2**20),
        cost_estimate=pl.CostEstimate(flops=10**10, bytes_accessed=6 * 10**7, transcendentals=0),
    )(*args)


class Place:
    def __init__(self, spread):
        self.spread = spread
        self.d, self.e = lax.axis_index("dp"), lax.axis_index("expert")
        self.t, self.f = self.d // spread, lax.rem(self.d, spread)
        self.y, self.c = self.e // 2, lax.rem(self.e, 2)
        self.above, self.below = self.t < LINE - 1, self.t > 0
        self.sibling = (self.d, self.e + 1 - 2 * self.c)
        self.across = (self.d, lax.rem(self.e + 2, 4))
        self.corner = (self.d, 3 - self.e)
        self.beside = (self.t * spread + 1 - self.f, self.e)
        self.mates = [(self.d, self.e), self.sibling, self.across, self.corner]

    def on_line(self, up):
        return (self.d + self.spread * (2 * up - 1), self.e)


def greet(always, place):
    barrier = pltpu.get_barrier_semaphore()
    for device in always:
        pl.semaphore_signal(barrier, inc=1, device_id=device, device_id_type=MESH)
    for up, there in ((1, place.above), (0, place.below)):

        @pl.when(there)
        def _(up=up):
            pl.semaphore_signal(barrier, inc=1, device_id=place.on_line(up), device_id_type=MESH)

    ends = place.above.astype(jnp.int32) + place.below.astype(jnp.int32)
    pl.semaphore_wait(barrier, len(always) + ends)


def remote(src, dst, send, recv, device):
    return pltpu.make_async_remote_copy(
        src_ref=src, dst_ref=dst, send_sem=send, recv_sem=recv, device_id=device, device_id_type=MESH)


def dma(*shape):
    return pltpu.SemaphoreType.DMA(shape)


def along(place, body, start=0):
    if start == 0:
        body(place.t)

    def step(k, carry):
        for t in (place.t + k, place.t - k):

            @pl.when(jnp.logical_and(t >= 0, t < LINE))
            def _(t=t):
                body(t)

        return carry

    lax.fori_loop(1, LINE, step, 0)


class Rider:
    partners = ()

    def begin(self):
        pass

    def ready(self):
        pass

    def after_first(self):
        pass

    def after_line(self):
        pass

    def after_relay(self):
        pass

    def finish(self):
        pass


class Line:
    def __init__(self, place, x, part, stage, arrived, final, returned, sems):
        self.p = place
        self.x, self.part, self.stage, self.arrived = x, part, stage, arrived
        self.final, self.returned = final, returned
        (self.out_send, self.x_recv, self.x_send, self.sum_send, self.sum_recv, self.ret_send, self.ret_recv) = sems

    @staticmethod
    def scratch(local, width):
        shape = (local, 4, CAP, width)
        return [
            pltpu.VMEM((local, LINE, 4, CAP, width), BF16),
            pltpu.VMEM((LINE,) + shape, F32),
            pltpu.VMEM((LINE,) + shape, BF16),
            pltpu.VMEM((2, LINE) + shape, BF16),
            pltpu.VMEM((4, local, CAP, width), BF16),
            dma(4), dma(LINE, 4), dma(2, LINE, 4), dma(LINE, 4), dma(2, LINE, 4), dma(4), dma(4),
        ]

    def slot_copy(self, out, i):
        to, p = self.p.mates[i], self.p
        return remote(out.at[to[1]], self.x.at[:, p.t, p.e], self.out_send.at[i], self.x_recv.at[p.t, p.e], to)

    def x_copy(self, up, s, b):
        at = self.x.at[:, s, b]
        return remote(at, at, self.x_send.at[up, s, b], self.x_recv.at[s, b], self.p.on_line(up))

    def sum_copy(self, up, s, b):
        return remote(self.stage.at[s, :, b], self.arrived.at[up, s, :, b], self.sum_send.at[s, b],
                      self.sum_recv.at[up, s, b], self.p.on_line(up))

    def ret_copy(self, i, to_mate=True):
        to = self.p.mates[i]
        row = self.p.e if to_mate else to[1]
        return remote(self.final.at[to[1]], self.returned.at[row], self.ret_send.at[i], self.ret_recv.at[row], to)

    def send_sum(self, up, s, b, total):
        self.stage[s, :, b] = total.astype(BF16)
        self.sum_copy(up, s, b).start()

    def relays(self):
        p = self.p

        @pl.when(jnp.logical_and(p.above, p.below))
        def _():
            up = jnp.where(p.t == 1, 1, 0)
            ahead = 2 * up - 1

            def on(kind, i):
                b = p.mates[i][1]
                s = {"near": p.t + ahead, "far": p.t + 2 * ahead, "back": p.t - ahead}[kind]
                way = 1 - up if kind == "back" else up
                self.sum_copy(way, s, b).wait_recv()
                self.send_sum(way, s, b, self.part[s, :, b] + self.arrived[way, s, :, b].astype(F32))

            for kind, i in (
                ("near", 0), ("near", 1), ("far", 0), ("far", 1), ("back", 0), ("far", 2), ("back", 1), ("far", 3),
                ("back", 2), ("near", 2), ("back", 3), ("near", 3),
            ):
                on(kind, i)

    def run(self, out, compute, kept, meanwhile, rider):
        p = self.p
        t, e = p.t, p.e
        blocks = [b for _, b in p.mates]
        greet(p.mates[1:] + list(rider.partners), p)
        for i in (2, 3, 1):
            self.slot_copy(out, i).start()
        self.x[:, t, e] = out[e]
        rider.begin()
        for i in range(4):
            if i:
                self.x_copy(0, t, blocks[i]).wait_recv()
            for up, there in ((0, p.below), (1, p.above)):

                @pl.when(there)
                def _(up=up, i=i):
                    self.x_copy(up, t, blocks[i]).start()

        rider.ready()
        lax.fori_loop(0, 2, lambda pair, carry: (compute(t, pair), carry)[1], 0)
        kept(t)
        rider.after_first()

        def step(n, carry):
            k = jnp.where(n < 2, 1, jnp.where(jnp.logical_or(n == 2, n == 5), 2, 3))
            half = jnp.where(jnp.logical_or(n == 1, n >= 4), 1, 0)
            pair = p.y + half - 2 * p.y * half
            first = jnp.where(half == 0, blocks[0], blocks[2])
            second = jnp.where(half == 0, blocks[1], blocks[3])
            for b in (first, second):
                for up, there, onward, before_end in ((0, t + k < LINE, p.below, t == 1), (1, t - k >= 0, p.above, t == LINE - 2)):
                    s = t - k if up else t + k
                    put_off = jnp.logical_and(before_end, n == 1)

                    @pl.when(there)
                    def _(up=up, onward=onward, s=s, b=b, put_off=put_off):
                        self.x_copy(up, s, b).wait_recv()

                        @pl.when(jnp.logical_and(onward, jnp.logical_not(put_off)))
                        def _():
                            self.x_copy(up, s, b).start()

            for up, before_end in ((0, t == 1), (1, t == LINE - 2)):

                @pl.when(jnp.logical_and(before_end, n == 5))
                def _(up=up):
                    for b in (first, second):
                        self.x_copy(up, t - 1 if up else t + 1, b).start()

            def side(up, carry):
                s = t + k - 2 * k * up

                @pl.when(jnp.logical_and(s >= 0, s < LINE))
                def _():
                    compute(s, pair)

                    @pl.when(half == 1)
                    def _():
                        kept(s)

                return carry

            lax.fori_loop(0, 2, side, 0)
            for up, starts, s in ((1, t == 0, k), (0, t == LINE - 1, LINE - 1 - k)):

                @pl.when(starts)
                def _(up=up, s=s):
                    for b in (first, second):
                        self.send_sum(up, s, b, self.part[s, :, b])

            return carry

        lax.fori_loop(0, 6, step, 0)
        rider.after_line()
        meanwhile()
        self.relays()
        rider.after_relay()
        for i, b in enumerate(blocks):
            for up, there in ((1, p.below), (0, p.above)):

                @pl.when(there)
                def _(up=up, b=b):
                    self.sum_copy(up, t, b).wait_recv()
                    self.part[t, :, b] = self.part[t, :, b] + self.arrived[up, t, :, b].astype(F32)

            if i:
                self.final[b] = self.part[t, :, b].astype(BF16)
                self.ret_copy(i).start()
            else:
                self.returned[e] = self.part[t, :, e].astype(BF16)

        def sent(s, carry):
            for i in range(4):
                for up, mine in ((0, jnp.logical_and(p.below, s >= t)), (1, jnp.logical_and(p.above, s <= t))):

                    @pl.when(mine)
                    def _(up=up, i=i):
                        self.x_copy(up, s, i).wait_send()

                @pl.when(s != t)
                def _(i=i):
                    self.sum_copy(0, s, i).wait_send()

            return carry

        for i in (1, 2, 3):
            self.slot_copy(out, i).wait_send()
        lax.fori_loop(0, LINE, sent, 0)
        rider.finish()
        for i in (1, 2, 3):
            self.ret_copy(i).wait_send()
            self.ret_copy(i, False).wait_recv()


def split(refs, *counts):
    out, at = [], 0
    for count in counts:
        out.append(refs[at : at + count])
        at += count
    return out + [refs[at:]]


def expert_forward_kernel(spread, parts, late, ride, out, *refs):
    own = 3 * parts - late
    weights_in, given, outs, late_out, whole, scratch, line_refs, sems, ride_refs = split(
        refs, own, 8 if ride else 0, 4, late, 5 if ride else 0, 3 * parts, 5, 7)
    weights_in = list(weights_in) + list(late_out)
    (g_all, u_all, keep_sem, load_sem), ride_refs = ride_refs[:4], ride_refs[4:]
    returned, x_keep, g_keep, u_keep = outs
    gate, up, down = scratch[:parts], scratch[parts : 2 * parts], scratch[2 * parts :]
    x, part, stage, arrived, final = line_refs
    local, _, _, _, width = x.shape
    rows = 2 * CAP
    p = Place(spread)
    line = Line(p, x, part, stage, arrived, final, returned, sems)
    rider = WeightRider(p, weights_in[-2:], given, whole, ride_refs) if late else Rider()

    def load(i):
        return pltpu.make_async_copy(weights_in[i], scratch[i], load_sem.at[i])

    for i in range(own):
        load(i).start()

    def keep_x(s):
        return pltpu.make_async_copy(x.at[:, s], x_keep.at[:, s], keep_sem.at[0, s])

    def keep_g(s):
        return pltpu.make_async_copy(g_all.at[s], g_keep.at[s], keep_sem.at[1, s])

    def keep_u(s):
        return pltpu.make_async_copy(u_all.at[s], u_keep.at[s], keep_sem.at[2, s])

    def kept(s):
        keep_x(s).start()
        keep_g(s).start()
        keep_u(s).start()

    def compute(s, pair):
        at = pl.multiple_of(pair * rows, rows)

        def one(l, carry):
            rows_in = x[l, s, pl.ds(2 * pair, 2)].reshape(rows, width)
            total = jnp.zeros((rows, width), F32)
            for q in range(parts):
                cols = gate[q].shape[2]
                here = slice(q * cols, (q + 1) * cols)
                g = dot_nn(rows_in, gate[q][l])
                u = dot_nn(rows_in, up[q][l])
                g_all[s, l, pl.ds(at, rows), here] = g
                u_all[s, l, pl.ds(at, rows), here] = u
                act = (g * jax.nn.sigmoid(g) * u).astype(BF16)
                total = total + dot_nn(act, down[q][l])
            part[s, l, pl.ds(2 * pair, 2)] = total.reshape(2, CAP, width)
            return carry

        lax.fori_loop(0, local, one, 0)

    class Loaded(Rider):
        partners = rider.partners
        after_first, after_line, after_relay, finish = (
            rider.after_first, rider.after_line, rider.after_relay, rider.finish)

        def begin(self):
            rider.begin()

        def ready(self):
            rider.ready()
            for i in range(own, 3 * parts):
                load(i).start()
            for i in range(3 * parts):
                load(i).wait()

    line.run(out, compute, kept, lambda: None, Loaded())
    for s in range(LINE):
        keep_x(s).wait()
        keep_g(s).wait()
        keep_u(s).wait()


def expert_backward_kernel(spread, parts, ride, out, *refs):
    loads_in, given, outs, ride_outs, loads, line_refs, sems, rest = split(
        refs, 3 + 3 * parts, 5 if ride else 0, 1 + 3 * parts, 4 if ride else 0, 3 + 3 * parts, 5, 7)
    (act_all, gg_all, gu_all), grads, (load_sem, grad_sem), ride_refs = split(rest, 3, 3 * parts, 2)
    returned, grads_out = outs[0], outs[1:]
    x_in, g_all, u_all = loads[:3]
    gate, up, down = loads[3 : 3 + parts], loads[3 + parts : 3 + 2 * parts], loads[3 + 2 * parts :]
    x, part, stage, arrived, final = line_refs
    local, _, _, _, width = x.shape
    rows = 2 * CAP
    p = Place(spread)
    line = Line(p, x, part, stage, arrived, final, returned, sems)
    rider = GradientRider(p, given, ride_outs, ride_refs) if ride else Rider()

    def load(i):
        return pltpu.make_async_copy(loads_in[i], loads[i], load_sem.at[i])

    def store(i, l):
        return pltpu.make_async_copy(grads[i].at[l], grads_out[i].at[l], grad_sem.at[i, l])

    for i in range(3 + 3 * parts):
        load(i).start()

    def compute(s, pair):
        at = pl.multiple_of(pair * rows, rows)
        into = pl.ds(pl.multiple_of((2 * s + pair) * rows, rows), rows)

        def one(l, carry):
            rows_in = x[l, s, pl.ds(2 * pair, 2)].reshape(rows, width)
            total = jnp.zeros((rows, width), F32)
            for q in range(parts):
                cols = gate[q].shape[2]
                here = slice(q * cols, (q + 1) * cols)
                g, u = g_all[s, l, pl.ds(at, rows), here], u_all[s, l, pl.ds(at, rows), here]
                g_act = dot_nt(rows_in, down[q][l])
                sigma = jax.nn.sigmoid(g)
                swish = g * sigma
                gg = (g_act * u * sigma * (1.0 + g * (1.0 - sigma))).astype(BF16)
                gu = (g_act * swish).astype(BF16)
                act_all[l, into, here] = (swish * u).astype(BF16)
                gg_all[l, into, here] = gg
                gu_all[l, into, here] = gu
                total = total + dot_nt(gg, gate[q][l]) + dot_nt(gu, up[q][l])
            part[s, l, pl.ds(2 * pair, 2)] = total.reshape(2, CAP, width)
            return carry

        lax.fori_loop(0, local, one, 0)

    def weights():
        def one(l, carry):
            x_rows = x_in[l].reshape(2 * LINE * rows, width)
            g_rows = x[l].reshape(2 * LINE * rows, width)
            for q in range(parts):
                cols = gate[q].shape[2]
                here = slice(q * cols, (q + 1) * cols)
                for i, value in (
                    (q, dot_tn(x_rows, gg_all[l, :, here])),
                    (parts + q, dot_tn(x_rows, gu_all[l, :, here])),
                    (2 * parts + q, dot_tn(act_all[l, :, here], g_rows)),
                ):
                    grads[i][l] = value.astype(grads[i].dtype)
                    store(i, l).start()
            return carry

        lax.fori_loop(0, local, one, 0)

    class Loaded(Rider):
        partners = rider.partners
        after_first, after_line, after_relay, finish = (
            rider.after_first, rider.after_line, rider.after_relay, rider.finish)

        def begin(self):
            rider.begin()

        def ready(self):
            for i in range(3 + 3 * parts):
                load(i).wait()

    line.run(out, compute, lambda s: None, weights, Loaded())
    for i in range(3 * parts):
        for l in range(local):
            store(i, l).wait()


def remote_params(call_id):
    return pltpu.CompilerParams(collective_id=call_id, has_side_effects=True, vmem_limit_bytes=61 * 2**20)


def struct(shape, dtype):
    return jax.ShapeDtypeStruct(tuple(shape), dtype)


def expert_forward(spread, call_id, out, weights, late=False, ride=None):
    parts = -(-len(weights) // 3)
    _, local, cap, width = out.shape
    columns = sum(w.shape[2] for w in weights[:parts])
    kept = (LINE, local, 4 * cap, columns)
    outs = [struct(out.shape, BF16), struct((local, LINE, 4, cap, width), BF16), struct(kept, F32), struct(kept, F32)]
    shapes = [w.shape for w in weights] + [weights[-1].shape] * late
    outs += [struct(weights[-1].shape, BF16)] * late
    scratch = [pltpu.VMEM(shape, BF16) for shape in shapes] + Line.scratch(local, width)
    scratch += [pltpu.VMEM(kept, F32), pltpu.VMEM(kept, F32), dma(3, LINE), dma(3 * parts)]
    more = ride or ()
    count = LINE * spread
    if ride:
        outs += [struct((count * s.shape[1], s.shape[2]), BF16) for s in ride[3:6]]
        outs += [struct(w.shape, BF16) for w in ride[6:]]
    if late:
        scratch += WeightRider.scratch(count if ride else 0)
    return pl.pallas_call(
        functools.partial(expert_forward_kernel, spread, parts, int(late), ride is not None),
        out_shape=outs,
        in_specs=[VMEM] + [ANY] * (len(weights) + len(more)),
        out_specs=[VMEM] + [ANY] * (len(outs) - 1),
        scratch_shapes=scratch,
        compiler_params=remote_params(call_id),
        cost_estimate=pl.CostEstimate(flops=2 * 10**10, bytes_accessed=2 * 10**8, transcendentals=0),
    )(out, *weights, *more)


def expert_backward(spread, call_id, out, kept, weights, ride=None):
    parts = len(weights) // 3
    _, local, cap, width = out.shape
    columns = sum(w.shape[2] for w in weights[:parts])
    loads = list(kept) + list(weights)
    grads = [(w.shape, F32 if i % parts == 0 else BF16) for i, w in enumerate(weights)]
    wide = pltpu.VMEM((local, LINE * 4 * cap, columns), BF16)
    outs = [struct(out.shape, BF16)] + [struct(*g) for g in grads]
    scratch = [pltpu.VMEM(a.shape, a.dtype) for a in loads] + Line.scratch(local, width)
    scratch += [wide] * 3 + [pltpu.VMEM(*g) for g in grads] + [dma(len(loads)), dma(len(grads), local)]
    more = ()
    if ride:
        more = ride
        depths = [g.shape[0] // (LINE * spread) for g in ride[:2]]
        outs.append(struct((LINE, spread, sum(depths) // 2, width // 2), F32))
        outs += [struct(g.shape, BF16) for g in ride[2:]]
        scratch += GradientRider.scratch(spread, depths, width)
    return pl.pallas_call(
        functools.partial(expert_backward_kernel, spread, parts, ride is not None),
        out_shape=outs,
        in_specs=[VMEM] + [ANY] * (len(loads) + len(more)),
        out_specs=[VMEM] + [ANY] * len(grads) + ([VMEM] + [ANY] * 3 if ride else []),
        scratch_shapes=scratch,
        compiler_params=remote_params(call_id),
        cost_estimate=pl.CostEstimate(flops=2 * 10**10, bytes_accessed=2 * 10**8, transcendentals=0),
    )(out, *loads, *more)


def from_partner(array, shift, spread, groups):
    pairs = [
        (t * spread + (f + shift) % spread, t * spread + f) for t in range(groups) for f in range(spread)
    ]
    return lax.ppermute(array, "dp", pairs)


def to_partner(array, shift, spread, groups):
    pairs = [
        (t * spread + f, t * spread + (f + shift) % spread) for t in range(groups) for f in range(spread)
    ]
    return lax.ppermute(array, "dp", pairs)


def pair_weights(shard, axis, spread):
    parts = [shard] + [from_partner(shard, i, spread, LINE) for i in range(1, spread)]
    if shard.shape[axis] % 128:
        return [jnp.concatenate(parts, axis=axis)]
    return parts


def pair_sum(parts, axis, spread, came=None):
    if came is not None:
        return parts[0] + came.astype(F32)
    if len(parts) == 1 and spread > 1:
        parts = jnp.split(parts[0], spread, axis=axis)
    total = parts[0]
    for i in range(1, spread):
        total = total + to_partner(parts[i].astype(BF16), i, spread, LINE).astype(F32)
    return total


class LineGather:
    def __init__(self, place, pairs, shards, quarters, sems):
        self.p, self.shards, self.quarters = place, shards, quarters
        self.send, self.recv, self.x_send, self.x_recv = sems
        self.columns = [place.f, 1 - place.f] if pairs else [0]

    @staticmethod
    def shapes(shards, columns):
        (a, wide), (b, _), (c, narrow) = shards
        return [(LINE, columns, a // 2, wide // 2), (LINE, columns, b // 2, wide // 2), (LINE, columns, c, narrow)]

    @staticmethod
    def scratch(columns):
        return [dma(2, LINE, columns, 3), dma(LINE, columns, 3), dma(3), dma(3)]

    def copy(self, kind, up, t, f):
        at = self.quarters[kind].at[t, f]
        return remote(at, at, self.send.at[up, t, f, kind], self.recv.at[t, f, kind], self.p.on_line(up))

    def x_copy(self, kind, f):
        at = self.quarters[kind].at[self.p.t, f]
        return remote(at, at, self.x_send.at[kind], self.x_recv.at[kind], self.p.beside)

    def both_ways(self, f):
        p = self.p
        for up, there in ((0, p.below), (1, p.above)):

            @pl.when(there)
            def _(up=up):
                for kind in range(3):
                    self.copy(kind, up, p.t, f).start()

    def begin(self):
        p, f = self.p, self.columns[0]
        for kind in (0, 1):
            half, wide = self.quarters[kind].shape[2:]
            self.quarters[kind][p.t, f] = self.shards[kind][
                pl.ds(pl.multiple_of(p.y * half, 16), half), pl.ds(pl.multiple_of(p.c * wide, 128), wide)]
        self.quarters[2][p.t, f] = self.shards[2][...]
        for kind in range(3 if len(self.columns) == 2 else 0):
            self.x_copy(kind, f).start()
        self.both_ways(f)

    def beside(self, then):
        for f in self.columns[1:]:
            for kind in range(3):
                self.x_copy(kind, f).wait_recv()
            self.both_ways(f)
            then(self.p.t, f)

    def step(self, k, then):
        p = self.p
        for f in self.columns:
            for up, there, onward in ((0, p.t + k < LINE, p.below), (1, p.t - k >= 0, p.above)):
                t = p.t - k if up else p.t + k

                @pl.when(there)
                def _(up=up, onward=onward, t=t, f=f):
                    for kind in range(3):
                        self.copy(kind, up, t, f).wait_recv()

                    @pl.when(onward)
                    def _():
                        for kind in range(3):
                            self.copy(kind, up, t, f).start()

                    then(t, f)

    def finish(self):
        p = self.p

        def line(t, carry):
            for up, mine in ((0, jnp.logical_and(p.below, t >= p.t)), (1, jnp.logical_and(p.above, t <= p.t))):

                @pl.when(mine)
                def _(up=up):
                    for f in self.columns:
                        for kind in range(3):
                            self.copy(kind, up, t, f).wait_send()

            return carry

        lax.fori_loop(0, LINE, line, 0)
        for f in self.columns[1:]:
            for kind in range(3):
                self.x_copy(kind, 1 - f).wait_send()


class Spread:
    def __init__(self, place, quarters, shards, whole, sems):
        self.p, self.quarters, self.shards, self.whole = place, quarters, shards, whole
        self.y_send, self.y_recv, self.c_send, self.c_recv, self.l_sem, self.s_sem = sems

    @staticmethod
    def scratch(count):
        return [dma(count, 2), dma(count, 2), dma(count, 2, 2), dma(count, 2, 2), dma(count, 3), dma(3)]

    def region(self, kind, s, y, c):
        depth = self.shards[kind].shape[0]
        if kind == 2:
            return self.whole[2].at[pl.ds(pl.multiple_of(s * depth, 16), depth)]
        half, wide = depth // 2, self.shards[kind].shape[1] // 2
        return self.whole[kind].at[
            pl.ds(pl.multiple_of(s * depth + y * half, 16), half), pl.ds(pl.multiple_of(c * wide, 128), wide)]

    def mine(self, kind, s):
        return self.region(kind, s, self.p.y, self.p.c)

    def y_copy(self, kind, src, s):
        return remote(src, self.mine(kind, s), self.y_send.at[s, kind], self.y_recv.at[s, kind], self.p.across)

    def y_came(self, kind, s):
        at = self.region(kind, s, 1 - self.p.y, self.p.c)
        return remote(at, at, self.y_send.at[s, kind], self.y_recv.at[s, kind], self.p.across)

    def c_copy(self, kind, src, s, y):
        return remote(src, self.region(kind, s, y, self.p.c), self.c_send.at[s, y, kind], self.c_recv.at[s, y, kind],
                      self.p.sibling)

    def c_came(self, kind, s, y):
        at = self.region(kind, s, y, 1 - self.p.c)
        return remote(at, at, self.c_send.at[s, y, kind], self.c_recv.at[s, y, kind], self.p.sibling)

    def local(self, kind, src, s):
        return pltpu.make_async_copy(src, self.mine(kind, s), self.l_sem.at[s, kind])

    def shard(self, kind):
        depth = self.shards[kind].shape[0]
        at = self.whole[kind].at[pl.ds(pl.multiple_of(self.p.d * depth, 16), depth)]
        return pltpu.make_async_copy(self.shards[kind], at, self.s_sem.at[kind])

    def own_shard(self):
        for kind in range(3):
            self.shard(kind).start()

    def push(self, s, sources, here=True):
        if here:
            for kind in range(3):
                self.local(kind, sources[kind], s).start()
        for kind in (0, 1):
            self.y_copy(kind, sources[kind], s).start()
            self.c_copy(kind, sources[kind], s, self.p.y).start()

    def across(self, s):
        for kind in (0, 1):
            self.y_came(kind, s).wait_recv()
            self.c_copy(kind, self.region(kind, s, 1 - self.p.y, self.p.c), s, 1 - self.p.y).start()

    def finish_shard(self, s, here=True):
        @pl.when(s != self.p.d)
        def _():
            for kind in range(3 if here else 0):
                self.local(kind, self.mine(kind, s), s).wait()
            for kind in (0, 1):
                self.y_came(kind, s).wait_send()
                for y in (0, 1):
                    self.c_came(kind, s, y).wait_send()
                    self.c_came(kind, s, y).wait_recv()

    def finish_own(self):
        for kind in range(3):
            self.shard(kind).wait()


class WeightRider:
    def __init__(self, place, down, given, whole, sems):
        self.p, self.quarters = place, given[:3]
        self.own, self.other = [down[0]] + list(given[6:]), [down[1]] + list(whole[3:])
        self.w_send, self.w_recv, *more = sems
        self.spread = None
        if given:
            shards = [ref.at[1] for ref in given[3:6]]
            self.x_send, self.x_recv, *more = more
            self.spread = Spread(place, self.quarters, shards, whole[:3], more)
        self.partners = [place.beside]

    @staticmethod
    def scratch(count):
        return [dma(3), dma(3)] + ([dma(LINE, 3), dma(LINE, 3)] + Spread.scratch(count) if count else [])

    def place_of(self, t):
        return t * self.p.spread + self.p.f

    def beside_of(self, t):
        return t * self.p.spread + 1 - self.p.f

    def x_copy(self, kind, t, s):
        return remote(self.quarters[kind].at[t, 0], self.spread.mine(kind, s), self.x_send.at[t, kind],
                      self.x_recv.at[t, kind], self.p.beside)

    def weight(self, i):
        return remote(self.own[i], self.other[i], self.w_send.at[i], self.w_recv.at[i], self.p.beside)

    def ready(self):
        self.weight(0).wait_recv()

    def begin(self):
        self.weight(0).start()
        if not self.spread:
            return
        self.spread.own_shard()

        def body(t):
            for kind in range(3):
                self.x_copy(kind, t, self.place_of(t)).start()

            @pl.when(t != self.p.t)
            def _():
                self.spread.push(self.place_of(t), [q.at[t, 0] for q in self.quarters])

        along(self.p, body)
        for i in (1, 2):
            self.weight(i).start()

    def after_first(self):
        pass

    def after_line(self):
        def body(t):
            s = self.beside_of(t)
            for kind in range(3):
                self.x_copy(kind, t, s).wait_recv()
            self.spread.push(s, [self.spread.mine(kind, s) for kind in range(3)], here=False)

        if self.spread:
            along(self.p, body)

    def after_relay(self):
        if self.spread:
            along(self.p, lambda t: self.spread.across(self.place_of(t)), start=1)
            along(self.p, lambda t: self.spread.across(self.beside_of(t)))

    def finish(self):
        self.weight(0).wait_send()
        if not self.spread:
            return
        self.spread.finish_own()
        for i in (1, 2):
            self.weight(i).wait()

        def line(t, carry):
            for kind in range(3):
                self.x_copy(kind, t, self.place_of(t)).wait_send()
            self.spread.finish_shard(self.place_of(t))
            self.spread.finish_shard(self.beside_of(t), here=False)
            return carry

        lax.fori_loop(0, LINE, line, 0)


def dense_gather_kernel(spread, qkv, out, small, routes, gate, *refs):
    p = Place(spread)
    whole, quarters1, (routes_all, partner), quarters0, sems0, sems1, (r_send, r_recv, w_send, w_recv), spread_sems = split(
        refs, 3, 3, 2, 3, 4, 4, 4)
    shards0, shards1 = ([ref.at[l] for ref in (qkv, out, small)] for l in (0, 1))
    line0 = LineGather(p, True, shards0, quarters0, sems0)
    line1 = LineGather(p, False, shards1, quarters1, sems1)
    spreading = Spread(p, quarters0, shards0, whole, spread_sems)
    greet(p.mates[1:] + [p.beside], p)

    def route_copy(i, row):
        return remote(routes, routes_all.at[row], r_send.at[i], r_recv.at[row], p.mates[i])

    def push(t, f):
        spreading.push(t * spread + f, [q.at[t, f] for q in quarters0])

    weight = remote(gate, partner, w_send.at[0], w_recv.at[0], p.beside)
    line0.begin()
    weight.start()
    routes_all[p.e] = routes[...]
    for i in (1, 2, 3):
        route_copy(i, p.e).start()
    spreading.own_shard()
    line0.beside(push)
    line1.begin()

    def step(k, carry):
        line0.step(k, push)
        line1.step(k, lambda t, f: None)
        return carry

    lax.fori_loop(1, LINE, step, 0)
    along(p, lambda t: spreading.across(t * spread + p.f), start=1)
    along(p, lambda t: spreading.across(t * spread + 1 - p.f))
    spreading.finish_own()
    lax.fori_loop(0, LINE * spread, lambda s, carry: (spreading.finish_shard(s), carry)[1], 0)
    line0.finish()
    line1.finish()
    weight.wait()
    for i in (1, 2, 3):
        route_copy(i, p.e).wait_send()
        route_copy(i, p.mates[i][1]).wait_recv()


def dense_gather(spread, call_id, arrays, routes, gate):
    count = spread * LINE
    shards = [a.shape[1:] for a in arrays]
    pairs, single = LineGather.shapes(shards, 2), LineGather.shapes(shards, 1)
    outs = [struct((count * rows, width), BF16) for rows, width in shards]
    outs += [struct(q, BF16) for q in single] + [struct((4,) + routes.shape, routes.dtype)]
    outs.append(struct(gate.shape, BF16))
    scratch = [pltpu.VMEM(q, BF16) for q in pairs] + LineGather.scratch(2) + LineGather.scratch(1)
    scratch += [dma(4), dma(4), dma(1), dma(1)]
    return pl.pallas_call(
        functools.partial(dense_gather_kernel, spread),
        out_shape=outs,
        in_specs=[VMEM] * 4 + [ANY],
        out_specs=[ANY] * 3 + [VMEM] * 4 + [ANY],
        scratch_shapes=scratch + Spread.scratch(count),
        compiler_params=remote_params(call_id),
    )(*arrays, routes, gate)


class Halve:
    def __init__(self, place, grads, quarter, scratch):
        self.p, self.grads, self.quarter = place, grads, quarter
        (self.mine, self.core, self.stage, self.came, self.l_sem, self.a_send, self.a_recv, self.y_send,
         self.y_recv) = scratch
        self.depths = [g.shape[0] // (LINE * place.spread) for g in grads]
        self.wide = grads[0].shape[1] // 2

    @staticmethod
    def scratch(spread, depths, width):
        count, rows, wide = LINE * spread, sum(depths) // 2, width // 2
        half = pltpu.VMEM((LINE, spread, rows, wide), BF16)
        everything = pltpu.VMEM((count * sum(depths), wide), BF16)
        return [everything, everything, half, half, dma(2), dma(2), dma(2), dma(LINE), dma(LINE)]

    def rows_of(self, kind):
        first = 0 if kind == 0 else self.grads[0].shape[0]
        return slice(first, first + self.grads[kind].shape[0])

    def lanes(self, c):
        return pl.ds(pl.multiple_of(c * self.wide, 128), self.wide)

    def local(self, kind):
        return pltpu.make_async_copy(
            self.grads[kind].at[:, self.lanes(self.p.c)], self.mine.at[self.rows_of(kind)], self.l_sem.at[kind])

    def a_copy(self, kind):
        return remote(self.grads[kind].at[:, self.lanes(1 - self.p.c)], self.core.at[self.rows_of(kind)],
                      self.a_send.at[kind], self.a_recv.at[kind], self.p.sibling)

    def y_copy(self, t):
        return remote(self.stage.at[t], self.came.at[t], self.y_send.at[t], self.y_recv.at[t], self.p.across)

    def pieces(self, t, f, y):
        s, row = t * self.p.spread + f, 0
        for kind, depth in enumerate(self.depths):
            at = self.rows_of(kind).start + s * depth + y * (depth // 2)
            here = pl.ds(pl.multiple_of(at, 16), depth // 2)
            yield slice(row, row + depth // 2), self.mine[here, :].astype(F32) + self.core[here, :].astype(F32)
            row += depth // 2

    def order(self, i):
        t = self.p.t
        down = LINE - 1 - i - jnp.where(LINE - 1 - i <= t, 1, 0)
        up = i + jnp.where(i >= t, 1, 0)
        return jnp.where(i == LINE - 1, t, jnp.where(t >= LINE // 2, up, down))

    def begin(self):
        for kind in (0, 1):
            self.a_copy(kind).start()
            self.local(kind).start()

    def after_first(self):
        for kind in (0, 1):
            self.a_copy(kind).wait_recv()
            self.local(kind).wait()

        def body(i, carry):
            t = self.order(i)
            for f in range(self.p.spread):
                for where, value in self.pieces(t, f, 1 - self.p.y):
                    self.stage[t, f, where] = value.astype(BF16)
            self.y_copy(t).start()
            return carry

        lax.fori_loop(0, LINE, body, 0)

        def own(t, carry):
            for f in range(self.p.spread):
                for where, value in self.pieces(t, f, self.p.y):
                    self.quarter[t, f, where] = value
            return carry

        lax.fori_loop(0, LINE, own, 0)

    def add(self, t):
        self.y_copy(t).wait_recv()
        self.quarter[t] = self.quarter[t] + self.came[t].astype(F32)

    def after_relay(self):
        lax.fori_loop(0, LINE, lambda i, carry: (self.add(self.order(i)), carry)[1], 0)

    def finish(self):
        for kind in (0, 1):
            self.a_copy(kind).wait_send()
        lax.fori_loop(0, LINE, lambda t, carry: (self.y_copy(t).wait_send(), carry)[1], 0)


class GradientRider:
    def __init__(self, place, given, outs, scratch):
        self.halve = Halve(place, given[:2], outs[0], scratch[:9])
        self.own, self.other = given[2:], outs[1:]
        self.p = place
        self.w_send, self.w_recv = scratch[9:]
        self.partners = [place.beside]

    @staticmethod
    def scratch(spread, depths, width):
        return Halve.scratch(spread, depths, width) + [dma(3), dma(3)]

    def weight(self, i):
        return remote(self.own[i], self.other[i], self.w_send.at[i], self.w_recv.at[i], self.p.beside)

    def begin(self):
        self.halve.begin()
        for i in range(3):
            self.weight(i).start()

    def after_first(self):
        self.halve.after_first()

    def after_line(self):
        pass

    def after_relay(self):
        self.halve.after_relay()

    def finish(self):
        self.halve.finish()
        for i in range(3):
            self.weight(i).wait()


class LineSum:
    def __init__(self, place, depths, quarter, sums, scratch):
        self.p, self.depths, self.quarter, self.sums = place, depths, quarter, sums
        (self.stage, self.came, self.stage_x, self.came_x, self.z_send, self.z_recv, self.x_send, self.x_recv,
         self.e_send, self.e_recv) = scratch
        self.wide = sums[0].shape[1] // 2

    @staticmethod
    def scratch(spread, depths, width):
        rows, wide = sum(depths) // 2, width // 2
        return [
            pltpu.VMEM((LINE, spread, rows, wide), BF16),
            pltpu.VMEM((2, LINE, spread, rows, wide), BF16),
            pltpu.VMEM((rows, wide), BF16),
            pltpu.VMEM((rows, wide), BF16),
            dma(LINE), dma(2, LINE), dma(1), dma(1), dma(3, 2), dma(3, 2),
        ]

    def lanes(self, c):
        return pl.ds(pl.multiple_of(c * self.wide, 128), self.wide)

    def z_copy(self, up, t):
        return remote(self.stage.at[t], self.came.at[up, t], self.z_send.at[t], self.z_recv.at[up, t], self.p.on_line(up))

    def x_copy(self):
        return remote(self.stage_x, self.came_x, self.x_send.at[0], self.x_recv.at[0], self.p.beside)

    def e_copy(self, i, kind, y, c):
        half = self.depths[kind] // 2
        at = self.sums[kind].at[pl.ds(pl.multiple_of(y * half, 8), half), self.lanes(c)]
        return remote(at, at, self.e_send.at[i, kind], self.e_recv.at[i, kind], self.p.across if i == 0 else self.p.sibling)

    def start(self, t):
        p = self.p
        for up, mine in ((1, jnp.logical_and(p.t == 0, t > 0)), (0, jnp.logical_and(p.t == LINE - 1, t < LINE - 1))):

            @pl.when(mine)
            def _(up=up):
                self.stage[t] = self.quarter[t].astype(BF16)
                self.z_copy(up, t).start()

    def relay(self, kind):
        p = self.p

        @pl.when(jnp.logical_and(p.above, p.below))
        def _():
            up = jnp.where(p.t == 1, 1, 0)
            ahead = 2 * up - 1
            t = {"near": p.t + ahead, "far": p.t + 2 * ahead, "back": p.t - ahead}[kind]
            way = 1 - up if kind == "back" else up
            self.z_copy(way, t).wait_recv()
            self.stage[t] = (self.quarter[t] + self.came[way, t].astype(F32)).astype(BF16)
            self.z_copy(way, t).start()

    def after_z(self):
        p = self.p

        for up, there in ((1, p.below), (0, p.above)):

            @pl.when(there)
            def _(up=up):
                self.z_copy(up, p.t).wait_recv()
                self.quarter[p.t] = self.quarter[p.t] + self.came[up, p.t].astype(F32)

        self.stage_x[...] = self.quarter[p.t, 1 - p.f].astype(BF16)
        self.x_copy().start()

    def after_x(self):
        p = self.p
        self.x_copy().wait_recv()
        row = 0
        for kind, depth in enumerate(self.depths):
            half = depth // 2
            value = self.quarter[p.t, p.f, row : row + half] + self.came_x[row : row + half].astype(F32)
            self.sums[kind][pl.ds(pl.multiple_of(p.y * half, 8), half), self.lanes(p.c)] = value
            row += half
        for i in (0, 1):
            for kind in (0, 1):
                self.e_copy(i, kind, p.y, p.c).start()

    def finish(self):
        p = self.p
        for kind in (0, 1):
            self.e_copy(0, kind, 1 - p.y, p.c).wait_recv()
            self.e_copy(2, kind, 1 - p.y, p.c).start()
        for kind in (0, 1):
            self.e_copy(0, kind, p.y, p.c).wait_send()
            self.e_copy(1, kind, p.y, p.c).wait_send()
            self.e_copy(1, kind, p.y, 1 - p.c).wait_recv()
            self.e_copy(2, kind, 1 - p.y, p.c).wait_send()
            self.e_copy(2, kind, 1 - p.y, 1 - p.c).wait_recv()
        self.x_copy().wait_send()

        def body(t, carry):
            @pl.when(t != p.t)
            def _():
                self.z_copy(0, t).wait_send()

            return carry

        lax.fori_loop(0, LINE, body, 0)


class SmallSum:
    def __init__(self, place, grads, total, scratch):
        self.p, self.grads, self.total = place, grads, total
        self.stage, self.came, self.send, self.recv = scratch
        p = place
        near = (p.d + p.spread - 2 * p.spread * lax.rem(p.t, 2), p.e)
        self.far = (lax.rem(p.d + 2 * p.spread, LINE * p.spread), p.e)
        self.partners = [p.sibling, p.across, near, self.far, p.beside]

    @staticmethod
    def scratch(rows, width):
        half = pltpu.VMEM((5, rows, width // 2), F32)
        return [half, half, dma(6), dma(6)]

    def lanes(self, c):
        wide = self.grads.shape[1] // 2
        return pl.ds(pl.multiple_of(c * wide, 128), wide)

    def copy(self, i):
        src = self.grads.at[:, self.lanes(1 - self.p.c)] if i == 0 else self.stage.at[i]
        return remote(src, self.came.at[i], self.send.at[i], self.recv.at[i], self.partners[i])

    def last(self, c):
        at = self.total.at[:, self.lanes(c)]
        return remote(at, at, self.send.at[5], self.recv.at[5], self.p.sibling)

    def step(self, i):
        if i == 0:
            self.copy(0).start()
            return
        self.copy(i - 1).wait_recv()
        mine = self.grads[:, self.lanes(self.p.c)] if i == 1 else self.stage[i - 1]
        value = mine + self.came[i - 1]
        if i < 5:
            self.stage[i] = value
            self.copy(i).start()
        else:
            self.total[:, self.lanes(self.p.c)] = value
            self.last(self.p.c).start()

    def finish(self):
        for i in range(5):
            self.copy(i).wait_send()
        self.last(self.p.c).wait_send()
        self.last(1 - self.p.c).wait_recv()


def dense_reduce_kernel(spread, depths, small0, small1, res, qkv0, out0, quarter1, small_sum, *refs):
    p = Place(spread)
    sums, (small, mine0, mine1), halve_refs, line0, line1, small_refs = split(refs, 2, 3, 9, 10, 10)
    sums0, sums1 = ([ref.at[l] for ref in sums] for l in (0, 1))
    halve = Halve(p, (qkv0, out0), mine0, halve_refs)
    sum0 = LineSum(p, depths, mine0, sums0, line0)
    sum1 = LineSum(p, depths, mine1, sums1, line1)
    little = SmallSum(p, small, small_sum, small_refs)
    greet([p.sibling, p.across, p.beside, little.far], p)
    halve.begin()
    rows = small0.shape[0]
    small[0:rows, :] = small0[...]
    small[rows : 2 * rows, :] = small1[...]
    small[2 * rows :, :] = jnp.zeros((16, small.shape[1]), F32)
    small[2 * rows :, 0:128] = res[0:16, :]
    little.step(0)
    mine1[...] = quarter1[...]
    for i in range(LINE):
        sum1.start(halve.order(i))
    little.step(1)
    halve.after_first()
    little.step(2)

    def arrive(i):
        halve.add(halve.order(i))
        sum0.start(halve.order(i))

    sum1.relay("far")
    sum1.relay("near")
    arrive(0)
    little.step(3)
    sum1.relay("back")
    arrive(1)
    sum0.relay("far")
    sum1.after_z()
    arrive(2)
    sum0.relay("near")
    sum0.relay("back")
    arrive(3)
    little.step(4)
    sum0.after_z()
    sum1.after_x()
    little.step(5)
    sum0.after_x()
    sum1.finish()
    halve.finish()
    little.finish()
    sum0.finish()


def dense_reduce(spread, call_id, smalls, grads0, quarter1):
    count = LINE * spread
    depths = [g.shape[0] // count for g in grads0]
    width = grads0[0].shape[1]
    small = (2 * smalls[0].shape[0] + 16, width)
    line = LineSum.scratch(spread, depths, width)
    mine = pltpu.VMEM(quarter1.shape, F32)
    scratch = [pltpu.VMEM(small, F32), mine, mine] + Halve.scratch(spread, depths, width) + line + line
    return pl.pallas_call(
        functools.partial(dense_reduce_kernel, spread, depths),
        out_shape=[struct(small, F32)] + [struct((2, depth, width), F32) for depth in depths],
        in_specs=[VMEM] * 3 + [ANY, ANY, VMEM],
        out_specs=[VMEM] * 3,
        scratch_shapes=scratch + SmallSum.scratch(*small),
        compiler_params=remote_params(call_id),
    )(*smalls, *grads0, quarter1)


def per_device(
    tokens, seq_lengths, block_perm, routes, norm_gains, w_qkv, w_out, w_router, w_residual, w_const, v_const,
    w_gate, w_up, w_down, cotangent,
):
    rows, width = tokens.shape
    owners = lax.axis_size("expert")
    shards = lax.axis_size("dp")
    spread = shards // LINE
    local = w_gate.shape[1]
    experts = local * owners
    layers = routes.shape[0]
    slots = experts * CAP
    place = lax.axis_index("expert")

    my_place = jnp.sum(jnp.where(jnp.arange(owners) == place, block_perm[0], 0))
    lengths = lax.dynamic_index_in_dim(seq_lengths[0], place, 0, keepdims=False)
    order = jnp.arange(lengths.shape[0])
    ends = jnp.sum(jnp.where(order[:, None] <= order[None, :], lengths[:, None], 0), axis=0)
    doc = jnp.sum((jnp.arange(rows)[:, None] >= ends[None, :]).astype(jnp.int32), axis=1)
    doc_col, doc_row = doc[:, None], doc[None, :]

    own = [[w[l].astype(BF16) for w in (w_gate, w_up, w_down)] for l in range(layers)]

    depth = w_out.shape[1]
    small = jnp.concatenate(
        [
            w_router, w_const[:, 0], w_const[:, 1], jnp.swapaxes(norm_gains, 1, 2), jnp.swapaxes(v_const, 1, 2),
            jnp.zeros((layers, depth, 108), F32),
        ],
        axis=2,
    ).astype(BF16)
    qkv_t = jnp.swapaxes(w_qkv, 1, 2).astype(BF16)
    out_rows = w_out.astype(BF16)
    in_kernels = spread == 2 and owners == 4 and qkv_t.shape[1] % 32 == 0 and depth % 32 == 0
    if in_kernels:
        packed_routes = jnp.zeros((8, 256), jnp.int32).at[: 2 * layers, :rows].set(
            jnp.swapaxes(routes, 1, 2).reshape(2 * layers, rows))
        *gathered, routes_all, gate = dense_gather(spread, 4, (qkv_t, out_rows, small), packed_routes, own[0][0])
        up_own, gate = lax.optimization_barrier((own[0][1], gate))
        weights = [[own[0][0], gate, up_own, from_partner(up_own, 1, spread, LINE), own[0][2]]]
        dense = [(gathered[2], gathered[0], gathered[1])]
        picked = lax.dynamic_index_in_dim(routes_all, my_place, 0, keepdims=False)
        my_routes = jnp.swapaxes(picked[: 2 * layers, :rows].reshape(layers, 2, rows), 1, 2)
    else:
        weights = [
            [part for w, axis in zip(own[l], (2, 2, 1)) for part in pair_weights(w, axis, spread)] for l in range(layers)]
        all_routes = lax.all_gather(routes, "expert", axis=0)
        my_routes = lax.dynamic_index_in_dim(all_routes, my_place, 0, keepdims=False)
        qkv_all = lax.all_gather(qkv_t, "dp", axis=1, tiled=True)
        out_all = lax.all_gather(out_rows, "dp", axis=1, tiled=True)
        small_all = lax.all_gather(small, "dp", axis=1, tiled=True)
        dense = [(small_all[l], qkv_all[l], out_all[l]) for l in range(layers)]

    w_res = jnp.zeros((128, 128), F32).at[: w_residual.shape[0], : w_residual.shape[1]].set(w_residual)

    cols = ((rows, width), F32)
    attention = [((rows, width), BF16), ((rows, 3 * width), BF16), ((HEADS, rows, rows), F32), ((rows, width), BF16)]
    per_token, sent = ((rows, 128), F32), ((slots, width), BF16)

    def group(array):
        return array.reshape(owners, local, CAP, width)

    attn_in0, qkv0, probs0, attn0, mid0, logits0, stat0, out = local_call(
        first_kernel, experts, (tokens, *dense[0], doc_col, doc_row, my_routes[0]),
        attention + [cols, per_token, per_token, sent])
    ride = (*gathered[3:], qkv_t, out_rows, small, *own[1][:2]) if in_kernels else None
    ret0, *kept0 = expert_forward(spread, 0, group(out), weights[0], in_kernels, ride)
    if in_kernels:
        kept0, down, (qkv_all, out_all, small_all), partner = kept0[:3], kept0[3], kept0[4:7], kept0[7:]
        weights[0].append(down)
        dense.append((small_all, qkv_all, out_all))
        weights.append([own[1][0], partner[0], own[1][1], partner[1], own[1][2]])
    ret0 = ret0.reshape(slots, width)
    stream1, attn_in1, qkv1, probs1, attn1, mid1, stat1, out = local_call(
        middle_kernel, experts,
        (mid0, dense[0][0], stat0, ret0, *dense[1], doc_col, doc_row, my_routes[1], logits0, w_res),
        [cols] + attention + [cols, per_token, sent])
    ret1, *kept1 = expert_forward(spread, 1, group(out), weights[1], in_kernels)
    if in_kernels:
        weights[1].append(kept1.pop())
    ret1 = ret1.reshape(slots, width)

    small_grads = ((24, width), F32)
    output, g_small1, extra, out, small_grad1, res_grad = local_call(
        turn_kernel, experts, (mid1, dense[1][0], stat1, ret1, cotangent, logits0, w_res),
        [((rows, width), BF16), per_token, per_token, sent, small_grads, ((128, 128), F32)])
    back, *expert_grads1 = expert_backward(spread, 2, group(out), kept1, weights[1])
    grad_type = BF16 if in_kernels else F32
    dense_grads = [((3 * width, width), grad_type), ((width, width), grad_type), small_grads]
    attention_scratch = [((rows, 3 * width), BF16), ((rows, width), BF16)]
    qkv_grad1, out_grad1, small_grad1, grad, g_small0, out, small_grad0 = local_call(
        between_kernel, experts,
        (cotangent, back.reshape(slots, width), g_small1, stat1, mid1, dense[1][0], stream1, dense[1][1], dense[1][2],
         attn_in1, qkv1, probs1, attn1, small_grad1, mid0, dense[0][0], stat0, ret0, extra),
        dense_grads + [cols, per_token, sent, small_grads], attention_scratch)
    ride = (qkv_grad1, out_grad1, *expert_grads1[1::2]) if in_kernels else None
    came = (None,) * 3
    back, *expert_grads0 = expert_backward(spread, 3, group(out), kept0, weights[0], ride)
    if in_kernels:
        expert_grads0, quarter1, came = expert_grads0[:6], expert_grads0[6], expert_grads0[7:]
    qkv_grad0, out_grad0, small_grad0, tokens_grad = local_call(
        last_kernel, experts,
        (grad, back.reshape(slots, width), g_small0, stat0, mid0, dense[0][0], tokens, dense[0][1], dense[0][2],
         attn_in0, qkv0, probs0, attn0, small_grad0),
        dense_grads + [cols], attention_scratch)

    expert_out = []
    for axis, at in ((2, 0), (2, 1), (1, 2)):
        per_layer = []
        for grads, sent_here in ((expert_grads0, None), (expert_grads1, came[at])):
            n = len(grads) // 3
            per_layer.append(pair_sum(grads[at * n : (at + 1) * n], axis, spread, sent_here))
        expert_out.append(jnp.stack(per_layer))
    gate_grad, up_grad, down_grad = expert_out
    if in_kernels:
        packed, qkv_grad, out_grad = dense_reduce(
            spread, 5, (small_grad0, small_grad1, res_grad), (qkv_grad0, out_grad0), quarter1)
    else:
        packed = jnp.concatenate([small_grad0, small_grad1, jnp.pad(res_grad[:16], ((0, 0), (0, width - 128)))])
        packed = lax.psum(packed, ("dp", "expert"))
        qkv_grad, out_grad = (
            lax.psum(lax.psum_scatter(jnp.stack(pair), "dp", scatter_dimension=1, tiled=True), "expert")
            for pair in ((qkv_grad0, qkv_grad1), (out_grad0, out_grad1)))
    mine = lax.dynamic_slice_in_dim(packed, lax.axis_index("dp") * depth, depth, axis=1)
    mine = jnp.stack([mine[:24], mine[24:48]])
    router_grad = jnp.swapaxes(mine[:, :CONST0], 1, 2)
    const_grad = jnp.swapaxes(mine[:, CONST0:GAIN0].reshape(layers, 2, 2, depth), 2, 3)
    residual_grad = packed[48 : 48 + CONST0, :CONST0]
    return (
        output, tokens_grad, mine[:, GAIN0 : GAIN0 + 2], jnp.swapaxes(qkv_grad, 1, 2), out_grad, router_grad,
        residual_grad, const_grad, mine[:, VECTOR0 : VECTOR0 + 2], gate_grad, up_grad, down_grad,
    )


def solution(mesh):
    in_specs = (
        P(("dp", "expert"), None), P("dp", None, None), P("dp", None), P(None, ("dp", "expert"), None),
        P(None, None, "dp"), P(None, None, "dp"), P(None, "dp", None), P(None, "dp", None), P(),
        P(None, None, "dp", None), P(None, None, "dp"), P(None, "expert", None, "dp"), P(None, "expert", None, "dp"),
        P(None, "expert", "dp", None), P(("dp", "expert"), None),
    )
    out_specs = (
        P(("dp", "expert"), None), P(("dp", "expert"), None), P(None, None, "dp"), P(None, None, "dp"),
        P(None, "dp", None), P(None, "dp", None), P(), P(None, None, "dp", None), P(None, None, "dp"),
        P(None, "expert", None, "dp"), P(None, "expert", None, "dp"), P(None, "expert", "dp", None),
    )
    return jax.shard_map(per_device, mesh=mesh, in_specs=in_specs, out_specs=out_specs, check_vma=False)
```

```python
import functools

import jax
import jax.numpy as jnp
from jax import lax
from jax.experimental import pallas as pl
from jax.experimental.pallas import tpu as pltpu
from jax.sharding import PartitionSpec as P

HEADS = 12
CAP = 48
LINE = 4
EPSILON = 1e-05
MASKED = -1e30
HIGH = lax.Precision.HIGHEST
F32 = jnp.float32
BF16 = jnp.bfloat16
MESH = pl.DeviceIdType.MESH
VMEM = pl.BlockSpec(memory_space=pltpu.VMEM)
ANY = pl.BlockSpec(memory_space=pl.ANY)

CONST0, GAIN0, VECTOR0 = 12, 16, 18
STAT = {
    name: i
    for i, name in enumerate(
        ("r0", "r1", "share0", "share1", "slot0", "slot1", "p00", "p01", "p10", "p11")
    )
}


SMEM = pl.BlockSpec(memory_space=pltpu.SMEM)


def dot_nn(a, b, **kw):
    return lax.dot_general(a, b, (((1,), (0,)), ((), ())), preferred_element_type=F32, **kw)


def dot_nt(a, b, **kw):
    return lax.dot_general(a, b, (((1,), (1,)), ((), ())), preferred_element_type=F32, **kw)


def dot_tn(a, b, **kw):
    return lax.dot_general(a, b, (((0,), (0,)), ((), ())), preferred_element_type=F32, **kw)


def lanes(rows, width=128):
    return lax.broadcasted_iota(jnp.int32, (rows, width), 1)


def rms_scale(values):
    return lax.rsqrt(jnp.mean(values * values, axis=-1, keepdims=True) + EPSILON)


def row_vectors(small):
    pick = lax.broadcasted_iota(jnp.int32, (8, 128), 0) + GAIN0 == lanes(8)
    rows = dot_nt(pick.astype(BF16), small)
    return rows[0:1], rows[1:2], rows[2:3], rows[3:4]


def stat_columns(stat):
    return {name: stat[:, i : i + 1] for name, i in STAT.items()}


def slot_picks(stat, slots):
    place = lanes(stat["slot0"].shape[0], slots).astype(F32)
    first = (place == stat["slot0"]).astype(BF16)
    second = (place == stat["slot1"]).astype(BF16)
    return first, second


def const_weights(stat, experts):
    out = []
    for kind in (experts + 1, experts + 2, experts + 3):
        out.append(
            stat["share0"] * (stat["r0"] == kind).astype(F32)
            + stat["share1"] * (stat["r1"] == kind).astype(F32)
        )
    return out


def doc_index(lengths, places):
    place, end = lax.axis_index("expert"), 0
    doc = jnp.zeros_like(places)
    for j in range(lengths.shape[2]):
        end = end + lengths[0, place, j]
        doc = doc + (places >= end).astype(jnp.int32)
    return doc


def block_routes(perm, routes_all, layer, rows):
    mine = routes_all[perm[0, lax.axis_index("expert")]].astype(F32)
    routes = jnp.transpose(mine)[:rows].astype(jnp.int32)
    return routes[:, 2 * layer : 2 * layer + 1], routes[:, 2 * layer + 1 : 2 * layer + 2]


def padded(w_res, ref):
    count = w_res.shape[0]
    ref[...] = jnp.zeros(ref.shape, F32)
    ref[0:count, 0:count] = w_res[...]
    return ref[...]


def attend_part(stream, small, w_qkv_t, w_out, lengths, attn_in_ref, qkv_ref, probs_ref, attn_ref):
    rows, width = stream.shape
    gain, _, _, _ = row_vectors(small)
    attn_in_ref[...] = (stream * rms_scale(stream) * gain).astype(BF16)

    def project(i, carry):
        at = pl.multiple_of(i * width, width)
        qkv_ref[:, pl.ds(at, width)] = dot_nt(
            attn_in_ref[...], w_qkv_t[pl.ds(at, width), :]
        ).astype(BF16)
        return carry

    lax.fori_loop(0, 3, project, 0)
    head_dim = width // HEADS
    factor = 1.0 / head_dim**0.5
    allowed = jnp.logical_and(
        doc_index(lengths, lax.broadcasted_iota(jnp.int32, (rows, 1), 0))
        == doc_index(lengths, lax.broadcasted_iota(jnp.int32, (1, rows), 1)),
        lax.broadcasted_iota(jnp.int32, (rows, rows), 0)
        >= lax.broadcasted_iota(jnp.int32, (rows, rows), 1),
    )

    def heads(i, carry):
        at = pl.multiple_of(i * 2 * head_dim, 2 * head_dim)
        query = qkv_ref[:, pl.ds(at, 2 * head_dim)]
        key = qkv_ref[:, pl.ds(pl.multiple_of(at + width, 128), 2 * head_dim)]
        value = qkv_ref[:, pl.ds(pl.multiple_of(at + 2 * width, 128), 2 * head_dim)]
        second = lanes(rows, 2 * head_dim) >= head_dim
        mixed = []
        for sub in (0, 1):
            mine = second if sub else jnp.logical_not(second)
            scores = dot_nt(jnp.where(mine, query, jnp.zeros_like(query)), key) * factor
            scores = jnp.where(allowed, scores, MASKED)
            exponent = jnp.exp(scores - jnp.max(scores, axis=-1, keepdims=True))
            probs = exponent / jnp.sum(exponent, axis=-1, keepdims=True)
            probs_ref[2 * i + sub] = probs
            mixed.append(dot_nn(probs.astype(BF16), value))
        attn_ref[:, pl.ds(at, 2 * head_dim)] = jnp.where(second, mixed[1], mixed[0]).astype(BF16)
        return carry

    lax.fori_loop(0, HEADS // 2, heads, 0, unroll=2)
    return stream + dot_nn(attn_ref[...], w_out[...])


def route_part(mid, small, routes, prev_logits, w_res, experts):
    rows = mid.shape[0]
    _, gain, _, _ = row_vectors(small)
    hidden = (mid * rms_scale(mid) * gain).astype(BF16)
    lane = lanes(rows)
    raw = dot_nn(hidden, small)
    logits = jnp.where(lane < CONST0, raw, 0.0)
    if prev_logits is not None:
        logits = logits + dot_nn(prev_logits, w_res, precision=HIGH)
    r0, r1 = routes
    hot0, hot1 = (lane == r0).astype(F32), (lane == r1).astype(F32)
    c0 = jnp.sum(hot0 * logits, axis=-1, keepdims=True)
    c1 = jnp.sum(hot1 * logits, axis=-1, keepdims=True)
    peak = jnp.maximum(c0, c1)
    e0, e1 = jnp.exp(c0 - peak), jnp.exp(c1 - peak)
    total = e0 + e1
    share0, share1 = e0 / total, e1 / total
    probs = []
    for j in (0, 1):
        a = raw[:, CONST0 + 2 * j : CONST0 + 2 * j + 1]
        b = raw[:, CONST0 + 2 * j + 1 : CONST0 + 2 * j + 2]
        top = jnp.maximum(a, b)
        ea, eb = jnp.exp(a - top), jnp.exp(b - top)
        probs += [ea / (ea + eb), eb / (ea + eb)]
    earlier = lax.broadcasted_iota(jnp.int32, (rows, rows), 0) > lax.broadcasted_iota(
        jnp.int32, (rows, rows), 1
    )
    before = dot_nn(earlier.astype(BF16), (hot0 + hot1).astype(BF16))
    f0, f1 = r0.astype(F32), r1.astype(F32)
    slot0 = jnp.where(
        r0 < experts, f0 * CAP + jnp.sum(before * hot0, axis=-1, keepdims=True), -1.0
    )
    slot1 = jnp.where(
        r1 < experts, f1 * CAP + jnp.sum(before * hot1, axis=-1, keepdims=True), -1.0
    )
    stat = jnp.zeros((rows, 128), F32)
    for i, column in enumerate([f0, f1, share0, share1, slot0, slot1] + probs):
        stat = jnp.where(lane == i, column, stat)
    first, second = slot_picks({"slot0": slot0, "slot1": slot1}, experts * CAP)
    outgoing = dot_tn(first + second, hidden).astype(BF16)
    return logits, stat, outgoing


def combine_part(mid, small, stat, returned, experts):
    _, gain, vec0, vec1 = row_vectors(small)
    hidden_full = mid * rms_scale(mid) * gain
    first, second = slot_picks(stat, experts * CAP)
    pair0, pair1 = dot_nn(first, returned), dot_nn(second, returned)
    copy, const0, const1 = const_weights(stat, experts)
    local = copy + const0 * stat["p00"] + const1 * stat["p10"]
    moe = stat["share0"] * pair0 + stat["share1"] * pair1 + local * hidden_full
    moe = moe + (const0 * stat["p01"]) * vec0 + (const1 * stat["p11"]) * vec1
    return mid + moe, hidden_full, pair0, pair1


def share_backward(grad, small, stat, hidden_full, pair0, pair1, extra, experts):
    rows = grad.shape[0]
    _, _, vec0, vec1 = row_vectors(small)
    first, second = slot_picks(stat, experts * CAP)
    lane = lanes(rows).astype(F32)
    rowsum = functools.partial(jnp.sum, axis=-1, keepdims=True)
    dot_hidden = rowsum(grad * hidden_full)
    dot_vec = (rowsum(grad * vec0), rowsum(grad * vec1))
    _, const0, const1 = const_weights(stat, experts)
    probs = ((stat["p00"], stat["p01"]), (stat["p10"], stat["p11"]))
    value = [probs[j][0] * dot_hidden + probs[j][1] * dot_vec[j] for j in (0, 1)]
    shares = []
    for r, pair in ((stat["r0"], pair0), (stat["r1"], pair1)):
        shares.append(
            rowsum(grad * pair)
            + (r == experts + 1).astype(F32) * dot_hidden
            + (r == experts + 2).astype(F32) * value[0]
            + (r == experts + 3).astype(F32) * value[1]
        )
    inner = stat["share0"] * shares[0] + stat["share1"] * shares[1]
    g_small = (lane == stat["r0"]).astype(F32) * (stat["share0"] * (shares[0] - inner))
    g_small = g_small + (lane == stat["r1"]).astype(F32) * (stat["share1"] * (shares[1] - inner))
    if extra is not None:
        g_small = g_small + extra
    g_logits = g_small
    for j, weight in ((0, const0), (1, const1)):
        q = (weight * dot_hidden, weight * dot_vec[j])
        mean = probs[j][0] * q[0] + probs[j][1] * q[1]
        for c in (0, 1):
            g_small = jnp.where(lane == CONST0 + 2 * j + c, probs[j][c] * (q[c] - mean), g_small)
    sent0 = (jnp.where(stat["r0"] < experts, stat["share0"], 0.0) * grad).astype(BF16)
    sent1 = (jnp.where(stat["r1"] < experts, stat["share1"], 0.0) * grad).astype(BF16)
    outgoing = (dot_tn(first, sent0) + dot_tn(second, sent1)).astype(BF16)
    hidden = hidden_full.astype(BF16).astype(F32)
    projections = dot_tn(g_small, hidden, precision=HIGH)
    vector0 = jnp.sum((const0 * stat["p01"]) * grad, axis=0, keepdims=True)
    vector1 = jnp.sum((const1 * stat["p11"]) * grad, axis=0, keepdims=True)
    return g_small, g_logits, outgoing, projections, vector0, vector1


def store_small(ref, projections, vector0, vector1):
    ref[0:16, :] = projections[0:16]
    ref[16:24, :] = jnp.zeros((8, ref.shape[1]), F32)
    ref[VECTOR0 : VECTOR0 + 1, :] = vector0
    ref[VECTOR0 + 1 : VECTOR0 + 2, :] = vector1


def first_kernel(experts, tokens, small, w_qkv_t, w_out, lengths, perm, routes_all,
                 attn_in, qkv, probs, attn, mid_ref, logits_ref, stat_ref, out_ref):
    mid = attend_part(tokens[...].astype(F32), small[...], w_qkv_t, w_out, lengths, attn_in, qkv, probs, attn)
    mid_ref[...] = mid
    routes = block_routes(perm, routes_all, 0, mid.shape[0])
    logits, stat, out = route_part(mid, small[...], routes, None, None, experts)
    logits_ref[...], stat_ref[...], out_ref[...] = logits, stat, out


def middle_kernel(experts, mid_in, small_in, stat_in, returned, small, w_qkv_t, w_out, lengths, perm, routes_all, logits_in, w_res,
                  stream_ref, attn_in, qkv, probs, attn, mid_ref, stat_ref, out_ref, res_ref):
    stream, _, _, _ = combine_part(mid_in[...], small_in[...], stat_columns(stat_in[...]), returned[...], experts)
    stream_ref[...] = stream
    mid = attend_part(stream, small[...], w_qkv_t, w_out, lengths, attn_in, qkv, probs, attn)
    mid_ref[...] = mid
    routes = block_routes(perm, routes_all, 1, mid.shape[0])
    _, stat, out = route_part(mid, small[...], routes, logits_in[...], padded(w_res, res_ref), experts)
    stat_ref[...], out_ref[...] = stat, out


def turn_kernel(experts, mid, small, stat_in, returned, cotangent, logits_in, w_res,
                output, g_small_ref, extra_ref, out_ref, small_grad, res_grad, res_ref):
    stat = stat_columns(stat_in[...])
    stream, hidden_full, pair0, pair1 = combine_part(mid[...], small[...], stat, returned[...], experts)
    output[...] = stream.astype(BF16)
    grad = cotangent[...].astype(F32)
    g_small, g_logits, out, projections, v0, v1 = share_backward(grad, small[...], stat, hidden_full, pair0, pair1, None, experts)
    g_small_ref[...] = g_small
    out_ref[...] = out
    store_small(small_grad, projections, v0, v1)
    res_grad[...] = dot_tn(logits_in[...], g_logits, precision=HIGH)
    extra_ref[...] = dot_nt(g_logits, padded(w_res, res_ref), precision=HIGH)


def layer_backward(experts, grad, back, g_small, stat, mid, small, stream, w_qkv_t, w_out, attn_in, qkv, probs, attn,
                   qkv_grad, out_grad, small_grad, g_qkv, g_attn):
    rows, width = mid.shape
    gain1, gain2, _, _ = row_vectors(small)
    first, second = slot_picks(stat, experts * CAP)
    copy, const0, const1 = const_weights(stat, experts)
    local = copy + const0 * stat["p00"] + const1 * stat["p10"]
    g_full = dot_nt(g_small, small.astype(F32), precision=HIGH) + dot_nn(first + second, back)
    g_full = g_full + grad * local
    s2 = rms_scale(mid)
    small_grad[GAIN0 + 1 : GAIN0 + 2, :] = jnp.sum(g_full * mid * s2, axis=0, keepdims=True)
    m = g_full * gain2
    g_mid = grad + s2 * m - mid * (s2 * s2 * s2 * jnp.mean(m * mid, axis=-1, keepdims=True))
    branch = g_mid.astype(BF16)
    out_grad[...] = dot_tn(attn[...], branch).astype(out_grad.dtype)
    g_attn[...] = dot_nt(branch, w_out[...]).astype(BF16)
    head_dim = width // HEADS
    factor = 1.0 / head_dim**0.5

    def heads(i, carry):
        at = pl.multiple_of(i * 2 * head_dim, 2 * head_dim)
        at_k = pl.multiple_of(at + width, 128)
        at_v = pl.multiple_of(at + 2 * width, 128)
        query = qkv[:, pl.ds(at, 2 * head_dim)]
        key = qkv[:, pl.ds(at_k, 2 * head_dim)]
        value = qkv[:, pl.ds(at_v, 2 * head_dim)]
        ga = g_attn[:, pl.ds(at, 2 * head_dim)]
        second_half = lanes(rows, 2 * head_dim) >= head_dim
        gq, gk, gv = [], [], []
        for sub in (0, 1):
            mine = second_half if sub else jnp.logical_not(second_half)
            p = probs[2 * i + sub]
            gp = dot_nt(jnp.where(mine, ga, jnp.zeros_like(ga)), value)
            gs = (p * (gp - jnp.sum(p * gp, axis=-1, keepdims=True))).astype(BF16)
            gq.append(dot_nn(gs, key))
            gk.append(dot_tn(gs, query))
            gv.append(dot_tn(p.astype(BF16), ga))
        g_qkv[:, pl.ds(at, 2 * head_dim)] = (jnp.where(second_half, gq[1], gq[0]) * factor).astype(BF16)
        g_qkv[:, pl.ds(at_k, 2 * head_dim)] = (jnp.where(second_half, gk[1], gk[0]) * factor).astype(BF16)
        g_qkv[:, pl.ds(at_v, 2 * head_dim)] = jnp.where(second_half, gv[1], gv[0]).astype(BF16)
        return carry

    lax.fori_loop(0, HEADS // 2, heads, 0, unroll=2)

    def weights(i, carry):
        at = pl.multiple_of(i * width, width)
        qkv_grad[pl.ds(at, width), :] = dot_tn(g_qkv[:, pl.ds(at, width)], attn_in[...]).astype(qkv_grad.dtype)
        return carry + dot_nn(g_qkv[:, pl.ds(at, width)], w_qkv_t[pl.ds(at, width), :])

    g_in = lax.fori_loop(0, 3, weights, jnp.zeros((rows, width), F32))
    s1 = rms_scale(stream)
    small_grad[GAIN0 : GAIN0 + 1, :] = jnp.sum(g_in * stream * s1, axis=0, keepdims=True)
    n = g_in * gain1
    return g_mid + s1 * n - stream * (s1 * s1 * s1 * jnp.mean(n * stream, axis=-1, keepdims=True))


def between_kernel(experts, cotangent, back, g_small, stat_in, mid, small, stream, w_qkv_t, w_out, attn_in, qkv, probs, attn, small_grad_in,
                   mid0, small0, stat0_in, returned0, extra,
                   qkv_grad, out_grad, small_grad, grad_ref, g_small0_ref, out_ref, small_grad0, g_qkv, g_attn):
    small_grad[...] = small_grad_in[...]
    grad = layer_backward(experts, cotangent[...].astype(F32), back[...], g_small[...], stat_columns(stat_in[...]), mid[...],
                          small[...], stream[...], w_qkv_t, w_out, attn_in, qkv, probs, attn, qkv_grad, out_grad, small_grad, g_qkv, g_attn)
    grad_ref[...] = grad
    stat0 = stat_columns(stat0_in[...])
    _, hidden_full, pair0, pair1 = combine_part(mid0[...], small0[...], stat0, returned0[...], experts)
    g_small0, _, out, projections, v0, v1 = share_backward(grad, small0[...], stat0, hidden_full, pair0, pair1, extra[...], experts)
    g_small0_ref[...] = g_small0
    out_ref[...] = out
    store_small(small_grad0, projections, v0, v1)


def last_kernel(experts, grad_in, back, g_small, stat_in, mid, small, tokens, w_qkv_t, w_out, attn_in, qkv, probs, attn, small_grad_in,
                qkv_grad, out_grad, small_grad, grad_ref, g_qkv, g_attn):
    small_grad[...] = small_grad_in[...]
    grad_ref[...] = layer_backward(experts, grad_in[...], back[...], g_small[...], stat_columns(stat_in[...]), mid[...], small[...],
                                   tokens[...].astype(F32), w_qkv_t, w_out, attn_in, qkv, probs, attn, qkv_grad, out_grad, small_grad,
                                   g_qkv, g_attn)


def local_call(kernel, experts, args, outs, scratch=(), scalars=()):
    return pl.pallas_call(
        functools.partial(kernel, experts),
        out_shape=[jax.ShapeDtypeStruct(shape, dtype) for shape, dtype in outs],
        in_specs=[SMEM if i in scalars else VMEM for i in range(len(args))],
        out_specs=[VMEM] * len(outs),
        scratch_shapes=[pltpu.VMEM(shape, dtype) for shape, dtype in scratch],
        compiler_params=pltpu.CompilerParams(vmem_limit_bytes=60 * 2**20),
        cost_estimate=pl.CostEstimate(flops=10**10, bytes_accessed=6 * 10**7, transcendentals=0),
    )(*args)


class Place:
    def __init__(self, spread):
        self.spread = spread
        self.d, self.e = lax.axis_index("dp"), lax.axis_index("expert")
        self.t, self.f = self.d // spread, lax.rem(self.d, spread)
        self.y, self.c = self.e // 2, lax.rem(self.e, 2)
        self.above, self.below = self.t < LINE - 1, self.t > 0
        self.inside = jnp.logical_and(self.above, self.below)
        self.up = jnp.where(self.t == 1, 1, 0)
        self.ahead = 2 * self.up - 1
        self.sibling = (self.d, self.e + 1 - 2 * self.c)
        self.across = (self.d, lax.rem(self.e + 2, 4))
        self.corner = (self.d, 3 - self.e)
        self.beside = (self.t * spread + 1 - self.f, self.e)
        self.mates = [(self.d, self.e), self.sibling, self.across, self.corner]

    def on_line(self, up):
        return (self.d + self.spread * (2 * up - 1), self.e)


def greet(always, place):
    barrier = pltpu.get_barrier_semaphore()
    for device in always:
        pl.semaphore_signal(barrier, inc=1, device_id=device, device_id_type=MESH)
    for up, there in ((1, place.above), (0, place.below)):

        @pl.when(there)
        def _(up=up):
            pl.semaphore_signal(barrier, inc=1, device_id=place.on_line(up), device_id_type=MESH)

    ends = place.above.astype(jnp.int32) + place.below.astype(jnp.int32)
    pl.semaphore_wait(barrier, len(always) + ends)


def remote(src, dst, send, recv, device):
    return pltpu.make_async_remote_copy(
        src_ref=src, dst_ref=dst, send_sem=send, recv_sem=recv, device_id=device, device_id_type=MESH)


def dma(*shape):
    return pltpu.SemaphoreType.DMA(shape)


def along(place, body, start=0):
    if start == 0:
        body(place.t)

    def step(k, carry):
        for t in (place.t + k, place.t - k):

            @pl.when(jnp.logical_and(t >= 0, t < LINE))
            def _(t=t):
                body(t)

        return carry

    lax.fori_loop(1, LINE, step, 0)


class Rider:
    partners = ()

    def begin(self):
        pass

    def ready(self):
        pass

    def after_first(self):
        pass

    def after_line(self):
        pass

    def after_relay(self):
        pass

    def finish(self):
        pass


class Line:
    def __init__(self, place, x, part, stage, arrived, final, returned, sems):
        self.p = place
        self.x, self.part, self.stage, self.arrived = x, part, stage, arrived
        self.final, self.returned = final, returned
        (self.out_send, self.x_recv, self.x_send, self.sum_send, self.sum_recv, self.ret_send, self.ret_recv) = sems

    @staticmethod
    def scratch(local, width):
        shape = (local, 4, CAP, width)
        return [
            pltpu.VMEM((local, LINE, 4, CAP, width), BF16),
            pltpu.VMEM((LINE,) + shape, F32),
            pltpu.VMEM((LINE,) + shape, BF16),
            pltpu.VMEM((2, LINE) + shape, BF16),
            pltpu.VMEM((4, local, CAP, width), BF16),
            dma(4), dma(LINE, 4), dma(2, LINE, 4), dma(LINE, 4), dma(2, LINE, 4), dma(4), dma(4),
        ]

    def slot_copy(self, out, i):
        to, p = self.p.mates[i], self.p
        return remote(out.at[to[1]], self.x.at[:, p.t, p.e], self.out_send.at[i], self.x_recv.at[p.t, p.e], to)

    def x_copy(self, up, s, b):
        at = self.x.at[:, s, b]
        return remote(at, at, self.x_send.at[up, s, b], self.x_recv.at[s, b], self.p.on_line(up))

    def sum_copy(self, up, s, b):
        return remote(self.stage.at[s, :, b], self.arrived.at[up, s, :, b], self.sum_send.at[s, b],
                      self.sum_recv.at[up, s, b], self.p.on_line(up))

    def ret_copy(self, i, to_mate=True):
        to = self.p.mates[i]
        row = self.p.e if to_mate else to[1]
        return remote(self.final.at[to[1]], self.returned.at[row], self.ret_send.at[i], self.ret_recv.at[row], to)

    def send_sum(self, up, s, b, total):
        self.stage[s, :, b] = total.astype(BF16)
        self.sum_copy(up, s, b).start()

    def relay(self, kind, i):
        p = self.p

        @pl.when(p.inside)
        def _():
            b = p.mates[i][1]
            s = {"near": p.t + p.ahead, "far": p.t + 2 * p.ahead, "back": p.t - p.ahead}[kind]
            way = 1 - p.up if kind == "back" else p.up
            self.sum_copy(way, s, b).wait_recv()
            self.send_sum(way, s, b, self.part[s, :, b] + self.arrived[way, s, :, b].astype(F32))

    def run(self, out, compute, kept, pieces, rider):
        p = self.p
        t, e = p.t, p.e
        blocks = [b for _, b in p.mates]
        greet(p.mates[1:] + list(rider.partners), p)
        for i in (2, 3, 1):
            self.slot_copy(out, i).start()
        self.x[:, t, e] = out[e]
        rider.begin()
        for i in range(4):
            if i:
                self.x_copy(0, t, blocks[i]).wait_recv()
            for up, there in ((0, p.below), (1, p.above)):

                @pl.when(there)
                def _(up=up, i=i):
                    self.x_copy(up, t, blocks[i]).start()

        rider.ready()

        def step(n, carry):
            k = jnp.where(n < 2, 1, jnp.where(jnp.logical_or(n == 2, n == 5), 2, 3))
            half = jnp.where(jnp.logical_or(n == 1, n >= 4), 1, 0)
            pair = p.y + half - 2 * p.y * half
            first = jnp.where(half == 0, blocks[0], blocks[2])
            second = jnp.where(half == 0, blocks[1], blocks[3])
            for b in (first, second):
                for up, there, onward, before_end in ((0, t + k < LINE, p.below, t == 1), (1, t - k >= 0, p.above, t == LINE - 2)):
                    s = t - k if up else t + k
                    put_off = jnp.logical_and(before_end, n == 1)

                    @pl.when(there)
                    def _(up=up, onward=onward, s=s, b=b, put_off=put_off):
                        self.x_copy(up, s, b).wait_recv()

                        @pl.when(jnp.logical_and(onward, jnp.logical_not(put_off)))
                        def _():
                            self.x_copy(up, s, b).start()

            for up, before_end in ((0, t == 1), (1, t == LINE - 2)):

                @pl.when(jnp.logical_and(before_end, n == 5))
                def _(up=up):
                    for b in (first, second):
                        self.x_copy(up, t - 1 if up else t + 1, b).start()

            @pl.when(jnp.logical_not(p.inside))
            def _():
                s = jnp.where(t == 0, k, LINE - 1 - k)
                compute(s, 2 * pair, 2)

                @pl.when(half == 1)
                def _():
                    kept(s)

            for up, starts, s in ((1, t == 0, k), (0, t == LINE - 1, LINE - 1 - k)):

                @pl.when(starts)
                def _(up=up, s=s):
                    for b in (first, second):
                        self.send_sum(up, s, b, self.part[s, :, b])

            rest = jnp.logical_and(p.inside, jnp.logical_or(n == 5, jnp.logical_and(n >= 1, n <= 2)))

            @pl.when(jnp.logical_or(n == 0, rest))
            def _():
                s = t + p.ahead * jnp.where(n == 0, 0, jnp.where(n == 1, 1, jnp.where(n == 2, -1, 2)))
                compute(s, 0, 4)
                kept(s)

            @pl.when(n == 0)
            def _():
                rider.after_first()

            return carry

        lax.fori_loop(0, 6, step, 0)
        rider.after_line()
        todo = list(pieces)
        for n, (kind, i) in enumerate((
            ("near", 0), ("near", 1), ("far", 0), ("far", 1), ("back", 0), ("far", 2), ("back", 1), ("far", 3),
            ("back", 2), ("near", 2), ("back", 3), ("near", 3),
        )):
            self.relay(kind, i)
            if n % 2 == 1 and todo:
                todo.pop(0)()
        for piece in todo:
            piece()
        rider.after_relay()
        for i, b in enumerate(blocks):
            for up, there in ((1, p.below), (0, p.above)):

                @pl.when(there)
                def _(up=up, b=b):
                    self.sum_copy(up, t, b).wait_recv()
                    self.part[t, :, b] = self.part[t, :, b] + self.arrived[up, t, :, b].astype(F32)

            if i:
                self.final[b] = self.part[t, :, b].astype(BF16)
                self.ret_copy(i).start()
            else:
                self.returned[e] = self.part[t, :, e].astype(BF16)

        def sent(s, carry):
            for i in range(4):
                for up, mine in ((0, jnp.logical_and(p.below, s >= t)), (1, jnp.logical_and(p.above, s <= t))):

                    @pl.when(mine)
                    def _(up=up, i=i):
                        self.x_copy(up, s, i).wait_send()

                @pl.when(s != t)
                def _(i=i):
                    self.sum_copy(0, s, i).wait_send()

            return carry

        for i in (1, 2, 3):
            self.slot_copy(out, i).wait_send()
        lax.fori_loop(0, LINE, sent, 0)
        rider.finish()
        for i in (1, 2, 3):
            self.ret_copy(i).wait_send()
            self.ret_copy(i, False).wait_recv()


def split(refs, *counts):
    out, at = [], 0
    for count in counts:
        out.append(refs[at : at + count])
        at += count
    return out + [refs[at:]]


def expert_forward_kernel(spread, parts, ride, out, *refs):
    weights_in, given, outs, whole, scratch, line_refs, sems, ride_refs = split(
        refs, 3 * parts, 9 if ride else 0, 4, 6 if ride else 0, 3 * parts, 5, 7)
    (g_all, u_all, keep_sem, load_sem), ride_refs = ride_refs[:4], ride_refs[4:]
    returned, x_keep, g_keep, u_keep = outs
    gate, up, down = scratch[:parts], scratch[parts : 2 * parts], scratch[2 * parts :]
    x, part, stage, arrived, final = line_refs
    local, _, _, _, width = x.shape
    p = Place(spread)
    line = Line(p, x, part, stage, arrived, final, returned, sems)
    rider = WeightRider(p, given, whole, ride_refs) if ride else Rider()

    def load(i):
        return pltpu.make_async_copy(weights_in[i], scratch[i], load_sem.at[i])

    for i in range(3 * parts):
        load(i).start()

    def keep_x(s):
        return pltpu.make_async_copy(x.at[:, s], x_keep.at[:, s], keep_sem.at[0, s])

    def keep_g(s):
        return pltpu.make_async_copy(g_all.at[s], g_keep.at[s], keep_sem.at[1, s])

    def keep_u(s):
        return pltpu.make_async_copy(u_all.at[s], u_keep.at[s], keep_sem.at[2, s])

    def kept(s):
        keep_x(s).start()
        keep_g(s).start()
        keep_u(s).start()

    def compute(s, first, count):
        rows = count * CAP
        at = pl.multiple_of(first * CAP, CAP)

        def one(l, carry):
            rows_in = x[l, s, pl.ds(first, count)].reshape(rows, width)
            total = jnp.zeros((rows, width), F32)
            for q in range(parts):
                cols = gate[q].shape[2]
                here = slice(q * cols, (q + 1) * cols)
                g = dot_nn(rows_in, gate[q][l])
                u = dot_nn(rows_in, up[q][l])
                g_all[s, l, pl.ds(at, rows), here] = g
                u_all[s, l, pl.ds(at, rows), here] = u
                act = (g * jax.nn.sigmoid(g) * u).astype(BF16)
                total = total + dot_nn(act, down[q][l])
            part[s, l, pl.ds(first, count)] = total.reshape(count, CAP, width)
            return carry

        lax.fori_loop(0, local, one, 0)

    class Loaded(Rider):
        partners = rider.partners
        after_first, after_line, after_relay, finish = (
            rider.after_first, rider.after_line, rider.after_relay, rider.finish)

        def begin(self):
            rider.begin()

        def ready(self):
            for i in range(3 * parts):
                load(i).wait()

    line.run(out, compute, kept, (), Loaded())
    for s in range(LINE):
        keep_x(s).wait()
        keep_g(s).wait()
        keep_u(s).wait()


def expert_backward_kernel(spread, parts, exchange, ride, out, *refs):
    loads_in, given, outs, came, ride_outs, loads, line_refs, sems, rest = split(
        refs, 3 + 3 * parts, 4 if ride else 0, 1 + 3 * parts - exchange, exchange, 3 if ride else 0, 3 + 3 * parts, 5, 7)
    (act_all, gg_all, gu_all), grads, (load_sem, grad_sem, w_send, w_recv), ride_refs = split(rest, 3, 3 * parts, 4)
    returned, grads_out = outs[0], list(outs[1:])
    if exchange:
        grads_out.insert(1, None)
    x_in, g_all, u_all = loads[:3]
    gate, up, down = loads[3 : 3 + parts], loads[3 + parts : 3 + 2 * parts], loads[3 + 2 * parts :]
    x, part, stage, arrived, final = line_refs
    local, _, _, _, width = x.shape
    p = Place(spread)
    line = Line(p, x, part, stage, arrived, final, returned, sems)
    rider = GradientRider(p, given, ride_outs, ride_refs) if ride else Rider()

    def load(i):
        return pltpu.make_async_copy(loads_in[i], loads[i], load_sem.at[i])

    def store(i, l):
        return pltpu.make_async_copy(grads[i].at[l], grads_out[i].at[l], grad_sem.at[i, l])

    for i in range(3 + 3 * parts):
        load(i).start()

    def compute(s, first, count):
        rows = count * CAP
        at = pl.multiple_of(first * CAP, CAP)
        into = pl.ds(pl.multiple_of((4 * s + first) * CAP, CAP), rows)

        def one(l, carry):
            rows_in = x[l, s, pl.ds(first, count)].reshape(rows, width)
            total = jnp.zeros((rows, width), F32)
            for q in range(parts):
                cols = gate[q].shape[2]
                here = slice(q * cols, (q + 1) * cols)
                g, u = g_all[s, l, pl.ds(at, rows), here], u_all[s, l, pl.ds(at, rows), here]
                g_act = dot_nt(rows_in, down[q][l])
                sigma = jax.nn.sigmoid(g)
                swish = g * sigma
                gg = (g_act * u * sigma * (1.0 + g * (1.0 - sigma))).astype(BF16)
                gu = (g_act * swish).astype(BF16)
                act_all[l, into, here] = (swish * u).astype(BF16)
                gg_all[l, into, here] = gg
                gu_all[l, into, here] = gu
                total = total + dot_nt(gg, gate[q][l]) + dot_nt(gu, up[q][l])
            part[s, l, pl.ds(first, count)] = total.reshape(count, CAP, width)
            return carry

        lax.fori_loop(0, local, one, 0)

    def weights(kind, l):
        x_rows, g_rows = (a[l].reshape(LINE * 4 * CAP, width) for a in (x_in, x))
        value = dot_tn(act_all[l], g_rows) if kind == 2 else dot_tn(x_rows, (gg_all, gu_all)[kind][l])
        for q in range(parts):
            i = kind * parts + q
            cols = gate[q].shape[2]
            here = slice(q * cols, (q + 1) * cols)
            grads[i][l] = (value[here] if kind == 2 else value[:, here]).astype(grads[i].dtype)
            if grads_out[i] is not None:
                store(i, l).start()
        if kind == 0 and l == local - 1:
            for copy in sent_gate():
                copy.start()

    def sent_gate():
        return [remote(grads[1], came[0], w_send.at[0], w_recv.at[0], p.beside)] if exchange else []

    class Loaded(Rider):
        partners = [p.beside] if exchange else []
        after_first, after_line, after_relay, finish = (
            rider.after_first, rider.after_line, rider.after_relay, rider.finish)

        def begin(self):
            rider.begin()

        def ready(self):
            for i in range(3 + 3 * parts):
                load(i).wait()

    pieces = [functools.partial(weights, kind, l) for kind in range(3) for l in range(local)]
    line.run(out, compute, lambda s: None, pieces, Loaded())
    for copy in sent_gate():
        copy.wait()
    for i in range(3 * parts):
        for l in range(local if grads_out[i] is not None else 0):
            store(i, l).wait()


def remote_params(call_id):
    return pltpu.CompilerParams(collective_id=call_id, has_side_effects=True, vmem_limit_bytes=61 * 2**20)


def struct(shape, dtype):
    return jax.ShapeDtypeStruct(tuple(shape), dtype)


def expert_forward(spread, call_id, out, weights, ride=None):
    parts = len(weights) // 3
    _, local, cap, width = out.shape
    columns = sum(w.shape[2] for w in weights[:parts])
    kept = (LINE, local, 4 * cap, columns)
    outs = [struct(out.shape, BF16), struct((local, LINE, 4, cap, width), BF16), struct(kept, F32), struct(kept, F32)]
    scratch = [pltpu.VMEM(w.shape, BF16) for w in weights] + Line.scratch(local, width)
    scratch += [pltpu.VMEM(kept, F32), pltpu.VMEM(kept, F32), dma(3, LINE), dma(3 * parts)]
    more = ride or ()
    count = LINE * spread
    if ride:
        outs += [struct((count * s.shape[1], s.shape[2]), BF16) for s in ride[3:6]]
        outs += [struct(w.shape, BF16) for w in ride[6:]]
        scratch += WeightRider.scratch(count)
    return pl.pallas_call(
        functools.partial(expert_forward_kernel, spread, parts, ride is not None),
        out_shape=outs,
        in_specs=[VMEM] + [ANY] * (len(weights) + len(more)),
        out_specs=[VMEM] + [ANY] * (len(outs) - 1),
        scratch_shapes=scratch,
        compiler_params=remote_params(call_id),
        cost_estimate=pl.CostEstimate(flops=2 * 10**10, bytes_accessed=2 * 10**8, transcendentals=0),
    )(out, *weights, *more)


def expert_backward(spread, call_id, out, kept, weights, exchange=False, ride=None):
    parts = len(weights) // 3
    _, local, cap, width = out.shape
    columns = sum(w.shape[2] for w in weights[:parts])
    loads = list(kept) + list(weights)
    grads = [(w.shape, F32 if i % parts == 0 else BF16) for i, w in enumerate(weights)]
    wide = pltpu.VMEM((local, LINE * 4 * cap, columns), BF16)
    outs = [struct(out.shape, BF16)] + [struct(*g) for i, g in enumerate(grads) if not exchange or i != 1]
    if exchange:
        outs.append(struct(*grads[1]))
    specs = [VMEM] + [ANY] * len(grads)
    scratch = [pltpu.VMEM(a.shape, a.dtype) for a in loads] + Line.scratch(local, width)
    scratch += [wide] * 3 + [pltpu.VMEM(*g) for g in grads] + [dma(len(loads)), dma(len(grads), local), dma(1), dma(1)]
    more = ride or ()
    if ride:
        depths = [g.shape[0] // (LINE * spread) for g in ride[:2]]
        outs.append(struct((LINE, spread, sum(depths) // 2, width // 2), F32))
        outs += [struct(g.shape, BF16) for g in ride[2:]]
        specs += [VMEM, ANY, ANY]
        scratch += GradientRider.scratch(spread, depths, width)
    return pl.pallas_call(
        functools.partial(expert_backward_kernel, spread, parts, int(exchange), ride is not None),
        out_shape=outs,
        in_specs=[VMEM] + [ANY] * (len(loads) + len(more)),
        out_specs=specs,
        scratch_shapes=scratch,
        compiler_params=remote_params(call_id),
        cost_estimate=pl.CostEstimate(flops=4 * 10**10, bytes_accessed=2 * 10**8, transcendentals=0),
    )(out, *loads, *more)


def from_partner(array, shift, spread, groups):
    pairs = [
        (t * spread + (f + shift) % spread, t * spread + f) for t in range(groups) for f in range(spread)
    ]
    return lax.ppermute(array, "dp", pairs)


def to_partner(array, shift, spread, groups):
    pairs = [
        (t * spread + f, t * spread + (f + shift) % spread) for t in range(groups) for f in range(spread)
    ]
    return lax.ppermute(array, "dp", pairs)


def pair_weights(shard, axis, spread):
    parts = [shard] + [from_partner(shard, i, spread, LINE) for i in range(1, spread)]
    if shard.shape[axis] % 128:
        return [jnp.concatenate(parts, axis=axis)]
    return parts


def pair_sum(parts, axis, spread):
    if len(parts) == 1 and spread > 1:
        parts = jnp.split(parts[0], spread, axis=axis)
    total = parts[0]
    for i in range(1, spread):
        total = total + to_partner(parts[i].astype(BF16), i, spread, LINE).astype(F32)
    return total


class LineGather:
    def __init__(self, place, pairs, shards, quarters, sems):
        self.p, self.shards, self.quarters = place, shards, quarters
        self.send, self.recv, self.x_send, self.x_recv = sems
        self.columns = [place.f, 1 - place.f] if pairs else [0]

    @staticmethod
    def shapes(shards, columns):
        (a, wide), (b, _), (c, narrow) = shards
        return [(LINE, columns, a // 2, wide // 2), (LINE, columns, b // 2, wide // 2), (LINE, columns, c, narrow)]

    @staticmethod
    def scratch(columns):
        return [dma(2, LINE, columns, 3), dma(LINE, columns, 3), dma(3), dma(3)]

    def copy(self, kind, up, t, f):
        at = self.quarters[kind].at[t, f]
        return remote(at, at, self.send.at[up, t, f, kind], self.recv.at[t, f, kind], self.p.on_line(up))

    def x_copy(self, kind, f):
        at = self.quarters[kind].at[self.p.t, f]
        return remote(at, at, self.x_send.at[kind], self.x_recv.at[kind], self.p.beside)

    def both_ways(self, f):
        p = self.p
        for up, there in ((0, p.below), (1, p.above)):

            @pl.when(there)
            def _(up=up):
                for kind in range(3):
                    self.copy(kind, up, p.t, f).start()

    def begin(self):
        p, f = self.p, self.columns[0]
        for kind in (0, 1):
            half, wide = self.quarters[kind].shape[2:]
            self.quarters[kind][p.t, f] = self.shards[kind][
                pl.ds(pl.multiple_of(p.y * half, 16), half), pl.ds(pl.multiple_of(p.c * wide, 128), wide)]
        self.quarters[2][p.t, f] = self.shards[2][...]
        for kind in range(3 if len(self.columns) == 2 else 0):
            self.x_copy(kind, f).start()
        self.both_ways(f)

    def beside(self, then):
        for f in self.columns[1:]:
            for kind in range(3):
                self.x_copy(kind, f).wait_recv()
            self.both_ways(f)
            then(self.p.t, f)

    def step(self, k, then):
        p = self.p
        for f in self.columns:
            for up, there, onward in ((0, p.t + k < LINE, p.below), (1, p.t - k >= 0, p.above)):
                t = p.t - k if up else p.t + k

                @pl.when(there)
                def _(up=up, onward=onward, t=t, f=f):
                    for kind in range(3):
                        self.copy(kind, up, t, f).wait_recv()

                    @pl.when(onward)
                    def _():
                        for kind in range(3):
                            self.copy(kind, up, t, f).start()

                    then(t, f)

    def finish(self):
        p = self.p

        def line(t, carry):
            for up, mine in ((0, jnp.logical_and(p.below, t >= p.t)), (1, jnp.logical_and(p.above, t <= p.t))):

                @pl.when(mine)
                def _(up=up):
                    for f in self.columns:
                        for kind in range(3):
                            self.copy(kind, up, t, f).wait_send()

            return carry

        lax.fori_loop(0, LINE, line, 0)
        for f in self.columns[1:]:
            for kind in range(3):
                self.x_copy(kind, 1 - f).wait_send()


class Spread:
    def __init__(self, place, quarters, shards, whole, sems):
        self.p, self.quarters, self.shards, self.whole = place, quarters, shards, whole
        self.y_send, self.y_recv, self.c_send, self.c_recv, self.l_sem, self.s_sem = sems

    @staticmethod
    def scratch(count):
        return [dma(count, 2), dma(count, 2), dma(count, 2, 2), dma(count, 2, 2), dma(count, 3), dma(3)]

    def region(self, kind, s, y, c):
        depth = self.shards[kind].shape[0]
        if kind == 2:
            return self.whole[2].at[pl.ds(pl.multiple_of(s * depth, 16), depth)]
        half, wide = depth // 2, self.shards[kind].shape[1] // 2
        return self.whole[kind].at[
            pl.ds(pl.multiple_of(s * depth + y * half, 16), half), pl.ds(pl.multiple_of(c * wide, 128), wide)]

    def mine(self, kind, s):
        return self.region(kind, s, self.p.y, self.p.c)

    def y_copy(self, kind, src, s):
        return remote(src, self.mine(kind, s), self.y_send.at[s, kind], self.y_recv.at[s, kind], self.p.across)

    def y_came(self, kind, s):
        at = self.region(kind, s, 1 - self.p.y, self.p.c)
        return remote(at, at, self.y_send.at[s, kind], self.y_recv.at[s, kind], self.p.across)

    def c_copy(self, kind, src, s, y):
        return remote(src, self.region(kind, s, y, self.p.c), self.c_send.at[s, y, kind], self.c_recv.at[s, y, kind],
                      self.p.sibling)

    def c_came(self, kind, s, y):
        at = self.region(kind, s, y, 1 - self.p.c)
        return remote(at, at, self.c_send.at[s, y, kind], self.c_recv.at[s, y, kind], self.p.sibling)

    def local(self, kind, src, s):
        return pltpu.make_async_copy(src, self.mine(kind, s), self.l_sem.at[s, kind])

    def shard(self, kind):
        depth = self.shards[kind].shape[0]
        at = self.whole[kind].at[pl.ds(pl.multiple_of(self.p.d * depth, 16), depth)]
        return pltpu.make_async_copy(self.shards[kind], at, self.s_sem.at[kind])

    def own_shard(self):
        for kind in range(3):
            self.shard(kind).start()

    def push(self, s, sources, here=True):
        if here:
            for kind in range(3):
                self.local(kind, sources[kind], s).start()
        for kind in (0, 1):
            self.y_copy(kind, sources[kind], s).start()
            self.c_copy(kind, sources[kind], s, self.p.y).start()

    def across(self, s):
        for kind in (0, 1):
            self.y_came(kind, s).wait_recv()
            self.c_copy(kind, self.region(kind, s, 1 - self.p.y, self.p.c), s, 1 - self.p.y).start()

    def finish_shard(self, s, here=True):
        @pl.when(s != self.p.d)
        def _():
            for kind in range(3 if here else 0):
                self.local(kind, self.mine(kind, s), s).wait()
            for kind in (0, 1):
                self.y_came(kind, s).wait_send()
                for y in (0, 1):
                    self.c_came(kind, s, y).wait_send()
                    self.c_came(kind, s, y).wait_recv()

    def finish_own(self):
        for kind in range(3):
            self.shard(kind).wait()


class WeightRider:
    def __init__(self, place, given, whole, sems):
        self.p, self.quarters, self.own, self.other = place, given[:3], given[6:], whole[3:]
        self.w_send, self.w_recv, self.x_send, self.x_recv, *more = sems
        self.spread = Spread(place, self.quarters, [ref.at[1] for ref in given[3:6]], whole[:3], more)
        self.partners = [place.beside]

    @staticmethod
    def scratch(count):
        return [dma(3), dma(3), dma(LINE, 3), dma(LINE, 3)] + Spread.scratch(count)

    def place_of(self, t):
        return t * self.p.spread + self.p.f

    def beside_of(self, t):
        return t * self.p.spread + 1 - self.p.f

    def x_copy(self, kind, t, s):
        return remote(self.quarters[kind].at[t, 0], self.spread.mine(kind, s), self.x_send.at[t, kind],
                      self.x_recv.at[t, kind], self.p.beside)

    def weight(self, i):
        return remote(self.own[i], self.other[i], self.w_send.at[i], self.w_recv.at[i], self.p.beside)

    def begin(self):
        self.spread.own_shard()

        def body(t):
            for kind in range(3):
                self.x_copy(kind, t, self.place_of(t)).start()

            @pl.when(t != self.p.t)
            def _():
                self.spread.push(self.place_of(t), [q.at[t, 0] for q in self.quarters])

        along(self.p, body)
        for i in range(3):
            self.weight(i).start()

    def after_first(self):
        pass

    def after_line(self):
        def body(t):
            s = self.beside_of(t)
            for kind in range(3):
                self.x_copy(kind, t, s).wait_recv()
            self.spread.push(s, [self.spread.mine(kind, s) for kind in range(3)], here=False)

        along(self.p, body)

    def after_relay(self):
        along(self.p, lambda t: self.spread.across(self.place_of(t)), start=1)
        along(self.p, lambda t: self.spread.across(self.beside_of(t)))

    def finish(self):
        self.spread.finish_own()
        for i in range(3):
            self.weight(i).wait()

        def line(t, carry):
            for kind in range(3):
                self.x_copy(kind, t, self.place_of(t)).wait_send()
            self.spread.finish_shard(self.place_of(t))
            self.spread.finish_shard(self.beside_of(t), here=False)
            return carry

        lax.fori_loop(0, LINE, line, 0)


def dense_gather_kernel(spread, qkv, out, small, routes, *refs):
    p = Place(spread)
    wide, whole, quarters1, (routes_all,), own, partner, quarters0, loaded, rounded, rest = split(refs, 3, 3, 3, 1, 6, 2, 3, 3, 3)
    sems0, sems1, (r_send, r_recv, w_send, w_recv, load_sem, own_sem), spread_sems = split(rest, 4, 4, 6)
    shards0, shards1 = ([ref.at[l] for ref in (qkv, out, small)] for l in (0, 1))
    line0 = LineGather(p, True, shards0, quarters0, sems0)
    line1 = LineGather(p, False, shards1, quarters1, sems1)
    spreading = Spread(p, quarters0, shards0, whole, spread_sems)

    def load(l, kind):
        return pltpu.make_async_copy(wide[kind].at[l], loaded[kind].at[l], load_sem.at[l, kind])

    def store(l, kind):
        return pltpu.make_async_copy(rounded[kind].at[l], own[3 * l + kind], own_sem.at[l, kind])

    def weight(kind):
        return remote(rounded[kind].at[0], partner[kind], w_send.at[kind], w_recv.at[kind], p.beside)

    def round_weights(l, kind):
        load(l, kind).wait()

        def one(i, carry):
            rounded[kind][l, i] = loaded[kind][l, i].astype(BF16)
            return carry

        lax.fori_loop(0, rounded[kind].shape[1], one, 0)
        store(l, kind).start()

    for l in (0, 1):
        for kind in range(3):
            load(l, kind).start()
    greet(p.mates[1:] + [p.beside], p)

    def route_copy(i, row):
        return remote(routes, routes_all.at[row], r_send.at[i], r_recv.at[row], p.mates[i])

    def push(t, f):
        spreading.push(t * spread + f, [q.at[t, f] for q in quarters0])

    line0.begin()
    for kind in (0, 1):
        round_weights(0, kind)
        weight(kind).start()
    routes_all[p.e] = routes[...]
    for i in (1, 2, 3):
        route_copy(i, p.e).start()
    spreading.own_shard()
    line0.beside(push)
    line1.begin()
    lax.fori_loop(1, LINE, lambda k, carry: (line0.step(k, push), carry)[1], 0)
    round_weights(0, 2)
    lax.fori_loop(1, LINE, lambda k, carry: (line1.step(k, lambda t, f: None), carry)[1], 0)
    for kind in range(3):
        round_weights(1, kind)
    along(p, lambda t: spreading.across(t * spread + p.f), start=1)
    along(p, lambda t: spreading.across(t * spread + 1 - p.f))
    spreading.finish_own()
    lax.fori_loop(0, LINE * spread, lambda s, carry: (spreading.finish_shard(s), carry)[1], 0)
    line0.finish()
    line1.finish()
    for l in (0, 1):
        for kind in range(3):
            store(l, kind).wait()
    for kind in (0, 1):
        weight(kind).wait()
    for i in (1, 2, 3):
        route_copy(i, p.e).wait_send()
        route_copy(i, p.mates[i][1]).wait_recv()


def dense_gather(spread, call_id, arrays, routes, wide):
    count = spread * LINE
    shards = [a.shape[1:] for a in arrays]
    pairs, single = LineGather.shapes(shards, 2), LineGather.shapes(shards, 1)
    outs = [struct((count * rows, width), BF16) for rows, width in shards]
    outs += [struct(q, BF16) for q in single] + [struct((4,) + routes.shape, routes.dtype)]
    outs += [struct(w.shape[1:], BF16) for w in wide] * 2 + [struct(w.shape[1:], BF16) for w in wide[:2]]
    scratch = [pltpu.VMEM(q, BF16) for q in pairs] + [pltpu.VMEM(w.shape, F32) for w in wide]
    scratch += [pltpu.VMEM(w.shape, BF16) for w in wide] + LineGather.scratch(2) + LineGather.scratch(1)
    scratch += [dma(4), dma(4), dma(2), dma(2), dma(2, 3), dma(2, 3)]
    return pl.pallas_call(
        functools.partial(dense_gather_kernel, spread),
        out_shape=outs,
        in_specs=[VMEM] * 4 + [ANY] * 3,
        out_specs=[ANY] * 3 + [VMEM] * 4 + [ANY] * 8,
        scratch_shapes=scratch + Spread.scratch(count),
        compiler_params=remote_params(call_id),
        cost_estimate=pl.CostEstimate(flops=10**10, bytes_accessed=10**8, transcendentals=0),
    )(*arrays, routes, *wide)


class Halve:
    def __init__(self, place, grads, quarter, scratch):
        self.p, self.grads, self.quarter = place, grads, quarter
        (self.mine, self.core, self.stage, self.came, self.l_sem, self.a_send, self.a_recv, self.y_send,
         self.y_recv) = scratch
        self.depths = [g.shape[0] // (LINE * place.spread) for g in grads]
        self.wide = grads[0].shape[1] // 2

    @staticmethod
    def scratch(spread, depths, width):
        count, rows, wide = LINE * spread, sum(depths) // 2, width // 2
        half = pltpu.VMEM((LINE, spread, rows, wide), BF16)
        everything = pltpu.VMEM((count * sum(depths), wide), BF16)
        return [everything, everything, half, half, dma(2), dma(2), dma(2), dma(LINE), dma(LINE)]

    def rows_of(self, kind):
        first = 0 if kind == 0 else self.grads[0].shape[0]
        return slice(first, first + self.grads[kind].shape[0])

    def lanes(self, c):
        return pl.ds(pl.multiple_of(c * self.wide, 128), self.wide)

    def local(self, kind):
        return pltpu.make_async_copy(
            self.grads[kind].at[:, self.lanes(self.p.c)], self.mine.at[self.rows_of(kind)], self.l_sem.at[kind])

    def a_copy(self, kind):
        return remote(self.grads[kind].at[:, self.lanes(1 - self.p.c)], self.core.at[self.rows_of(kind)],
                      self.a_send.at[kind], self.a_recv.at[kind], self.p.sibling)

    def y_copy(self, t):
        return remote(self.stage.at[t], self.came.at[t], self.y_send.at[t], self.y_recv.at[t], self.p.across)

    def pieces(self, t, f, y):
        s, row = t * self.p.spread + f, 0
        for kind, depth in enumerate(self.depths):
            at = self.rows_of(kind).start + s * depth + y * (depth // 2)
            here = pl.ds(pl.multiple_of(at, 16), depth // 2)
            yield slice(row, row + depth // 2), self.mine[here, :].astype(F32) + self.core[here, :].astype(F32)
            row += depth // 2

    def order(self, i):
        t = self.p.t
        down = LINE - 1 - i - jnp.where(LINE - 1 - i <= t, 1, 0)
        up = i + jnp.where(i >= t, 1, 0)
        return jnp.where(i == LINE - 1, t, jnp.where(t >= LINE // 2, up, down))

    def begin(self):
        for kind in (0, 1):
            self.a_copy(kind).start()
            self.local(kind).start()

    def after_first(self):
        for kind in (0, 1):
            self.a_copy(kind).wait_recv()
            self.local(kind).wait()

        def body(i, carry):
            t = self.order(i)
            for f in range(self.p.spread):
                for where, value in self.pieces(t, f, 1 - self.p.y):
                    self.stage[t, f, where] = value.astype(BF16)
            self.y_copy(t).start()
            return carry

        lax.fori_loop(0, LINE, body, 0)

        def own(t, carry):
            for f in range(self.p.spread):
                for where, value in self.pieces(t, f, self.p.y):
                    self.quarter[t, f, where] = value
            return carry

        lax.fori_loop(0, LINE, own, 0)

    def add(self, t):
        self.y_copy(t).wait_recv()
        self.quarter[t] = self.quarter[t] + self.came[t].astype(F32)

    def after_relay(self):
        lax.fori_loop(0, LINE, lambda i, carry: (self.add(self.order(i)), carry)[1], 0)

    def finish(self):
        for kind in (0, 1):
            self.a_copy(kind).wait_send()
        lax.fori_loop(0, LINE, lambda t, carry: (self.y_copy(t).wait_send(), carry)[1], 0)


class GradientRider:
    def __init__(self, place, given, outs, scratch):
        self.halve = Halve(place, given[:2], outs[0], scratch[:9])
        self.own, self.other = given[2:], outs[1:]
        self.p = place
        self.w_send, self.w_recv = scratch[9:]

    @staticmethod
    def scratch(spread, depths, width):
        return Halve.scratch(spread, depths, width) + [dma(2), dma(2)]

    def weight(self, i):
        return remote(self.own[i], self.other[i], self.w_send.at[i], self.w_recv.at[i], self.p.beside)

    def begin(self):
        self.halve.begin()
        for i in range(2):
            self.weight(i).start()

    def after_first(self):
        self.halve.after_first()

    def after_line(self):
        pass

    def after_relay(self):
        self.halve.after_relay()

    def finish(self):
        self.halve.finish()
        for i in range(2):
            self.weight(i).wait()


class LineSum:
    def __init__(self, place, depths, quarter, sums, scratch):
        self.p, self.depths, self.quarter, self.sums = place, depths, quarter, sums
        (self.stage, self.came, self.stage_x, self.came_x, self.z_send, self.z_recv, self.x_send, self.x_recv,
         self.e_send, self.e_recv) = scratch
        self.wide = sums[0].shape[1] // 2

    @staticmethod
    def scratch(spread, depths, width):
        rows, wide = sum(depths) // 2, width // 2
        return [
            pltpu.VMEM((LINE, spread, rows, wide), BF16),
            pltpu.VMEM((2, LINE, spread, rows, wide), BF16),
            pltpu.VMEM((rows, wide), BF16),
            pltpu.VMEM((rows, wide), BF16),
            dma(LINE), dma(2, LINE), dma(1), dma(1), dma(3, 2), dma(3, 2),
        ]

    def lanes(self, c):
        return pl.ds(pl.multiple_of(c * self.wide, 128), self.wide)

    def z_copy(self, up, t):
        return remote(self.stage.at[t], self.came.at[up, t], self.z_send.at[t], self.z_recv.at[up, t], self.p.on_line(up))

    def x_copy(self):
        return remote(self.stage_x, self.came_x, self.x_send.at[0], self.x_recv.at[0], self.p.beside)

    def e_copy(self, i, kind, y, c):
        half = self.depths[kind] // 2
        at = self.sums[kind].at[pl.ds(pl.multiple_of(y * half, 8), half), self.lanes(c)]
        return remote(at, at, self.e_send.at[i, kind], self.e_recv.at[i, kind], self.p.across if i == 0 else self.p.sibling)

    def start(self, t):
        p = self.p
        for up, mine in ((1, jnp.logical_and(p.t == 0, t > 0)), (0, jnp.logical_and(p.t == LINE - 1, t < LINE - 1))):

            @pl.when(mine)
            def _(up=up):
                self.stage[t] = self.quarter[t].astype(BF16)
                self.z_copy(up, t).start()

    def relay(self, kind):
        p = self.p

        @pl.when(p.inside)
        def _():
            t = {"near": p.t + p.ahead, "far": p.t + 2 * p.ahead, "back": p.t - p.ahead}[kind]
            way = 1 - p.up if kind == "back" else p.up
            self.z_copy(way, t).wait_recv()
            self.stage[t] = (self.quarter[t] + self.came[way, t].astype(F32)).astype(BF16)
            self.z_copy(way, t).start()

    def after_z(self):
        p = self.p

        for up, there in ((1, p.below), (0, p.above)):

            @pl.when(there)
            def _(up=up):
                self.z_copy(up, p.t).wait_recv()
                self.quarter[p.t] = self.quarter[p.t] + self.came[up, p.t].astype(F32)

        self.stage_x[...] = self.quarter[p.t, 1 - p.f].astype(BF16)
        self.x_copy().start()

    def after_x(self):
        p = self.p
        self.x_copy().wait_recv()
        row = 0
        for kind, depth in enumerate(self.depths):
            half = depth // 2
            value = self.quarter[p.t, p.f, row : row + half] + self.came_x[row : row + half].astype(F32)
            self.sums[kind][pl.ds(pl.multiple_of(p.y * half, 8), half), self.lanes(p.c)] = value
            row += half
        for i in (0, 1):
            for kind in (0, 1):
                self.e_copy(i, kind, p.y, p.c).start()

    def finish(self):
        p = self.p
        for kind in (0, 1):
            self.e_copy(0, kind, 1 - p.y, p.c).wait_recv()
            self.e_copy(2, kind, 1 - p.y, p.c).start()
        for kind in (0, 1):
            self.e_copy(0, kind, p.y, p.c).wait_send()
            self.e_copy(1, kind, p.y, p.c).wait_send()
            self.e_copy(1, kind, p.y, 1 - p.c).wait_recv()
            self.e_copy(2, kind, 1 - p.y, p.c).wait_send()
            self.e_copy(2, kind, 1 - p.y, 1 - p.c).wait_recv()
        self.x_copy().wait_send()

        def body(t, carry):
            @pl.when(t != p.t)
            def _():
                self.z_copy(0, t).wait_send()

            return carry

        lax.fori_loop(0, LINE, body, 0)


class SmallSum:
    def __init__(self, place, grads, total, scratch):
        self.p, self.grads, self.total = place, grads, total
        self.stage, self.came, self.send, self.recv = scratch
        p = place
        near = (p.d + p.spread - 2 * p.spread * lax.rem(p.t, 2), p.e)
        self.far = (lax.rem(p.d + 2 * p.spread, LINE * p.spread), p.e)
        self.partners = [p.sibling, p.across, near, self.far, p.beside]

    @staticmethod
    def scratch(rows, width):
        half = pltpu.VMEM((5, rows, width // 2), F32)
        return [half, half, dma(6), dma(6)]

    def lanes(self, c):
        wide = self.grads.shape[1] // 2
        return pl.ds(pl.multiple_of(c * wide, 128), wide)

    def copy(self, i):
        src = self.grads.at[:, self.lanes(1 - self.p.c)] if i == 0 else self.stage.at[i]
        return remote(src, self.came.at[i], self.send.at[i], self.recv.at[i], self.partners[i])

    def last(self, c):
        at = self.total.at[:, self.lanes(c)]
        return remote(at, at, self.send.at[5], self.recv.at[5], self.p.sibling)

    def step(self, i):
        if i == 0:
            self.copy(0).start()
            return
        self.copy(i - 1).wait_recv()
        mine = self.grads[:, self.lanes(self.p.c)] if i == 1 else self.stage[i - 1]
        value = mine + self.came[i - 1]
        if i < 5:
            self.stage[i] = value
            self.copy(i).start()
        else:
            self.total[:, self.lanes(self.p.c)] = value
            self.last(self.p.c).start()

    def finish(self):
        for i in range(5):
            self.copy(i).wait_send()
        self.last(self.p.c).wait_send()
        self.last(1 - self.p.c).wait_recv()


def dense_reduce_kernel(spread, depths, small0, small1, res, qkv0, out0, quarter1, up0, down0, small_sum, *refs):
    p = Place(spread)
    sums, came, (small, mine0, mine1), (w_send, w_recv), halve_refs, line0, line1, small_refs = split(refs, 2, 2, 3, 2, 9, 10, 10)
    sums0, sums1 = ([ref.at[l] for ref in sums] for l in (0, 1))
    halve = Halve(p, (qkv0, out0), mine0, halve_refs)
    sum0 = LineSum(p, depths, mine0, sums0, line0)
    sum1 = LineSum(p, depths, mine1, sums1, line1)
    little = SmallSum(p, small, small_sum, small_refs)
    weights = [remote(w, came[i], w_send.at[i], w_recv.at[i], p.beside) for i, w in enumerate((up0, down0))]
    greet([p.sibling, p.across, p.beside, little.far], p)
    halve.begin()
    for copy in weights:
        copy.start()
    rows = small0.shape[0]
    small[0:rows, :] = small0[...]
    small[rows : 2 * rows, :] = small1[...]
    small[2 * rows :, :] = jnp.zeros((16, small.shape[1]), F32)
    small[2 * rows :, 0:128] = res[0:16, :]
    little.step(0)
    mine1[...] = quarter1[...]
    for i in range(LINE):
        sum1.start(halve.order(i))
    little.step(1)
    halve.after_first()
    little.step(2)

    def arrive(i):
        halve.add(halve.order(i))
        sum0.start(halve.order(i))

    sum1.relay("far")
    sum1.relay("near")
    arrive(0)
    little.step(3)
    sum1.relay("back")
    arrive(1)
    sum0.relay("far")
    sum1.after_z()
    arrive(2)
    sum0.relay("near")
    sum0.relay("back")
    arrive(3)
    little.step(4)
    sum0.after_z()
    sum1.after_x()
    little.step(5)
    sum0.after_x()
    sum1.finish()
    halve.finish()
    little.finish()
    sum0.finish()
    for copy in weights:
        copy.wait()


def dense_reduce(spread, call_id, smalls, grads0, quarter1, weights0):
    count = LINE * spread
    depths = [g.shape[0] // count for g in grads0]
    width = grads0[0].shape[1]
    small = (2 * smalls[0].shape[0] + 16, width)
    line = LineSum.scratch(spread, depths, width)
    mine = pltpu.VMEM(quarter1.shape, F32)
    scratch = [pltpu.VMEM(small, F32), mine, mine, dma(2), dma(2)] + Halve.scratch(spread, depths, width) + line + line
    return pl.pallas_call(
        functools.partial(dense_reduce_kernel, spread, depths),
        out_shape=[struct(small, F32)] + [struct((2, depth, width), F32) for depth in depths]
        + [struct(w.shape, BF16) for w in weights0],
        in_specs=[VMEM] * 3 + [ANY, ANY, VMEM, ANY, ANY],
        out_specs=[VMEM] * 3 + [ANY] * 2,
        scratch_shapes=scratch + SmallSum.scratch(*small),
        compiler_params=remote_params(call_id),
        cost_estimate=pl.CostEstimate(flops=2 * 10**10, bytes_accessed=2 * 10**8, transcendentals=0),
    )(*smalls, *grads0, quarter1, *weights0)


def per_device(
    tokens, seq_lengths, block_perm, routes, norm_gains, w_qkv, w_out, w_router, w_residual, w_const, v_const,
    w_gate, w_up, w_down, cotangent,
):
    rows, width = tokens.shape
    owners = lax.axis_size("expert")
    shards = lax.axis_size("dp")
    spread = shards // LINE
    local = w_gate.shape[1]
    experts = local * owners
    layers = routes.shape[0]
    slots = experts * CAP

    packed_routes = jnp.zeros((8, -(-rows // 128) * 128), jnp.int32).at[: 2 * layers, :rows].set(
        jnp.swapaxes(routes, 1, 2).reshape(2 * layers, rows))

    depth = w_out.shape[1]
    small = jnp.concatenate(
        [
            w_router, w_const[:, 0], w_const[:, 1], jnp.swapaxes(norm_gains, 1, 2), jnp.swapaxes(v_const, 1, 2),
            jnp.zeros((layers, depth, 108), F32),
        ],
        axis=2,
    ).astype(BF16)
    qkv_t = jnp.swapaxes(w_qkv, 1, 2).astype(BF16)
    out_rows = w_out.astype(BF16)
    in_kernels = spread == 2 and owners == 4 and qkv_t.shape[1] % 32 == 0 and depth % 32 == 0
    if in_kernels:
        *gathered, routes_all, g0, u0, d0, g1, u1, d1, gate, up = dense_gather(
            spread, 4, (qkv_t, out_rows, small), packed_routes, (w_gate, w_up, w_down))
        weights = [[g0, gate, u0, up, d0, from_partner(d0, 1, spread, LINE)]]
        dense = [(gathered[2], gathered[0], gathered[1])]
    else:
        weights = []
        for l in range(layers):
            own = [(w_gate[l].astype(BF16), 2), (w_up[l].astype(BF16), 2), (w_down[l].astype(BF16), 1)]
            weights.append([part for w, axis in own for part in pair_weights(w, axis, spread)])
        routes_all = lax.all_gather(packed_routes, "expert", axis=0)
        qkv_all = lax.all_gather(qkv_t, "dp", axis=1, tiled=True)
        out_all = lax.all_gather(out_rows, "dp", axis=1, tiled=True)
        small_all = lax.all_gather(small, "dp", axis=1, tiled=True)
        dense = [(small_all[l], qkv_all[l], out_all[l]) for l in range(layers)]

    cols = ((rows, width), F32)
    attention = [((rows, width), BF16), ((rows, 3 * width), BF16), ((HEADS, rows, rows), F32), ((rows, width), BF16)]
    residual = ((128, 128), F32)
    per_token, sent = ((rows, 128), F32), ((slots, width), BF16)

    def group(array):
        return array.reshape(owners, local, CAP, width)

    attn_in0, qkv0, probs0, attn0, mid0, logits0, stat0, out = local_call(
        first_kernel, experts, (tokens, *dense[0], seq_lengths, block_perm, routes_all),
        attention + [cols, per_token, per_token, sent], scalars=(4, 5))
    ride = (*gathered[3:], qkv_t, out_rows, small, g1, u1, d1) if in_kernels else None
    ret0, *kept0 = expert_forward(spread, 0, group(out), weights[0], ride)
    if in_kernels:
        kept0, (qkv_all, out_all, small_all), (gate, up, down) = kept0[:3], kept0[3:6], kept0[6:]
        dense.append((small_all, qkv_all, out_all))
        weights.append([g1, gate, u1, up, d1, down])
    ret0 = ret0.reshape(slots, width)
    stream1, attn_in1, qkv1, probs1, attn1, mid1, stat1, out = local_call(
        middle_kernel, experts,
        (mid0, dense[0][0], stat0, ret0, *dense[1], seq_lengths, block_perm, routes_all, logits0, w_residual),
        [cols] + attention + [cols, per_token, sent], [residual], scalars=(7, 8))
    ret1, *kept1 = expert_forward(spread, 1, group(out), weights[1])
    ret1 = ret1.reshape(slots, width)

    small_grads = ((24, width), F32)
    output, g_small1, extra, out, small_grad1, res_grad = local_call(
        turn_kernel, experts, (mid1, dense[1][0], stat1, ret1, cotangent, logits0, w_residual),
        [((rows, width), BF16), per_token, per_token, sent, small_grads, residual], [residual])
    back, *expert_grads1 = expert_backward(spread, 2, group(out), kept1, weights[1], in_kernels)
    ride = None
    grad_type = BF16 if in_kernels else F32
    dense_grads = [((3 * width, width), grad_type), ((width, width), grad_type), small_grads]
    attention_scratch = [((rows, 3 * width), BF16), ((rows, width), BF16)]
    qkv_grad1, out_grad1, small_grad1, grad, g_small0, out, small_grad0 = local_call(
        between_kernel, experts,
        (cotangent, back.reshape(slots, width), g_small1, stat1, mid1, dense[1][0], stream1, dense[1][1], dense[1][2],
         attn_in1, qkv1, probs1, attn1, small_grad1, mid0, dense[0][0], stat0, ret0, extra),
        dense_grads + [cols, per_token, sent, small_grads], attention_scratch)
    if in_kernels:
        gate1, up1, up1_sent, down1, down1_sent, gate1_came = expert_grads1
        ride = (qkv_grad1, out_grad1, up1_sent, down1_sent)
    back, *expert_grads0 = expert_backward(spread, 3, group(out), kept0, weights[0], in_kernels, ride)
    qkv_grad0, out_grad0, small_grad0, tokens_grad = local_call(
        last_kernel, experts,
        (grad, back.reshape(slots, width), g_small0, stat0, mid0, dense[0][0], tokens, dense[0][1], dense[0][2],
         attn_in0, qkv0, probs0, attn0, small_grad0),
        dense_grads + [cols], attention_scratch)

    if in_kernels:
        gate0, up0, up0_sent, down0, down0_sent, gate0_came, quarter1, up1_came, down1_came = expert_grads0
        packed, qkv_grad, out_grad, up0_came, down0_came = dense_reduce(
            spread, 5, (small_grad0, small_grad1, res_grad), (qkv_grad0, out_grad0), quarter1, (up0_sent, down0_sent))
        pairs = (
            ((gate0, gate0_came), (gate1, gate1_came)), ((up0, up0_came), (up1, up1_came)),
            ((down0, down0_came), (down1, down1_came)))
        gate_grad, up_grad, down_grad = (
            jnp.stack([mine + came.astype(F32) for mine, came in layer]) for layer in pairs)
    else:
        gate_grad, up_grad, down_grad = (
            jnp.stack([
                pair_sum(grads[at * len(grads) // 3 : (at + 1) * len(grads) // 3], axis, spread)
                for grads in (expert_grads0, expert_grads1)])
            for axis, at in ((2, 0), (2, 1), (1, 2)))
        packed = jnp.concatenate([small_grad0, small_grad1, jnp.pad(res_grad[:16], ((0, 0), (0, width - 128)))])
        packed = lax.psum(packed, ("dp", "expert"))
        qkv_grad, out_grad = (
            lax.psum(lax.psum_scatter(jnp.stack(pair), "dp", scatter_dimension=1, tiled=True), "expert")
            for pair in ((qkv_grad0, qkv_grad1), (out_grad0, out_grad1)))
    mine = lax.dynamic_slice_in_dim(packed, lax.axis_index("dp") * depth, depth, axis=1)
    mine = jnp.stack([mine[:24], mine[24:48]])
    router_grad = jnp.swapaxes(mine[:, :CONST0], 1, 2)
    const_grad = jnp.swapaxes(mine[:, CONST0:GAIN0].reshape(layers, 2, 2, depth), 2, 3)
    residual_grad = packed[48 : 48 + CONST0, :CONST0]
    return (
        output, tokens_grad, mine[:, GAIN0 : GAIN0 + 2], jnp.swapaxes(qkv_grad, 1, 2), out_grad, router_grad,
        residual_grad, const_grad, mine[:, VECTOR0 : VECTOR0 + 2], gate_grad, up_grad, down_grad,
    )


def solution(mesh):
    in_specs = (
        P(("dp", "expert"), None), P("dp", None, None), P("dp", None), P(None, ("dp", "expert"), None),
        P(None, None, "dp"), P(None, None, "dp"), P(None, "dp", None), P(None, "dp", None), P(),
        P(None, None, "dp", None), P(None, None, "dp"), P(None, "expert", None, "dp"), P(None, "expert", None, "dp"),
        P(None, "expert", "dp", None), P(("dp", "expert"), None),
    )
    out_specs = (
        P(("dp", "expert"), None), P(("dp", "expert"), None), P(None, None, "dp"), P(None, None, "dp"),
        P(None, "dp", None), P(None, "dp", None), P(), P(None, None, "dp", None), P(None, None, "dp"),
        P(None, "expert", None, "dp"), P(None, "expert", None, "dp"), P(None, "expert", "dp", None),
    )
    return jax.shard_map(per_device, mesh=mesh, in_specs=in_specs, out_specs=out_specs, check_vma=False)
```

```python
import functools

import jax
import jax.numpy as jnp
from jax import lax
from jax.experimental import pallas as pl
from jax.experimental.pallas import tpu as pltpu
from jax.sharding import PartitionSpec as P

HEADS = 12
CAP = 48
LINE = 4
EPSILON = 1e-05
MASKED = -1e30
HIGH = lax.Precision.HIGHEST
F32 = jnp.float32
BF16 = jnp.bfloat16
MESH = pl.DeviceIdType.MESH
VMEM = pl.BlockSpec(memory_space=pltpu.VMEM)
ANY = pl.BlockSpec(memory_space=pl.ANY)

CONST0, GAIN0, VECTOR0 = 12, 16, 18
STAT = {
    name: i
    for i, name in enumerate(
        ("r0", "r1", "share0", "share1", "slot0", "slot1", "p00", "p01", "p10", "p11")
    )
}


SMEM = pl.BlockSpec(memory_space=pltpu.SMEM)


def dot_nn(a, b, **kw):
    return lax.dot_general(a, b, (((1,), (0,)), ((), ())), preferred_element_type=F32, **kw)


def dot_nt(a, b, **kw):
    return lax.dot_general(a, b, (((1,), (1,)), ((), ())), preferred_element_type=F32, **kw)


def dot_tn(a, b, **kw):
    return lax.dot_general(a, b, (((0,), (0,)), ((), ())), preferred_element_type=F32, **kw)


def lanes(rows, width=128):
    return lax.broadcasted_iota(jnp.int32, (rows, width), 1)


def rms_scale(values):
    return lax.rsqrt(jnp.mean(values * values, axis=-1, keepdims=True) + EPSILON)


def row_vectors(small):
    pick = lax.broadcasted_iota(jnp.int32, (8, 128), 0) + GAIN0 == lanes(8)
    rows = dot_nt(pick.astype(BF16), small)
    return rows[0:1], rows[1:2], rows[2:3], rows[3:4]


def stat_columns(stat):
    return {name: stat[:, i : i + 1] for name, i in STAT.items()}


def slot_picks(stat, slots):
    place = lanes(stat["slot0"].shape[0], slots).astype(F32)
    first = (place == stat["slot0"]).astype(BF16)
    second = (place == stat["slot1"]).astype(BF16)
    return first, second


def const_weights(stat, experts):
    out = []
    for kind in (experts + 1, experts + 2, experts + 3):
        out.append(
            stat["share0"] * (stat["r0"] == kind).astype(F32)
            + stat["share1"] * (stat["r1"] == kind).astype(F32)
        )
    return out


def doc_index(lengths, places):
    place, end = lax.axis_index("expert"), 0
    doc = jnp.zeros_like(places)
    for j in range(lengths.shape[2]):
        end = end + lengths[0, place, j]
        doc = doc + (places >= end).astype(jnp.int32)
    return doc


def block_routes(perm, routes_all, layer, rows):
    mine = routes_all[perm[0, lax.axis_index("expert")]].astype(F32)
    routes = jnp.transpose(mine)[:rows].astype(jnp.int32)
    return routes[:, 2 * layer : 2 * layer + 1], routes[:, 2 * layer + 1 : 2 * layer + 2]


def padded(w_res, ref):
    count = w_res.shape[0]
    ref[...] = jnp.zeros(ref.shape, F32)
    ref[0:count, 0:count] = w_res[...]
    return ref[...]


def attend_part(stream, small, w_qkv_t, w_out, lengths, attn_in_ref, qkv_ref, probs_ref, attn_ref):
    rows, width = stream.shape
    gain, _, _, _ = row_vectors(small)
    attn_in_ref[...] = (stream * rms_scale(stream) * gain).astype(BF16)

    def project(i, carry):
        at = pl.multiple_of(i * width, width)
        qkv_ref[:, pl.ds(at, width)] = dot_nt(
            attn_in_ref[...], w_qkv_t[pl.ds(at, width), :]
        ).astype(BF16)
        return carry

    lax.fori_loop(0, 3, project, 0, unroll=True)
    head_dim = width // HEADS
    factor = 1.0 / head_dim**0.5
    allowed = jnp.logical_and(
        doc_index(lengths, lax.broadcasted_iota(jnp.int32, (rows, 1), 0))
        == doc_index(lengths, lax.broadcasted_iota(jnp.int32, (1, rows), 1)),
        lax.broadcasted_iota(jnp.int32, (rows, rows), 0)
        >= lax.broadcasted_iota(jnp.int32, (rows, rows), 1),
    )

    def heads(i, carry):
        at = pl.multiple_of(i * 2 * head_dim, 2 * head_dim)
        query = qkv_ref[:, pl.ds(at, 2 * head_dim)]
        key = qkv_ref[:, pl.ds(pl.multiple_of(at + width, 128), 2 * head_dim)]
        value = qkv_ref[:, pl.ds(pl.multiple_of(at + 2 * width, 128), 2 * head_dim)]
        second = lanes(rows, 2 * head_dim) >= head_dim
        mixed = []
        for sub in (0, 1):
            mine = second if sub else jnp.logical_not(second)
            scores = dot_nt(jnp.where(mine, query, jnp.zeros_like(query)), key) * factor
            scores = jnp.where(allowed, scores, MASKED)
            exponent = jnp.exp(scores - jnp.max(scores, axis=-1, keepdims=True))
            probs = exponent / jnp.sum(exponent, axis=-1, keepdims=True)
            probs_ref[2 * i + sub] = probs
            mixed.append(dot_nn(probs.astype(BF16), value))
        attn_ref[:, pl.ds(at, 2 * head_dim)] = jnp.where(second, mixed[1], mixed[0]).astype(BF16)
        return carry

    lax.fori_loop(0, HEADS // 2, heads, 0, unroll=True)
    return stream + dot_nn(attn_ref[...], w_out[...])


def route_part(mid, small, routes, prev_logits, w_res, experts):
    rows = mid.shape[0]
    _, gain, _, _ = row_vectors(small)
    hidden = (mid * rms_scale(mid) * gain).astype(BF16)
    lane = lanes(rows)
    raw = dot_nn(hidden, small)
    logits = jnp.where(lane < CONST0, raw, 0.0)
    if prev_logits is not None:
        logits = logits + dot_nn(prev_logits, w_res, precision=HIGH)
    r0, r1 = routes
    hot0, hot1 = (lane == r0).astype(F32), (lane == r1).astype(F32)
    c0 = jnp.sum(hot0 * logits, axis=-1, keepdims=True)
    c1 = jnp.sum(hot1 * logits, axis=-1, keepdims=True)
    peak = jnp.maximum(c0, c1)
    e0, e1 = jnp.exp(c0 - peak), jnp.exp(c1 - peak)
    total = e0 + e1
    share0, share1 = e0 / total, e1 / total
    probs = []
    for j in (0, 1):
        a = raw[:, CONST0 + 2 * j : CONST0 + 2 * j + 1]
        b = raw[:, CONST0 + 2 * j + 1 : CONST0 + 2 * j + 2]
        top = jnp.maximum(a, b)
        ea, eb = jnp.exp(a - top), jnp.exp(b - top)
        probs += [ea / (ea + eb), eb / (ea + eb)]
    earlier = lax.broadcasted_iota(jnp.int32, (rows, rows), 0) > lax.broadcasted_iota(
        jnp.int32, (rows, rows), 1
    )
    before = dot_nn(earlier.astype(BF16), (hot0 + hot1).astype(BF16))
    f0, f1 = r0.astype(F32), r1.astype(F32)
    slot0 = jnp.where(
        r0 < experts, f0 * CAP + jnp.sum(before * hot0, axis=-1, keepdims=True), -1.0
    )
    slot1 = jnp.where(
        r1 < experts, f1 * CAP + jnp.sum(before * hot1, axis=-1, keepdims=True), -1.0
    )
    stat = jnp.zeros((rows, 128), F32)
    for i, column in enumerate([f0, f1, share0, share1, slot0, slot1] + probs):
        stat = jnp.where(lane == i, column, stat)
    first, second = slot_picks({"slot0": slot0, "slot1": slot1}, experts * CAP)
    outgoing = dot_tn(first + second, hidden).astype(BF16)
    return logits, stat, outgoing


def combine_part(mid, small, stat, returned, experts):
    _, gain, vec0, vec1 = row_vectors(small)
    hidden_full = mid * rms_scale(mid) * gain
    first, second = slot_picks(stat, experts * CAP)
    pair0, pair1 = dot_nn(first, returned), dot_nn(second, returned)
    copy, const0, const1 = const_weights(stat, experts)
    local = copy + const0 * stat["p00"] + const1 * stat["p10"]
    moe = stat["share0"] * pair0 + stat["share1"] * pair1 + local * hidden_full
    moe = moe + (const0 * stat["p01"]) * vec0 + (const1 * stat["p11"]) * vec1
    return mid + moe, hidden_full, pair0, pair1


def share_backward(grad, small, stat, hidden_full, pair0, pair1, extra, experts):
    rows = grad.shape[0]
    _, _, vec0, vec1 = row_vectors(small)
    first, second = slot_picks(stat, experts * CAP)
    lane = lanes(rows).astype(F32)
    rowsum = functools.partial(jnp.sum, axis=-1, keepdims=True)
    dot_hidden = rowsum(grad * hidden_full)
    dot_vec = (rowsum(grad * vec0), rowsum(grad * vec1))
    _, const0, const1 = const_weights(stat, experts)
    probs = ((stat["p00"], stat["p01"]), (stat["p10"], stat["p11"]))
    value = [probs[j][0] * dot_hidden + probs[j][1] * dot_vec[j] for j in (0, 1)]
    shares = []
    for r, pair in ((stat["r0"], pair0), (stat["r1"], pair1)):
        shares.append(
            rowsum(grad * pair)
            + (r == experts + 1).astype(F32) * dot_hidden
            + (r == experts + 2).astype(F32) * value[0]
            + (r == experts + 3).astype(F32) * value[1]
        )
    inner = stat["share0"] * shares[0] + stat["share1"] * shares[1]
    g_small = (lane == stat["r0"]).astype(F32) * (stat["share0"] * (shares[0] - inner))
    g_small = g_small + (lane == stat["r1"]).astype(F32) * (stat["share1"] * (shares[1] - inner))
    if extra is not None:
        g_small = g_small + extra
    g_logits = g_small
    for j, weight in ((0, const0), (1, const1)):
        q = (weight * dot_hidden, weight * dot_vec[j])
        mean = probs[j][0] * q[0] + probs[j][1] * q[1]
        for c in (0, 1):
            g_small = jnp.where(lane == CONST0 + 2 * j + c, probs[j][c] * (q[c] - mean), g_small)
    sent0 = (jnp.where(stat["r0"] < experts, stat["share0"], 0.0) * grad).astype(BF16)
    sent1 = (jnp.where(stat["r1"] < experts, stat["share1"], 0.0) * grad).astype(BF16)
    outgoing = (dot_tn(first, sent0) + dot_tn(second, sent1)).astype(BF16)
    hidden = hidden_full.astype(BF16).astype(F32)
    projections = dot_tn(g_small, hidden, precision=HIGH)
    vector0 = jnp.sum((const0 * stat["p01"]) * grad, axis=0, keepdims=True)
    vector1 = jnp.sum((const1 * stat["p11"]) * grad, axis=0, keepdims=True)
    return g_small, g_logits, outgoing, projections, vector0, vector1


def store_small(ref, projections, vector0, vector1):
    ref[0:16, :] = projections[0:16]
    ref[16:24, :] = jnp.zeros((8, ref.shape[1]), F32)
    ref[VECTOR0 : VECTOR0 + 1, :] = vector0
    ref[VECTOR0 + 1 : VECTOR0 + 2, :] = vector1


def first_kernel(experts, tokens, small, w_qkv_t, w_out, lengths, perm, routes_all,
                 attn_in, qkv, probs, attn, mid_ref, logits_ref, stat_ref, out_ref):
    mid = attend_part(tokens[...].astype(F32), small[...], w_qkv_t, w_out, lengths, attn_in, qkv, probs, attn)
    mid_ref[...] = mid
    routes = block_routes(perm, routes_all, 0, mid.shape[0])
    logits, stat, out = route_part(mid, small[...], routes, None, None, experts)
    logits_ref[...], stat_ref[...], out_ref[...] = logits, stat, out


def middle_kernel(experts, mid_in, small_in, stat_in, returned, small, w_qkv_t, w_out, lengths, perm, routes_all, logits_in, w_res,
                  stream_ref, attn_in, qkv, probs, attn, mid_ref, stat_ref, out_ref, res_ref):
    stream, _, _, _ = combine_part(mid_in[...], small_in[...], stat_columns(stat_in[...]), returned[...], experts)
    stream_ref[...] = stream
    mid = attend_part(stream, small[...], w_qkv_t, w_out, lengths, attn_in, qkv, probs, attn)
    mid_ref[...] = mid
    routes = block_routes(perm, routes_all, 1, mid.shape[0])
    _, stat, out = route_part(mid, small[...], routes, logits_in[...], padded(w_res, res_ref), experts)
    stat_ref[...], out_ref[...] = stat, out


def turn_kernel(experts, mid, small, stat_in, returned, cotangent, logits_in, w_res,
                output, g_small_ref, extra_ref, out_ref, small_grad, res_grad, res_ref):
    stat = stat_columns(stat_in[...])
    stream, hidden_full, pair0, pair1 = combine_part(mid[...], small[...], stat, returned[...], experts)
    output[...] = stream.astype(BF16)
    grad = cotangent[...].astype(F32)
    g_small, g_logits, out, projections, v0, v1 = share_backward(grad, small[...], stat, hidden_full, pair0, pair1, None, experts)
    g_small_ref[...] = g_small
    out_ref[...] = out
    store_small(small_grad, projections, v0, v1)
    res_grad[...] = dot_tn(logits_in[...], g_logits, precision=HIGH)
    extra_ref[...] = dot_nt(g_logits, padded(w_res, res_ref), precision=HIGH)


def layer_backward(experts, grad, back, g_small, stat, mid, small, stream, w_qkv_t, w_out, attn_in, qkv, probs, attn,
                   qkv_grad, out_grad, small_grad, g_qkv, g_attn):
    rows, width = mid.shape
    gain1, gain2, _, _ = row_vectors(small)
    first, second = slot_picks(stat, experts * CAP)
    copy, const0, const1 = const_weights(stat, experts)
    local = copy + const0 * stat["p00"] + const1 * stat["p10"]
    g_full = dot_nt(g_small, small.astype(F32), precision=HIGH) + dot_nn(first + second, back)
    g_full = g_full + grad * local
    s2 = rms_scale(mid)
    small_grad[GAIN0 + 1 : GAIN0 + 2, :] = jnp.sum(g_full * mid * s2, axis=0, keepdims=True)
    m = g_full * gain2
    g_mid = grad + s2 * m - mid * (s2 * s2 * s2 * jnp.mean(m * mid, axis=-1, keepdims=True))
    branch = g_mid.astype(BF16)
    out_grad[...] = dot_tn(attn[...], branch).astype(out_grad.dtype)
    g_attn[...] = dot_nt(branch, w_out[...]).astype(BF16)
    head_dim = width // HEADS
    factor = 1.0 / head_dim**0.5

    def heads(i, carry):
        at = pl.multiple_of(i * 2 * head_dim, 2 * head_dim)
        at_k = pl.multiple_of(at + width, 128)
        at_v = pl.multiple_of(at + 2 * width, 128)
        query = qkv[:, pl.ds(at, 2 * head_dim)]
        key = qkv[:, pl.ds(at_k, 2 * head_dim)]
        value = qkv[:, pl.ds(at_v, 2 * head_dim)]
        ga = g_attn[:, pl.ds(at, 2 * head_dim)]
        second_half = lanes(rows, 2 * head_dim) >= head_dim
        gq, gk, gv = [], [], []
        for sub in (0, 1):
            mine = second_half if sub else jnp.logical_not(second_half)
            p = probs[2 * i + sub]
            gp = dot_nt(jnp.where(mine, ga, jnp.zeros_like(ga)), value)
            gs = (p * (gp - jnp.sum(p * gp, axis=-1, keepdims=True))).astype(BF16)
            gq.append(dot_nn(gs, key))
            gk.append(dot_tn(gs, query))
            gv.append(dot_tn(p.astype(BF16), ga))
        g_qkv[:, pl.ds(at, 2 * head_dim)] = (jnp.where(second_half, gq[1], gq[0]) * factor).astype(BF16)
        g_qkv[:, pl.ds(at_k, 2 * head_dim)] = (jnp.where(second_half, gk[1], gk[0]) * factor).astype(BF16)
        g_qkv[:, pl.ds(at_v, 2 * head_dim)] = jnp.where(second_half, gv[1], gv[0]).astype(BF16)
        return carry

    lax.fori_loop(0, HEADS // 2, heads, 0, unroll=True)

    def weights(i, carry):
        at = pl.multiple_of(i * width, width)
        qkv_grad[pl.ds(at, width), :] = dot_tn(g_qkv[:, pl.ds(at, width)], attn_in[...]).astype(qkv_grad.dtype)
        return carry + dot_nn(g_qkv[:, pl.ds(at, width)], w_qkv_t[pl.ds(at, width), :])

    g_in = lax.fori_loop(0, 3, weights, jnp.zeros((rows, width), F32))
    s1 = rms_scale(stream)
    small_grad[GAIN0 : GAIN0 + 1, :] = jnp.sum(g_in * stream * s1, axis=0, keepdims=True)
    n = g_in * gain1
    return g_mid + s1 * n - stream * (s1 * s1 * s1 * jnp.mean(n * stream, axis=-1, keepdims=True))


def between_kernel(experts, cotangent, back, g_small, stat_in, mid, small, stream, w_qkv_t, w_out, attn_in, qkv, probs, attn, small_grad_in,
                   mid0, small0, stat0_in, returned0, extra,
                   qkv_grad, out_grad, small_grad, grad_ref, g_small0_ref, out_ref, small_grad0, g_qkv, g_attn):
    small_grad[...] = small_grad_in[...]
    grad = layer_backward(experts, cotangent[...].astype(F32), back[...], g_small[...], stat_columns(stat_in[...]), mid[...],
                          small[...], stream[...], w_qkv_t, w_out, attn_in, qkv, probs, attn, qkv_grad, out_grad, small_grad, g_qkv, g_attn)
    grad_ref[...] = grad
    stat0 = stat_columns(stat0_in[...])
    _, hidden_full, pair0, pair1 = combine_part(mid0[...], small0[...], stat0, returned0[...], experts)
    g_small0, _, out, projections, v0, v1 = share_backward(grad, small0[...], stat0, hidden_full, pair0, pair1, extra[...], experts)
    g_small0_ref[...] = g_small0
    out_ref[...] = out
    store_small(small_grad0, projections, v0, v1)


def last_kernel(experts, grad_in, back, g_small, stat_in, mid, small, tokens, w_qkv_t, w_out, attn_in, qkv, probs, attn, small_grad_in,
                qkv_grad, out_grad, small_grad, grad_ref, g_qkv, g_attn):
    small_grad[...] = small_grad_in[...]
    grad_ref[...] = layer_backward(experts, grad_in[...], back[...], g_small[...], stat_columns(stat_in[...]), mid[...], small[...],
                                   tokens[...].astype(F32), w_qkv_t, w_out, attn_in, qkv, probs, attn, qkv_grad, out_grad, small_grad,
                                   g_qkv, g_attn)


def local_call(kernel, experts, args, outs, scratch=(), scalars=()):
    return pl.pallas_call(
        functools.partial(kernel, experts),
        out_shape=[jax.ShapeDtypeStruct(shape, dtype) for shape, dtype in outs],
        in_specs=[SMEM if i in scalars else VMEM for i in range(len(args))],
        out_specs=[VMEM] * len(outs),
        scratch_shapes=[pltpu.VMEM(shape, dtype) for shape, dtype in scratch],
        compiler_params=pltpu.CompilerParams(vmem_limit_bytes=60 * 2**20),
        cost_estimate=pl.CostEstimate(flops=10**10, bytes_accessed=6 * 10**7, transcendentals=0),
    )(*args)


class Place:
    def __init__(self, spread):
        self.spread = spread
        self.d, self.e = lax.axis_index("dp"), lax.axis_index("expert")
        self.t, self.f = self.d // spread, lax.rem(self.d, spread)
        self.y, self.c = self.e // 2, lax.rem(self.e, 2)
        self.above, self.below = self.t < LINE - 1, self.t > 0
        self.inside = jnp.logical_and(self.above, self.below)
        self.up = jnp.where(self.t == 1, 1, 0)
        self.ahead = 2 * self.up - 1
        self.sibling = (self.d, self.e + 1 - 2 * self.c)
        self.across = (self.d, lax.rem(self.e + 2, 4))
        self.corner = (self.d, 3 - self.e)
        self.beside = (self.t * spread + 1 - self.f, self.e)
        self.mates = [(self.d, self.e), self.sibling, self.across, self.corner]

    def block(self, i):
        return pick(i, [e for _, e in self.mates])

    def on_line(self, up):
        return (self.d + self.spread * (2 * up - 1), self.e)


def pick(index, values):
    out = values[-1]
    for n in range(len(values) - 2, -1, -1):
        out = jnp.where(index == n, values[n], out)
    return out


def greet(always, place):
    barrier = pltpu.get_barrier_semaphore()
    for device in always:
        pl.semaphore_signal(barrier, inc=1, device_id=device, device_id_type=MESH)
    for up, there in ((1, place.above), (0, place.below)):

        @pl.when(there)
        def _(up=up):
            pl.semaphore_signal(barrier, inc=1, device_id=place.on_line(up), device_id_type=MESH)

    ends = place.above.astype(jnp.int32) + place.below.astype(jnp.int32)
    pl.semaphore_wait(barrier, len(always) + ends)


def remote(src, dst, send, recv, device):
    return pltpu.make_async_remote_copy(
        src_ref=src, dst_ref=dst, send_sem=send, recv_sem=recv, device_id=device, device_id_type=MESH)


def dma(*shape):
    return pltpu.SemaphoreType.DMA(shape)


def along(place, body, start=0):
    if start == 0:
        body(place.t)

    def step(k, carry):
        for t in (place.t + k, place.t - k):

            @pl.when(jnp.logical_and(t >= 0, t < LINE))
            def _(t=t):
                body(t)

        return carry

    lax.fori_loop(1, LINE, step, 0)


class Rider:
    partners = ()

    def begin(self):
        pass

    def ready(self):
        pass

    def after_first(self):
        pass

    def after_line(self):
        pass

    def after_relay(self):
        pass

    def finish(self):
        pass


class Line:
    def __init__(self, place, x, part, stage, arrived, final, returned, sems):
        self.p = place
        self.x, self.part, self.stage, self.arrived = x, part, stage, arrived
        self.final, self.returned = final, returned
        (self.out_send, self.x_recv, self.x_send, self.sum_send, self.sum_recv, self.ret_send, self.ret_recv) = sems

    @staticmethod
    def scratch(local, width):
        shape = (local, 4, CAP, width)
        return [
            pltpu.VMEM((local, LINE, 4, CAP, width), BF16),
            pltpu.VMEM((LINE,) + shape, F32),
            pltpu.VMEM((LINE,) + shape, BF16),
            pltpu.VMEM((2, LINE) + shape, BF16),
            pltpu.VMEM((4, local, CAP, width), BF16),
            dma(4), dma(LINE, 4), dma(2, LINE, 4), dma(LINE, 4), dma(2, LINE, 4), dma(4), dma(4),
        ]

    def slot_copy(self, out, i):
        to, p = self.p.mates[i], self.p
        return remote(out.at[to[1]], self.x.at[:, p.t, p.e], self.out_send.at[i], self.x_recv.at[p.t, p.e], to)

    def x_copy(self, up, s, b):
        at = self.x.at[:, s, b]
        return remote(at, at, self.x_send.at[up, s, b], self.x_recv.at[s, b], self.p.on_line(up))

    def sum_copy(self, up, s, b):
        return remote(self.stage.at[s, :, b], self.arrived.at[up, s, :, b], self.sum_send.at[s, b],
                      self.sum_recv.at[up, s, b], self.p.on_line(up))

    def ret_copy(self, i, to_mate=True):
        to = self.p.block(i)
        row = self.p.e if to_mate else to
        return remote(self.final.at[to], self.returned.at[row], self.ret_send.at[i], self.ret_recv.at[row], (self.p.d, to))

    def send_sum(self, up, s, b, total):
        self.stage[s, :, b] = total.astype(BF16)
        self.sum_copy(up, s, b).start()

    def relay(self, n):
        p = self.p
        kind = pick(n, (0, 0, 1, 1, 2, 1, 2, 1, 2, 0, 2, 0))
        b = p.block(pick(n, (0, 1, 0, 1, 0, 2, 1, 3, 2, 2, 3, 3)))
        s = p.t + p.ahead * pick(kind, (1, 2, -1))
        way = jnp.where(kind == 2, 1 - p.up, p.up)

        @pl.when(p.inside)
        def _():
            self.sum_copy(way, s, b).wait_recv()
            self.send_sum(way, s, b, self.part[s, :, b] + self.arrived[way, s, :, b].astype(F32))

    def run(self, out, compute, kept, pieces, rider):
        p = self.p
        t, e = p.t, p.e
        blocks = [b for _, b in p.mates]
        greet(p.mates[1:] + list(rider.partners), p)
        for i in (2, 3, 1):
            self.slot_copy(out, i).start()
        self.x[:, t, e] = out[e]
        rider.begin()
        for i in range(4):
            if i:
                self.x_copy(0, t, blocks[i]).wait_recv()
            for up, there in ((0, p.below), (1, p.above)):

                @pl.when(there)
                def _(up=up, i=i):
                    self.x_copy(up, t, blocks[i]).start()

        rider.ready()

        def step(n, carry):
            k = jnp.where(n < 2, 1, jnp.where(jnp.logical_or(n == 2, n == 5), 2, 3))
            half = jnp.where(jnp.logical_or(n == 1, n >= 4), 1, 0)
            pair = p.y + half - 2 * p.y * half
            first = jnp.where(half == 0, blocks[0], blocks[2])
            second = jnp.where(half == 0, blocks[1], blocks[3])
            for b in (first, second):
                for up, there, onward, before_end in ((0, t + k < LINE, p.below, t == 1), (1, t - k >= 0, p.above, t == LINE - 2)):
                    s = t - k if up else t + k
                    put_off = jnp.logical_and(before_end, n == 1)

                    @pl.when(there)
                    def _(up=up, onward=onward, s=s, b=b, put_off=put_off):
                        self.x_copy(up, s, b).wait_recv()

                        @pl.when(jnp.logical_and(onward, jnp.logical_not(put_off)))
                        def _():
                            self.x_copy(up, s, b).start()

            for up, before_end in ((0, t == 1), (1, t == LINE - 2)):

                @pl.when(jnp.logical_and(before_end, n == 5))
                def _(up=up):
                    for b in (first, second):
                        self.x_copy(up, t - 1 if up else t + 1, b).start()

            @pl.when(jnp.logical_not(p.inside))
            def _():
                s = jnp.where(t == 0, k, LINE - 1 - k)
                compute(s, 2 * pair, 2)

                @pl.when(half == 1)
                def _():
                    kept(s)

            for up, starts, s in ((1, t == 0, k), (0, t == LINE - 1, LINE - 1 - k)):

                @pl.when(starts)
                def _(up=up, s=s):
                    for b in (first, second):
                        self.send_sum(up, s, b, self.part[s, :, b])

            rest = jnp.logical_and(p.inside, jnp.logical_or(n == 5, jnp.logical_and(n >= 1, n <= 2)))

            @pl.when(jnp.logical_or(n == 0, rest))
            def _():
                s = t + p.ahead * jnp.where(n == 0, 0, jnp.where(n == 1, 1, jnp.where(n == 2, -1, 2)))
                compute(s, 0, 4)
                kept(s)

            @pl.when(n == 0)
            def _():
                rider.after_first()

            return carry

        lax.fori_loop(0, 6, step, 0)
        rider.after_line()

        def passing(n, carry):
            self.relay(n)
            pieces(n)
            return carry

        lax.fori_loop(0, 12, passing, 0)
        rider.after_relay()

        def end(i, carry):
            b = p.block(i)
            for up, there in ((1, p.below), (0, p.above)):

                @pl.when(there)
                def _(up=up):
                    self.sum_copy(up, t, b).wait_recv()
                    self.part[t, :, b] = self.part[t, :, b] + self.arrived[up, t, :, b].astype(F32)

            self.final[b] = self.part[t, :, b].astype(BF16)

            @pl.when(i > 0)
            def _():
                self.ret_copy(i).start()

            return carry

        lax.fori_loop(0, 4, end, 0)
        self.returned[e] = self.final[e]

        def sent(n, carry):
            s, b = n // 4, lax.rem(n, 4)
            for up, mine in ((0, jnp.logical_and(p.below, s >= t)), (1, jnp.logical_and(p.above, s <= t))):

                @pl.when(mine)
                def _(up=up):
                    self.x_copy(up, s, b).wait_send()

            @pl.when(s != t)
            def _():
                self.sum_copy(0, s, b).wait_send()

            return carry

        for i in (1, 2, 3):
            self.slot_copy(out, i).wait_send()
        lax.fori_loop(0, 4 * LINE, sent, 0)
        rider.finish()
        for i in (1, 2, 3):
            self.ret_copy(i).wait_send()
            self.ret_copy(i, False).wait_recv()


def split(refs, *counts):
    out, at = [], 0
    for count in counts:
        out.append(refs[at : at + count])
        at += count
    return out + [refs[at:]]


def expert_forward_kernel(spread, parts, late, ride, out, *refs):
    weights_in, given, outs, late_out, whole, scratch, line_refs, sems, ride_refs = split(
        refs, 3 * parts, 8 if ride else 0, 4, late, 5 if ride else 0, 3 * parts, 5, 7)
    (g_all, u_all, keep_sem, load_sem, late_sem), ride_refs = ride_refs[:5], ride_refs[5:]
    returned, x_keep, g_keep, u_keep = outs
    gate, up, down = scratch[:parts], scratch[parts : 2 * parts], scratch[2 * parts :]
    x, part, stage, arrived, final = line_refs
    local, _, _, _, width = x.shape
    p = Place(spread)
    line = Line(p, x, part, stage, arrived, final, returned, sems)
    rider = WeightRider(p, given, whole, ride_refs) if ride else Rider()

    def load(i):
        given = weights_in[i].shape[0]
        return pltpu.make_async_copy(weights_in[i], scratch[i].at[0:given], load_sem.at[i])

    for i in range(3 * parts):
        load(i).start()

    def late_copy():
        return remote(weights_in[-2].at[1:local], scratch[-1].at[1:local], late_sem.at[0], late_sem.at[1], p.beside)

    def late_store():
        return pltpu.make_async_copy(scratch[-1], late_out[0], late_sem.at[2])

    def keep_x(s):
        return pltpu.make_async_copy(x.at[:, s], x_keep.at[:, s], keep_sem.at[0, s])

    def keep_g(s):
        return pltpu.make_async_copy(g_all.at[s], g_keep.at[s], keep_sem.at[1, s])

    def keep_u(s):
        return pltpu.make_async_copy(u_all.at[s], u_keep.at[s], keep_sem.at[2, s])

    def kept(s):
        keep_x(s).start()
        keep_g(s).start()
        keep_u(s).start()

    def compute(s, first, count):
        rows = count * CAP
        at = pl.multiple_of(first * CAP, CAP)

        def one(l, carry):
            rows_in = x[l, s, pl.ds(first, count)].reshape(rows, width)
            total = jnp.zeros((rows, width), F32)
            for q in range(parts):
                cols = gate[q].shape[2]
                here = slice(q * cols, (q + 1) * cols)
                g = dot_nn(rows_in, gate[q][l])
                u = dot_nn(rows_in, up[q][l])
                g_all[s, l, pl.ds(at, rows), here] = g
                u_all[s, l, pl.ds(at, rows), here] = u
                act = (g * jax.nn.sigmoid(g) * u).astype(BF16)
                total = total + dot_nn(act, down[q][l])
            part[s, l, pl.ds(first, count)] = total.reshape(count, CAP, width)
            return carry

        lax.fori_loop(0, local, one, 0)

    class Loaded(Rider):
        partners = [p.beside] if late else []
        after_first, after_line, after_relay = rider.after_first, rider.after_line, rider.after_relay

        def begin(self):
            if late:
                late_copy().start()
            rider.begin()

        def ready(self):
            for i in range(3 * parts):
                load(i).wait()
            if late:
                late_copy().wait_recv()
                late_store().start()

        def finish(self):
            rider.finish()
            if late:
                late_copy().wait_send()
                late_store().wait()

    line.run(out, compute, kept, lambda n: None, Loaded())
    for s in range(LINE):
        keep_x(s).wait()
        keep_g(s).wait()
        keep_u(s).wait()


def expert_backward_kernel(spread, parts, exchange, ride, out, *refs):
    loads_in, given, outs, came, ride_outs, loads, line_refs, sems, rest = split(
        refs, 3 + 3 * parts, 4 if ride else 0, 1 + 3 * parts - exchange, exchange, 3 if ride else 0, 3 + 3 * parts, 5, 7)
    (act_all, gg_all, gu_all), grads, (load_sem, grad_sem, w_send, w_recv), ride_refs = split(rest, 3, 3 * parts, 4)
    returned, grads_out = outs[0], list(outs[1:])
    if exchange:
        grads_out.insert(1, None)
    x_in, g_all, u_all = loads[:3]
    gate, up, down = loads[3 : 3 + parts], loads[3 + parts : 3 + 2 * parts], loads[3 + 2 * parts :]
    x, part, stage, arrived, final = line_refs
    local, _, _, _, width = x.shape
    p = Place(spread)
    line = Line(p, x, part, stage, arrived, final, returned, sems)
    rider = GradientRider(p, given, ride_outs, ride_refs) if ride else Rider()

    def load(i):
        return pltpu.make_async_copy(loads_in[i], loads[i], load_sem.at[i])

    def store(i, l):
        return pltpu.make_async_copy(grads[i].at[l], grads_out[i].at[l], grad_sem.at[i, l])

    for i in range(3 + 3 * parts):
        load(i).start()

    def compute(s, first, count):
        rows = count * CAP
        at = pl.multiple_of(first * CAP, CAP)
        into = pl.ds(pl.multiple_of((4 * s + first) * CAP, CAP), rows)

        def one(l, carry):
            rows_in = x[l, s, pl.ds(first, count)].reshape(rows, width)
            total = jnp.zeros((rows, width), F32)
            for q in range(parts):
                cols = gate[q].shape[2]
                here = slice(q * cols, (q + 1) * cols)
                g, u = g_all[s, l, pl.ds(at, rows), here], u_all[s, l, pl.ds(at, rows), here]
                g_act = dot_nt(rows_in, down[q][l])
                sigma = jax.nn.sigmoid(g)
                swish = g * sigma
                gg = (g_act * u * sigma * (1.0 + g * (1.0 - sigma))).astype(BF16)
                gu = (g_act * swish).astype(BF16)
                act_all[l, into, here] = (swish * u).astype(BF16)
                gg_all[l, into, here] = gg
                gu_all[l, into, here] = gu
                total = total + dot_nt(gg, gate[q][l]) + dot_nt(gu, up[q][l])
            part[s, l, pl.ds(first, count)] = total.reshape(count, CAP, width)
            return carry

        lax.fori_loop(0, local, one, 0)

    def weights(kind, l):
        x_rows, g_rows = (a[l].reshape(LINE * 4 * CAP, width) for a in (x_in, x))
        value = dot_tn(act_all[l], g_rows) if kind == 2 else dot_tn(x_rows, (gg_all, gu_all)[kind][l])
        for q in range(parts):
            i = kind * parts + q
            cols = gate[q].shape[2]
            here = slice(q * cols, (q + 1) * cols)
            grads[i][l] = (value[here] if kind == 2 else value[:, here]).astype(grads[i].dtype)
            if grads_out[i] is not None:
                store(i, l).start()

    def pieces(n):
        for kind in range(3):
            at = n - 1 - 2 * local * kind

            @pl.when(jnp.logical_and(lax.rem(n, 2) == 1, jnp.logical_and(at >= 0, at < 2 * local)))
            def _(kind=kind, at=at):
                weights(kind, at // 2)

        @pl.when(n == 2 * local - 1)
        def _():
            for copy in sent_gate():
                copy.start()

    def sent_gate():
        return [remote(grads[1], came[0], w_send.at[0], w_recv.at[0], p.beside)] if exchange else []

    class Loaded(Rider):
        partners = [p.beside] if exchange else []
        after_first, after_line, after_relay, finish = (
            rider.after_first, rider.after_line, rider.after_relay, rider.finish)

        def begin(self):
            rider.begin()

        def ready(self):
            for i in range(3 + 3 * parts):
                load(i).wait()

    line.run(out, compute, lambda s: None, pieces, Loaded())
    for copy in sent_gate():
        copy.wait()
    for i in range(3 * parts):
        for l in range(local if grads_out[i] is not None else 0):
            store(i, l).wait()


def remote_params(call_id):
    return pltpu.CompilerParams(collective_id=call_id, has_side_effects=True, vmem_limit_bytes=61 * 2**20)


def struct(shape, dtype):
    return jax.ShapeDtypeStruct(tuple(shape), dtype)


def expert_forward(spread, call_id, out, weights, late=False, ride=None):
    parts = len(weights) // 3
    _, local, cap, width = out.shape
    columns = sum(w.shape[2] for w in weights[:parts])
    kept = (LINE, local, 4 * cap, columns)
    outs = [struct(out.shape, BF16), struct((local, LINE, 4, cap, width), BF16), struct(kept, F32), struct(kept, F32)]
    outs += [struct(weights[-2].shape, BF16)] * late
    scratch = [pltpu.VMEM((local,) + w.shape[1:], BF16) for w in weights] + Line.scratch(local, width)
    scratch += [pltpu.VMEM(kept, F32), pltpu.VMEM(kept, F32), dma(3, LINE), dma(3 * parts), dma(3)]
    more = ride or ()
    count = LINE * spread
    if ride:
        outs += [struct((count * s.shape[1], s.shape[2]), BF16) for s in ride[3:6]]
        outs += [struct(w.shape, BF16) for w in ride[6:]]
        scratch += WeightRider.scratch(count)
    return pl.pallas_call(
        functools.partial(expert_forward_kernel, spread, parts, int(late), ride is not None),
        out_shape=outs,
        in_specs=[VMEM] + [ANY] * (len(weights) + len(more)),
        out_specs=[VMEM] + [ANY] * (len(outs) - 1),
        scratch_shapes=scratch,
        compiler_params=remote_params(call_id),
        cost_estimate=pl.CostEstimate(flops=2 * 10**10, bytes_accessed=2 * 10**8, transcendentals=0),
    )(out, *weights, *more)


def expert_backward(spread, call_id, out, kept, weights, exchange=False, ride=None):
    parts = len(weights) // 3
    _, local, cap, width = out.shape
    columns = sum(w.shape[2] for w in weights[:parts])
    loads = list(kept) + list(weights)
    grads = [(w.shape, F32 if i % parts == 0 else BF16) for i, w in enumerate(weights)]
    wide = pltpu.VMEM((local, LINE * 4 * cap, columns), BF16)
    outs = [struct(out.shape, BF16)] + [struct(*g) for i, g in enumerate(grads) if not exchange or i != 1]
    if exchange:
        outs.append(struct(*grads[1]))
    specs = [VMEM] + [ANY] * len(grads)
    scratch = [pltpu.VMEM(a.shape, a.dtype) for a in loads] + Line.scratch(local, width)
    scratch += [wide] * 3 + [pltpu.VMEM(*g) for g in grads] + [dma(len(loads)), dma(len(grads), local), dma(1), dma(1)]
    more = ride or ()
    if ride:
        depths = [g.shape[0] // (LINE * spread) for g in ride[:2]]
        outs.append(struct((LINE, spread, sum(depths) // 2, width // 2), F32))
        outs += [struct(g.shape, BF16) for g in ride[2:]]
        specs += [VMEM, ANY, ANY]
        scratch += GradientRider.scratch(spread, depths, width)
    return pl.pallas_call(
        functools.partial(expert_backward_kernel, spread, parts, int(exchange), ride is not None),
        out_shape=outs,
        in_specs=[VMEM] + [ANY] * (len(loads) + len(more)),
        out_specs=specs,
        scratch_shapes=scratch,
        compiler_params=remote_params(call_id),
        cost_estimate=pl.CostEstimate(flops=4 * 10**10, bytes_accessed=2 * 10**8, transcendentals=0),
    )(out, *loads, *more)


def from_partner(array, shift, spread, groups):
    pairs = [
        (t * spread + (f + shift) % spread, t * spread + f) for t in range(groups) for f in range(spread)
    ]
    return lax.ppermute(array, "dp", pairs)


def to_partner(array, shift, spread, groups):
    pairs = [
        (t * spread + f, t * spread + (f + shift) % spread) for t in range(groups) for f in range(spread)
    ]
    return lax.ppermute(array, "dp", pairs)


def pair_weights(shard, axis, spread):
    parts = [shard] + [from_partner(shard, i, spread, LINE) for i in range(1, spread)]
    if shard.shape[axis] % 128:
        return [jnp.concatenate(parts, axis=axis)]
    return parts


def pair_sum(parts, axis, spread):
    if len(parts) == 1 and spread > 1:
        parts = jnp.split(parts[0], spread, axis=axis)
    total = parts[0]
    for i in range(1, spread):
        total = total + to_partner(parts[i].astype(BF16), i, spread, LINE).astype(F32)
    return total


class LineGather:
    def __init__(self, place, pairs, shards, quarters, sems):
        self.p, self.shards, self.quarters = place, shards, quarters
        self.send, self.recv, self.x_send, self.x_recv = sems
        self.columns = [place.f, 1 - place.f] if pairs else [0]

    @staticmethod
    def shapes(shards, columns):
        (a, wide), (b, _), (c, narrow) = shards
        return [(LINE, columns, a // 2, wide // 2), (LINE, columns, b // 2, wide // 2), (LINE, columns, c, narrow)]

    @staticmethod
    def scratch(columns):
        return [dma(2, LINE, columns, 3), dma(LINE, columns, 3), dma(3), dma(3)]

    def copy(self, kind, up, t, f):
        at = self.quarters[kind].at[t, f]
        return remote(at, at, self.send.at[up, t, f, kind], self.recv.at[t, f, kind], self.p.on_line(up))

    def x_copy(self, kind, f):
        at = self.quarters[kind].at[self.p.t, f]
        return remote(at, at, self.x_send.at[kind], self.x_recv.at[kind], self.p.beside)

    def both_ways(self, f):
        p = self.p
        for up, there in ((0, p.below), (1, p.above)):

            @pl.when(there)
            def _(up=up):
                for kind in range(3):
                    self.copy(kind, up, p.t, f).start()

    def begin(self):
        p, f = self.p, self.columns[0]
        for kind in (0, 1):
            half, wide = self.quarters[kind].shape[2:]
            self.quarters[kind][p.t, f] = self.shards[kind][
                pl.ds(pl.multiple_of(p.y * half, 16), half), pl.ds(pl.multiple_of(p.c * wide, 128), wide)]
        self.quarters[2][p.t, f] = self.shards[2][...]
        for kind in range(3 if len(self.columns) == 2 else 0):
            self.x_copy(kind, f).start()
        self.both_ways(f)

    def beside(self, then):
        for f in self.columns[1:]:
            for kind in range(3):
                self.x_copy(kind, f).wait_recv()
            self.both_ways(f)
            then(self.p.t, f)

    def step(self, k, then):
        p = self.p
        for f in self.columns:
            for up, there, onward in ((0, p.t + k < LINE, p.below), (1, p.t - k >= 0, p.above)):
                t = p.t - k if up else p.t + k

                @pl.when(there)
                def _(up=up, onward=onward, t=t, f=f):
                    for kind in range(3):
                        self.copy(kind, up, t, f).wait_recv()

                    @pl.when(onward)
                    def _():
                        for kind in range(3):
                            self.copy(kind, up, t, f).start()

                    then(t, f)

    def finish(self):
        p = self.p

        def line(t, carry):
            for up, mine in ((0, jnp.logical_and(p.below, t >= p.t)), (1, jnp.logical_and(p.above, t <= p.t))):

                @pl.when(mine)
                def _(up=up):
                    for f in self.columns:
                        for kind in range(3):
                            self.copy(kind, up, t, f).wait_send()

            return carry

        lax.fori_loop(0, LINE, line, 0)
        for f in self.columns[1:]:
            for kind in range(3):
                self.x_copy(kind, 1 - f).wait_send()


class Spread:
    def __init__(self, place, quarters, shards, whole, sems):
        self.p, self.quarters, self.shards, self.whole = place, quarters, shards, whole
        self.y_send, self.y_recv, self.c_send, self.c_recv, self.l_sem, self.s_sem = sems

    @staticmethod
    def scratch(count):
        return [dma(count, 2), dma(count, 2), dma(count, 2, 2), dma(count, 2, 2), dma(count, 3), dma(3)]

    def region(self, kind, s, y, c):
        depth = self.shards[kind].shape[0]
        if kind == 2:
            return self.whole[2].at[pl.ds(pl.multiple_of(s * depth, 16), depth)]
        half, wide = depth // 2, self.shards[kind].shape[1] // 2
        return self.whole[kind].at[
            pl.ds(pl.multiple_of(s * depth + y * half, 16), half), pl.ds(pl.multiple_of(c * wide, 128), wide)]

    def mine(self, kind, s):
        return self.region(kind, s, self.p.y, self.p.c)

    def y_copy(self, kind, src, s):
        return remote(src, self.mine(kind, s), self.y_send.at[s, kind], self.y_recv.at[s, kind], self.p.across)

    def y_came(self, kind, s):
        at = self.region(kind, s, 1 - self.p.y, self.p.c)
        return remote(at, at, self.y_send.at[s, kind], self.y_recv.at[s, kind], self.p.across)

    def c_copy(self, kind, src, s, y):
        return remote(src, self.region(kind, s, y, self.p.c), self.c_send.at[s, y, kind], self.c_recv.at[s, y, kind],
                      self.p.sibling)

    def c_came(self, kind, s, y):
        at = self.region(kind, s, y, 1 - self.p.c)
        return remote(at, at, self.c_send.at[s, y, kind], self.c_recv.at[s, y, kind], self.p.sibling)

    def local(self, kind, src, s):
        return pltpu.make_async_copy(src, self.mine(kind, s), self.l_sem.at[s, kind])

    def shard(self, kind):
        depth = self.shards[kind].shape[0]
        at = self.whole[kind].at[pl.ds(pl.multiple_of(self.p.d * depth, 16), depth)]
        return pltpu.make_async_copy(self.shards[kind], at, self.s_sem.at[kind])

    def own_shard(self):
        for kind in range(3):
            self.shard(kind).start()

    def push(self, s, sources, here=True):
        if here:
            for kind in range(3):
                self.local(kind, sources[kind], s).start()
        for kind in (0, 1):
            self.y_copy(kind, sources[kind], s).start()
            self.c_copy(kind, sources[kind], s, self.p.y).start()

    def across(self, s):
        for kind in (0, 1):
            self.y_came(kind, s).wait_recv()
            self.c_copy(kind, self.region(kind, s, 1 - self.p.y, self.p.c), s, 1 - self.p.y).start()

    def finish_shard(self, s, here=True):
        @pl.when(s != self.p.d)
        def _():
            for kind in range(3 if here else 0):
                self.local(kind, self.mine(kind, s), s).wait()
            for kind in (0, 1):
                self.y_came(kind, s).wait_send()
                for y in (0, 1):
                    self.c_came(kind, s, y).wait_send()
                    self.c_came(kind, s, y).wait_recv()

    def finish_own(self):
        for kind in range(3):
            self.shard(kind).wait()


class WeightRider:
    def __init__(self, place, given, whole, sems):
        self.p, self.quarters, self.own, self.other = place, given[:3], given[6:], whole[3:]
        self.w_send, self.w_recv, self.x_send, self.x_recv, *more = sems
        self.spread = Spread(place, self.quarters, [ref.at[1] for ref in given[3:6]], whole[:3], more)

    @staticmethod
    def scratch(count):
        return [dma(2), dma(2), dma(LINE, 3), dma(LINE, 3)] + Spread.scratch(count)

    def place_of(self, t):
        return t * self.p.spread + self.p.f

    def beside_of(self, t):
        return t * self.p.spread + 1 - self.p.f

    def x_copy(self, kind, t, s):
        return remote(self.quarters[kind].at[t, 0], self.spread.mine(kind, s), self.x_send.at[t, kind],
                      self.x_recv.at[t, kind], self.p.beside)

    def weight(self, i):
        return remote(self.own[i], self.other[i], self.w_send.at[i], self.w_recv.at[i], self.p.beside)

    def begin(self):
        self.spread.own_shard()

        def body(t):
            for kind in range(3):
                self.x_copy(kind, t, self.place_of(t)).start()

            @pl.when(t != self.p.t)
            def _():
                self.spread.push(self.place_of(t), [q.at[t, 0] for q in self.quarters])

        along(self.p, body)
        for i in range(2):
            self.weight(i).start()

    def after_first(self):
        pass

    def after_line(self):
        def body(t):
            s = self.beside_of(t)
            for kind in range(3):
                self.x_copy(kind, t, s).wait_recv()
            self.spread.push(s, [self.spread.mine(kind, s) for kind in range(3)], here=False)

        along(self.p, body)

    def after_relay(self):
        along(self.p, lambda t: self.spread.across(self.place_of(t)), start=1)
        along(self.p, lambda t: self.spread.across(self.beside_of(t)))

    def finish(self):
        self.spread.finish_own()
        for i in range(2):
            self.weight(i).wait()

        def line(t, carry):
            for kind in range(3):
                self.x_copy(kind, t, self.place_of(t)).wait_send()
            self.spread.finish_shard(self.place_of(t))
            self.spread.finish_shard(self.beside_of(t), here=False)
            return carry

        lax.fori_loop(0, LINE, line, 0)


def dense_gather_kernel(spread, qkv, out, small, routes, *refs):
    p = Place(spread)
    wide, whole, quarters1, (routes_all,), own, firsts, partner, quarters0, loaded, rounded, rest = split(
        refs, 3, 3, 3, 1, 6, 2, 2, 3, 3, 3)
    sems0, sems1, (r_send, r_recv, w_send, w_recv, load_sem, own_sem, first_sem), spread_sems = split(rest, 4, 4, 7)
    shards0, shards1 = ([ref.at[l] for ref in (qkv, out, small)] for l in (0, 1))
    line0 = LineGather(p, True, shards0, quarters0, sems0)
    line1 = LineGather(p, False, shards1, quarters1, sems1)
    spreading = Spread(p, quarters0, shards0, whole, spread_sems)

    def load(l, kind):
        return pltpu.make_async_copy(wide[kind].at[l], loaded[kind].at[l], load_sem.at[l, kind])

    def store(l, kind):
        return pltpu.make_async_copy(rounded[kind].at[l], own[3 * l + kind], own_sem.at[l, kind])

    def first(l):
        return pltpu.make_async_copy(rounded[2].at[l, 0:1], firsts[l], first_sem.at[l])

    def weight(kind):
        return remote(rounded[kind].at[0], partner[kind], w_send.at[kind], w_recv.at[kind], p.beside)

    def round_weights(l, kind):
        load(l, kind).wait()

        def one(i, carry):
            rounded[kind][l, i] = loaded[kind][l, i].astype(BF16)
            return carry

        lax.fori_loop(0, rounded[kind].shape[1], one, 0)
        store(l, kind).start()
        if kind == 2:
            first(l).start()

    for l in (0, 1):
        for kind in range(3):
            load(l, kind).start()
    greet(p.mates[1:] + [p.beside], p)

    def route_copy(i, row):
        return remote(routes, routes_all.at[row], r_send.at[i], r_recv.at[row], p.mates[i])

    def push(t, f):
        spreading.push(t * spread + f, [q.at[t, f] for q in quarters0])

    line0.begin()
    for kind in (0, 1):
        round_weights(0, kind)
        weight(kind).start()
    routes_all[p.e] = routes[...]
    for i in (1, 2, 3):
        route_copy(i, p.e).start()
    spreading.own_shard()
    line0.beside(push)
    line1.begin()
    lax.fori_loop(1, LINE, lambda k, carry: (line0.step(k, push), carry)[1], 0)
    round_weights(0, 2)
    lax.fori_loop(1, LINE, lambda k, carry: (line1.step(k, lambda t, f: None), carry)[1], 0)
    for kind in range(3):
        round_weights(1, kind)
    along(p, lambda t: spreading.across(t * spread + p.f), start=1)
    along(p, lambda t: spreading.across(t * spread + 1 - p.f))
    spreading.finish_own()
    lax.fori_loop(0, LINE * spread, lambda s, carry: (spreading.finish_shard(s), carry)[1], 0)
    line0.finish()
    line1.finish()
    for l in (0, 1):
        for kind in range(3):
            store(l, kind).wait()
        first(l).wait()
    for kind in (0, 1):
        weight(kind).wait()
    for i in (1, 2, 3):
        route_copy(i, p.e).wait_send()
        route_copy(i, p.mates[i][1]).wait_recv()


def dense_gather(spread, call_id, arrays, routes, wide):
    count = spread * LINE
    shards = [a.shape[1:] for a in arrays]
    pairs, single = LineGather.shapes(shards, 2), LineGather.shapes(shards, 1)
    outs = [struct((count * rows, width), BF16) for rows, width in shards]
    outs += [struct(q, BF16) for q in single] + [struct((4,) + routes.shape, routes.dtype)]
    outs += [struct(w.shape[1:], BF16) for w in wide] * 2 + [struct((1,) + wide[2].shape[2:], BF16)] * 2
    outs += [struct(w.shape[1:], BF16) for w in wide[:2]]
    scratch = [pltpu.VMEM(q, BF16) for q in pairs] + [pltpu.VMEM(w.shape, F32) for w in wide]
    scratch += [pltpu.VMEM(w.shape, BF16) for w in wide] + LineGather.scratch(2) + LineGather.scratch(1)
    scratch += [dma(4), dma(4), dma(2), dma(2), dma(2, 3), dma(2, 3), dma(2)]
    return pl.pallas_call(
        functools.partial(dense_gather_kernel, spread),
        out_shape=outs,
        in_specs=[VMEM] * 4 + [ANY] * 3,
        out_specs=[ANY] * 3 + [VMEM] * 4 + [ANY] * 10,
        scratch_shapes=scratch + Spread.scratch(count),
        compiler_params=remote_params(call_id),
        cost_estimate=pl.CostEstimate(flops=10**10, bytes_accessed=10**8, transcendentals=0),
    )(*arrays, routes, *wide)


class Halve:
    def __init__(self, place, grads, quarter, scratch):
        self.p, self.grads, self.quarter = place, grads, quarter
        (self.mine, self.core, self.stage, self.came, self.l_sem, self.a_send, self.a_recv, self.y_send,
         self.y_recv) = scratch
        self.depths = [g.shape[0] // (LINE * place.spread) for g in grads]
        self.wide = grads[0].shape[1] // 2

    @staticmethod
    def scratch(spread, depths, width):
        count, rows, wide = LINE * spread, sum(depths) // 2, width // 2
        half = pltpu.VMEM((LINE, spread, rows, wide), BF16)
        everything = pltpu.VMEM((count * sum(depths), wide), BF16)
        return [everything, everything, half, half, dma(2), dma(2), dma(2), dma(LINE), dma(LINE)]

    def rows_of(self, kind):
        first = 0 if kind == 0 else self.grads[0].shape[0]
        return slice(first, first + self.grads[kind].shape[0])

    def lanes(self, c):
        return pl.ds(pl.multiple_of(c * self.wide, 128), self.wide)

    def local(self, kind):
        return pltpu.make_async_copy(
            self.grads[kind].at[:, self.lanes(self.p.c)], self.mine.at[self.rows_of(kind)], self.l_sem.at[kind])

    def a_copy(self, kind):
        return remote(self.grads[kind].at[:, self.lanes(1 - self.p.c)], self.core.at[self.rows_of(kind)],
                      self.a_send.at[kind], self.a_recv.at[kind], self.p.sibling)

    def y_copy(self, t):
        return remote(self.stage.at[t], self.came.at[t], self.y_send.at[t], self.y_recv.at[t], self.p.across)

    def pieces(self, t, f, y):
        s, row = t * self.p.spread + f, 0
        for kind, depth in enumerate(self.depths):
            at = self.rows_of(kind).start + s * depth + y * (depth // 2)
            here = pl.ds(pl.multiple_of(at, 16), depth // 2)
            yield slice(row, row + depth // 2), self.mine[here, :].astype(F32) + self.core[here, :].astype(F32)
            row += depth // 2

    def order(self, i):
        t = self.p.t
        down = LINE - 1 - i - jnp.where(LINE - 1 - i <= t, 1, 0)
        up = i + jnp.where(i >= t, 1, 0)
        return jnp.where(i == LINE - 1, t, jnp.where(t >= LINE // 2, up, down))

    def begin(self):
        for kind in (0, 1):
            self.a_copy(kind).start()
            self.local(kind).start()

    def after_first(self):
        for kind in (0, 1):
            self.a_copy(kind).wait_recv()
            self.local(kind).wait()

        def body(i, carry):
            t = self.order(i)
            for f in range(self.p.spread):
                for where, value in self.pieces(t, f, 1 - self.p.y):
                    self.stage[t, f, where] = value.astype(BF16)
            self.y_copy(t).start()
            return carry

        lax.fori_loop(0, LINE, body, 0)

        def own(t, carry):
            for f in range(self.p.spread):
                for where, value in self.pieces(t, f, self.p.y):
                    self.quarter[t, f, where] = value
            return carry

        lax.fori_loop(0, LINE, own, 0)

    def add(self, t):
        self.y_copy(t).wait_recv()
        self.quarter[t] = self.quarter[t] + self.came[t].astype(F32)

    def after_relay(self):
        lax.fori_loop(0, LINE, lambda i, carry: (self.add(self.order(i)), carry)[1], 0)

    def finish(self):
        for kind in (0, 1):
            self.a_copy(kind).wait_send()
        lax.fori_loop(0, LINE, lambda t, carry: (self.y_copy(t).wait_send(), carry)[1], 0)


class GradientRider:
    def __init__(self, place, given, outs, scratch):
        self.halve = Halve(place, given[:2], outs[0], scratch[:9])
        self.own, self.other = given[2:], outs[1:]
        self.p = place
        self.w_send, self.w_recv = scratch[9:]

    @staticmethod
    def scratch(spread, depths, width):
        return Halve.scratch(spread, depths, width) + [dma(2), dma(2)]

    def weight(self, i):
        return remote(self.own[i], self.other[i], self.w_send.at[i], self.w_recv.at[i], self.p.beside)

    def begin(self):
        self.halve.begin()
        for i in range(2):
            self.weight(i).start()

    def after_first(self):
        self.halve.after_first()

    def after_line(self):
        pass

    def after_relay(self):
        self.halve.after_relay()

    def finish(self):
        self.halve.finish()
        for i in range(2):
            self.weight(i).wait()


class LineSum:
    def __init__(self, place, depths, quarter, sums, scratch):
        self.p, self.depths, self.quarter, self.sums = place, depths, quarter, sums
        (self.stage, self.came, self.stage_x, self.came_x, self.z_send, self.z_recv, self.x_send, self.x_recv,
         self.e_send, self.e_recv) = scratch
        self.wide = sums[0].shape[1] // 2

    @staticmethod
    def scratch(spread, depths, width):
        rows, wide = sum(depths) // 2, width // 2
        return [
            pltpu.VMEM((LINE, spread, rows, wide), BF16),
            pltpu.VMEM((2, LINE, spread, rows, wide), BF16),
            pltpu.VMEM((rows, wide), BF16),
            pltpu.VMEM((rows, wide), BF16),
            dma(LINE), dma(2, LINE), dma(1), dma(1), dma(3, 2), dma(3, 2),
        ]

    def lanes(self, c):
        return pl.ds(pl.multiple_of(c * self.wide, 128), self.wide)

    def z_copy(self, up, t):
        return remote(self.stage.at[t], self.came.at[up, t], self.z_send.at[t], self.z_recv.at[up, t], self.p.on_line(up))

    def x_copy(self):
        return remote(self.stage_x, self.came_x, self.x_send.at[0], self.x_recv.at[0], self.p.beside)

    def e_copy(self, i, kind, y, c):
        half = self.depths[kind] // 2
        at = self.sums[kind].at[pl.ds(pl.multiple_of(y * half, 8), half), self.lanes(c)]
        return remote(at, at, self.e_send.at[i, kind], self.e_recv.at[i, kind], self.p.across if i == 0 else self.p.sibling)

    def start(self, t):
        p = self.p
        for up, mine in ((1, jnp.logical_and(p.t == 0, t > 0)), (0, jnp.logical_and(p.t == LINE - 1, t < LINE - 1))):

            @pl.when(mine)
            def _(up=up):
                self.stage[t] = self.quarter[t].astype(BF16)
                self.z_copy(up, t).start()

    def relay(self, kind):
        p = self.p

        @pl.when(p.inside)
        def _():
            t = {"near": p.t + p.ahead, "far": p.t + 2 * p.ahead, "back": p.t - p.ahead}[kind]
            way = 1 - p.up if kind == "back" else p.up
            self.z_copy(way, t).wait_recv()
            self.stage[t] = (self.quarter[t] + self.came[way, t].astype(F32)).astype(BF16)
            self.z_copy(way, t).start()

    def after_z(self):
        p = self.p

        for up, there in ((1, p.below), (0, p.above)):

            @pl.when(there)
            def _(up=up):
                self.z_copy(up, p.t).wait_recv()
                self.quarter[p.t] = self.quarter[p.t] + self.came[up, p.t].astype(F32)

        self.stage_x[...] = self.quarter[p.t, 1 - p.f].astype(BF16)
        self.x_copy().start()

    def after_x(self):
        p = self.p
        self.x_copy().wait_recv()
        row = 0
        for kind, depth in enumerate(self.depths):
            half = depth // 2
            value = self.quarter[p.t, p.f, row : row + half] + self.came_x[row : row + half].astype(F32)
            self.sums[kind][pl.ds(pl.multiple_of(p.y * half, 8), half), self.lanes(p.c)] = value
            row += half
        for i in (0, 1):
            for kind in (0, 1):
                self.e_copy(i, kind, p.y, p.c).start()

    def finish(self):
        p = self.p
        for kind in (0, 1):
            self.e_copy(0, kind, 1 - p.y, p.c).wait_recv()
            self.e_copy(2, kind, 1 - p.y, p.c).start()
        for kind in (0, 1):
            self.e_copy(0, kind, p.y, p.c).wait_send()
            self.e_copy(1, kind, p.y, p.c).wait_send()
            self.e_copy(1, kind, p.y, 1 - p.c).wait_recv()
            self.e_copy(2, kind, 1 - p.y, p.c).wait_send()
            self.e_copy(2, kind, 1 - p.y, 1 - p.c).wait_recv()
        self.x_copy().wait_send()

        def body(t, carry):
            @pl.when(t != p.t)
            def _():
                self.z_copy(0, t).wait_send()

            return carry

        lax.fori_loop(0, LINE, body, 0)


class SmallSum:
    def __init__(self, place, grads, total, scratch):
        self.p, self.grads, self.total = place, grads, total
        self.stage, self.came, self.send, self.recv = scratch
        p = place
        near = (p.d + p.spread - 2 * p.spread * lax.rem(p.t, 2), p.e)
        self.far = (lax.rem(p.d + 2 * p.spread, LINE * p.spread), p.e)
        self.partners = [p.sibling, p.across, near, self.far, p.beside]

    @staticmethod
    def scratch(rows, width):
        half = pltpu.VMEM((5, rows, width // 2), F32)
        return [half, half, dma(6), dma(6)]

    def lanes(self, c):
        wide = self.grads.shape[1] // 2
        return pl.ds(pl.multiple_of(c * wide, 128), wide)

    def copy(self, i):
        src = self.grads.at[:, self.lanes(1 - self.p.c)] if i == 0 else self.stage.at[i]
        return remote(src, self.came.at[i], self.send.at[i], self.recv.at[i], self.partners[i])

    def last(self, c):
        at = self.total.at[:, self.lanes(c)]
        return remote(at, at, self.send.at[5], self.recv.at[5], self.p.sibling)

    def step(self, i):
        if i == 0:
            self.copy(0).start()
            return
        self.copy(i - 1).wait_recv()
        mine = self.grads[:, self.lanes(self.p.c)] if i == 1 else self.stage[i - 1]
        value = mine + self.came[i - 1]
        if i < 5:
            self.stage[i] = value
            self.copy(i).start()
        else:
            self.total[:, self.lanes(self.p.c)] = value
            self.last(self.p.c).start()

    def finish(self):
        for i in range(5):
            self.copy(i).wait_send()
        self.last(self.p.c).wait_send()
        self.last(1 - self.p.c).wait_recv()


def dense_reduce_kernel(spread, depths, small0, small1, res, qkv0, out0, quarter1, up0, down0, small_sum, *refs):
    p = Place(spread)
    sums, came, (small, mine0, mine1), (w_send, w_recv), halve_refs, line0, line1, small_refs = split(refs, 2, 2, 3, 2, 9, 10, 10)
    sums0, sums1 = ([ref.at[l] for ref in sums] for l in (0, 1))
    halve = Halve(p, (qkv0, out0), mine0, halve_refs)
    sum0 = LineSum(p, depths, mine0, sums0, line0)
    sum1 = LineSum(p, depths, mine1, sums1, line1)
    little = SmallSum(p, small, small_sum, small_refs)
    weights = [remote(w, came[i], w_send.at[i], w_recv.at[i], p.beside) for i, w in enumerate((up0, down0))]
    greet([p.sibling, p.across, p.beside, little.far], p)
    halve.begin()
    for copy in weights:
        copy.start()
    rows = small0.shape[0]
    small[0:rows, :] = small0[...]
    small[rows : 2 * rows, :] = small1[...]
    small[2 * rows :, :] = jnp.zeros((16, small.shape[1]), F32)
    small[2 * rows :, 0:128] = res[0:16, :]
    little.step(0)
    mine1[...] = quarter1[...]
    for i in range(LINE):
        sum1.start(halve.order(i))
    little.step(1)
    halve.after_first()
    little.step(2)

    def arrive(i):
        halve.add(halve.order(i))
        sum0.start(halve.order(i))

    sum1.relay("far")
    sum1.relay("near")
    arrive(0)
    little.step(3)
    sum1.relay("back")
    arrive(1)
    sum0.relay("far")
    sum1.after_z()
    arrive(2)
    sum0.relay("near")
    sum0.relay("back")
    arrive(3)
    little.step(4)
    sum0.after_z()
    sum1.after_x()
    little.step(5)
    sum0.after_x()
    sum1.finish()
    halve.finish()
    little.finish()
    sum0.finish()
    for copy in weights:
        copy.wait()


def dense_reduce(spread, call_id, smalls, grads0, quarter1, weights0):
    count = LINE * spread
    depths = [g.shape[0] // count for g in grads0]
    width = grads0[0].shape[1]
    small = (2 * smalls[0].shape[0] + 16, width)
    line = LineSum.scratch(spread, depths, width)
    mine = pltpu.VMEM(quarter1.shape, F32)
    scratch = [pltpu.VMEM(small, F32), mine, mine, dma(2), dma(2)] + Halve.scratch(spread, depths, width) + line + line
    return pl.pallas_call(
        functools.partial(dense_reduce_kernel, spread, depths),
        out_shape=[struct(small, F32)] + [struct((2, depth, width), F32) for depth in depths]
        + [struct(w.shape, BF16) for w in weights0],
        in_specs=[VMEM] * 3 + [ANY, ANY, VMEM, ANY, ANY],
        out_specs=[VMEM] * 3 + [ANY] * 2,
        scratch_shapes=scratch + SmallSum.scratch(*small),
        compiler_params=remote_params(call_id),
        cost_estimate=pl.CostEstimate(flops=2 * 10**10, bytes_accessed=2 * 10**8, transcendentals=0),
    )(*smalls, *grads0, quarter1, *weights0)


def per_device(
    tokens, seq_lengths, block_perm, routes, norm_gains, w_qkv, w_out, w_router, w_residual, w_const, v_const,
    w_gate, w_up, w_down, cotangent,
):
    rows, width = tokens.shape
    owners = lax.axis_size("expert")
    shards = lax.axis_size("dp")
    spread = shards // LINE
    local = w_gate.shape[1]
    experts = local * owners
    layers = routes.shape[0]
    slots = experts * CAP

    packed_routes = jnp.zeros((8, -(-rows // 128) * 128), jnp.int32).at[: 2 * layers, :rows].set(
        jnp.swapaxes(routes, 1, 2).reshape(2 * layers, rows))

    depth = w_out.shape[1]
    small = jnp.concatenate(
        [
            w_router, w_const[:, 0], w_const[:, 1], jnp.swapaxes(norm_gains, 1, 2), jnp.swapaxes(v_const, 1, 2),
            jnp.zeros((layers, depth, 108), F32),
        ],
        axis=2,
    ).astype(BF16)
    qkv_t = jnp.swapaxes(w_qkv, 1, 2).astype(BF16)
    out_rows = w_out.astype(BF16)
    in_kernels = spread == 2 and owners == 4 and qkv_t.shape[1] % 32 == 0 and depth % 32 == 0
    if in_kernels:
        *gathered, routes_all, g0, u0, d0, g1, u1, d1, first0, first1, gate, up = dense_gather(
            spread, 4, (qkv_t, out_rows, small), packed_routes, (w_gate, w_up, w_down))
        weights = [[g0, gate, u0, up, d0, from_partner(first0, 1, spread, LINE)]]
        dense = [(gathered[2], gathered[0], gathered[1])]
    else:
        weights = []
        for l in range(layers):
            own = [(w_gate[l].astype(BF16), 2), (w_up[l].astype(BF16), 2), (w_down[l].astype(BF16), 1)]
            weights.append([part for w, axis in own for part in pair_weights(w, axis, spread)])
        routes_all = lax.all_gather(packed_routes, "expert", axis=0)
        qkv_all = lax.all_gather(qkv_t, "dp", axis=1, tiled=True)
        out_all = lax.all_gather(out_rows, "dp", axis=1, tiled=True)
        small_all = lax.all_gather(small, "dp", axis=1, tiled=True)
        dense = [(small_all[l], qkv_all[l], out_all[l]) for l in range(layers)]

    cols = ((rows, width), F32)
    attention = [((rows, width), BF16), ((rows, 3 * width), BF16), ((HEADS, rows, rows), F32), ((rows, width), BF16)]
    residual = ((128, 128), F32)
    per_token, sent = ((rows, 128), F32), ((slots, width), BF16)

    def group(array):
        return array.reshape(owners, local, CAP, width)

    attn_in0, qkv0, probs0, attn0, mid0, logits0, stat0, out = local_call(
        first_kernel, experts, (tokens, *dense[0], seq_lengths, block_perm, routes_all),
        attention + [cols, per_token, per_token, sent], scalars=(4, 5))
    ride = (*gathered[3:], qkv_t, out_rows, small, g1, u1) if in_kernels else None
    ret0, *kept0 = expert_forward(spread, 0, group(out), weights[0], in_kernels, ride)
    if in_kernels:
        kept0, weights[0][5], (qkv_all, out_all, small_all), (gate, up) = kept0[:3], kept0[3], kept0[4:7], kept0[7:]
        dense.append((small_all, qkv_all, out_all))
        first1, ret0 = lax.optimization_barrier((first1, ret0))
        weights.append([g1, gate, u1, up, d1, from_partner(first1, 1, spread, LINE)])
    ret0 = ret0.reshape(slots, width)
    stream1, attn_in1, qkv1, probs1, attn1, mid1, stat1, out = local_call(
        middle_kernel, experts,
        (mid0, dense[0][0], stat0, ret0, *dense[1], seq_lengths, block_perm, routes_all, logits0, w_residual),
        [cols] + attention + [cols, per_token, sent], [residual], scalars=(7, 8))
    ret1, *kept1 = expert_forward(spread, 1, group(out), weights[1], in_kernels)
    if in_kernels:
        weights[1][5] = kept1.pop()
    ret1 = ret1.reshape(slots, width)

    small_grads = ((24, width), F32)
    output, g_small1, extra, out, small_grad1, res_grad = local_call(
        turn_kernel, experts, (mid1, dense[1][0], stat1, ret1, cotangent, logits0, w_residual),
        [((rows, width), BF16), per_token, per_token, sent, small_grads, residual], [residual])
    back, *expert_grads1 = expert_backward(spread, 2, group(out), kept1, weights[1], in_kernels)
    ride = None
    grad_type = BF16 if in_kernels else F32
    dense_grads = [((3 * width, width), grad_type), ((width, width), grad_type), small_grads]
    attention_scratch = [((rows, 3 * width), BF16), ((rows, width), BF16)]
    qkv_grad1, out_grad1, small_grad1, grad, g_small0, out, small_grad0 = local_call(
        between_kernel, experts,
        (cotangent, back.reshape(slots, width), g_small1, stat1, mid1, dense[1][0], stream1, dense[1][1], dense[1][2],
         attn_in1, qkv1, probs1, attn1, small_grad1, mid0, dense[0][0], stat0, ret0, extra),
        dense_grads + [cols, per_token, sent, small_grads], attention_scratch)
    if in_kernels:
        gate1, up1, up1_sent, down1, down1_sent, gate1_came = expert_grads1
        ride = (qkv_grad1, out_grad1, up1_sent, down1_sent)
    back, *expert_grads0 = expert_backward(spread, 3, group(out), kept0, weights[0], in_kernels, ride)
    qkv_grad0, out_grad0, small_grad0, tokens_grad = local_call(
        last_kernel, experts,
        (grad, back.reshape(slots, width), g_small0, stat0, mid0, dense[0][0], tokens, dense[0][1], dense[0][2],
         attn_in0, qkv0, probs0, attn0, small_grad0),
        dense_grads + [cols], attention_scratch)

    if in_kernels:
        gate0, up0, up0_sent, down0, down0_sent, gate0_came, quarter1, up1_came, down1_came = expert_grads0
        packed, qkv_grad, out_grad, up0_came, down0_came = dense_reduce(
            spread, 5, (small_grad0, small_grad1, res_grad), (qkv_grad0, out_grad0), quarter1, (up0_sent, down0_sent))
        pairs = (
            ((gate0, gate0_came), (gate1, gate1_came)), ((up0, up0_came), (up1, up1_came)),
            ((down0, down0_came), (down1, down1_came)))
        gate_grad, up_grad, down_grad = (
            jnp.stack([mine + came.astype(F32) for mine, came in layer]) for layer in pairs)
    else:
        gate_grad, up_grad, down_grad = (
            jnp.stack([
                pair_sum(grads[at * len(grads) // 3 : (at + 1) * len(grads) // 3], axis, spread)
                for grads in (expert_grads0, expert_grads1)])
            for axis, at in ((2, 0), (2, 1), (1, 2)))
        packed = jnp.concatenate([small_grad0, small_grad1, jnp.pad(res_grad[:16], ((0, 0), (0, width - 128)))])
        packed = lax.psum(packed, ("dp", "expert"))
        qkv_grad, out_grad = (
            lax.psum(lax.psum_scatter(jnp.stack(pair), "dp", scatter_dimension=1, tiled=True), "expert")
            for pair in ((qkv_grad0, qkv_grad1), (out_grad0, out_grad1)))
    mine = lax.dynamic_slice_in_dim(packed, lax.axis_index("dp") * depth, depth, axis=1)
    mine = jnp.stack([mine[:24], mine[24:48]])
    router_grad = jnp.swapaxes(mine[:, :CONST0], 1, 2)
    const_grad = jnp.swapaxes(mine[:, CONST0:GAIN0].reshape(layers, 2, 2, depth), 2, 3)
    residual_grad = packed[48 : 48 + CONST0, :CONST0]
    return (
        output, tokens_grad, mine[:, GAIN0 : GAIN0 + 2], jnp.swapaxes(qkv_grad, 1, 2), out_grad, router_grad,
        residual_grad, const_grad, mine[:, VECTOR0 : VECTOR0 + 2], gate_grad, up_grad, down_grad,
    )


def solution(mesh):
    in_specs = (
        P(("dp", "expert"), None), P("dp", None, None), P("dp", None), P(None, ("dp", "expert"), None),
        P(None, None, "dp"), P(None, None, "dp"), P(None, "dp", None), P(None, "dp", None), P(),
        P(None, None, "dp", None), P(None, None, "dp"), P(None, "expert", None, "dp"), P(None, "expert", None, "dp"),
        P(None, "expert", "dp", None), P(("dp", "expert"), None),
    )
    out_specs = (
        P(("dp", "expert"), None), P(("dp", "expert"), None), P(None, None, "dp"), P(None, None, "dp"),
        P(None, "dp", None), P(None, "dp", None), P(), P(None, None, "dp", None), P(None, None, "dp"),
        P(None, "expert", None, "dp"), P(None, "expert", None, "dp"), P(None, "expert", "dp", None),
    )
    return jax.shard_map(per_device, mesh=mesh, in_specs=in_specs, out_specs=out_specs, check_vma=False)
```

```python
import functools

import jax
import jax.numpy as jnp
from jax import lax
from jax.experimental import pallas as pl
from jax.experimental.pallas import tpu as pltpu
from jax.sharding import PartitionSpec as P

HEADS = 12
CAP = 48
LINE = 4
EPSILON = 1e-05
MASKED = -1e30
HIGH = lax.Precision.HIGHEST
F32 = jnp.float32
BF16 = jnp.bfloat16
MESH = pl.DeviceIdType.MESH
VMEM = pl.BlockSpec(memory_space=pltpu.VMEM)
ANY = pl.BlockSpec(memory_space=pl.ANY)

CONST0, GAIN0, VECTOR0 = 12, 16, 18
STAT = {
    name: i
    for i, name in enumerate(
        ("r0", "r1", "share0", "share1", "slot0", "slot1", "p00", "p01", "p10", "p11")
    )
}


SMEM = pl.BlockSpec(memory_space=pltpu.SMEM)


def dot_nn(a, b, **kw):
    return lax.dot_general(a, b, (((1,), (0,)), ((), ())), preferred_element_type=F32, **kw)


def dot_nt(a, b, **kw):
    return lax.dot_general(a, b, (((1,), (1,)), ((), ())), preferred_element_type=F32, **kw)


def dot_tn(a, b, **kw):
    return lax.dot_general(a, b, (((0,), (0,)), ((), ())), preferred_element_type=F32, **kw)


def lanes(rows, width=128):
    return lax.broadcasted_iota(jnp.int32, (rows, width), 1)


def rms_scale(values):
    return lax.rsqrt(jnp.mean(values * values, axis=-1, keepdims=True) + EPSILON)


def row_vectors(small):
    pick = lax.broadcasted_iota(jnp.int32, (8, 128), 0) + GAIN0 == lanes(8)
    rows = dot_nt(pick.astype(BF16), small)
    return rows[0:1], rows[1:2], rows[2:3], rows[3:4]


def stat_columns(stat):
    return {name: stat[:, i : i + 1] for name, i in STAT.items()}


def slot_picks(stat, slots):
    place = lanes(stat["slot0"].shape[0], slots).astype(F32)
    first = (place == stat["slot0"]).astype(BF16)
    second = (place == stat["slot1"]).astype(BF16)
    return first, second


def const_weights(stat, experts):
    out = []
    for kind in (experts + 1, experts + 2, experts + 3):
        out.append(
            stat["share0"] * (stat["r0"] == kind).astype(F32)
            + stat["share1"] * (stat["r1"] == kind).astype(F32)
        )
    return out


def doc_index(lengths, places):
    place, end = lax.axis_index("expert"), 0
    doc = jnp.zeros_like(places)
    for j in range(lengths.shape[2]):
        end = end + lengths[0, place, j]
        doc = doc + (places >= end).astype(jnp.int32)
    return doc


def block_routes(perm, routes_all, layer, rows):
    mine = routes_all[perm[0, lax.axis_index("expert")]].astype(F32)
    routes = jnp.transpose(mine)[:rows].astype(jnp.int32)
    return routes[:, 2 * layer : 2 * layer + 1], routes[:, 2 * layer + 1 : 2 * layer + 2]


def padded(w_res, ref):
    count = w_res.shape[0]
    ref[...] = jnp.zeros(ref.shape, F32)
    ref[0:count, 0:count] = w_res[...]
    return ref[...]


def attend_part(stream, small, w_qkv_t, w_out, lengths, attn_in_ref, qkv_ref, probs_ref, attn_ref):
    rows, width = stream.shape
    gain, _, _, _ = row_vectors(small)
    attn_in_ref[...] = (stream * rms_scale(stream) * gain).astype(BF16)

    def project(i, carry):
        at = pl.multiple_of(i * width, width)
        qkv_ref[:, pl.ds(at, width)] = dot_nt(
            attn_in_ref[...], w_qkv_t[pl.ds(at, width), :]
        ).astype(BF16)
        return carry

    lax.fori_loop(0, 3, project, 0, unroll=True)
    head_dim = width // HEADS
    factor = 1.0 / head_dim**0.5
    allowed = jnp.logical_and(
        doc_index(lengths, lax.broadcasted_iota(jnp.int32, (rows, 1), 0))
        == doc_index(lengths, lax.broadcasted_iota(jnp.int32, (1, rows), 1)),
        lax.broadcasted_iota(jnp.int32, (rows, rows), 0)
        >= lax.broadcasted_iota(jnp.int32, (rows, rows), 1),
    )

    def heads(i, carry):
        at = pl.multiple_of(i * 2 * head_dim, 2 * head_dim)
        query = qkv_ref[:, pl.ds(at, 2 * head_dim)]
        key = qkv_ref[:, pl.ds(pl.multiple_of(at + width, 128), 2 * head_dim)]
        value = qkv_ref[:, pl.ds(pl.multiple_of(at + 2 * width, 128), 2 * head_dim)]
        second = lanes(rows, 2 * head_dim) >= head_dim
        mixed = []
        for sub in (0, 1):
            mine = second if sub else jnp.logical_not(second)
            scores = dot_nt(jnp.where(mine, query, jnp.zeros_like(query)), key) * factor
            scores = jnp.where(allowed, scores, MASKED)
            exponent = jnp.exp(scores - jnp.max(scores, axis=-1, keepdims=True))
            probs = exponent / jnp.sum(exponent, axis=-1, keepdims=True)
            probs_ref[2 * i + sub] = probs
            mixed.append(dot_nn(probs.astype(BF16), value))
        attn_ref[:, pl.ds(at, 2 * head_dim)] = jnp.where(second, mixed[1], mixed[0]).astype(BF16)
        return carry

    lax.fori_loop(0, HEADS // 2, heads, 0, unroll=True)
    return stream + dot_nn(attn_ref[...], w_out[...])


def route_part(mid, small, routes, prev_logits, w_res, experts):
    rows = mid.shape[0]
    _, gain, _, _ = row_vectors(small)
    hidden = (mid * rms_scale(mid) * gain).astype(BF16)
    lane = lanes(rows)
    raw = dot_nn(hidden, small)
    logits = jnp.where(lane < CONST0, raw, 0.0)
    if prev_logits is not None:
        logits = logits + dot_nn(prev_logits, w_res, precision=HIGH)
    r0, r1 = routes
    hot0, hot1 = (lane == r0).astype(F32), (lane == r1).astype(F32)
    c0 = jnp.sum(hot0 * logits, axis=-1, keepdims=True)
    c1 = jnp.sum(hot1 * logits, axis=-1, keepdims=True)
    peak = jnp.maximum(c0, c1)
    e0, e1 = jnp.exp(c0 - peak), jnp.exp(c1 - peak)
    total = e0 + e1
    share0, share1 = e0 / total, e1 / total
    probs = []
    for j in (0, 1):
        a = raw[:, CONST0 + 2 * j : CONST0 + 2 * j + 1]
        b = raw[:, CONST0 + 2 * j + 1 : CONST0 + 2 * j + 2]
        top = jnp.maximum(a, b)
        ea, eb = jnp.exp(a - top), jnp.exp(b - top)
        probs += [ea / (ea + eb), eb / (ea + eb)]
    earlier = lax.broadcasted_iota(jnp.int32, (rows, rows), 0) > lax.broadcasted_iota(
        jnp.int32, (rows, rows), 1
    )
    before = dot_nn(earlier.astype(BF16), (hot0 + hot1).astype(BF16))
    f0, f1 = r0.astype(F32), r1.astype(F32)
    slot0 = jnp.where(
        r0 < experts, f0 * CAP + jnp.sum(before * hot0, axis=-1, keepdims=True), -1.0
    )
    slot1 = jnp.where(
        r1 < experts, f1 * CAP + jnp.sum(before * hot1, axis=-1, keepdims=True), -1.0
    )
    stat = jnp.zeros((rows, 128), F32)
    for i, column in enumerate([f0, f1, share0, share1, slot0, slot1] + probs):
        stat = jnp.where(lane == i, column, stat)
    first, second = slot_picks({"slot0": slot0, "slot1": slot1}, experts * CAP)
    outgoing = dot_tn(first + second, hidden).astype(BF16)
    return logits, stat, outgoing


def combine_part(mid, small, stat, returned, experts):
    _, gain, vec0, vec1 = row_vectors(small)
    hidden_full = mid * rms_scale(mid) * gain
    first, second = slot_picks(stat, experts * CAP)
    pair0, pair1 = dot_nn(first, returned), dot_nn(second, returned)
    copy, const0, const1 = const_weights(stat, experts)
    local = copy + const0 * stat["p00"] + const1 * stat["p10"]
    moe = stat["share0"] * pair0 + stat["share1"] * pair1 + local * hidden_full
    moe = moe + (const0 * stat["p01"]) * vec0 + (const1 * stat["p11"]) * vec1
    return mid + moe, hidden_full, pair0, pair1


def share_backward(grad, small, stat, hidden_full, pair0, pair1, extra, experts):
    rows = grad.shape[0]
    _, _, vec0, vec1 = row_vectors(small)
    first, second = slot_picks(stat, experts * CAP)
    lane = lanes(rows).astype(F32)
    rowsum = functools.partial(jnp.sum, axis=-1, keepdims=True)
    dot_hidden = rowsum(grad * hidden_full)
    dot_vec = (rowsum(grad * vec0), rowsum(grad * vec1))
    _, const0, const1 = const_weights(stat, experts)
    probs = ((stat["p00"], stat["p01"]), (stat["p10"], stat["p11"]))
    value = [probs[j][0] * dot_hidden + probs[j][1] * dot_vec[j] for j in (0, 1)]
    shares = []
    for r, pair in ((stat["r0"], pair0), (stat["r1"], pair1)):
        shares.append(
            rowsum(grad * pair)
            + (r == experts + 1).astype(F32) * dot_hidden
            + (r == experts + 2).astype(F32) * value[0]
            + (r == experts + 3).astype(F32) * value[1]
        )
    inner = stat["share0"] * shares[0] + stat["share1"] * shares[1]
    g_small = (lane == stat["r0"]).astype(F32) * (stat["share0"] * (shares[0] - inner))
    g_small = g_small + (lane == stat["r1"]).astype(F32) * (stat["share1"] * (shares[1] - inner))
    if extra is not None:
        g_small = g_small + extra
    g_logits = g_small
    for j, weight in ((0, const0), (1, const1)):
        q = (weight * dot_hidden, weight * dot_vec[j])
        mean = probs[j][0] * q[0] + probs[j][1] * q[1]
        for c in (0, 1):
            g_small = jnp.where(lane == CONST0 + 2 * j + c, probs[j][c] * (q[c] - mean), g_small)
    sent0 = (jnp.where(stat["r0"] < experts, stat["share0"], 0.0) * grad).astype(BF16)
    sent1 = (jnp.where(stat["r1"] < experts, stat["share1"], 0.0) * grad).astype(BF16)
    outgoing = (dot_tn(first, sent0) + dot_tn(second, sent1)).astype(BF16)
    hidden = hidden_full.astype(BF16).astype(F32)
    projections = dot_tn(g_small, hidden, precision=HIGH)
    vector0 = jnp.sum((const0 * stat["p01"]) * grad, axis=0, keepdims=True)
    vector1 = jnp.sum((const1 * stat["p11"]) * grad, axis=0, keepdims=True)
    return g_small, g_logits, outgoing, projections, vector0, vector1


def store_small(ref, projections, vector0, vector1):
    ref[0:16, :] = projections[0:16]
    ref[16:24, :] = jnp.zeros((8, ref.shape[1]), F32)
    ref[VECTOR0 : VECTOR0 + 1, :] = vector0
    ref[VECTOR0 + 1 : VECTOR0 + 2, :] = vector1


def first_kernel(experts, tokens, small, w_qkv_t, w_out, lengths, perm, routes_all,
                 attn_in, qkv, probs, attn, mid_ref, logits_ref, stat_ref, out_ref):
    mid = attend_part(tokens[...].astype(F32), small[...], w_qkv_t, w_out, lengths, attn_in, qkv, probs, attn)
    mid_ref[...] = mid
    routes = block_routes(perm, routes_all, 0, mid.shape[0])
    logits, stat, out = route_part(mid, small[...], routes, None, None, experts)
    logits_ref[...], stat_ref[...], out_ref[...] = logits, stat, out


def middle_kernel(experts, mid_in, small_in, stat_in, returned, small, w_qkv_t, w_out, lengths, perm, routes_all, logits_in, w_res,
                  stream_ref, attn_in, qkv, probs, attn, mid_ref, stat_ref, out_ref, res_ref):
    stream, _, _, _ = combine_part(mid_in[...], small_in[...], stat_columns(stat_in[...]), returned[...], experts)
    stream_ref[...] = stream
    mid = attend_part(stream, small[...], w_qkv_t, w_out, lengths, attn_in, qkv, probs, attn)
    mid_ref[...] = mid
    routes = block_routes(perm, routes_all, 1, mid.shape[0])
    _, stat, out = route_part(mid, small[...], routes, logits_in[...], padded(w_res, res_ref), experts)
    stat_ref[...], out_ref[...] = stat, out


def turn_kernel(experts, mid, small, stat_in, returned, cotangent, logits_in, w_res,
                output, g_small_ref, extra_ref, out_ref, small_grad, res_grad, res_ref):
    stat = stat_columns(stat_in[...])
    stream, hidden_full, pair0, pair1 = combine_part(mid[...], small[...], stat, returned[...], experts)
    output[...] = stream.astype(BF16)
    grad = cotangent[...].astype(F32)
    g_small, g_logits, out, projections, v0, v1 = share_backward(grad, small[...], stat, hidden_full, pair0, pair1, None, experts)
    g_small_ref[...] = g_small
    out_ref[...] = out
    store_small(small_grad, projections, v0, v1)
    res_grad[...] = dot_tn(logits_in[...], g_logits, precision=HIGH)
    extra_ref[...] = dot_nt(g_logits, padded(w_res, res_ref), precision=HIGH)


def layer_backward(experts, grad, back, g_small, stat, mid, small, stream, w_qkv_t, w_out, attn_in, qkv, probs, attn,
                   qkv_grad, out_grad, small_grad, g_qkv, g_attn):
    rows, width = mid.shape
    gain1, gain2, _, _ = row_vectors(small)
    first, second = slot_picks(stat, experts * CAP)
    copy, const0, const1 = const_weights(stat, experts)
    local = copy + const0 * stat["p00"] + const1 * stat["p10"]
    g_full = dot_nt(g_small, small.astype(F32), precision=HIGH) + dot_nn(first + second, back)
    g_full = g_full + grad * local
    s2 = rms_scale(mid)
    small_grad[GAIN0 + 1 : GAIN0 + 2, :] = jnp.sum(g_full * mid * s2, axis=0, keepdims=True)
    m = g_full * gain2
    g_mid = grad + s2 * m - mid * (s2 * s2 * s2 * jnp.mean(m * mid, axis=-1, keepdims=True))
    branch = g_mid.astype(BF16)
    out_grad[...] = dot_tn(attn[...], branch).astype(out_grad.dtype)
    g_attn[...] = dot_nt(branch, w_out[...]).astype(BF16)
    head_dim = width // HEADS
    factor = 1.0 / head_dim**0.5

    def heads(i, carry):
        at = pl.multiple_of(i * 2 * head_dim, 2 * head_dim)
        at_k = pl.multiple_of(at + width, 128)
        at_v = pl.multiple_of(at + 2 * width, 128)
        query = qkv[:, pl.ds(at, 2 * head_dim)]
        key = qkv[:, pl.ds(at_k, 2 * head_dim)]
        value = qkv[:, pl.ds(at_v, 2 * head_dim)]
        ga = g_attn[:, pl.ds(at, 2 * head_dim)]
        second_half = lanes(rows, 2 * head_dim) >= head_dim
        gq, gk, gv = [], [], []
        for sub in (0, 1):
            mine = second_half if sub else jnp.logical_not(second_half)
            p = probs[2 * i + sub]
            gp = dot_nt(jnp.where(mine, ga, jnp.zeros_like(ga)), value)
            gs = (p * (gp - jnp.sum(p * gp, axis=-1, keepdims=True))).astype(BF16)
            gq.append(dot_nn(gs, key))
            gk.append(dot_tn(gs, query))
            gv.append(dot_tn(p.astype(BF16), ga))
        g_qkv[:, pl.ds(at, 2 * head_dim)] = (jnp.where(second_half, gq[1], gq[0]) * factor).astype(BF16)
        g_qkv[:, pl.ds(at_k, 2 * head_dim)] = (jnp.where(second_half, gk[1], gk[0]) * factor).astype(BF16)
        g_qkv[:, pl.ds(at_v, 2 * head_dim)] = jnp.where(second_half, gv[1], gv[0]).astype(BF16)
        return carry

    lax.fori_loop(0, HEADS // 2, heads, 0, unroll=True)

    def weights(i, carry):
        at = pl.multiple_of(i * width, width)
        qkv_grad[pl.ds(at, width), :] = dot_tn(g_qkv[:, pl.ds(at, width)], attn_in[...]).astype(qkv_grad.dtype)
        return carry + dot_nn(g_qkv[:, pl.ds(at, width)], w_qkv_t[pl.ds(at, width), :])

    g_in = lax.fori_loop(0, 3, weights, jnp.zeros((rows, width), F32))
    s1 = rms_scale(stream)
    small_grad[GAIN0 : GAIN0 + 1, :] = jnp.sum(g_in * stream * s1, axis=0, keepdims=True)
    n = g_in * gain1
    return g_mid + s1 * n - stream * (s1 * s1 * s1 * jnp.mean(n * stream, axis=-1, keepdims=True))


def between_kernel(experts, cotangent, back, g_small, stat_in, mid, small, stream, w_qkv_t, w_out, attn_in, qkv, probs, attn, small_grad_in,
                   mid0, small0, stat0_in, returned0, extra,
                   qkv_grad, out_grad, small_grad, grad_ref, g_small0_ref, out_ref, small_grad0, g_qkv, g_attn):
    small_grad[...] = small_grad_in[...]
    grad = layer_backward(experts, cotangent[...].astype(F32), back[...], g_small[...], stat_columns(stat_in[...]), mid[...],
                          small[...], stream[...], w_qkv_t, w_out, attn_in, qkv, probs, attn, qkv_grad, out_grad, small_grad, g_qkv, g_attn)
    grad_ref[...] = grad
    stat0 = stat_columns(stat0_in[...])
    _, hidden_full, pair0, pair1 = combine_part(mid0[...], small0[...], stat0, returned0[...], experts)
    g_small0, _, out, projections, v0, v1 = share_backward(grad, small0[...], stat0, hidden_full, pair0, pair1, extra[...], experts)
    g_small0_ref[...] = g_small0
    out_ref[...] = out
    store_small(small_grad0, projections, v0, v1)


def last_kernel(experts, grad_in, back, g_small, stat_in, mid, small, tokens, w_qkv_t, w_out, attn_in, qkv, probs, attn, small_grad_in,
                qkv_grad, out_grad, small_grad, grad_ref, g_qkv, g_attn):
    small_grad[...] = small_grad_in[...]
    grad_ref[...] = layer_backward(experts, grad_in[...], back[...], g_small[...], stat_columns(stat_in[...]), mid[...], small[...],
                                   tokens[...].astype(F32), w_qkv_t, w_out, attn_in, qkv, probs, attn, qkv_grad, out_grad, small_grad,
                                   g_qkv, g_attn)


def local_call(kernel, experts, args, outs, scratch=(), scalars=()):
    return pl.pallas_call(
        functools.partial(kernel, experts),
        out_shape=[jax.ShapeDtypeStruct(shape, dtype) for shape, dtype in outs],
        in_specs=[SMEM if i in scalars else VMEM for i in range(len(args))],
        out_specs=[VMEM] * len(outs),
        scratch_shapes=[pltpu.VMEM(shape, dtype) for shape, dtype in scratch],
        compiler_params=pltpu.CompilerParams(vmem_limit_bytes=60 * 2**20),
        cost_estimate=pl.CostEstimate(flops=10**10, bytes_accessed=6 * 10**7, transcendentals=0),
    )(*args)


class Place:
    def __init__(self, spread):
        self.spread = spread
        self.d, self.e = lax.axis_index("dp"), lax.axis_index("expert")
        self.t, self.f = self.d // spread, lax.rem(self.d, spread)
        self.y, self.c = self.e // 2, lax.rem(self.e, 2)
        self.above, self.below = self.t < LINE - 1, self.t > 0
        self.inside = jnp.logical_and(self.above, self.below)
        self.up = jnp.where(self.t == 1, 1, 0)
        self.ahead = 2 * self.up - 1
        self.sibling = (self.d, self.e + 1 - 2 * self.c)
        self.across = (self.d, lax.rem(self.e + 2, 4))
        self.corner = (self.d, 3 - self.e)
        self.beside = (self.t * spread + 1 - self.f, self.e)
        self.mates = [(self.d, self.e), self.sibling, self.across, self.corner]

    def block(self, i):
        return pick(i, [e for _, e in self.mates])

    def on_line(self, up):
        return (self.d + self.spread * (2 * up - 1), self.e)


def pick(index, values):
    out = values[-1]
    for n in range(len(values) - 2, -1, -1):
        out = jnp.where(index == n, values[n], out)
    return out


def greet(always, place):
    barrier = pltpu.get_barrier_semaphore()
    for device in always:
        pl.semaphore_signal(barrier, inc=1, device_id=device, device_id_type=MESH)
    for up, there in ((1, place.above), (0, place.below)):

        @pl.when(there)
        def _(up=up):
            pl.semaphore_signal(barrier, inc=1, device_id=place.on_line(up), device_id_type=MESH)

    ends = place.above.astype(jnp.int32) + place.below.astype(jnp.int32)
    pl.semaphore_wait(barrier, len(always) + ends)


def remote(src, dst, send, recv, device):
    return pltpu.make_async_remote_copy(
        src_ref=src, dst_ref=dst, send_sem=send, recv_sem=recv, device_id=device, device_id_type=MESH)


def dma(*shape):
    return pltpu.SemaphoreType.DMA(shape)


def along(place, body, start=0):
    if start == 0:
        body(place.t)

    def step(k, carry):
        for t in (place.t + k, place.t - k):

            @pl.when(jnp.logical_and(t >= 0, t < LINE))
            def _(t=t):
                body(t)

        return carry

    lax.fori_loop(1, LINE, step, 0)


class Rider:
    partners = ()

    def begin(self):
        pass

    def ready(self):
        pass

    def after_first(self):
        pass

    def after_line(self):
        pass

    def after_relay(self):
        pass

    def finish(self):
        pass


class Line:
    def __init__(self, place, x, part, stage, arrived, final, returned, sems):
        self.p = place
        self.x, self.part, self.stage, self.arrived = x, part, stage, arrived
        self.final, self.returned = final, returned
        (self.out_send, self.x_recv, self.x_send, self.sum_send, self.sum_recv, self.ret_send, self.ret_recv) = sems

    @staticmethod
    def scratch(local, width):
        shape = (local, 4, CAP, width)
        return [
            pltpu.VMEM((local, LINE, 4, CAP, width), BF16),
            pltpu.VMEM((LINE,) + shape, F32),
            pltpu.VMEM((LINE,) + shape, BF16),
            pltpu.VMEM((2, LINE) + shape, BF16),
            pltpu.VMEM((4, local, CAP, width), BF16),
            dma(4), dma(LINE, 4), dma(2, LINE, 4), dma(LINE, 4), dma(2, LINE, 4), dma(4), dma(4),
        ]

    def slot_copy(self, out, i):
        to, p = self.p.mates[i], self.p
        return remote(out.at[to[1]], self.x.at[:, p.t, p.e], self.out_send.at[i], self.x_recv.at[p.t, p.e], to)

    def x_copy(self, up, s, b):
        at = self.x.at[:, s, b]
        return remote(at, at, self.x_send.at[up, s, b], self.x_recv.at[s, b], self.p.on_line(up))

    def sum_copy(self, up, s, b):
        return remote(self.stage.at[s, :, b], self.arrived.at[up, s, :, b], self.sum_send.at[s, b],
                      self.sum_recv.at[up, s, b], self.p.on_line(up))

    def ret_copy(self, i, to_mate=True):
        to = self.p.block(i)
        row = self.p.e if to_mate else to
        return remote(self.final.at[to], self.returned.at[row], self.ret_send.at[i], self.ret_recv.at[row], (self.p.d, to))

    def send_sum(self, up, s, b, total):
        self.stage[s, :, b] = total.astype(BF16)
        self.sum_copy(up, s, b).start()

    def relay(self, n):
        p = self.p
        kind = pick(n, (0, 0, 1, 1, 2, 1, 2, 1, 2, 0, 2, 0))
        b = p.block(pick(n, (0, 1, 0, 1, 0, 2, 1, 3, 2, 2, 3, 3)))
        s = p.t + p.ahead * pick(kind, (1, 2, -1))
        way = jnp.where(kind == 2, 1 - p.up, p.up)

        @pl.when(p.inside)
        def _():
            self.sum_copy(way, s, b).wait_recv()
            self.send_sum(way, s, b, self.part[s, :, b] + self.arrived[way, s, :, b].astype(F32))

    def run(self, out, compute, kept, pieces, rider):
        p = self.p
        t, e = p.t, p.e
        blocks = [b for _, b in p.mates]
        greet(p.mates[1:] + list(rider.partners), p)
        for i in (2, 3, 1):
            self.slot_copy(out, i).start()
        self.x[:, t, e] = out[e]
        rider.begin()
        for i in range(4):
            if i:
                self.x_copy(0, t, blocks[i]).wait_recv()
            for up, there in ((0, p.below), (1, p.above)):

                @pl.when(there)
                def _(up=up, i=i):
                    self.x_copy(up, t, blocks[i]).start()

        rider.ready()

        def step(n, carry):
            k = jnp.where(n < 2, 1, jnp.where(jnp.logical_or(n == 2, n == 5), 2, 3))
            half = jnp.where(jnp.logical_or(n == 1, n >= 4), 1, 0)
            pair = p.y + half - 2 * p.y * half
            first = jnp.where(half == 0, blocks[0], blocks[2])
            second = jnp.where(half == 0, blocks[1], blocks[3])
            for b in (first, second):
                for up, there, onward, before_end in ((0, t + k < LINE, p.below, t == 1), (1, t - k >= 0, p.above, t == LINE - 2)):
                    s = t - k if up else t + k
                    put_off = jnp.logical_and(before_end, n == 1)

                    @pl.when(there)
                    def _(up=up, onward=onward, s=s, b=b, put_off=put_off):
                        self.x_copy(up, s, b).wait_recv()

                        @pl.when(jnp.logical_and(onward, jnp.logical_not(put_off)))
                        def _():
                            self.x_copy(up, s, b).start()

            for up, before_end in ((0, t == 1), (1, t == LINE - 2)):

                @pl.when(jnp.logical_and(before_end, n == 5))
                def _(up=up):
                    for b in (first, second):
                        self.x_copy(up, t - 1 if up else t + 1, b).start()

            @pl.when(jnp.logical_not(p.inside))
            def _():
                s = jnp.where(t == 0, k, LINE - 1 - k)
                compute(s, 2 * pair, 2)

                @pl.when(half == 1)
                def _():
                    kept(s)

            for up, starts, s in ((1, t == 0, k), (0, t == LINE - 1, LINE - 1 - k)):

                @pl.when(starts)
                def _(up=up, s=s):
                    for b in (first, second):
                        self.send_sum(up, s, b, self.part[s, :, b])

            rest = jnp.logical_and(p.inside, jnp.logical_or(n == 5, jnp.logical_and(n >= 1, n <= 2)))

            @pl.when(jnp.logical_or(n == 0, rest))
            def _():
                s = t + p.ahead * jnp.where(n == 0, 0, jnp.where(n == 1, 1, jnp.where(n == 2, -1, 2)))
                compute(s, 0, 4)
                kept(s)

            @pl.when(n == 0)
            def _():
                rider.after_first()

            return carry

        lax.fori_loop(0, 6, step, 0)
        rider.after_line()

        def passing(n, carry):
            self.relay(n)
            pieces(n)
            return carry

        lax.fori_loop(0, 12, passing, 0)
        rider.after_relay()

        def end(i, carry):
            b = p.block(i)
            for up, there in ((1, p.below), (0, p.above)):

                @pl.when(there)
                def _(up=up):
                    self.sum_copy(up, t, b).wait_recv()
                    self.part[t, :, b] = self.part[t, :, b] + self.arrived[up, t, :, b].astype(F32)

            self.final[b] = self.part[t, :, b].astype(BF16)

            @pl.when(i > 0)
            def _():
                self.ret_copy(i).start()

            return carry

        lax.fori_loop(0, 4, end, 0)
        self.returned[e] = self.final[e]

        def sent(n, carry):
            s, b = n // 4, lax.rem(n, 4)
            for up, mine in ((0, jnp.logical_and(p.below, s >= t)), (1, jnp.logical_and(p.above, s <= t))):

                @pl.when(mine)
                def _(up=up):
                    self.x_copy(up, s, b).wait_send()

            @pl.when(s != t)
            def _():
                self.sum_copy(0, s, b).wait_send()

            return carry

        for i in (1, 2, 3):
            self.slot_copy(out, i).wait_send()
        lax.fori_loop(0, 4 * LINE, sent, 0)
        rider.finish()
        for i in (1, 2, 3):
            self.ret_copy(i).wait_send()
            self.ret_copy(i, False).wait_recv()


def split(refs, *counts):
    out, at = [], 0
    for count in counts:
        out.append(refs[at : at + count])
        at += count
    return out + [refs[at:]]


def expert_forward_kernel(spread, parts, late, ride, out, *refs):
    weights_in, given, outs, late_out, whole, scratch, line_refs, sems, ride_refs = split(
        refs, 3 * parts, 8 if ride else 0, 4, late, 5 if ride else 0, 3 * parts, 5, 7)
    (g_all, u_all, keep_sem, load_sem, late_sem), ride_refs = ride_refs[:5], ride_refs[5:]
    returned, x_keep, g_keep, u_keep = outs
    gate, up, down = scratch[:parts], scratch[parts : 2 * parts], scratch[2 * parts :]
    x, part, stage, arrived, final = line_refs
    local, _, _, _, width = x.shape
    p = Place(spread)
    line = Line(p, x, part, stage, arrived, final, returned, sems)
    rider = WeightRider(p, given, whole, ride_refs) if ride else Rider()

    def load(i):
        given = weights_in[i].shape[0]
        return pltpu.make_async_copy(weights_in[i], scratch[i].at[0:given], load_sem.at[i])

    for i in range(3 * parts):
        load(i).start()

    def late_copy():
        return remote(weights_in[-2].at[1:local], scratch[-1].at[1:local], late_sem.at[0], late_sem.at[1], p.beside)

    def late_store():
        return pltpu.make_async_copy(scratch[-1], late_out[0], late_sem.at[2])

    def keep_x(s):
        return pltpu.make_async_copy(x.at[:, s], x_keep.at[:, s], keep_sem.at[0, s])

    def keep_g(s):
        return pltpu.make_async_copy(g_all.at[s], g_keep.at[s], keep_sem.at[1, s])

    def keep_u(s):
        return pltpu.make_async_copy(u_all.at[s], u_keep.at[s], keep_sem.at[2, s])

    def kept(s):
        keep_x(s).start()
        keep_g(s).start()
        keep_u(s).start()

    def compute(s, first, count):
        rows = count * CAP
        at = pl.multiple_of(first * CAP, CAP)

        def one(l, carry):
            rows_in = x[l, s, pl.ds(first, count)].reshape(rows, width)
            total = jnp.zeros((rows, width), F32)
            for q in range(parts):
                cols = gate[q].shape[2]
                here = slice(q * cols, (q + 1) * cols)
                g = dot_nn(rows_in, gate[q][l])
                u = dot_nn(rows_in, up[q][l])
                g_all[s, l, pl.ds(at, rows), here] = g
                u_all[s, l, pl.ds(at, rows), here] = u
                act = (g * jax.nn.sigmoid(g) * u).astype(BF16)
                total = total + dot_nn(act, down[q][l])
            part[s, l, pl.ds(first, count)] = total.reshape(count, CAP, width)
            return carry

        lax.fori_loop(0, local, one, 0)

    class Loaded(Rider):
        partners = [p.beside] if late else []
        after_first, after_line, after_relay = rider.after_first, rider.after_line, rider.after_relay

        def begin(self):
            if late:
                late_copy().start()
            rider.begin()

        def ready(self):
            for i in range(3 * parts):
                load(i).wait()
            if late:
                late_copy().wait_recv()
                late_store().start()

        def finish(self):
            rider.finish()
            if late:
                late_copy().wait_send()
                late_store().wait()

    line.run(out, compute, kept, lambda n: None, Loaded())
    for s in range(LINE):
        keep_x(s).wait()
        keep_g(s).wait()
        keep_u(s).wait()


def expert_backward_kernel(spread, parts, exchange, ride, out, *refs):
    loads_in, given, outs, came, ride_outs, loads, line_refs, sems, rest = split(
        refs, 3 + 3 * parts, 4 if ride else 0, 1 + 3 * parts - exchange, exchange, 3 if ride else 0, 3 + 3 * parts, 5, 7)
    (act_all, gg_all, gu_all), grads, (load_sem, grad_sem, w_send, w_recv), ride_refs = split(rest, 3, 3 * parts, 4)
    returned, grads_out = outs[0], list(outs[1:])
    if exchange:
        grads_out.insert(1, None)
    x_in, g_all, u_all = loads[:3]
    gate, up, down = loads[3 : 3 + parts], loads[3 + parts : 3 + 2 * parts], loads[3 + 2 * parts :]
    x, part, stage, arrived, final = line_refs
    local, _, _, _, width = x.shape
    p = Place(spread)
    line = Line(p, x, part, stage, arrived, final, returned, sems)
    rider = GradientRider(p, given, ride_outs, ride_refs) if ride else Rider()

    def load(i):
        return pltpu.make_async_copy(loads_in[i], loads[i], load_sem.at[i])

    def store(i, l):
        return pltpu.make_async_copy(grads[i].at[l], grads_out[i].at[l], grad_sem.at[i, l])

    for i in range(3 + 3 * parts):
        load(i).start()

    def compute(s, first, count):
        rows = count * CAP
        at = pl.multiple_of(first * CAP, CAP)
        into = pl.ds(pl.multiple_of((4 * s + first) * CAP, CAP), rows)

        def one(l, carry):
            rows_in = x[l, s, pl.ds(first, count)].reshape(rows, width)
            total = jnp.zeros((rows, width), F32)
            for q in range(parts):
                cols = gate[q].shape[2]
                here = slice(q * cols, (q + 1) * cols)
                g, u = g_all[s, l, pl.ds(at, rows), here], u_all[s, l, pl.ds(at, rows), here]
                g_act = dot_nt(rows_in, down[q][l])
                sigma = jax.nn.sigmoid(g)
                swish = g * sigma
                gg = (g_act * u * sigma * (1.0 + g * (1.0 - sigma))).astype(BF16)
                gu = (g_act * swish).astype(BF16)
                act_all[l, into, here] = (swish * u).astype(BF16)
                gg_all[l, into, here] = gg
                gu_all[l, into, here] = gu
                total = total + dot_nt(gg, gate[q][l]) + dot_nt(gu, up[q][l])
            part[s, l, pl.ds(first, count)] = total.reshape(count, CAP, width)
            return carry

        lax.fori_loop(0, local, one, 0)

    def weights(kind, l):
        x_rows, g_rows = (a[l].reshape(LINE * 4 * CAP, width) for a in (x_in, x))
        value = dot_tn(act_all[l], g_rows) if kind == 2 else dot_tn(x_rows, (gg_all, gu_all)[kind][l])
        for q in range(parts):
            i = kind * parts + q
            cols = gate[q].shape[2]
            here = slice(q * cols, (q + 1) * cols)
            grads[i][l] = (value[here] if kind == 2 else value[:, here]).astype(grads[i].dtype)
            if grads_out[i] is not None:
                store(i, l).start()

    def pieces(n):
        for kind in range(3):
            at = n - 1 - 2 * local * kind

            @pl.when(jnp.logical_and(lax.rem(n, 2) == 1, jnp.logical_and(at >= 0, at < 2 * local)))
            def _(kind=kind, at=at):
                weights(kind, at // 2)

        @pl.when(n == 2 * local - 1)
        def _():
            for copy in sent_gate():
                copy.start()

    def sent_gate():
        return [remote(grads[1], came[0], w_send.at[0], w_recv.at[0], p.beside)] if exchange else []

    class Loaded(Rider):
        partners = [p.beside] if exchange else []
        after_first, after_line, after_relay, finish = (
            rider.after_first, rider.after_line, rider.after_relay, rider.finish)

        def begin(self):
            rider.begin()

        def ready(self):
            for i in range(3 + 3 * parts):
                load(i).wait()

    line.run(out, compute, lambda s: None, pieces, Loaded())
    for copy in sent_gate():
        copy.wait()
    for i in range(3 * parts):
        for l in range(local if grads_out[i] is not None else 0):
            store(i, l).wait()


def remote_params(call_id):
    return pltpu.CompilerParams(collective_id=call_id, has_side_effects=True, vmem_limit_bytes=61 * 2**20)


def struct(shape, dtype):
    return jax.ShapeDtypeStruct(tuple(shape), dtype)


def expert_forward(spread, call_id, out, weights, late=False, ride=None):
    parts = len(weights) // 3
    _, local, cap, width = out.shape
    columns = sum(w.shape[2] for w in weights[:parts])
    kept = (LINE, local, 4 * cap, columns)
    outs = [struct(out.shape, BF16), struct((local, LINE, 4, cap, width), BF16), struct(kept, F32), struct(kept, F32)]
    outs += [struct(weights[-2].shape, BF16)] * late
    scratch = [pltpu.VMEM((local,) + w.shape[1:], BF16) for w in weights] + Line.scratch(local, width)
    scratch += [pltpu.VMEM(kept, F32), pltpu.VMEM(kept, F32), dma(3, LINE), dma(3 * parts), dma(3)]
    more = ride or ()
    count = LINE * spread
    if ride:
        outs += [struct((count * s.shape[0], s.shape[1]), BF16) for s in ride[3:6]]
        outs += [struct(w.shape, BF16) for w in ride[6:]]
        scratch += WeightRider.scratch(count)
    return pl.pallas_call(
        functools.partial(expert_forward_kernel, spread, parts, int(late), ride is not None),
        out_shape=outs,
        in_specs=[VMEM] + [ANY] * (len(weights) + len(more)),
        out_specs=[VMEM] + [ANY] * (len(outs) - 1),
        scratch_shapes=scratch,
        compiler_params=remote_params(call_id),
        cost_estimate=pl.CostEstimate(flops=2 * 10**10, bytes_accessed=2 * 10**8, transcendentals=0),
    )(out, *weights, *more)


def expert_backward(spread, call_id, out, kept, weights, exchange=False, ride=None):
    parts = len(weights) // 3
    _, local, cap, width = out.shape
    columns = sum(w.shape[2] for w in weights[:parts])
    loads = list(kept) + list(weights)
    grads = [(w.shape, F32 if i % parts == 0 else BF16) for i, w in enumerate(weights)]
    wide = pltpu.VMEM((local, LINE * 4 * cap, columns), BF16)
    outs = [struct(out.shape, BF16)] + [struct(*g) for i, g in enumerate(grads) if not exchange or i != 1]
    if exchange:
        outs.append(struct(*grads[1]))
    specs = [VMEM] + [ANY] * len(grads)
    scratch = [pltpu.VMEM(a.shape, a.dtype) for a in loads] + Line.scratch(local, width)
    scratch += [wide] * 3 + [pltpu.VMEM(*g) for g in grads] + [dma(len(loads)), dma(len(grads), local), dma(1), dma(1)]
    more = ride or ()
    if ride:
        depths = [g.shape[0] // (LINE * spread) for g in ride[:2]]
        outs.append(struct((LINE, spread, sum(depths) // 2, width // 2), F32))
        outs += [struct(g.shape, BF16) for g in ride[2:]]
        specs += [VMEM, ANY, ANY]
        scratch += GradientRider.scratch(spread, depths, width)
    return pl.pallas_call(
        functools.partial(expert_backward_kernel, spread, parts, int(exchange), ride is not None),
        out_shape=outs,
        in_specs=[VMEM] + [ANY] * (len(loads) + len(more)),
        out_specs=specs,
        scratch_shapes=scratch,
        compiler_params=remote_params(call_id),
        cost_estimate=pl.CostEstimate(flops=4 * 10**10, bytes_accessed=2 * 10**8, transcendentals=0),
    )(out, *loads, *more)


def from_partner(array, shift, spread, groups):
    pairs = [
        (t * spread + (f + shift) % spread, t * spread + f) for t in range(groups) for f in range(spread)
    ]
    return lax.ppermute(array, "dp", pairs)


def to_partner(array, shift, spread, groups):
    pairs = [
        (t * spread + f, t * spread + (f + shift) % spread) for t in range(groups) for f in range(spread)
    ]
    return lax.ppermute(array, "dp", pairs)


def pair_weights(shard, axis, spread):
    parts = [shard] + [from_partner(shard, i, spread, LINE) for i in range(1, spread)]
    if shard.shape[axis] % 128:
        return [jnp.concatenate(parts, axis=axis)]
    return parts


def pair_sum(parts, axis, spread):
    if len(parts) == 1 and spread > 1:
        parts = jnp.split(parts[0], spread, axis=axis)
    total = parts[0]
    for i in range(1, spread):
        total = total + to_partner(parts[i].astype(BF16), i, spread, LINE).astype(F32)
    return total


class LineGather:
    def __init__(self, place, pairs, shards, quarters, sems):
        self.p, self.shards, self.quarters = place, shards, quarters
        self.send, self.recv, self.x_send, self.x_recv = sems
        self.columns = [place.f, 1 - place.f] if pairs else [0]

    @staticmethod
    def shapes(shards, columns):
        (a, wide), (b, _), (c, narrow) = shards
        return [(LINE, columns, a // 2, wide // 2), (LINE, columns, b // 2, wide // 2), (LINE, columns, c, narrow)]

    @staticmethod
    def scratch(columns):
        return [dma(2, LINE, columns, 3), dma(LINE, columns, 3), dma(3), dma(3)]

    def copy(self, kind, up, t, f):
        at = self.quarters[kind].at[t, f]
        return remote(at, at, self.send.at[up, t, f, kind], self.recv.at[t, f, kind], self.p.on_line(up))

    def x_copy(self, kind, f):
        at = self.quarters[kind].at[self.p.t, f]
        return remote(at, at, self.x_send.at[kind], self.x_recv.at[kind], self.p.beside)

    def both_ways(self, f):
        p = self.p
        for up, there in ((0, p.below), (1, p.above)):

            @pl.when(there)
            def _(up=up):
                for kind in range(3):
                    self.copy(kind, up, p.t, f).start()

    def begin(self):
        p, f = self.p, self.columns[0]
        for kind in (0, 1):
            half, wide = self.quarters[kind].shape[2:]
            self.quarters[kind][p.t, f] = self.shards[kind][
                pl.ds(pl.multiple_of(p.y * half, 16), half), pl.ds(pl.multiple_of(p.c * wide, 128), wide)]
        self.quarters[2][p.t, f] = self.shards[2][...]
        for kind in range(3 if len(self.columns) == 2 else 0):
            self.x_copy(kind, f).start()
        self.both_ways(f)

    def beside(self, then):
        for f in self.columns[1:]:
            for kind in range(3):
                self.x_copy(kind, f).wait_recv()
            self.both_ways(f)
            then(self.p.t, f)

    def step(self, k, then):
        p = self.p
        for f in self.columns:
            for up, there, onward in ((0, p.t + k < LINE, p.below), (1, p.t - k >= 0, p.above)):
                t = p.t - k if up else p.t + k

                @pl.when(there)
                def _(up=up, onward=onward, t=t, f=f):
                    for kind in range(3):
                        self.copy(kind, up, t, f).wait_recv()

                    @pl.when(onward)
                    def _():
                        for kind in range(3):
                            self.copy(kind, up, t, f).start()

                    then(t, f)

    def finish(self):
        p = self.p

        def line(t, carry):
            for up, mine in ((0, jnp.logical_and(p.below, t >= p.t)), (1, jnp.logical_and(p.above, t <= p.t))):

                @pl.when(mine)
                def _(up=up):
                    for f in self.columns:
                        for kind in range(3):
                            self.copy(kind, up, t, f).wait_send()

            return carry

        lax.fori_loop(0, LINE, line, 0)
        for f in self.columns[1:]:
            for kind in range(3):
                self.x_copy(kind, 1 - f).wait_send()


class Spread:
    def __init__(self, place, quarters, shards, whole, sems):
        self.p, self.quarters, self.shards, self.whole = place, quarters, shards, whole
        self.y_send, self.y_recv, self.c_send, self.c_recv, self.l_sem, self.s_sem = sems

    @staticmethod
    def scratch(count):
        return [dma(count, 2), dma(count, 2), dma(count, 2, 2), dma(count, 2, 2), dma(count, 3), dma(3)]

    def region(self, kind, s, y, c):
        depth = self.shards[kind].shape[0]
        if kind == 2:
            return self.whole[2].at[pl.ds(pl.multiple_of(s * depth, 16), depth)]
        half, wide = depth // 2, self.shards[kind].shape[1] // 2
        return self.whole[kind].at[
            pl.ds(pl.multiple_of(s * depth + y * half, 16), half), pl.ds(pl.multiple_of(c * wide, 128), wide)]

    def mine(self, kind, s):
        return self.region(kind, s, self.p.y, self.p.c)

    def y_copy(self, kind, src, s):
        return remote(src, self.mine(kind, s), self.y_send.at[s, kind], self.y_recv.at[s, kind], self.p.across)

    def y_came(self, kind, s):
        at = self.region(kind, s, 1 - self.p.y, self.p.c)
        return remote(at, at, self.y_send.at[s, kind], self.y_recv.at[s, kind], self.p.across)

    def c_copy(self, kind, src, s, y):
        return remote(src, self.region(kind, s, y, self.p.c), self.c_send.at[s, y, kind], self.c_recv.at[s, y, kind],
                      self.p.sibling)

    def c_came(self, kind, s, y):
        at = self.region(kind, s, y, 1 - self.p.c)
        return remote(at, at, self.c_send.at[s, y, kind], self.c_recv.at[s, y, kind], self.p.sibling)

    def local(self, kind, src, s):
        return pltpu.make_async_copy(src, self.mine(kind, s), self.l_sem.at[s, kind])

    def shard(self, kind):
        depth = self.shards[kind].shape[0]
        at = self.whole[kind].at[pl.ds(pl.multiple_of(self.p.d * depth, 16), depth)]
        return pltpu.make_async_copy(self.shards[kind], at, self.s_sem.at[kind])

    def own_shard(self):
        for kind in range(3):
            self.shard(kind).start()

    def push(self, s, sources, here=True):
        if here:
            for kind in range(3):
                self.local(kind, sources[kind], s).start()
        for kind in (0, 1):
            self.y_copy(kind, sources[kind], s).start()
            self.c_copy(kind, sources[kind], s, self.p.y).start()

    def across(self, s):
        for kind in (0, 1):
            self.y_came(kind, s).wait_recv()
            self.c_copy(kind, self.region(kind, s, 1 - self.p.y, self.p.c), s, 1 - self.p.y).start()

    def finish_shard(self, s, here=True):
        @pl.when(s != self.p.d)
        def _():
            for kind in range(3 if here else 0):
                self.local(kind, self.mine(kind, s), s).wait()
            for kind in (0, 1):
                self.y_came(kind, s).wait_send()
                for y in (0, 1):
                    self.c_came(kind, s, y).wait_send()
                    self.c_came(kind, s, y).wait_recv()

    def finish_own(self):
        for kind in range(3):
            self.shard(kind).wait()


class WeightRider:
    def __init__(self, place, given, whole, sems):
        self.p, self.quarters, self.own, self.other = place, given[:3], given[6:], whole[3:]
        self.w_send, self.w_recv, self.x_send, self.x_recv, *more = sems
        self.spread = Spread(place, self.quarters, given[3:6], whole[:3], more)

    @staticmethod
    def scratch(count):
        return [dma(2), dma(2), dma(LINE, 3), dma(LINE, 3)] + Spread.scratch(count)

    def place_of(self, t):
        return t * self.p.spread + self.p.f

    def beside_of(self, t):
        return t * self.p.spread + 1 - self.p.f

    def x_copy(self, kind, t, s):
        return remote(self.quarters[kind].at[t, 0], self.spread.mine(kind, s), self.x_send.at[t, kind],
                      self.x_recv.at[t, kind], self.p.beside)

    def weight(self, i):
        return remote(self.own[i], self.other[i], self.w_send.at[i], self.w_recv.at[i], self.p.beside)

    def begin(self):
        self.spread.own_shard()

        def body(t):
            for kind in range(3):
                self.x_copy(kind, t, self.place_of(t)).start()

            @pl.when(t != self.p.t)
            def _():
                self.spread.push(self.place_of(t), [q.at[t, 0] for q in self.quarters])

        along(self.p, body)
        for i in range(2):
            self.weight(i).start()

    def after_first(self):
        pass

    def after_line(self):
        def body(t):
            s = self.beside_of(t)
            for kind in range(3):
                self.x_copy(kind, t, s).wait_recv()
            self.spread.push(s, [self.spread.mine(kind, s) for kind in range(3)], here=False)

        along(self.p, body)

    def after_relay(self):
        along(self.p, lambda t: self.spread.across(self.place_of(t)), start=1)
        along(self.p, lambda t: self.spread.across(self.beside_of(t)))

    def finish(self):
        self.spread.finish_own()
        for i in range(2):
            self.weight(i).wait()

        def line(t, carry):
            for kind in range(3):
                self.x_copy(kind, t, self.place_of(t)).wait_send()
            self.spread.finish_shard(self.place_of(t))
            self.spread.finish_shard(self.beside_of(t), here=False)
            return carry

        lax.fori_loop(0, LINE, line, 0)


def pack_small(l, router, const, gains, vectors, rows, small):
    rows[...] = jnp.zeros(rows.shape, F32)
    for r in range(router.shape[0]):
        rows[r : r + 1, :] = router[r, l : l + 1, :]
    for j in (0, 1):
        rows[CONST0 + 2 * j : CONST0 + 2 * j + 2, :] = const[l, j]
    rows[GAIN0 : GAIN0 + 2, :] = gains[l]
    rows[VECTOR0 : VECTOR0 + 2, :] = vectors[l]
    place = lax.broadcasted_iota(jnp.int32, (rows.shape[0], 128), 0) == lanes(rows.shape[0])
    small[l] = dot_tn(rows[...].astype(BF16), place.astype(BF16)).astype(BF16)


def dense_gather_kernel(spread, qkv_wide, out_wide, router, const, gains, vectors, routes, *refs):
    p = Place(spread)
    wide, whole, quarters1, (routes_all,), own, firsts, partner, shards1_out, quarters0, loaded, rounded, shards, (rows,), rest = split(
        refs, 3, 3, 3, 1, 6, 2, 2, 3, 3, 3, 3, 3, 1)
    qkv, out, small = shards
    sems0, sems1, (r_send, r_recv, w_send, w_recv, load_sem, own_sem, first_sem, shard_sem), spread_sems = split(rest, 4, 4, 8)
    shards0, shards1 = ([ref.at[l] for ref in (qkv, out, small)] for l in (0, 1))
    line0 = LineGather(p, True, shards0, quarters0, sems0)
    line1 = LineGather(p, False, shards1, quarters1, sems1)
    spreading = Spread(p, quarters0, shards0, whole, spread_sems)

    def load(l, kind):
        return pltpu.make_async_copy(wide[kind].at[l], loaded[kind].at[l], load_sem.at[l, kind])

    def store(l, kind):
        return pltpu.make_async_copy(rounded[kind].at[l], own[3 * l + kind], own_sem.at[l, kind])

    def first(l):
        return pltpu.make_async_copy(rounded[2].at[l, 0:1], firsts[l], first_sem.at[l])

    def weight(kind):
        return remote(rounded[kind].at[0], partner[kind], w_send.at[kind], w_recv.at[kind], p.beside)

    def round_weights(l, kind):
        load(l, kind).wait()

        def one(i, carry):
            rounded[kind][l, i] = loaded[kind][l, i].astype(BF16)
            return carry

        lax.fori_loop(0, rounded[kind].shape[1], one, 0)
        store(l, kind).start()
        if kind == 2:
            first(l).start()

    def shard1(kind):
        return pltpu.make_async_copy(shards[kind].at[1], shards1_out[kind], shard_sem.at[kind])

    for l in (0, 1):
        for kind in range(3):
            load(l, kind).start()
    for l in (0, 1):
        qkv[l], out[l] = qkv_wide[l].astype(BF16), out_wide[l].astype(BF16)
        pack_small(l, router, const, gains, vectors, rows, small)
    for kind in range(3):
        shard1(kind).start()
    greet(p.mates[1:] + [p.beside], p)

    def route_copy(i, row):
        return remote(routes, routes_all.at[row], r_send.at[i], r_recv.at[row], p.mates[i])

    def push(t, f):
        spreading.push(t * spread + f, [q.at[t, f] for q in quarters0])

    line0.begin()
    for kind in (0, 1):
        round_weights(0, kind)
        weight(kind).start()
    routes_all[p.e] = routes[...]
    for i in (1, 2, 3):
        route_copy(i, p.e).start()
    spreading.own_shard()
    line0.beside(push)
    line1.begin()
    lax.fori_loop(1, LINE, lambda k, carry: (line0.step(k, push), carry)[1], 0)
    round_weights(0, 2)
    lax.fori_loop(1, LINE, lambda k, carry: (line1.step(k, lambda t, f: None), carry)[1], 0)
    for kind in range(3):
        round_weights(1, kind)
    along(p, lambda t: spreading.across(t * spread + p.f), start=1)
    along(p, lambda t: spreading.across(t * spread + 1 - p.f))
    spreading.finish_own()
    lax.fori_loop(0, LINE * spread, lambda s, carry: (spreading.finish_shard(s), carry)[1], 0)
    line0.finish()
    line1.finish()
    for l in (0, 1):
        for kind in range(3):
            store(l, kind).wait()
        first(l).wait()
    for kind in (0, 1):
        weight(kind).wait()
    for kind in range(3):
        shard1(kind).wait()
    for i in (1, 2, 3):
        route_copy(i, p.e).wait_send()
        route_copy(i, p.mates[i][1]).wait_recv()


def dense_gather(spread, call_id, arrays, routes, wide):
    count = spread * LINE
    layers, depth = arrays[1].shape[:2]
    shards = [arrays[0].shape[1:], arrays[1].shape[1:], (depth, 128)]
    pairs, single = LineGather.shapes(shards, 2), LineGather.shapes(shards, 1)
    outs = [struct((count * rows, width), BF16) for rows, width in shards]
    outs += [struct(q, BF16) for q in single] + [struct((4,) + routes.shape, routes.dtype)]
    outs += [struct(w.shape[1:], BF16) for w in wide] * 2 + [struct((1,) + wide[2].shape[2:], BF16)] * 2
    outs += [struct(w.shape[1:], BF16) for w in wide[:2]] + [struct(s, BF16) for s in shards]
    scratch = [pltpu.VMEM(q, BF16) for q in pairs] + [pltpu.VMEM(w.shape, F32) for w in wide]
    scratch += [pltpu.VMEM(w.shape, BF16) for w in wide] + [pltpu.VMEM((layers,) + s, BF16) for s in shards]
    scratch += [pltpu.VMEM((32, depth), F32)] + LineGather.scratch(2) + LineGather.scratch(1)
    scratch += [dma(4), dma(4), dma(2), dma(2), dma(2, 3), dma(2, 3), dma(2), dma(3)]
    return pl.pallas_call(
        functools.partial(dense_gather_kernel, spread),
        out_shape=outs,
        in_specs=[VMEM] * (len(arrays) + 1) + [ANY] * 3,
        out_specs=[ANY] * 3 + [VMEM] * 4 + [ANY] * 13,
        scratch_shapes=scratch + Spread.scratch(count),
        compiler_params=remote_params(call_id),
        cost_estimate=pl.CostEstimate(flops=10**10, bytes_accessed=10**8, transcendentals=0),
    )(*arrays, routes, *wide)


class Halve:
    def __init__(self, place, grads, quarter, scratch):
        self.p, self.grads, self.quarter = place, grads, quarter
        (self.mine, self.core, self.stage, self.came, self.l_sem, self.a_send, self.a_recv, self.y_send,
         self.y_recv) = scratch
        self.depths = [g.shape[0] // (LINE * place.spread) for g in grads]
        self.wide = grads[0].shape[1] // 2

    @staticmethod
    def scratch(spread, depths, width):
        count, rows, wide = LINE * spread, sum(depths) // 2, width // 2
        half = pltpu.VMEM((LINE, spread, rows, wide), BF16)
        everything = pltpu.VMEM((count * sum(depths), wide), BF16)
        return [everything, everything, half, half, dma(2), dma(2), dma(2), dma(LINE), dma(LINE)]

    def rows_of(self, kind):
        first = 0 if kind == 0 else self.grads[0].shape[0]
        return slice(first, first + self.grads[kind].shape[0])

    def lanes(self, c):
        return pl.ds(pl.multiple_of(c * self.wide, 128), self.wide)

    def local(self, kind):
        return pltpu.make_async_copy(
            self.grads[kind].at[:, self.lanes(self.p.c)], self.mine.at[self.rows_of(kind)], self.l_sem.at[kind])

    def a_copy(self, kind):
        return remote(self.grads[kind].at[:, self.lanes(1 - self.p.c)], self.core.at[self.rows_of(kind)],
                      self.a_send.at[kind], self.a_recv.at[kind], self.p.sibling)

    def y_copy(self, t):
        return remote(self.stage.at[t], self.came.at[t], self.y_send.at[t], self.y_recv.at[t], self.p.across)

    def pieces(self, t, f, y):
        s, row = t * self.p.spread + f, 0
        for kind, depth in enumerate(self.depths):
            at = self.rows_of(kind).start + s * depth + y * (depth // 2)
            here = pl.ds(pl.multiple_of(at, 16), depth // 2)
            yield slice(row, row + depth // 2), self.mine[here, :].astype(F32) + self.core[here, :].astype(F32)
            row += depth // 2

    def order(self, i):
        t = self.p.t
        down = LINE - 1 - i - jnp.where(LINE - 1 - i <= t, 1, 0)
        up = i + jnp.where(i >= t, 1, 0)
        return jnp.where(i == LINE - 1, t, jnp.where(t >= LINE // 2, up, down))

    def begin(self):
        for kind in (0, 1):
            self.a_copy(kind).start()
            self.local(kind).start()

    def after_first(self):
        for kind in (0, 1):
            self.a_copy(kind).wait_recv()
            self.local(kind).wait()

        def body(i, carry):
            t = self.order(i)
            for f in range(self.p.spread):
                for where, value in self.pieces(t, f, 1 - self.p.y):
                    self.stage[t, f, where] = value.astype(BF16)
            self.y_copy(t).start()
            return carry

        lax.fori_loop(0, LINE, body, 0)

        def own(t, carry):
            for f in range(self.p.spread):
                for where, value in self.pieces(t, f, self.p.y):
                    self.quarter[t, f, where] = value
            return carry

        lax.fori_loop(0, LINE, own, 0)

    def add(self, t):
        self.y_copy(t).wait_recv()
        self.quarter[t] = self.quarter[t] + self.came[t].astype(F32)

    def after_relay(self):
        lax.fori_loop(0, LINE, lambda i, carry: (self.add(self.order(i)), carry)[1], 0)

    def finish(self):
        for kind in (0, 1):
            self.a_copy(kind).wait_send()
        lax.fori_loop(0, LINE, lambda t, carry: (self.y_copy(t).wait_send(), carry)[1], 0)


class GradientRider:
    def __init__(self, place, given, outs, scratch):
        self.halve = Halve(place, given[:2], outs[0], scratch[:9])
        self.own, self.other = given[2:], outs[1:]
        self.p = place
        self.w_send, self.w_recv = scratch[9:]

    @staticmethod
    def scratch(spread, depths, width):
        return Halve.scratch(spread, depths, width) + [dma(2), dma(2)]

    def weight(self, i):
        return remote(self.own[i], self.other[i], self.w_send.at[i], self.w_recv.at[i], self.p.beside)

    def begin(self):
        self.halve.begin()
        for i in range(2):
            self.weight(i).start()

    def after_first(self):
        self.halve.after_first()

    def after_line(self):
        pass

    def after_relay(self):
        self.halve.after_relay()

    def finish(self):
        self.halve.finish()
        for i in range(2):
            self.weight(i).wait()


class LineSum:
    def __init__(self, place, depths, quarter, sums, scratch):
        self.p, self.depths, self.quarter, self.sums = place, depths, quarter, sums
        (self.stage, self.came, self.stage_x, self.came_x, self.z_send, self.z_recv, self.x_send, self.x_recv,
         self.e_send, self.e_recv) = scratch
        self.wide = sums[0].shape[1] // 2

    @staticmethod
    def scratch(spread, depths, width):
        rows, wide = sum(depths) // 2, width // 2
        return [
            pltpu.VMEM((LINE, spread, rows, wide), BF16),
            pltpu.VMEM((2, LINE, spread, rows, wide), BF16),
            pltpu.VMEM((rows, wide), BF16),
            pltpu.VMEM((rows, wide), BF16),
            dma(LINE), dma(2, LINE), dma(1), dma(1), dma(3, 2), dma(3, 2),
        ]

    def lanes(self, c):
        return pl.ds(pl.multiple_of(c * self.wide, 128), self.wide)

    def z_copy(self, up, t):
        return remote(self.stage.at[t], self.came.at[up, t], self.z_send.at[t], self.z_recv.at[up, t], self.p.on_line(up))

    def x_copy(self):
        return remote(self.stage_x, self.came_x, self.x_send.at[0], self.x_recv.at[0], self.p.beside)

    def e_copy(self, i, kind, y, c):
        half = self.depths[kind] // 2
        at = self.sums[kind].at[pl.ds(pl.multiple_of(y * half, 8), half), self.lanes(c)]
        return remote(at, at, self.e_send.at[i, kind], self.e_recv.at[i, kind], self.p.across if i == 0 else self.p.sibling)

    def start(self, t):
        p = self.p
        for up, mine in ((1, jnp.logical_and(p.t == 0, t > 0)), (0, jnp.logical_and(p.t == LINE - 1, t < LINE - 1))):

            @pl.when(mine)
            def _(up=up):
                self.stage[t] = self.quarter[t].astype(BF16)
                self.z_copy(up, t).start()

    def relay(self, kind):
        p = self.p

        @pl.when(p.inside)
        def _():
            t = {"near": p.t + p.ahead, "far": p.t + 2 * p.ahead, "back": p.t - p.ahead}[kind]
            way = 1 - p.up if kind == "back" else p.up
            self.z_copy(way, t).wait_recv()
            self.stage[t] = (self.quarter[t] + self.came[way, t].astype(F32)).astype(BF16)
            self.z_copy(way, t).start()

    def after_z(self):
        p = self.p

        for up, there in ((1, p.below), (0, p.above)):

            @pl.when(there)
            def _(up=up):
                self.z_copy(up, p.t).wait_recv()
                self.quarter[p.t] = self.quarter[p.t] + self.came[up, p.t].astype(F32)

        self.stage_x[...] = self.quarter[p.t, 1 - p.f].astype(BF16)
        self.x_copy().start()

    def after_x(self):
        p = self.p
        self.x_copy().wait_recv()
        row = 0
        for kind, depth in enumerate(self.depths):
            half = depth // 2
            value = self.quarter[p.t, p.f, row : row + half] + self.came_x[row : row + half].astype(F32)
            self.sums[kind][pl.ds(pl.multiple_of(p.y * half, 8), half), self.lanes(p.c)] = value
            row += half
        for i in (0, 1):
            for kind in (0, 1):
                self.e_copy(i, kind, p.y, p.c).start()

    def finish(self):
        p = self.p
        for kind in (0, 1):
            self.e_copy(0, kind, 1 - p.y, p.c).wait_recv()
            self.e_copy(2, kind, 1 - p.y, p.c).start()
        for kind in (0, 1):
            self.e_copy(0, kind, p.y, p.c).wait_send()
            self.e_copy(1, kind, p.y, p.c).wait_send()
            self.e_copy(1, kind, p.y, 1 - p.c).wait_recv()
            self.e_copy(2, kind, 1 - p.y, p.c).wait_send()
            self.e_copy(2, kind, 1 - p.y, 1 - p.c).wait_recv()
        self.x_copy().wait_send()

        def body(t, carry):
            @pl.when(t != p.t)
            def _():
                self.z_copy(0, t).wait_send()

            return carry

        lax.fori_loop(0, LINE, body, 0)


class SmallSum:
    def __init__(self, place, grads, total, scratch):
        self.p, self.grads, self.total = place, grads, total
        self.stage, self.came, self.send, self.recv = scratch
        p = place
        near = (p.d + p.spread - 2 * p.spread * lax.rem(p.t, 2), p.e)
        self.far = (lax.rem(p.d + 2 * p.spread, LINE * p.spread), p.e)
        self.partners = [p.sibling, p.across, near, self.far, p.beside]

    @staticmethod
    def scratch(rows, width):
        half = pltpu.VMEM((5, rows, width // 2), F32)
        return [half, half, dma(6), dma(6)]

    def lanes(self, c):
        wide = self.grads.shape[1] // 2
        return pl.ds(pl.multiple_of(c * wide, 128), wide)

    def copy(self, i):
        src = self.grads.at[:, self.lanes(1 - self.p.c)] if i == 0 else self.stage.at[i]
        return remote(src, self.came.at[i], self.send.at[i], self.recv.at[i], self.partners[i])

    def last(self, c):
        at = self.total.at[:, self.lanes(c)]
        return remote(at, at, self.send.at[5], self.recv.at[5], self.p.sibling)

    def step(self, i):
        if i == 0:
            self.copy(0).start()
            return
        self.copy(i - 1).wait_recv()
        mine = self.grads[:, self.lanes(self.p.c)] if i == 1 else self.stage[i - 1]
        value = mine + self.came[i - 1]
        if i < 5:
            self.stage[i] = value
            self.copy(i).start()
        else:
            self.total[:, self.lanes(self.p.c)] = value
            self.last(self.p.c).start()

    def finish(self):
        for i in range(5):
            self.copy(i).wait_send()
        self.last(self.p.c).wait_send()
        self.last(1 - self.p.c).wait_recv()


def dense_reduce_kernel(spread, depths, small0, small1, res, qkv0, out0, quarter1, up0, down0, small_sum, *refs):
    p = Place(spread)
    sums, came, (small, mine0, mine1), (w_send, w_recv), halve_refs, line0, line1, small_refs = split(refs, 2, 2, 3, 2, 9, 10, 10)
    sums0, sums1 = ([ref.at[l] for ref in sums] for l in (0, 1))
    halve = Halve(p, (qkv0, out0), mine0, halve_refs)
    sum0 = LineSum(p, depths, mine0, sums0, line0)
    sum1 = LineSum(p, depths, mine1, sums1, line1)
    little = SmallSum(p, small, small_sum, small_refs)
    weights = [remote(w, came[i], w_send.at[i], w_recv.at[i], p.beside) for i, w in enumerate((up0, down0))]
    greet([p.sibling, p.across, p.beside, little.far], p)
    halve.begin()
    for copy in weights:
        copy.start()
    rows = small0.shape[0]
    small[0:rows, :] = small0[...]
    small[rows : 2 * rows, :] = small1[...]
    small[2 * rows :, :] = jnp.zeros((16, small.shape[1]), F32)
    small[2 * rows :, 0:128] = res[0:16, :]
    little.step(0)
    mine1[...] = quarter1[...]
    for i in range(LINE):
        sum1.start(halve.order(i))
    little.step(1)
    halve.after_first()
    little.step(2)

    def arrive(i):
        halve.add(halve.order(i))
        sum0.start(halve.order(i))

    sum1.relay("far")
    sum1.relay("near")
    arrive(0)
    little.step(3)
    sum1.relay("back")
    arrive(1)
    sum0.relay("far")
    sum1.after_z()
    arrive(2)
    sum0.relay("near")
    sum0.relay("back")
    arrive(3)
    little.step(4)
    sum0.after_z()
    sum1.after_x()
    little.step(5)
    sum0.after_x()
    sum1.finish()
    halve.finish()
    little.finish()
    sum0.finish()
    for copy in weights:
        copy.wait()


def dense_reduce(spread, call_id, smalls, grads0, quarter1, weights0):
    count = LINE * spread
    depths = [g.shape[0] // count for g in grads0]
    width = grads0[0].shape[1]
    small = (2 * smalls[0].shape[0] + 16, width)
    line = LineSum.scratch(spread, depths, width)
    mine = pltpu.VMEM(quarter1.shape, F32)
    scratch = [pltpu.VMEM(small, F32), mine, mine, dma(2), dma(2)] + Halve.scratch(spread, depths, width) + line + line
    return pl.pallas_call(
        functools.partial(dense_reduce_kernel, spread, depths),
        out_shape=[struct(small, F32)] + [struct((2, depth, width), F32) for depth in depths]
        + [struct(w.shape, BF16) for w in weights0],
        in_specs=[VMEM] * 3 + [ANY, ANY, VMEM, ANY, ANY],
        out_specs=[VMEM] * 3 + [ANY] * 2,
        scratch_shapes=scratch + SmallSum.scratch(*small),
        compiler_params=remote_params(call_id),
        cost_estimate=pl.CostEstimate(flops=2 * 10**10, bytes_accessed=2 * 10**8, transcendentals=0),
    )(*smalls, *grads0, quarter1, *weights0)


def stack_kernel(qkv, out, *refs):
    parts, (qkv_out, out_out, *stacked) = refs[:12], refs[12:]
    qkv_out[...], out_out[...] = qkv[...], out[...]
    for kind, ref in enumerate(stacked):
        for l in (0, 1):
            mine, came = parts[4 * kind + 2 * l], parts[4 * kind + 2 * l + 1]
            ref[l] = mine[...] + came[...].astype(F32)


def stack_results(qkv, out, parts):
    flat = [part for kind in parts for layer in kind for part in layer]
    local, steps = flat[0].shape[0], 2

    def rows_of(shape, lead):
        block = (shape[0] if lead else 1, *((1,) if lead else ()), shape[-2] // steps, shape[-1])
        if lead:
            return pl.BlockSpec(block, lambda l, n: (0, l, n, 0))
        return pl.BlockSpec(block, lambda l, n: (l, n, 0))

    stacked = [(2,) + kind[0][0].shape for kind in parts]
    return pl.pallas_call(
        stack_kernel,
        out_shape=[struct(a.shape, F32) for a in (qkv, out)] + [struct(s, F32) for s in stacked],
        grid=(local, steps),
        in_specs=[rows_of(a.shape, False) for a in (qkv, out, *flat)],
        out_specs=[rows_of(a.shape, False) for a in (qkv, out)] + [rows_of(s, True) for s in stacked],
        compiler_params=pltpu.CompilerParams(vmem_limit_bytes=60 * 2**20),
        cost_estimate=pl.CostEstimate(flops=10**7, bytes_accessed=3 * 10**7, transcendentals=0),
    )(qkv, out, *flat)


def per_device(
    tokens, seq_lengths, block_perm, routes, norm_gains, w_qkv, w_out, w_router, w_residual, w_const, v_const,
    w_gate, w_up, w_down, cotangent,
):
    rows, width = tokens.shape
    owners = lax.axis_size("expert")
    shards = lax.axis_size("dp")
    spread = shards // LINE
    local = w_gate.shape[1]
    experts = local * owners
    layers = routes.shape[0]
    slots = experts * CAP

    packed_routes = jnp.zeros((8, -(-rows // 128) * 128), jnp.int32).at[: 2 * layers, :rows].set(
        jnp.swapaxes(routes, 1, 2).reshape(2 * layers, rows))

    depth = w_out.shape[1]
    qkv_t = jnp.swapaxes(w_qkv, 1, 2)
    in_kernels = spread == 2 and owners == 4 and layers == local == 2 and qkv_t.shape[1] % 32 == 0 and depth % 32 == 0
    if in_kernels:
        arrays = (qkv_t, w_out, jnp.transpose(w_router, (2, 0, 1)), jnp.swapaxes(w_const, 2, 3), norm_gains, v_const)
        *gathered, routes_all, g0, u0, d0, g1, u1, d1, first0, first1, gate, up, qkv1_own, out1_own, small1_own = dense_gather(
            spread, 4, arrays, packed_routes, (w_gate, w_up, w_down))
        weights = [[g0, gate, u0, up, d0, from_partner(first0, 1, spread, LINE)]]
        dense = [(gathered[2], gathered[0], gathered[1])]
    else:
        weights = []
        for l in range(layers):
            own = [(w_gate[l].astype(BF16), 2), (w_up[l].astype(BF16), 2), (w_down[l].astype(BF16), 1)]
            weights.append([part for w, axis in own for part in pair_weights(w, axis, spread)])
        small = jnp.concatenate(
            [
                w_router, w_const[:, 0], w_const[:, 1], jnp.swapaxes(norm_gains, 1, 2), jnp.swapaxes(v_const, 1, 2),
                jnp.zeros((layers, depth, 108), F32),
            ],
            axis=2,
        ).astype(BF16)
        routes_all = lax.all_gather(packed_routes, "expert", axis=0)
        qkv_all = lax.all_gather(qkv_t.astype(BF16), "dp", axis=1, tiled=True)
        out_all = lax.all_gather(w_out.astype(BF16), "dp", axis=1, tiled=True)
        small_all = lax.all_gather(small, "dp", axis=1, tiled=True)
        dense = [(small_all[l], qkv_all[l], out_all[l]) for l in range(layers)]

    cols = ((rows, width), F32)
    attention = [((rows, width), BF16), ((rows, 3 * width), BF16), ((HEADS, rows, rows), F32), ((rows, width), BF16)]
    residual = ((128, 128), F32)
    per_token, sent = ((rows, 128), F32), ((slots, width), BF16)

    def group(array):
        return array.reshape(owners, local, CAP, width)

    attn_in0, qkv0, probs0, attn0, mid0, logits0, stat0, out = local_call(
        first_kernel, experts, (tokens, *dense[0], seq_lengths, block_perm, routes_all),
        attention + [cols, per_token, per_token, sent], scalars=(4, 5))
    ride = (*gathered[3:], qkv1_own, out1_own, small1_own, g1, u1) if in_kernels else None
    ret0, *kept0 = expert_forward(spread, 0, group(out), weights[0], in_kernels, ride)
    if in_kernels:
        kept0, weights[0][5], (qkv_all, out_all, small_all), (gate, up) = kept0[:3], kept0[3], kept0[4:7], kept0[7:]
        dense.append((small_all, qkv_all, out_all))
        first1, ret0 = lax.optimization_barrier((first1, ret0))
        weights.append([g1, gate, u1, up, d1, from_partner(first1, 1, spread, LINE)])
    ret0 = ret0.reshape(slots, width)
    stream1, attn_in1, qkv1, probs1, attn1, mid1, stat1, out = local_call(
        middle_kernel, experts,
        (mid0, dense[0][0], stat0, ret0, *dense[1], seq_lengths, block_perm, routes_all, logits0, w_residual),
        [cols] + attention + [cols, per_token, sent], [residual], scalars=(7, 8))
    ret1, *kept1 = expert_forward(spread, 1, group(out), weights[1], in_kernels)
    if in_kernels:
        weights[1][5] = kept1.pop()
    ret1 = ret1.reshape(slots, width)

    small_grads = ((24, width), F32)
    output, g_small1, extra, out, small_grad1, res_grad = local_call(
        turn_kernel, experts, (mid1, dense[1][0], stat1, ret1, cotangent, logits0, w_residual),
        [((rows, width), BF16), per_token, per_token, sent, small_grads, residual], [residual])
    back, *expert_grads1 = expert_backward(spread, 2, group(out), kept1, weights[1], in_kernels)
    ride = None
    grad_type = BF16 if in_kernels else F32
    dense_grads = [((3 * width, width), grad_type), ((width, width), grad_type), small_grads]
    attention_scratch = [((rows, 3 * width), BF16), ((rows, width), BF16)]
    qkv_grad1, out_grad1, small_grad1, grad, g_small0, out, small_grad0 = local_call(
        between_kernel, experts,
        (cotangent, back.reshape(slots, width), g_small1, stat1, mid1, dense[1][0], stream1, dense[1][1], dense[1][2],
         attn_in1, qkv1, probs1, attn1, small_grad1, mid0, dense[0][0], stat0, ret0, extra),
        dense_grads + [cols, per_token, sent, small_grads], attention_scratch)
    if in_kernels:
        gate1, up1, up1_sent, down1, down1_sent, gate1_came = expert_grads1
        ride = (qkv_grad1, out_grad1, up1_sent, down1_sent)
    back, *expert_grads0 = expert_backward(spread, 3, group(out), kept0, weights[0], in_kernels, ride)
    qkv_grad0, out_grad0, small_grad0, tokens_grad = local_call(
        last_kernel, experts,
        (grad, back.reshape(slots, width), g_small0, stat0, mid0, dense[0][0], tokens, dense[0][1], dense[0][2],
         attn_in0, qkv0, probs0, attn0, small_grad0),
        dense_grads + [cols], attention_scratch)

    if in_kernels:
        gate0, up0, up0_sent, down0, down0_sent, gate0_came, quarter1, up1_came, down1_came = expert_grads0
        packed, qkv_grad, out_grad, up0_came, down0_came = dense_reduce(
            spread, 5, (small_grad0, small_grad1, res_grad), (qkv_grad0, out_grad0), quarter1, (up0_sent, down0_sent))
        pairs = (
            ((gate0, gate0_came), (gate1, gate1_came)), ((up0, up0_came), (up1, up1_came)),
            ((down0, down0_came), (down1, down1_came)))
        qkv_grad, out_grad, gate_grad, up_grad, down_grad = stack_results(qkv_grad, out_grad, pairs)
    else:
        gate_grad, up_grad, down_grad = (
            jnp.stack([
                pair_sum(grads[at * len(grads) // 3 : (at + 1) * len(grads) // 3], axis, spread)
                for grads in (expert_grads0, expert_grads1)])
            for axis, at in ((2, 0), (2, 1), (1, 2)))
        packed = jnp.concatenate([small_grad0, small_grad1, jnp.pad(res_grad[:16], ((0, 0), (0, width - 128)))])
        packed = lax.psum(packed, ("dp", "expert"))
        qkv_grad, out_grad = (
            lax.psum(lax.psum_scatter(jnp.stack(pair), "dp", scatter_dimension=1, tiled=True), "expert")
            for pair in ((qkv_grad0, qkv_grad1), (out_grad0, out_grad1)))
    mine = lax.dynamic_slice_in_dim(packed, lax.axis_index("dp") * depth, depth, axis=1)
    mine = jnp.stack([mine[:24], mine[24:48]])
    router_grad = jnp.swapaxes(mine[:, :CONST0], 1, 2)
    const_grad = jnp.swapaxes(mine[:, CONST0:GAIN0].reshape(layers, 2, 2, depth), 2, 3)
    residual_grad = packed[48 : 48 + CONST0, :CONST0]
    return (
        output, tokens_grad, mine[:, GAIN0 : GAIN0 + 2], jnp.swapaxes(qkv_grad, 1, 2), out_grad, router_grad,
        residual_grad, const_grad, mine[:, VECTOR0 : VECTOR0 + 2], gate_grad, up_grad, down_grad,
    )


def solution(mesh):
    in_specs = (
        P(("dp", "expert"), None), P("dp", None, None), P("dp", None), P(None, ("dp", "expert"), None),
        P(None, None, "dp"), P(None, None, "dp"), P(None, "dp", None), P(None, "dp", None), P(),
        P(None, None, "dp", None), P(None, None, "dp"), P(None, "expert", None, "dp"), P(None, "expert", None, "dp"),
        P(None, "expert", "dp", None), P(("dp", "expert"), None),
    )
    out_specs = (
        P(("dp", "expert"), None), P(("dp", "expert"), None), P(None, None, "dp"), P(None, None, "dp"),
        P(None, "dp", None), P(None, "dp", None), P(), P(None, None, "dp", None), P(None, None, "dp"),
        P(None, "expert", None, "dp"), P(None, "expert", None, "dp"), P(None, "expert", "dp", None),
    )
    return jax.shard_map(per_device, mesh=mesh, in_specs=in_specs, out_specs=out_specs, check_vma=False)
```

```python
import functools

import jax
import jax.numpy as jnp
from jax import lax
from jax.experimental import pallas as pl
from jax.experimental.pallas import tpu as pltpu
from jax.sharding import PartitionSpec as P

HEADS = 12
CAP = 48
LINE = 4
EPSILON = 1e-05
MASKED = -1e30
HIGH = lax.Precision.HIGHEST
F32 = jnp.float32
BF16 = jnp.bfloat16
MESH = pl.DeviceIdType.MESH
VMEM = pl.BlockSpec(memory_space=pltpu.VMEM)
ANY = pl.BlockSpec(memory_space=pl.ANY)

CONST0, GAIN0, VECTOR0 = 12, 16, 18
STAT = {
    name: i
    for i, name in enumerate(
        ("r0", "r1", "share0", "share1", "slot0", "slot1", "p00", "p01", "p10", "p11")
    )
}


SMEM = pl.BlockSpec(memory_space=pltpu.SMEM)


def dot_nn(a, b, **kw):
    return lax.dot_general(a, b, (((1,), (0,)), ((), ())), preferred_element_type=F32, **kw)


def dot_nt(a, b, **kw):
    return lax.dot_general(a, b, (((1,), (1,)), ((), ())), preferred_element_type=F32, **kw)


def dot_tn(a, b, **kw):
    return lax.dot_general(a, b, (((0,), (0,)), ((), ())), preferred_element_type=F32, **kw)


def thirds(values):
    out = []
    for _ in range(3):
        out.append(values.astype(BF16))
        values = values - out[-1].astype(F32)
    return out


def lanes(rows, width=128):
    return lax.broadcasted_iota(jnp.int32, (rows, width), 1)


def rms_scale(values):
    return lax.rsqrt(jnp.mean(values * values, axis=-1, keepdims=True) + EPSILON)


def row_vectors(small):
    pick = lax.broadcasted_iota(jnp.int32, (8, 128), 0) + GAIN0 == lanes(8)
    rows = dot_nt(pick.astype(BF16), small)
    return rows[0:1], rows[1:2], rows[2:3], rows[3:4]


def stat_columns(stat):
    return {name: stat[:, i : i + 1] for name, i in STAT.items()}


def slot_picks(stat, slots):
    place = lanes(stat["slot0"].shape[0], slots).astype(F32)
    first = (place == stat["slot0"]).astype(BF16)
    second = (place == stat["slot1"]).astype(BF16)
    return first, second


def const_weights(stat, experts):
    out = []
    for kind in (experts + 1, experts + 2, experts + 3):
        out.append(
            stat["share0"] * (stat["r0"] == kind).astype(F32)
            + stat["share1"] * (stat["r1"] == kind).astype(F32)
        )
    return out


def doc_index(lengths, places):
    place, end = lax.axis_index("expert"), 0
    doc = jnp.zeros_like(places)
    for j in range(lengths.shape[2]):
        end = end + lengths[0, place, j]
        doc = doc + (places >= end).astype(jnp.int32)
    return doc


def block_routes(perm, routes_all, layer, rows):
    mine = routes_all[perm[0, lax.axis_index("expert")]].astype(F32)
    routes = jnp.transpose(mine)[:rows].astype(jnp.int32)
    return routes[:, 2 * layer : 2 * layer + 1], routes[:, 2 * layer + 1 : 2 * layer + 2]


def padded(w_res, ref):
    count = w_res.shape[0]
    ref[...] = jnp.zeros(ref.shape, F32)
    ref[0:count, 0:count] = w_res[...]
    return ref[...]


def attend_part(stream, small, w_qkv_t, w_out, lengths, attn_in_ref, qkv_ref, probs_ref, attn_ref):
    rows, width = stream.shape
    gain, _, _, _ = row_vectors(small)
    attn_in_ref[...] = (stream * rms_scale(stream) * gain).astype(BF16)

    def project(i, carry):
        at = pl.multiple_of(i * width, width)
        qkv_ref[:, pl.ds(at, width)] = dot_nt(
            attn_in_ref[...], w_qkv_t[pl.ds(at, width), :]
        ).astype(BF16)
        return carry

    lax.fori_loop(0, 3, project, 0, unroll=True)
    head_dim = width // HEADS
    factor = 1.0 / head_dim**0.5
    allowed = jnp.logical_and(
        doc_index(lengths, lax.broadcasted_iota(jnp.int32, (rows, 1), 0))
        == doc_index(lengths, lax.broadcasted_iota(jnp.int32, (1, rows), 1)),
        lax.broadcasted_iota(jnp.int32, (rows, rows), 0)
        >= lax.broadcasted_iota(jnp.int32, (rows, rows), 1),
    )

    def heads(i, carry):
        at = pl.multiple_of(i * 2 * head_dim, 2 * head_dim)
        query = qkv_ref[:, pl.ds(at, 2 * head_dim)]
        key = qkv_ref[:, pl.ds(pl.multiple_of(at + width, 128), 2 * head_dim)]
        value = qkv_ref[:, pl.ds(pl.multiple_of(at + 2 * width, 128), 2 * head_dim)]
        second = lanes(rows, 2 * head_dim) >= head_dim
        mixed = []
        for sub in (0, 1):
            mine = second if sub else jnp.logical_not(second)
            scores = dot_nt(jnp.where(mine, query, jnp.zeros_like(query)), key) * factor
            scores = jnp.where(allowed, scores, MASKED)
            exponent = jnp.exp(scores - jnp.max(scores, axis=-1, keepdims=True))
            probs = exponent / jnp.sum(exponent, axis=-1, keepdims=True)
            probs_ref[2 * i + sub] = probs
            mixed.append(dot_nn(probs.astype(BF16), value))
        attn_ref[:, pl.ds(at, 2 * head_dim)] = jnp.where(second, mixed[1], mixed[0]).astype(BF16)
        return carry

    lax.fori_loop(0, HEADS // 2, heads, 0, unroll=True)
    return stream + dot_nn(attn_ref[...], w_out[...])


def route_part(mid, small, routes, prev_logits, w_res, experts):
    rows = mid.shape[0]
    _, gain, _, _ = row_vectors(small)
    hidden = (mid * rms_scale(mid) * gain).astype(BF16)
    lane = lanes(rows)
    raw = dot_nn(hidden, small)
    logits = jnp.where(lane < CONST0, raw, 0.0)
    if prev_logits is not None:
        logits = logits + dot_nn(prev_logits, w_res, precision=HIGH)
    r0, r1 = routes
    hot0, hot1 = (lane == r0).astype(F32), (lane == r1).astype(F32)
    c0 = jnp.sum(hot0 * logits, axis=-1, keepdims=True)
    c1 = jnp.sum(hot1 * logits, axis=-1, keepdims=True)
    peak = jnp.maximum(c0, c1)
    e0, e1 = jnp.exp(c0 - peak), jnp.exp(c1 - peak)
    total = e0 + e1
    share0, share1 = e0 / total, e1 / total
    probs = []
    for j in (0, 1):
        a = raw[:, CONST0 + 2 * j : CONST0 + 2 * j + 1]
        b = raw[:, CONST0 + 2 * j + 1 : CONST0 + 2 * j + 2]
        top = jnp.maximum(a, b)
        ea, eb = jnp.exp(a - top), jnp.exp(b - top)
        probs += [ea / (ea + eb), eb / (ea + eb)]
    earlier = lax.broadcasted_iota(jnp.int32, (rows, rows), 0) > lax.broadcasted_iota(
        jnp.int32, (rows, rows), 1
    )
    before = dot_nn(earlier.astype(BF16), (hot0 + hot1).astype(BF16))
    f0, f1 = r0.astype(F32), r1.astype(F32)
    slot0 = jnp.where(
        r0 < experts, f0 * CAP + jnp.sum(before * hot0, axis=-1, keepdims=True), -1.0
    )
    slot1 = jnp.where(
        r1 < experts, f1 * CAP + jnp.sum(before * hot1, axis=-1, keepdims=True), -1.0
    )
    stat = jnp.zeros((rows, 128), F32)
    for i, column in enumerate([f0, f1, share0, share1, slot0, slot1] + probs):
        stat = jnp.where(lane == i, column, stat)
    first, second = slot_picks({"slot0": slot0, "slot1": slot1}, experts * CAP)
    outgoing = dot_tn(first + second, hidden).astype(BF16)
    return logits, stat, outgoing


def combine_part(mid, small, stat, returned, experts):
    _, gain, vec0, vec1 = row_vectors(small)
    hidden_full = mid * rms_scale(mid) * gain
    first, second = slot_picks(stat, experts * CAP)
    pair0, pair1 = dot_nn(first, returned), dot_nn(second, returned)
    copy, const0, const1 = const_weights(stat, experts)
    local = copy + const0 * stat["p00"] + const1 * stat["p10"]
    moe = stat["share0"] * pair0 + stat["share1"] * pair1 + local * hidden_full
    moe = moe + (const0 * stat["p01"]) * vec0 + (const1 * stat["p11"]) * vec1
    return mid + moe, hidden_full, pair0, pair1


def share_backward(grad, small, stat, hidden_full, pair0, pair1, extra, experts):
    rows = grad.shape[0]
    _, _, vec0, vec1 = row_vectors(small)
    first, second = slot_picks(stat, experts * CAP)
    lane = lanes(rows).astype(F32)
    rowsum = functools.partial(jnp.sum, axis=-1, keepdims=True)
    dot_hidden = rowsum(grad * hidden_full)
    dot_vec = (rowsum(grad * vec0), rowsum(grad * vec1))
    _, const0, const1 = const_weights(stat, experts)
    probs = ((stat["p00"], stat["p01"]), (stat["p10"], stat["p11"]))
    value = [probs[j][0] * dot_hidden + probs[j][1] * dot_vec[j] for j in (0, 1)]
    shares = []
    for r, pair in ((stat["r0"], pair0), (stat["r1"], pair1)):
        shares.append(
            rowsum(grad * pair)
            + (r == experts + 1).astype(F32) * dot_hidden
            + (r == experts + 2).astype(F32) * value[0]
            + (r == experts + 3).astype(F32) * value[1]
        )
    inner = stat["share0"] * shares[0] + stat["share1"] * shares[1]
    g_small = (lane == stat["r0"]).astype(F32) * (stat["share0"] * (shares[0] - inner))
    g_small = g_small + (lane == stat["r1"]).astype(F32) * (stat["share1"] * (shares[1] - inner))
    if extra is not None:
        g_small = g_small + extra
    g_logits = g_small
    for j, weight in ((0, const0), (1, const1)):
        q = (weight * dot_hidden, weight * dot_vec[j])
        mean = probs[j][0] * q[0] + probs[j][1] * q[1]
        for c in (0, 1):
            g_small = jnp.where(lane == CONST0 + 2 * j + c, probs[j][c] * (q[c] - mean), g_small)
    sent0 = (jnp.where(stat["r0"] < experts, stat["share0"], 0.0) * grad).astype(BF16)
    sent1 = (jnp.where(stat["r1"] < experts, stat["share1"], 0.0) * grad).astype(BF16)
    outgoing = (dot_tn(first, sent0) + dot_tn(second, sent1)).astype(BF16)
    hidden = hidden_full.astype(BF16)
    projections = sum(dot_tn(part, hidden) for part in thirds(g_small)[::-1])
    vector0 = jnp.sum((const0 * stat["p01"]) * grad, axis=0, keepdims=True)
    vector1 = jnp.sum((const1 * stat["p11"]) * grad, axis=0, keepdims=True)
    return g_small, g_logits, outgoing, projections, vector0, vector1


def store_small(ref, projections, vector0, vector1):
    ref[0:16, :] = projections[0:16]
    ref[16:24, :] = jnp.zeros((8, ref.shape[1]), F32)
    ref[VECTOR0 : VECTOR0 + 1, :] = vector0
    ref[VECTOR0 + 1 : VECTOR0 + 2, :] = vector1


def first_kernel(experts, tokens, small, w_qkv_t, w_out, lengths, perm, routes_all,
                 attn_in, qkv, probs, attn, mid_ref, logits_ref, stat_ref, out_ref):
    mid = attend_part(tokens[...].astype(F32), small[...], w_qkv_t, w_out, lengths, attn_in, qkv, probs, attn)
    mid_ref[...] = mid
    routes = block_routes(perm, routes_all, 0, mid.shape[0])
    logits, stat, out = route_part(mid, small[...], routes, None, None, experts)
    logits_ref[...], stat_ref[...], out_ref[...] = logits, stat, out


def middle_kernel(experts, mid_in, small_in, stat_in, returned, small, w_qkv_t, w_out, lengths, perm, routes_all, logits_in, w_res,
                  stream_ref, attn_in, qkv, probs, attn, mid_ref, stat_ref, out_ref, res_ref):
    stream, _, _, _ = combine_part(mid_in[...], small_in[...], stat_columns(stat_in[...]), returned[...], experts)
    stream_ref[...] = stream
    mid = attend_part(stream, small[...], w_qkv_t, w_out, lengths, attn_in, qkv, probs, attn)
    mid_ref[...] = mid
    routes = block_routes(perm, routes_all, 1, mid.shape[0])
    _, stat, out = route_part(mid, small[...], routes, logits_in[...], padded(w_res, res_ref), experts)
    stat_ref[...], out_ref[...] = stat, out


def turn_kernel(experts, mid, small, stat_in, returned, cotangent, logits_in, w_res,
                output, g_small_ref, extra_ref, out_ref, small_grad, res_grad, res_ref):
    stat = stat_columns(stat_in[...])
    stream, hidden_full, pair0, pair1 = combine_part(mid[...], small[...], stat, returned[...], experts)
    output[...] = stream.astype(BF16)
    grad = cotangent[...].astype(F32)
    g_small, g_logits, out, projections, v0, v1 = share_backward(grad, small[...], stat, hidden_full, pair0, pair1, None, experts)
    g_small_ref[...] = g_small
    out_ref[...] = out
    store_small(small_grad, projections, v0, v1)
    res_grad[...] = dot_tn(logits_in[...], g_logits, precision=HIGH)
    extra_ref[...] = dot_nt(g_logits, padded(w_res, res_ref), precision=HIGH)


def layer_backward(experts, grad, back, g_small, stat, mid, small, stream, w_qkv_t, w_out, attn_in, qkv, probs, attn,
                   qkv_grad, out_grad, small_grad, g_qkv, g_attn):
    rows, width = mid.shape
    gain1, gain2, _, _ = row_vectors(small)
    first, second = slot_picks(stat, experts * CAP)
    copy, const0, const1 = const_weights(stat, experts)
    local = copy + const0 * stat["p00"] + const1 * stat["p10"]
    g_full = sum(dot_nt(part, small) for part in thirds(g_small)[::-1]) + dot_nn(first + second, back)
    g_full = g_full + grad * local
    s2 = rms_scale(mid)
    small_grad[GAIN0 + 1 : GAIN0 + 2, :] = jnp.sum(g_full * mid * s2, axis=0, keepdims=True)
    m = g_full * gain2
    g_mid = grad + s2 * m - mid * (s2 * s2 * s2 * jnp.mean(m * mid, axis=-1, keepdims=True))
    branch = g_mid.astype(BF16)
    out_grad[...] = dot_tn(attn[...], branch).astype(out_grad.dtype)
    g_attn[...] = dot_nt(branch, w_out[...]).astype(BF16)
    head_dim = width // HEADS
    factor = 1.0 / head_dim**0.5

    def heads(i, carry):
        at = pl.multiple_of(i * 2 * head_dim, 2 * head_dim)
        at_k = pl.multiple_of(at + width, 128)
        at_v = pl.multiple_of(at + 2 * width, 128)
        query = qkv[:, pl.ds(at, 2 * head_dim)]
        key = qkv[:, pl.ds(at_k, 2 * head_dim)]
        value = qkv[:, pl.ds(at_v, 2 * head_dim)]
        ga = g_attn[:, pl.ds(at, 2 * head_dim)]
        second_half = lanes(rows, 2 * head_dim) >= head_dim
        gq, gk, gv = [], [], []
        for sub in (0, 1):
            mine = second_half if sub else jnp.logical_not(second_half)
            p = probs[2 * i + sub]
            gp = dot_nt(jnp.where(mine, ga, jnp.zeros_like(ga)), value)
            gs = (p * (gp - jnp.sum(p * gp, axis=-1, keepdims=True))).astype(BF16)
            gq.append(dot_nn(gs, key))
            gk.append(dot_tn(gs, query))
            gv.append(dot_tn(p.astype(BF16), ga))
        g_qkv[:, pl.ds(at, 2 * head_dim)] = (jnp.where(second_half, gq[1], gq[0]) * factor).astype(BF16)
        g_qkv[:, pl.ds(at_k, 2 * head_dim)] = (jnp.where(second_half, gk[1], gk[0]) * factor).astype(BF16)
        g_qkv[:, pl.ds(at_v, 2 * head_dim)] = jnp.where(second_half, gv[1], gv[0]).astype(BF16)
        return carry

    lax.fori_loop(0, HEADS // 2, heads, 0, unroll=True)

    def weights(i, carry):
        at = pl.multiple_of(i * width, width)
        qkv_grad[pl.ds(at, width), :] = dot_tn(g_qkv[:, pl.ds(at, width)], attn_in[...]).astype(qkv_grad.dtype)
        return carry + dot_nn(g_qkv[:, pl.ds(at, width)], w_qkv_t[pl.ds(at, width), :])

    g_in = lax.fori_loop(0, 3, weights, jnp.zeros((rows, width), F32))
    s1 = rms_scale(stream)
    small_grad[GAIN0 : GAIN0 + 1, :] = jnp.sum(g_in * stream * s1, axis=0, keepdims=True)
    n = g_in * gain1
    return g_mid + s1 * n - stream * (s1 * s1 * s1 * jnp.mean(n * stream, axis=-1, keepdims=True))


def between_kernel(experts, cotangent, back, g_small, stat_in, mid, small, stream, w_qkv_t, w_out, attn_in, qkv, probs, attn, small_grad_in,
                   mid0, small0, stat0_in, returned0, extra,
                   qkv_grad, out_grad, small_grad, grad_ref, g_small0_ref, out_ref, small_grad0, g_qkv, g_attn):
    small_grad[...] = small_grad_in[...]
    grad = layer_backward(experts, cotangent[...].astype(F32), back[...], g_small[...], stat_columns(stat_in[...]), mid[...],
                          small[...], stream[...], w_qkv_t, w_out, attn_in, qkv, probs, attn, qkv_grad, out_grad, small_grad, g_qkv, g_attn)
    grad_ref[...] = grad
    stat0 = stat_columns(stat0_in[...])
    _, hidden_full, pair0, pair1 = combine_part(mid0[...], small0[...], stat0, returned0[...], experts)
    g_small0, _, out, projections, v0, v1 = share_backward(grad, small0[...], stat0, hidden_full, pair0, pair1, extra[...], experts)
    g_small0_ref[...] = g_small0
    out_ref[...] = out
    store_small(small_grad0, projections, v0, v1)


def last_kernel(experts, grad_in, back, g_small, stat_in, mid, small, tokens, w_qkv_t, w_out, attn_in, qkv, probs, attn, small_grad_in,
                qkv_grad, out_grad, small_grad, grad_ref, g_qkv, g_attn):
    small_grad[...] = small_grad_in[...]
    grad_ref[...] = layer_backward(experts, grad_in[...], back[...], g_small[...], stat_columns(stat_in[...]), mid[...], small[...],
                                   tokens[...].astype(F32), w_qkv_t, w_out, attn_in, qkv, probs, attn, qkv_grad, out_grad, small_grad,
                                   g_qkv, g_attn)


def local_call(kernel, experts, args, outs, scratch=(), scalars=()):
    return pl.pallas_call(
        functools.partial(kernel, experts),
        out_shape=[jax.ShapeDtypeStruct(shape, dtype) for shape, dtype in outs],
        in_specs=[SMEM if i in scalars else VMEM for i in range(len(args))],
        out_specs=[VMEM] * len(outs),
        scratch_shapes=[pltpu.VMEM(shape, dtype) for shape, dtype in scratch],
        compiler_params=pltpu.CompilerParams(vmem_limit_bytes=60 * 2**20),
        cost_estimate=pl.CostEstimate(flops=10**10, bytes_accessed=6 * 10**7, transcendentals=0),
    )(*args)


class Place:
    def __init__(self, spread):
        self.spread = spread
        self.d, self.e = lax.axis_index("dp"), lax.axis_index("expert")
        self.t, self.f = self.d // spread, lax.rem(self.d, spread)
        self.y, self.c = self.e // 2, lax.rem(self.e, 2)
        self.above, self.below = self.t < LINE - 1, self.t > 0
        self.inside = jnp.logical_and(self.above, self.below)
        self.up = jnp.where(self.t == 1, 1, 0)
        self.ahead = 2 * self.up - 1
        self.sibling = (self.d, self.e + 1 - 2 * self.c)
        self.across = (self.d, lax.rem(self.e + 2, 4))
        self.corner = (self.d, 3 - self.e)
        self.beside = (self.t * spread + 1 - self.f, self.e)
        self.mates = [(self.d, self.e), self.sibling, self.across, self.corner]

    def block(self, i):
        return pick(i, [e for _, e in self.mates])

    def on_line(self, up):
        return (self.d + self.spread * (2 * up - 1), self.e)


def pick(index, values):
    out = values[-1]
    for n in range(len(values) - 2, -1, -1):
        out = jnp.where(index == n, values[n], out)
    return out


def greet(always, place, meanwhile=lambda: None):
    barrier = pltpu.get_barrier_semaphore()
    for device in always:
        pl.semaphore_signal(barrier, inc=1, device_id=device, device_id_type=MESH)
    for up, there in ((1, place.above), (0, place.below)):

        @pl.when(there)
        def _(up=up):
            pl.semaphore_signal(barrier, inc=1, device_id=place.on_line(up), device_id_type=MESH)

    meanwhile()
    ends = place.above.astype(jnp.int32) + place.below.astype(jnp.int32)
    pl.semaphore_wait(barrier, len(always) + ends)


def remote(src, dst, send, recv, device):
    return pltpu.make_async_remote_copy(
        src_ref=src, dst_ref=dst, send_sem=send, recv_sem=recv, device_id=device, device_id_type=MESH)


def dma(*shape):
    return pltpu.SemaphoreType.DMA(shape)


def along(place, body, start=0):
    if start == 0:
        body(place.t)

    def step(k, carry):
        for t in (place.t + k, place.t - k):

            @pl.when(jnp.logical_and(t >= 0, t < LINE))
            def _(t=t):
                body(t)

        return carry

    lax.fori_loop(1, LINE, step, 0)


class Rider:
    partners = ()

    def begin(self):
        pass

    def ready(self):
        pass

    def after_first(self):
        pass

    def after_line(self):
        pass

    def after_relay(self):
        pass

    def finish(self):
        pass


class Line:
    def __init__(self, place, x, part, stage, arrived, final, returned, sems):
        self.p = place
        self.x, self.part, self.stage, self.arrived = x, part, stage, arrived
        self.final, self.returned = final, returned
        (self.out_send, self.x_recv, self.x_send, self.sum_send, self.sum_recv, self.ret_send, self.ret_recv) = sems

    @staticmethod
    def scratch(local, width):
        shape = (local, 4, CAP, width)
        return [
            pltpu.VMEM((local, LINE, 4, CAP, width), BF16),
            pltpu.VMEM((LINE,) + shape, F32),
            pltpu.VMEM((LINE,) + shape, BF16),
            pltpu.VMEM((2, LINE) + shape, BF16),
            pltpu.VMEM((4, local, CAP, width), BF16),
            dma(4), dma(LINE, 4), dma(2, LINE, 4), dma(LINE, 4), dma(2, LINE, 4), dma(4), dma(4),
        ]

    def slot_copy(self, out, i):
        to, p = self.p.mates[i], self.p
        return remote(out.at[to[1]], self.x.at[:, p.t, p.e], self.out_send.at[i], self.x_recv.at[p.t, p.e], to)

    def x_copy(self, up, s, b):
        at = self.x.at[:, s, b]
        return remote(at, at, self.x_send.at[up, s, b], self.x_recv.at[s, b], self.p.on_line(up))

    def sum_copy(self, up, s, b):
        return remote(self.stage.at[s, :, b], self.arrived.at[up, s, :, b], self.sum_send.at[s, b],
                      self.sum_recv.at[up, s, b], self.p.on_line(up))

    def ret_copy(self, i, to_mate=True):
        to = self.p.block(i)
        row = self.p.e if to_mate else to
        return remote(self.final.at[to], self.returned.at[row], self.ret_send.at[i], self.ret_recv.at[row], (self.p.d, to))

    def send_sum(self, up, s, b, total):
        self.stage[s, :, b] = total.astype(BF16)
        self.sum_copy(up, s, b).start()

    def relay(self, n):
        p = self.p
        kind = pick(n, (0, 0, 1, 1, 2, 1, 2, 1, 2, 0, 2, 0))
        b = p.block(pick(n, (0, 1, 0, 1, 0, 2, 1, 3, 2, 2, 3, 3)))
        s = p.t + p.ahead * pick(kind, (1, 2, -1))
        way = jnp.where(kind == 2, 1 - p.up, p.up)

        @pl.when(p.inside)
        def _():
            self.sum_copy(way, s, b).wait_recv()
            self.send_sum(way, s, b, self.part[s, :, b] + self.arrived[way, s, :, b].astype(F32))

    def run(self, out, compute, kept, pieces, rider):
        p = self.p
        t, e = p.t, p.e
        blocks = [b for _, b in p.mates]
        greet(p.mates[1:] + list(rider.partners), p)
        for i in (2, 3, 1):
            self.slot_copy(out, i).start()
        self.x[:, t, e] = out[e]
        rider.begin()
        for i in range(4):
            if i:
                self.x_copy(0, t, blocks[i]).wait_recv()
            for up, there in ((0, p.below), (1, p.above)):

                @pl.when(there)
                def _(up=up, i=i):
                    self.x_copy(up, t, blocks[i]).start()

        rider.ready()

        def step(n, carry):
            k = jnp.where(n < 2, 1, jnp.where(jnp.logical_or(n == 2, n == 5), 2, 3))
            half = jnp.where(jnp.logical_or(n == 1, n >= 4), 1, 0)
            pair = p.y + half - 2 * p.y * half
            first = jnp.where(half == 0, blocks[0], blocks[2])
            second = jnp.where(half == 0, blocks[1], blocks[3])
            for b in (first, second):
                for up, there, onward, before_end in ((0, t + k < LINE, p.below, t == 1), (1, t - k >= 0, p.above, t == LINE - 2)):
                    s = t - k if up else t + k
                    put_off = jnp.logical_and(before_end, n == 1)

                    @pl.when(there)
                    def _(up=up, onward=onward, s=s, b=b, put_off=put_off):
                        self.x_copy(up, s, b).wait_recv()

                        @pl.when(jnp.logical_and(onward, jnp.logical_not(put_off)))
                        def _():
                            self.x_copy(up, s, b).start()

            for up, before_end in ((0, t == 1), (1, t == LINE - 2)):

                @pl.when(jnp.logical_and(before_end, n == 5))
                def _(up=up):
                    for b in (first, second):
                        self.x_copy(up, t - 1 if up else t + 1, b).start()

            @pl.when(jnp.logical_not(p.inside))
            def _():
                s = jnp.where(t == 0, k, LINE - 1 - k)
                compute(s, 2 * pair, 2)

                @pl.when(half == 1)
                def _():
                    kept(s)

            for up, starts, s in ((1, t == 0, k), (0, t == LINE - 1, LINE - 1 - k)):

                @pl.when(starts)
                def _(up=up, s=s):
                    for b in (first, second):
                        self.send_sum(up, s, b, self.part[s, :, b])

            rest = jnp.logical_and(p.inside, jnp.logical_or(n == 5, jnp.logical_and(n >= 1, n <= 2)))

            @pl.when(jnp.logical_or(n == 0, rest))
            def _():
                s = t + p.ahead * jnp.where(n == 0, 0, jnp.where(n == 1, 1, jnp.where(n == 2, -1, 2)))
                compute(s, 0, 4)
                kept(s)

            @pl.when(n == 0)
            def _():
                rider.after_first()

            return carry

        lax.fori_loop(0, 6, step, 0)
        rider.after_line()

        def passing(n, carry):
            self.relay(n)
            pieces(n)
            return carry

        lax.fori_loop(0, 12, passing, 0)
        rider.after_relay()

        def end(i, carry):
            b = p.block(i)
            for up, there in ((1, p.below), (0, p.above)):

                @pl.when(there)
                def _(up=up):
                    self.sum_copy(up, t, b).wait_recv()
                    self.part[t, :, b] = self.part[t, :, b] + self.arrived[up, t, :, b].astype(F32)

            self.final[b] = self.part[t, :, b].astype(BF16)

            @pl.when(i > 0)
            def _():
                self.ret_copy(i).start()

            return carry

        lax.fori_loop(0, 4, end, 0)
        self.returned[e] = self.final[e]

        def sent(n, carry):
            s, b = n // 4, lax.rem(n, 4)
            for up, mine in ((0, jnp.logical_and(p.below, s >= t)), (1, jnp.logical_and(p.above, s <= t))):

                @pl.when(mine)
                def _(up=up):
                    self.x_copy(up, s, b).wait_send()

            @pl.when(s != t)
            def _():
                self.sum_copy(0, s, b).wait_send()

            return carry

        for i in (1, 2, 3):
            self.slot_copy(out, i).wait_send()
        lax.fori_loop(0, 4 * LINE, sent, 0)
        rider.finish()
        for i in (1, 2, 3):
            self.ret_copy(i).wait_send()
            self.ret_copy(i, False).wait_recv()


def split(refs, *counts):
    out, at = [], 0
    for count in counts:
        out.append(refs[at : at + count])
        at += count
    return out + [refs[at:]]


def expert_forward_kernel(spread, parts, late, ride, out, *refs):
    weights_in, given, outs, late_out, whole, scratch, line_refs, sems, ride_refs = split(
        refs, 3 * parts, 8 if ride else 0, 4, late, 5 if ride else 0, 3 * parts, 5, 7)
    (g_all, u_all, keep_sem, load_sem, late_sem), ride_refs = ride_refs[:5], ride_refs[5:]
    returned, x_keep, g_keep, u_keep = outs
    gate, up, down = scratch[:parts], scratch[parts : 2 * parts], scratch[2 * parts :]
    x, part, stage, arrived, final = line_refs
    local, _, _, _, width = x.shape
    p = Place(spread)
    line = Line(p, x, part, stage, arrived, final, returned, sems)
    rider = WeightRider(p, given, whole, ride_refs) if ride else Rider()

    def load(i):
        given = weights_in[i].shape[0]
        return pltpu.make_async_copy(weights_in[i], scratch[i].at[0:given], load_sem.at[i])

    for i in range(3 * parts):
        load(i).start()

    def late_copy():
        return remote(weights_in[-2].at[1:local], scratch[-1].at[1:local], late_sem.at[0], late_sem.at[1], p.beside)

    def late_store():
        return pltpu.make_async_copy(scratch[-1], late_out[0], late_sem.at[2])

    def keep_x(s):
        return pltpu.make_async_copy(x.at[:, s], x_keep.at[:, s], keep_sem.at[0, s])

    def keep_g(s):
        return pltpu.make_async_copy(g_all.at[s], g_keep.at[s], keep_sem.at[1, s])

    def keep_u(s):
        return pltpu.make_async_copy(u_all.at[s], u_keep.at[s], keep_sem.at[2, s])

    def kept(s):
        keep_x(s).start()
        keep_g(s).start()
        keep_u(s).start()

    def compute(s, first, count):
        rows = count * CAP
        at = pl.multiple_of(first * CAP, CAP)

        def one(l, carry):
            rows_in = x[l, s, pl.ds(first, count)].reshape(rows, width)
            total = jnp.zeros((rows, width), F32)
            for q in range(parts):
                cols = gate[q].shape[2]
                here = slice(q * cols, (q + 1) * cols)
                g = dot_nn(rows_in, gate[q][l])
                u = dot_nn(rows_in, up[q][l])
                g_all[s, l, pl.ds(at, rows), here] = g
                u_all[s, l, pl.ds(at, rows), here] = u
                act = (g * jax.nn.sigmoid(g) * u).astype(BF16)
                total = total + dot_nn(act, down[q][l])
            part[s, l, pl.ds(first, count)] = total.reshape(count, CAP, width)
            return carry

        lax.fori_loop(0, local, one, 0)

    class Loaded(Rider):
        partners = [p.beside] if late else []
        after_first, after_line, after_relay = rider.after_first, rider.after_line, rider.after_relay

        def begin(self):
            if late:
                late_copy().start()
            rider.begin()

        def ready(self):
            for i in range(3 * parts):
                load(i).wait()
            if late:
                late_copy().wait_recv()
                late_store().start()

        def finish(self):
            rider.finish()
            if late:
                late_copy().wait_send()
                late_store().wait()

    line.run(out, compute, kept, lambda n: None, Loaded())
    for s in range(LINE):
        keep_x(s).wait()
        keep_g(s).wait()
        keep_u(s).wait()


def expert_backward_kernel(spread, parts, exchange, ride, out, *refs):
    loads_in, given, outs, came, ride_outs, loads, line_refs, sems, rest = split(
        refs, 3 + 3 * parts, 4 if ride else 0, 1 + 3 * parts - exchange, exchange, 3 if ride else 0, 3 + 3 * parts, 5, 7)
    (act_all, gg_all, gu_all), grads, (load_sem, grad_sem, w_send, w_recv), ride_refs = split(rest, 3, 3 * parts, 4)
    returned, grads_out = outs[0], list(outs[1:])
    if exchange:
        grads_out.insert(1, None)
    x_in, g_all, u_all = loads[:3]
    gate, up, down = loads[3 : 3 + parts], loads[3 + parts : 3 + 2 * parts], loads[3 + 2 * parts :]
    x, part, stage, arrived, final = line_refs
    local, _, _, _, width = x.shape
    p = Place(spread)
    line = Line(p, x, part, stage, arrived, final, returned, sems)
    rider = GradientRider(p, given, ride_outs, ride_refs) if ride else Rider()

    def load(i):
        return pltpu.make_async_copy(loads_in[i], loads[i], load_sem.at[i])

    def store(i, l):
        return pltpu.make_async_copy(grads[i].at[l], grads_out[i].at[l], grad_sem.at[i, l])

    for i in range(3 + 3 * parts):
        load(i).start()

    def compute(s, first, count):
        rows = count * CAP
        at = pl.multiple_of(first * CAP, CAP)
        into = pl.ds(pl.multiple_of((4 * s + first) * CAP, CAP), rows)

        def one(l, carry):
            rows_in = x[l, s, pl.ds(first, count)].reshape(rows, width)
            total = jnp.zeros((rows, width), F32)
            for q in range(parts):
                cols = gate[q].shape[2]
                here = slice(q * cols, (q + 1) * cols)
                g, u = g_all[s, l, pl.ds(at, rows), here], u_all[s, l, pl.ds(at, rows), here]
                g_act = dot_nt(rows_in, down[q][l])
                sigma = jax.nn.sigmoid(g)
                swish = g * sigma
                gg = (g_act * u * sigma * (1.0 + g * (1.0 - sigma))).astype(BF16)
                gu = (g_act * swish).astype(BF16)
                act_all[l, into, here] = (swish * u).astype(BF16)
                gg_all[l, into, here] = gg
                gu_all[l, into, here] = gu
                total = total + dot_nt(gg, gate[q][l]) + dot_nt(gu, up[q][l])
            part[s, l, pl.ds(first, count)] = total.reshape(count, CAP, width)
            return carry

        lax.fori_loop(0, local, one, 0)

    def weights(kind, l):
        x_rows, g_rows = (a[l].reshape(LINE * 4 * CAP, width) for a in (x_in, x))
        value = dot_tn(act_all[l], g_rows) if kind == 2 else dot_tn(x_rows, (gg_all, gu_all)[kind][l])
        for q in range(parts):
            i = kind * parts + q
            cols = gate[q].shape[2]
            here = slice(q * cols, (q + 1) * cols)
            grads[i][l] = (value[here] if kind == 2 else value[:, here]).astype(grads[i].dtype)
            if grads_out[i] is not None:
                store(i, l).start()

    def pieces(n):
        for kind in range(3):
            at = n - 1 - 2 * local * kind

            @pl.when(jnp.logical_and(lax.rem(n, 2) == 1, jnp.logical_and(at >= 0, at < 2 * local)))
            def _(kind=kind, at=at):
                weights(kind, at // 2)

        @pl.when(n == 2 * local - 1)
        def _():
            for copy in sent_gate():
                copy.start()

    def sent_gate():
        return [remote(grads[1], came[0], w_send.at[0], w_recv.at[0], p.beside)] if exchange else []

    class Loaded(Rider):
        partners = [p.beside] if exchange else []
        after_first, after_line, after_relay, finish = (
            rider.after_first, rider.after_line, rider.after_relay, rider.finish)

        def begin(self):
            rider.begin()

        def ready(self):
            for i in range(3 + 3 * parts):
                load(i).wait()

    line.run(out, compute, lambda s: None, pieces, Loaded())
    for copy in sent_gate():
        copy.wait()
    for i in range(3 * parts):
        for l in range(local if grads_out[i] is not None else 0):
            store(i, l).wait()


def remote_params(call_id):
    return pltpu.CompilerParams(collective_id=call_id, has_side_effects=True, vmem_limit_bytes=61 * 2**20)


def struct(shape, dtype):
    return jax.ShapeDtypeStruct(tuple(shape), dtype)


def expert_forward(spread, call_id, out, weights, late=False, ride=None):
    parts = len(weights) // 3
    _, local, cap, width = out.shape
    columns = sum(w.shape[2] for w in weights[:parts])
    kept = (LINE, local, 4 * cap, columns)
    outs = [struct(out.shape, BF16), struct((local, LINE, 4, cap, width), BF16), struct(kept, F32), struct(kept, F32)]
    outs += [struct(weights[-2].shape, BF16)] * late
    scratch = [pltpu.VMEM((local,) + w.shape[1:], BF16) for w in weights] + Line.scratch(local, width)
    scratch += [pltpu.VMEM(kept, F32), pltpu.VMEM(kept, F32), dma(3, LINE), dma(3 * parts), dma(3)]
    more = ride or ()
    count = LINE * spread
    if ride:
        outs += [struct((count * s.shape[0], s.shape[1]), BF16) for s in ride[3:6]]
        outs += [struct(w.shape, BF16) for w in ride[6:]]
        scratch += WeightRider.scratch(count)
    return pl.pallas_call(
        functools.partial(expert_forward_kernel, spread, parts, int(late), ride is not None),
        out_shape=outs,
        in_specs=[VMEM] + [ANY] * (len(weights) - 1) + [VMEM if late else ANY] + [ANY] * len(more),
        out_specs=[VMEM] + [ANY] * (len(outs) - 1),
        scratch_shapes=scratch,
        compiler_params=remote_params(call_id),
        cost_estimate=pl.CostEstimate(flops=2 * 10**10, bytes_accessed=2 * 10**8, transcendentals=0),
    )(out, *weights, *more)


def expert_backward(spread, call_id, out, kept, weights, exchange=False, ride=None):
    parts = len(weights) // 3
    _, local, cap, width = out.shape
    columns = sum(w.shape[2] for w in weights[:parts])
    loads = list(kept) + list(weights)
    grads = [(w.shape, F32 if i % parts == 0 else BF16) for i, w in enumerate(weights)]
    wide = pltpu.VMEM((local, LINE * 4 * cap, columns), BF16)
    outs = [struct(out.shape, BF16)] + [struct(*g) for i, g in enumerate(grads) if not exchange or i != 1]
    if exchange:
        outs.append(struct(*grads[1]))
    specs = [VMEM] + [ANY] * len(grads)
    scratch = [pltpu.VMEM(a.shape, a.dtype) for a in loads] + Line.scratch(local, width)
    scratch += [wide] * 3 + [pltpu.VMEM(*g) for g in grads] + [dma(len(loads)), dma(len(grads), local), dma(1), dma(1)]
    more = ride or ()
    if ride:
        depths = [g.shape[0] // (LINE * spread) for g in ride[:2]]
        outs.append(struct((LINE, spread, sum(depths) // 2, width // 2), F32))
        outs += [struct(g.shape, BF16) for g in ride[2:]]
        specs += [VMEM, ANY, ANY]
        scratch += GradientRider.scratch(spread, depths, width)
    return pl.pallas_call(
        functools.partial(expert_backward_kernel, spread, parts, int(exchange), ride is not None),
        out_shape=outs,
        in_specs=[VMEM] + [ANY] * (len(loads) + len(more)),
        out_specs=specs,
        scratch_shapes=scratch,
        compiler_params=remote_params(call_id),
        cost_estimate=pl.CostEstimate(flops=4 * 10**10, bytes_accessed=2 * 10**8, transcendentals=0),
    )(out, *loads, *more)


def from_partner(array, shift, spread, groups):
    pairs = [
        (t * spread + (f + shift) % spread, t * spread + f) for t in range(groups) for f in range(spread)
    ]
    return lax.ppermute(array, "dp", pairs)


def to_partner(array, shift, spread, groups):
    pairs = [
        (t * spread + f, t * spread + (f + shift) % spread) for t in range(groups) for f in range(spread)
    ]
    return lax.ppermute(array, "dp", pairs)


def pair_weights(shard, axis, spread):
    parts = [shard] + [from_partner(shard, i, spread, LINE) for i in range(1, spread)]
    if shard.shape[axis] % 128:
        return [jnp.concatenate(parts, axis=axis)]
    return parts


def pair_sum(parts, axis, spread):
    if len(parts) == 1 and spread > 1:
        parts = jnp.split(parts[0], spread, axis=axis)
    total = parts[0]
    for i in range(1, spread):
        total = total + to_partner(parts[i].astype(BF16), i, spread, LINE).astype(F32)
    return total


class LineGather:
    def __init__(self, place, pairs, shards, quarters, sems):
        self.p, self.shards, self.quarters = place, shards, quarters
        self.send, self.recv, self.x_send, self.x_recv = sems
        self.columns = [place.f, 1 - place.f] if pairs else [0]

    @staticmethod
    def shapes(shards, columns):
        (a, wide), (b, _), (c, narrow) = shards
        return [(LINE, columns, a // 2, wide // 2), (LINE, columns, b // 2, wide // 2), (LINE, columns, c, narrow)]

    @staticmethod
    def scratch(columns):
        return [dma(2, LINE, columns, 3), dma(LINE, columns, 3), dma(3), dma(3)]

    def copy(self, kind, up, t, f):
        at = self.quarters[kind].at[t, f]
        return remote(at, at, self.send.at[up, t, f, kind], self.recv.at[t, f, kind], self.p.on_line(up))

    def x_copy(self, kind, f):
        at = self.quarters[kind].at[self.p.t, f]
        return remote(at, at, self.x_send.at[kind], self.x_recv.at[kind], self.p.beside)

    def both_ways(self, f):
        p = self.p
        for up, there in ((0, p.below), (1, p.above)):

            @pl.when(there)
            def _(up=up):
                for kind in range(3):
                    self.copy(kind, up, p.t, f).start()

    def begin(self):
        p, f = self.p, self.columns[0]
        for kind in (0, 1):
            half, wide = self.quarters[kind].shape[2:]
            self.quarters[kind][p.t, f] = self.shards[kind][
                pl.ds(pl.multiple_of(p.y * half, 16), half), pl.ds(pl.multiple_of(p.c * wide, 128), wide)]
        self.quarters[2][p.t, f] = self.shards[2][...]
        for kind in range(3 if len(self.columns) == 2 else 0):
            self.x_copy(kind, f).start()
        self.both_ways(f)

    def beside(self, then):
        for f in self.columns[1:]:
            for kind in range(3):
                self.x_copy(kind, f).wait_recv()
            self.both_ways(f)
            then(self.p.t, f)

    def step(self, k, then):
        p = self.p
        for f in self.columns:
            for up, there, onward in ((0, p.t + k < LINE, p.below), (1, p.t - k >= 0, p.above)):
                t = p.t - k if up else p.t + k

                @pl.when(there)
                def _(up=up, onward=onward, t=t, f=f):
                    for kind in range(3):
                        self.copy(kind, up, t, f).wait_recv()

                    @pl.when(onward)
                    def _():
                        for kind in range(3):
                            self.copy(kind, up, t, f).start()

                    then(t, f)

    def finish(self):
        p = self.p

        def line(t, carry):
            for up, mine in ((0, jnp.logical_and(p.below, t >= p.t)), (1, jnp.logical_and(p.above, t <= p.t))):

                @pl.when(mine)
                def _(up=up):
                    for f in self.columns:
                        for kind in range(3):
                            self.copy(kind, up, t, f).wait_send()

            return carry

        lax.fori_loop(0, LINE, line, 0)
        for f in self.columns[1:]:
            for kind in range(3):
                self.x_copy(kind, 1 - f).wait_send()


class Spread:
    def __init__(self, place, quarters, shards, whole, sems):
        self.p, self.quarters, self.shards, self.whole = place, quarters, shards, whole
        self.y_send, self.y_recv, self.c_send, self.c_recv, self.l_sem, self.s_sem = sems

    @staticmethod
    def scratch(count):
        return [dma(count, 2), dma(count, 2), dma(count, 2, 2), dma(count, 2, 2), dma(count, 3), dma(3)]

    def region(self, kind, s, y, c):
        depth = self.shards[kind].shape[0]
        if kind == 2:
            return self.whole[2].at[pl.ds(pl.multiple_of(s * depth, 16), depth)]
        half, wide = depth // 2, self.shards[kind].shape[1] // 2
        return self.whole[kind].at[
            pl.ds(pl.multiple_of(s * depth + y * half, 16), half), pl.ds(pl.multiple_of(c * wide, 128), wide)]

    def mine(self, kind, s):
        return self.region(kind, s, self.p.y, self.p.c)

    def y_copy(self, kind, src, s):
        return remote(src, self.mine(kind, s), self.y_send.at[s, kind], self.y_recv.at[s, kind], self.p.across)

    def y_came(self, kind, s):
        at = self.region(kind, s, 1 - self.p.y, self.p.c)
        return remote(at, at, self.y_send.at[s, kind], self.y_recv.at[s, kind], self.p.across)

    def c_copy(self, kind, src, s, y):
        return remote(src, self.region(kind, s, y, self.p.c), self.c_send.at[s, y, kind], self.c_recv.at[s, y, kind],
                      self.p.sibling)

    def c_came(self, kind, s, y):
        at = self.region(kind, s, y, 1 - self.p.c)
        return remote(at, at, self.c_send.at[s, y, kind], self.c_recv.at[s, y, kind], self.p.sibling)

    def local(self, kind, src, s):
        return pltpu.make_async_copy(src, self.mine(kind, s), self.l_sem.at[s, kind])

    def shard(self, kind):
        depth = self.shards[kind].shape[0]
        at = self.whole[kind].at[pl.ds(pl.multiple_of(self.p.d * depth, 16), depth)]
        return pltpu.make_async_copy(self.shards[kind], at, self.s_sem.at[kind])

    def own_shard(self):
        for kind in range(3):
            self.shard(kind).start()

    def push(self, s, sources, here=True):
        if here:
            for kind in range(3):
                self.local(kind, sources[kind], s).start()
        for kind in (0, 1):
            self.y_copy(kind, sources[kind], s).start()
            self.c_copy(kind, sources[kind], s, self.p.y).start()

    def across(self, s):
        for kind in (0, 1):
            self.y_came(kind, s).wait_recv()
            self.c_copy(kind, self.region(kind, s, 1 - self.p.y, self.p.c), s, 1 - self.p.y).start()

    def finish_shard(self, s, here=True):
        @pl.when(s != self.p.d)
        def _():
            for kind in range(3 if here else 0):
                self.local(kind, self.mine(kind, s), s).wait()
            for kind in (0, 1):
                self.y_came(kind, s).wait_send()
                for y in (0, 1):
                    self.c_came(kind, s, y).wait_send()
                    self.c_came(kind, s, y).wait_recv()

    def finish_own(self):
        for kind in range(3):
            self.shard(kind).wait()


class WeightRider:
    def __init__(self, place, given, whole, sems):
        self.p, self.quarters, self.own, self.other = place, given[:3], given[6:], whole[3:]
        self.w_send, self.w_recv, self.x_send, self.x_recv, *more = sems
        self.spread = Spread(place, self.quarters, given[3:6], whole[:3], more)

    @staticmethod
    def scratch(count):
        return [dma(2), dma(2), dma(LINE, 3), dma(LINE, 3)] + Spread.scratch(count)

    def place_of(self, t):
        return t * self.p.spread + self.p.f

    def beside_of(self, t):
        return t * self.p.spread + 1 - self.p.f

    def x_copy(self, kind, t, s):
        return remote(self.quarters[kind].at[t, 0], self.spread.mine(kind, s), self.x_send.at[t, kind],
                      self.x_recv.at[t, kind], self.p.beside)

    def weight(self, i):
        return remote(self.own[i], self.other[i], self.w_send.at[i], self.w_recv.at[i], self.p.beside)

    def begin(self):
        self.spread.own_shard()

        def body(t):
            for kind in range(3):
                self.x_copy(kind, t, self.place_of(t)).start()

            @pl.when(t != self.p.t)
            def _():
                self.spread.push(self.place_of(t), [q.at[t, 0] for q in self.quarters])

        along(self.p, body)
        for i in range(2):
            self.weight(i).start()

    def after_first(self):
        pass

    def after_line(self):
        def body(t):
            s = self.beside_of(t)
            for kind in range(3):
                self.x_copy(kind, t, s).wait_recv()
            self.spread.push(s, [self.spread.mine(kind, s) for kind in range(3)], here=False)

        along(self.p, body)

    def after_relay(self):
        along(self.p, lambda t: self.spread.across(self.place_of(t)), start=1)
        along(self.p, lambda t: self.spread.across(self.beside_of(t)))

    def finish(self):
        self.spread.finish_own()
        for i in range(2):
            self.weight(i).wait()

        def line(t, carry):
            for kind in range(3):
                self.x_copy(kind, t, self.place_of(t)).wait_send()
            self.spread.finish_shard(self.place_of(t))
            self.spread.finish_shard(self.beside_of(t), here=False)
            return carry

        lax.fori_loop(0, LINE, line, 0)


def pack_small(l, router, const, gains, vectors, rows, small):
    rows[...] = jnp.zeros(rows.shape, F32)
    for r in range(router.shape[0]):
        rows[r : r + 1, :] = router[r, l : l + 1, :]
    for j in (0, 1):
        rows[CONST0 + 2 * j : CONST0 + 2 * j + 2, :] = const[l, j]
    rows[GAIN0 : GAIN0 + 2, :] = gains[l]
    rows[VECTOR0 : VECTOR0 + 2, :] = vectors[l]
    place = lax.broadcasted_iota(jnp.int32, (rows.shape[0], 128), 0) == lanes(rows.shape[0])
    small[l] = dot_tn(rows[...].astype(BF16), place.astype(BF16)).astype(BF16)


def dense_gather_kernel(spread, qkv_wide, out_wide, router, const, gains, vectors, routes_in, *refs):
    p = Place(spread)
    wide, whole, quarters1, (routes_all,), own, firsts, partner, shards1_out, quarters0, loaded, rounded, shards, (rows, routes), rest = split(
        refs, 3, 3, 3, 1, 6, 2, 2, 3, 3, 3, 3, 3, 2)
    qkv, out, small = shards
    sems0, sems1, (r_send, r_recv, w_send, w_recv, load_sem, own_sem, first_sem, shard_sem), spread_sems = split(rest, 4, 4, 8)
    shards0, shards1 = ([ref.at[l] for ref in (qkv, out, small)] for l in (0, 1))
    line0 = LineGather(p, True, shards0, quarters0, sems0)
    line1 = LineGather(p, False, shards1, quarters1, sems1)
    spreading = Spread(p, quarters0, shards0, whole, spread_sems)

    def load(l, kind):
        return pltpu.make_async_copy(wide[kind].at[l], loaded[kind].at[l], load_sem.at[l, kind])

    def store(l, kind):
        return pltpu.make_async_copy(rounded[kind].at[l], own[3 * l + kind], own_sem.at[l, kind])

    def first(l):
        return pltpu.make_async_copy(rounded[2].at[l, 0:1], firsts[l], first_sem.at[l])

    def weight(kind):
        return remote(rounded[kind].at[0], partner[kind], w_send.at[kind], w_recv.at[kind], p.beside)

    def round_weights(l, kind):
        load(l, kind).wait()

        def one(i, carry):
            rounded[kind][l, i] = loaded[kind][l, i].astype(BF16)
            return carry

        lax.fori_loop(0, rounded[kind].shape[1], one, 0)
        store(l, kind).start()
        if kind == 2:
            first(l).start()

    def shard1(kind):
        return pltpu.make_async_copy(shards[kind].at[1], shards1_out[kind], shard_sem.at[kind])

    for l in (0, 1):
        for kind in range(3):
            load(l, kind).start()
    def round_shards():
        for l in (0, 1):
            qkv[l], out[l] = qkv_wide[l].astype(BF16), out_wide[l].astype(BF16)
            pack_small(l, router, const, gains, vectors, rows, small)
        for kind in range(3):
            shard1(kind).start()
        routes[...] = jnp.zeros(routes.shape, jnp.int32)
        for l in (0, 1):
            routes[2 * l : 2 * l + 2, 0 : routes_in.shape[2]] = routes_in[l]

    greet(p.mates[1:] + [p.beside], p, round_shards)

    def route_copy(i, row):
        return remote(routes, routes_all.at[row], r_send.at[i], r_recv.at[row], p.mates[i])

    def push(t, f):
        spreading.push(t * spread + f, [q.at[t, f] for q in quarters0])

    line0.begin()
    for kind in (0, 1):
        round_weights(0, kind)
        weight(kind).start()
    routes_all[p.e] = routes[...]
    for i in (1, 2, 3):
        route_copy(i, p.e).start()
    spreading.own_shard()
    line0.beside(push)
    line1.begin()
    lax.fori_loop(1, LINE, lambda k, carry: (line0.step(k, push), carry)[1], 0)
    round_weights(0, 2)
    lax.fori_loop(1, LINE, lambda k, carry: (line1.step(k, lambda t, f: None), carry)[1], 0)
    for kind in range(3):
        round_weights(1, kind)
    along(p, lambda t: spreading.across(t * spread + p.f), start=1)
    along(p, lambda t: spreading.across(t * spread + 1 - p.f))
    spreading.finish_own()
    lax.fori_loop(0, LINE * spread, lambda s, carry: (spreading.finish_shard(s), carry)[1], 0)
    line0.finish()
    line1.finish()
    for l in (0, 1):
        for kind in range(3):
            store(l, kind).wait()
        first(l).wait()
    for kind in (0, 1):
        weight(kind).wait()
    for kind in range(3):
        shard1(kind).wait()
    for i in (1, 2, 3):
        route_copy(i, p.e).wait_send()
        route_copy(i, p.mates[i][1]).wait_recv()


def dense_gather(spread, call_id, arrays, routes, wide):
    count = spread * LINE
    layers, depth = arrays[1].shape[:2]
    shards = [arrays[0].shape[1:], arrays[1].shape[1:], (depth, 128)]
    pairs, single = LineGather.shapes(shards, 2), LineGather.shapes(shards, 1)
    outs = [struct((count * rows, width), BF16) for rows, width in shards]
    packed = (8, -(-routes.shape[2] // 128) * 128)
    outs += [struct(q, BF16) for q in single] + [struct((4,) + packed, jnp.int32)]
    outs += [struct(w.shape[1:], BF16) for w in wide] * 2 + [struct((1,) + wide[2].shape[2:], BF16)] * 2
    outs += [struct(w.shape[1:], BF16) for w in wide[:2]] + [struct(s, BF16) for s in shards]
    scratch = [pltpu.VMEM(q, BF16) for q in pairs] + [pltpu.VMEM(w.shape, F32) for w in wide]
    scratch += [pltpu.VMEM(w.shape, BF16) for w in wide] + [pltpu.VMEM((layers,) + s, BF16) for s in shards]
    scratch += [pltpu.VMEM((32, depth), F32), pltpu.VMEM(packed, jnp.int32)] + LineGather.scratch(2) + LineGather.scratch(1)
    scratch += [dma(4), dma(4), dma(2), dma(2), dma(2, 3), dma(2, 3), dma(2), dma(3)]
    return pl.pallas_call(
        functools.partial(dense_gather_kernel, spread),
        out_shape=outs,
        in_specs=[VMEM] * (len(arrays) + 1) + [ANY] * 3,
        out_specs=[ANY] * 3 + [VMEM] * 4 + [ANY] * 13,
        scratch_shapes=scratch + Spread.scratch(count),
        compiler_params=remote_params(call_id),
        cost_estimate=pl.CostEstimate(flops=10**10, bytes_accessed=10**8, transcendentals=0),
    )(*arrays, routes, *wide)


class Halve:
    def __init__(self, place, grads, quarter, scratch):
        self.p, self.grads, self.quarter = place, grads, quarter
        (self.mine, self.core, self.stage, self.came, self.l_sem, self.a_send, self.a_recv, self.y_send,
         self.y_recv) = scratch
        self.depths = [g.shape[0] // (LINE * place.spread) for g in grads]
        self.wide = grads[0].shape[1] // 2

    @staticmethod
    def scratch(spread, depths, width):
        count, rows, wide = LINE * spread, sum(depths) // 2, width // 2
        half = pltpu.VMEM((LINE, spread, rows, wide), BF16)
        everything = pltpu.VMEM((count * sum(depths), wide), BF16)
        return [everything, everything, half, half, dma(2), dma(2), dma(2), dma(LINE), dma(LINE)]

    def rows_of(self, kind):
        first = 0 if kind == 0 else self.grads[0].shape[0]
        return slice(first, first + self.grads[kind].shape[0])

    def lanes(self, c):
        return pl.ds(pl.multiple_of(c * self.wide, 128), self.wide)

    def local(self, kind):
        return pltpu.make_async_copy(
            self.grads[kind].at[:, self.lanes(self.p.c)], self.mine.at[self.rows_of(kind)], self.l_sem.at[kind])

    def a_copy(self, kind):
        return remote(self.grads[kind].at[:, self.lanes(1 - self.p.c)], self.core.at[self.rows_of(kind)],
                      self.a_send.at[kind], self.a_recv.at[kind], self.p.sibling)

    def y_copy(self, t):
        return remote(self.stage.at[t], self.came.at[t], self.y_send.at[t], self.y_recv.at[t], self.p.across)

    def pieces(self, t, f, y):
        s, row = t * self.p.spread + f, 0
        for kind, depth in enumerate(self.depths):
            at = self.rows_of(kind).start + s * depth + y * (depth // 2)
            here = pl.ds(pl.multiple_of(at, 16), depth // 2)
            yield slice(row, row + depth // 2), self.mine[here, :].astype(F32) + self.core[here, :].astype(F32)
            row += depth // 2

    def order(self, i):
        t = self.p.t
        down = LINE - 1 - i - jnp.where(LINE - 1 - i <= t, 1, 0)
        up = i + jnp.where(i >= t, 1, 0)
        return jnp.where(i == LINE - 1, t, jnp.where(t >= LINE // 2, up, down))

    def begin(self):
        for kind in (0, 1):
            self.a_copy(kind).start()
            self.local(kind).start()

    def after_first(self):
        for kind in (0, 1):
            self.a_copy(kind).wait_recv()
            self.local(kind).wait()

        def body(i, carry):
            t = self.order(i)
            for f in range(self.p.spread):
                for where, value in self.pieces(t, f, 1 - self.p.y):
                    self.stage[t, f, where] = value.astype(BF16)
            self.y_copy(t).start()
            return carry

        lax.fori_loop(0, LINE, body, 0)

        def own(t, carry):
            for f in range(self.p.spread):
                for where, value in self.pieces(t, f, self.p.y):
                    self.quarter[t, f, where] = value
            return carry

        lax.fori_loop(0, LINE, own, 0)

    def add(self, t):
        self.y_copy(t).wait_recv()
        self.quarter[t] = self.quarter[t] + self.came[t].astype(F32)

    def after_relay(self):
        lax.fori_loop(0, LINE, lambda i, carry: (self.add(self.order(i)), carry)[1], 0)

    def finish(self):
        for kind in (0, 1):
            self.a_copy(kind).wait_send()
        lax.fori_loop(0, LINE, lambda t, carry: (self.y_copy(t).wait_send(), carry)[1], 0)


class GradientRider:
    def __init__(self, place, given, outs, scratch):
        self.halve = Halve(place, given[:2], outs[0], scratch[:9])
        self.own, self.other = given[2:], outs[1:]
        self.p = place
        self.w_send, self.w_recv = scratch[9:]

    @staticmethod
    def scratch(spread, depths, width):
        return Halve.scratch(spread, depths, width) + [dma(2), dma(2)]

    def weight(self, i):
        return remote(self.own[i], self.other[i], self.w_send.at[i], self.w_recv.at[i], self.p.beside)

    def begin(self):
        self.halve.begin()
        for i in range(2):
            self.weight(i).start()

    def after_first(self):
        self.halve.after_first()

    def after_line(self):
        pass

    def after_relay(self):
        self.halve.after_relay()

    def finish(self):
        self.halve.finish()
        for i in range(2):
            self.weight(i).wait()


class LineSum:
    def __init__(self, place, depths, quarter, sums, scratch):
        self.p, self.depths, self.quarter, self.sums = place, depths, quarter, sums
        (self.stage, self.came, self.stage_x, self.came_x, self.z_send, self.z_recv, self.x_send, self.x_recv,
         self.e_send, self.e_recv) = scratch
        self.wide = sums[0].shape[1] // 2

    @staticmethod
    def scratch(spread, depths, width):
        rows, wide = sum(depths) // 2, width // 2
        return [
            pltpu.VMEM((LINE, spread, rows, wide), BF16),
            pltpu.VMEM((2, LINE, spread, rows, wide), BF16),
            pltpu.VMEM((rows, wide), BF16),
            pltpu.VMEM((rows, wide), BF16),
            dma(LINE), dma(2, LINE), dma(1), dma(1), dma(3, 2), dma(3, 2),
        ]

    def lanes(self, c):
        return pl.ds(pl.multiple_of(c * self.wide, 128), self.wide)

    def z_copy(self, up, t):
        return remote(self.stage.at[t], self.came.at[up, t], self.z_send.at[t], self.z_recv.at[up, t], self.p.on_line(up))

    def x_copy(self):
        return remote(self.stage_x, self.came_x, self.x_send.at[0], self.x_recv.at[0], self.p.beside)

    def e_copy(self, i, kind, y, c):
        half = self.depths[kind] // 2
        at = self.sums[kind].at[pl.ds(pl.multiple_of(y * half, 8), half), self.lanes(c)]
        return remote(at, at, self.e_send.at[i, kind], self.e_recv.at[i, kind], self.p.across if i == 0 else self.p.sibling)

    def start(self, t):
        p = self.p
        for up, mine in ((1, jnp.logical_and(p.t == 0, t > 0)), (0, jnp.logical_and(p.t == LINE - 1, t < LINE - 1))):

            @pl.when(mine)
            def _(up=up):
                self.stage[t] = self.quarter[t].astype(BF16)
                self.z_copy(up, t).start()

    def relay(self, kind):
        p = self.p

        @pl.when(p.inside)
        def _():
            t = {"near": p.t + p.ahead, "far": p.t + 2 * p.ahead, "back": p.t - p.ahead}[kind]
            way = 1 - p.up if kind == "back" else p.up
            self.z_copy(way, t).wait_recv()
            self.stage[t] = (self.quarter[t] + self.came[way, t].astype(F32)).astype(BF16)
            self.z_copy(way, t).start()

    def after_z(self):
        p = self.p

        for up, there in ((1, p.below), (0, p.above)):

            @pl.when(there)
            def _(up=up):
                self.z_copy(up, p.t).wait_recv()
                self.quarter[p.t] = self.quarter[p.t] + self.came[up, p.t].astype(F32)

        self.stage_x[...] = self.quarter[p.t, 1 - p.f].astype(BF16)
        self.x_copy().start()

    def after_x(self):
        p = self.p
        self.x_copy().wait_recv()
        row = 0
        for kind, depth in enumerate(self.depths):
            half = depth // 2
            value = self.quarter[p.t, p.f, row : row + half] + self.came_x[row : row + half].astype(F32)
            self.sums[kind][pl.ds(pl.multiple_of(p.y * half, 8), half), self.lanes(p.c)] = value
            row += half
        for i in (0, 1):
            for kind in (0, 1):
                self.e_copy(i, kind, p.y, p.c).start()

    def finish(self):
        p = self.p
        for kind in (0, 1):
            self.e_copy(0, kind, 1 - p.y, p.c).wait_recv()
            self.e_copy(2, kind, 1 - p.y, p.c).start()
        for kind in (0, 1):
            self.e_copy(0, kind, p.y, p.c).wait_send()
            self.e_copy(1, kind, p.y, p.c).wait_send()
            self.e_copy(1, kind, p.y, 1 - p.c).wait_recv()
            self.e_copy(2, kind, 1 - p.y, p.c).wait_send()
            self.e_copy(2, kind, 1 - p.y, 1 - p.c).wait_recv()
        self.x_copy().wait_send()

        def body(t, carry):
            @pl.when(t != p.t)
            def _():
                self.z_copy(0, t).wait_send()

            return carry

        lax.fori_loop(0, LINE, body, 0)


class SmallSum:
    def __init__(self, place, grads, total, scratch):
        self.p, self.grads, self.total = place, grads, total
        self.stage, self.came, self.send, self.recv = scratch
        p = place
        near = (p.d + p.spread - 2 * p.spread * lax.rem(p.t, 2), p.e)
        self.far = (lax.rem(p.d + 2 * p.spread, LINE * p.spread), p.e)
        self.partners = [p.sibling, p.across, near, self.far, p.beside]

    @staticmethod
    def scratch(rows, width):
        half = pltpu.VMEM((5, rows, width // 2), F32)
        return [half, half, dma(6), dma(6)]

    def lanes(self, c):
        wide = self.grads.shape[1] // 2
        return pl.ds(pl.multiple_of(c * wide, 128), wide)

    def copy(self, i):
        src = self.grads.at[:, self.lanes(1 - self.p.c)] if i == 0 else self.stage.at[i]
        return remote(src, self.came.at[i], self.send.at[i], self.recv.at[i], self.partners[i])

    def last(self, c):
        at = self.total.at[:, self.lanes(c)]
        return remote(at, at, self.send.at[5], self.recv.at[5], self.p.sibling)

    def step(self, i):
        if i == 0:
            self.copy(0).start()
            return
        self.copy(i - 1).wait_recv()
        mine = self.grads[:, self.lanes(self.p.c)] if i == 1 else self.stage[i - 1]
        value = mine + self.came[i - 1]
        if i < 5:
            self.stage[i] = value
            self.copy(i).start()
        else:
            self.total[:, self.lanes(self.p.c)] = value
            self.last(self.p.c).start()

    def finish(self):
        for i in range(5):
            self.copy(i).wait_send()
        self.last(self.p.c).wait_send()
        self.last(1 - self.p.c).wait_recv()


def dense_reduce_kernel(spread, depths, small0, small1, res, qkv0, out0, quarter1, up0, down0, small_sum, *refs):
    p = Place(spread)
    sums, came, (small, mine0, mine1), (w_send, w_recv), halve_refs, line0, line1, small_refs = split(refs, 2, 2, 3, 2, 9, 10, 10)
    sums0, sums1 = ([ref.at[l] for ref in sums] for l in (0, 1))
    halve = Halve(p, (qkv0, out0), mine0, halve_refs)
    sum0 = LineSum(p, depths, mine0, sums0, line0)
    sum1 = LineSum(p, depths, mine1, sums1, line1)
    little = SmallSum(p, small, small_sum, small_refs)
    weights = [remote(w, came[i], w_send.at[i], w_recv.at[i], p.beside) for i, w in enumerate((up0, down0))]
    greet([p.sibling, p.across, p.beside, little.far], p)
    halve.begin()
    for copy in weights:
        copy.start()
    rows = small0.shape[0]
    small[0:rows, :] = small0[...]
    small[rows : 2 * rows, :] = small1[...]
    small[2 * rows :, :] = jnp.zeros((16, small.shape[1]), F32)
    small[2 * rows :, 0:128] = res[0:16, :]
    little.step(0)
    mine1[...] = quarter1[...]
    for i in range(LINE):
        sum1.start(halve.order(i))
    little.step(1)
    halve.after_first()
    little.step(2)

    def arrive(i):
        halve.add(halve.order(i))
        sum0.start(halve.order(i))

    sum1.relay("far")
    sum1.relay("near")
    arrive(0)
    little.step(3)
    sum1.relay("back")
    arrive(1)
    sum0.relay("far")
    sum1.after_z()
    arrive(2)
    sum0.relay("near")
    sum0.relay("back")
    arrive(3)
    little.step(4)
    sum0.after_z()
    sum1.after_x()
    little.step(5)
    sum0.after_x()
    sum1.finish()
    halve.finish()
    little.finish()
    sum0.finish()
    for copy in weights:
        copy.wait()


def dense_reduce(spread, call_id, smalls, grads0, quarter1, weights0):
    count = LINE * spread
    depths = [g.shape[0] // count for g in grads0]
    width = grads0[0].shape[1]
    small = (2 * smalls[0].shape[0] + 16, width)
    line = LineSum.scratch(spread, depths, width)
    mine = pltpu.VMEM(quarter1.shape, F32)
    scratch = [pltpu.VMEM(small, F32), mine, mine, dma(2), dma(2)] + Halve.scratch(spread, depths, width) + line + line
    return pl.pallas_call(
        functools.partial(dense_reduce_kernel, spread, depths),
        out_shape=[struct(small, F32)] + [struct((2, depth, width), F32) for depth in depths]
        + [struct(w.shape, BF16) for w in weights0],
        in_specs=[VMEM] * 3 + [ANY, ANY, VMEM, ANY, ANY],
        out_specs=[VMEM] * 3 + [ANY] * 2,
        scratch_shapes=scratch + SmallSum.scratch(*small),
        compiler_params=remote_params(call_id),
        cost_estimate=pl.CostEstimate(flops=2 * 10**10, bytes_accessed=2 * 10**8, transcendentals=0),
    )(*smalls, *grads0, quarter1, *weights0)


def stack_kernel(small, qkv, out, *refs):
    parts, (qkv_out, out_out, *stacked), (router, const, gains, vectors, residual) = split(refs, 12, 5)
    qkv_out[...], out_out[...] = qkv[...], out[...]
    for kind, ref in enumerate(stacked):
        for l in (0, 1):
            mine, came = parts[4 * kind + 2 * l], parts[4 * kind + 2 * l + 1]
            ref[l] = mine[...] + came[...].astype(F32)

    @pl.when(jnp.logical_and(pl.program_id(0) == 0, pl.program_id(1) == 0))
    def _():
        depth, width = gains.shape[2], small.shape[1]
        here = lanes(depth, width) == lax.axis_index("dp") * depth + lax.broadcasted_iota(jnp.int32, (depth, width), 0)
        rows = dot_nt(small[...], here.astype(F32), precision=HIGH)
        for l in (0, 1):
            first = 24 * l
            for r in range(CONST0):
                router[r, l : l + 1, :] = rows[first + r : first + r + 1]
            for j in (0, 1):
                at = first + CONST0 + 2 * j
                const[l, j] = rows[at : at + 2]
            gains[l] = rows[first + GAIN0 : first + GAIN0 + 2]
            vectors[l] = rows[first + VECTOR0 : first + VECTOR0 + 2]
        residual[...] = small[48 : 48 + CONST0, 0:CONST0]


def stack_results(small, qkv, out, parts, depth):
    flat = [part for kind in parts for layer in kind for part in layer]
    local, steps = flat[0].shape[0], 2

    def rows_of(shape, lead=None):
        rows, wide = shape[-2] // steps, shape[-1]
        if lead:
            return pl.BlockSpec((lead, 1, rows, wide), lambda l, n: (0, l, n, 0))
        return pl.BlockSpec((1, rows, wide), lambda l, n: (l, n, 0))

    def whole(shape):
        return pl.BlockSpec(shape, lambda l, n: (0,) * len(shape))

    stacked = [(2,) + kind[0][0].shape for kind in parts]
    little = [(CONST0, 2, depth), (2, 2, 2, depth), (2, 2, depth), (2, 2, depth), (CONST0, CONST0)]
    return pl.pallas_call(
        stack_kernel,
        out_shape=[struct(a.shape, F32) for a in (qkv, out)] + [struct(s, F32) for s in stacked + little],
        grid=(local, steps),
        in_specs=[whole(small.shape)] + [rows_of(a.shape) for a in (qkv, out, *flat)],
        out_specs=[rows_of(a.shape) for a in (qkv, out)] + [rows_of(s, 2) for s in stacked] + [whole(s) for s in little],
        compiler_params=pltpu.CompilerParams(vmem_limit_bytes=60 * 2**20),
        cost_estimate=pl.CostEstimate(flops=10**7, bytes_accessed=3 * 10**7, transcendentals=0),
    )(small, qkv, out, *flat)


def per_device(
    tokens, seq_lengths, block_perm, routes, norm_gains, w_qkv, w_out, w_router, w_residual, w_const, v_const,
    w_gate, w_up, w_down, cotangent,
):
    rows, width = tokens.shape
    owners = lax.axis_size("expert")
    shards = lax.axis_size("dp")
    spread = shards // LINE
    local = w_gate.shape[1]
    experts = local * owners
    layers = routes.shape[0]
    slots = experts * CAP

    depth = w_out.shape[1]
    qkv_t = jnp.swapaxes(w_qkv, 1, 2)
    in_kernels = spread == 2 and owners == 4 and layers == local == 2 and qkv_t.shape[1] % 32 == 0 and depth % 32 == 0
    if in_kernels:
        arrays = (qkv_t, w_out, jnp.transpose(w_router, (2, 0, 1)), jnp.swapaxes(w_const, 2, 3), norm_gains, v_const)
        *gathered, routes_all, g0, u0, d0, g1, u1, d1, first0, first1, gate, up, qkv1_own, out1_own, small1_own = dense_gather(
            spread, 4, arrays, jnp.swapaxes(routes, 1, 2), (w_gate, w_up, w_down))
        weights = [[g0, gate, u0, up, d0, from_partner(first0, 1, spread, LINE)]]
        dense = [(gathered[2], gathered[0], gathered[1])]
    else:
        weights = []
        for l in range(layers):
            own = [(w_gate[l].astype(BF16), 2), (w_up[l].astype(BF16), 2), (w_down[l].astype(BF16), 1)]
            weights.append([part for w, axis in own for part in pair_weights(w, axis, spread)])
        small = jnp.concatenate(
            [
                w_router, w_const[:, 0], w_const[:, 1], jnp.swapaxes(norm_gains, 1, 2), jnp.swapaxes(v_const, 1, 2),
                jnp.zeros((layers, depth, 108), F32),
            ],
            axis=2,
        ).astype(BF16)
        packed_routes = jnp.zeros((8, -(-rows // 128) * 128), jnp.int32).at[: 2 * layers, :rows].set(
            jnp.swapaxes(routes, 1, 2).reshape(2 * layers, rows))
        routes_all = lax.all_gather(packed_routes, "expert", axis=0)
        qkv_all = lax.all_gather(qkv_t.astype(BF16), "dp", axis=1, tiled=True)
        out_all = lax.all_gather(w_out.astype(BF16), "dp", axis=1, tiled=True)
        small_all = lax.all_gather(small, "dp", axis=1, tiled=True)
        dense = [(small_all[l], qkv_all[l], out_all[l]) for l in range(layers)]

    cols = ((rows, width), F32)
    attention = [((rows, width), BF16), ((rows, 3 * width), BF16), ((HEADS, rows, rows), F32), ((rows, width), BF16)]
    residual = ((128, 128), F32)
    per_token, sent = ((rows, 128), F32), ((slots, width), BF16)

    def group(array):
        return array.reshape(owners, local, CAP, width)

    attn_in0, qkv0, probs0, attn0, mid0, logits0, stat0, out = local_call(
        first_kernel, experts, (tokens, *dense[0], seq_lengths, block_perm, routes_all),
        attention + [cols, per_token, per_token, sent], scalars=(4, 5))
    ride = (*gathered[3:], qkv1_own, out1_own, small1_own, g1, u1) if in_kernels else None
    ret0, *kept0 = expert_forward(spread, 0, group(out), weights[0], in_kernels, ride)
    if in_kernels:
        kept0, weights[0][5], (qkv_all, out_all, small_all), (gate, up) = kept0[:3], kept0[3], kept0[4:7], kept0[7:]
        dense.append((small_all, qkv_all, out_all))
        first1, ret0 = lax.optimization_barrier((first1, ret0))
        weights.append([g1, gate, u1, up, d1, from_partner(first1, 1, spread, LINE)])
    ret0 = ret0.reshape(slots, width)
    stream1, attn_in1, qkv1, probs1, attn1, mid1, stat1, out = local_call(
        middle_kernel, experts,
        (mid0, dense[0][0], stat0, ret0, *dense[1], seq_lengths, block_perm, routes_all, logits0, w_residual),
        [cols] + attention + [cols, per_token, sent], [residual], scalars=(7, 8))
    ret1, *kept1 = expert_forward(spread, 1, group(out), weights[1], in_kernels)
    if in_kernels:
        weights[1][5] = kept1.pop()
    ret1 = ret1.reshape(slots, width)

    small_grads = ((24, width), F32)
    output, g_small1, extra, out, small_grad1, res_grad = local_call(
        turn_kernel, experts, (mid1, dense[1][0], stat1, ret1, cotangent, logits0, w_residual),
        [((rows, width), BF16), per_token, per_token, sent, small_grads, residual], [residual])
    back, *expert_grads1 = expert_backward(spread, 2, group(out), kept1, weights[1], in_kernels)
    ride = None
    grad_type = BF16 if in_kernels else F32
    dense_grads = [((3 * width, width), grad_type), ((width, width), grad_type), small_grads]
    attention_scratch = [((rows, 3 * width), BF16), ((rows, width), BF16)]
    qkv_grad1, out_grad1, small_grad1, grad, g_small0, out, small_grad0 = local_call(
        between_kernel, experts,
        (cotangent, back.reshape(slots, width), g_small1, stat1, mid1, dense[1][0], stream1, dense[1][1], dense[1][2],
         attn_in1, qkv1, probs1, attn1, small_grad1, mid0, dense[0][0], stat0, ret0, extra),
        dense_grads + [cols, per_token, sent, small_grads], attention_scratch)
    if in_kernels:
        gate1, up1, up1_sent, down1, down1_sent, gate1_came = expert_grads1
        ride = (qkv_grad1, out_grad1, up1_sent, down1_sent)
    back, *expert_grads0 = expert_backward(spread, 3, group(out), kept0, weights[0], in_kernels, ride)
    qkv_grad0, out_grad0, small_grad0, tokens_grad = local_call(
        last_kernel, experts,
        (grad, back.reshape(slots, width), g_small0, stat0, mid0, dense[0][0], tokens, dense[0][1], dense[0][2],
         attn_in0, qkv0, probs0, attn0, small_grad0),
        dense_grads + [cols], attention_scratch)

    if in_kernels:
        gate0, up0, up0_sent, down0, down0_sent, gate0_came, quarter1, up1_came, down1_came = expert_grads0
        packed, qkv_grad, out_grad, up0_came, down0_came = dense_reduce(
            spread, 5, (small_grad0, small_grad1, res_grad), (qkv_grad0, out_grad0), quarter1, (up0_sent, down0_sent))
        pairs = (
            ((gate0, gate0_came), (gate1, gate1_came)), ((up0, up0_came), (up1, up1_came)),
            ((down0, down0_came), (down1, down1_came)))
        qkv_grad, out_grad, gate_grad, up_grad, down_grad, router_grad, const_grad, gains_grad, vector_grad, residual_grad = (
            stack_results(packed, qkv_grad, out_grad, pairs, depth))
        router_grad = jnp.transpose(router_grad, (1, 2, 0))
        const_grad = jnp.swapaxes(const_grad, 2, 3)
    else:
        gate_grad, up_grad, down_grad = (
            jnp.stack([
                pair_sum(grads[at * len(grads) // 3 : (at + 1) * len(grads) // 3], axis, spread)
                for grads in (expert_grads0, expert_grads1)])
            for axis, at in ((2, 0), (2, 1), (1, 2)))
        packed = jnp.concatenate([small_grad0, small_grad1, jnp.pad(res_grad[:16], ((0, 0), (0, width - 128)))])
        packed = lax.psum(packed, ("dp", "expert"))
        qkv_grad, out_grad = (
            lax.psum(lax.psum_scatter(jnp.stack(pair), "dp", scatter_dimension=1, tiled=True), "expert")
            for pair in ((qkv_grad0, qkv_grad1), (out_grad0, out_grad1)))
        mine = lax.dynamic_slice_in_dim(packed, lax.axis_index("dp") * depth, depth, axis=1)
        mine = jnp.stack([mine[:24], mine[24:48]])
        router_grad = jnp.swapaxes(mine[:, :CONST0], 1, 2)
        const_grad = jnp.swapaxes(mine[:, CONST0:GAIN0].reshape(layers, 2, 2, depth), 2, 3)
        residual_grad = packed[48 : 48 + CONST0, :CONST0]
        gains_grad, vector_grad = mine[:, GAIN0 : GAIN0 + 2], mine[:, VECTOR0 : VECTOR0 + 2]
    return (
        output, tokens_grad, gains_grad, jnp.swapaxes(qkv_grad, 1, 2), out_grad, router_grad,
        residual_grad, const_grad, vector_grad, gate_grad, up_grad, down_grad,
    )


def solution(mesh):
    in_specs = (
        P(("dp", "expert"), None), P("dp", None, None), P("dp", None), P(None, ("dp", "expert"), None),
        P(None, None, "dp"), P(None, None, "dp"), P(None, "dp", None), P(None, "dp", None), P(),
        P(None, None, "dp", None), P(None, None, "dp"), P(None, "expert", None, "dp"), P(None, "expert", None, "dp"),
        P(None, "expert", "dp", None), P(("dp", "expert"), None),
    )
    out_specs = (
        P(("dp", "expert"), None), P(("dp", "expert"), None), P(None, None, "dp"), P(None, None, "dp"),
        P(None, "dp", None), P(None, "dp", None), P(), P(None, None, "dp", None), P(None, None, "dp"),
        P(None, "expert", None, "dp"), P(None, "expert", None, "dp"), P(None, "expert", "dp", None),
    )
    return jax.shard_map(per_device, mesh=mesh, in_specs=in_specs, out_specs=out_specs, check_vma=False)
```

```python
import functools

import jax
import jax.numpy as jnp
from jax import lax
from jax.experimental import pallas as pl
from jax.experimental.pallas import tpu as pltpu
from jax.sharding import PartitionSpec as P

HEADS = 12
CAP = 48
LINE = 4
EPSILON = 1e-05
MASKED = -1e30
HIGH = lax.Precision.HIGHEST
F32 = jnp.float32
BF16 = jnp.bfloat16
MESH = pl.DeviceIdType.MESH
VMEM = pl.BlockSpec(memory_space=pltpu.VMEM)
ANY = pl.BlockSpec(memory_space=pl.ANY)

CONST0, GAIN0, VECTOR0 = 12, 16, 18
STAT = {
    name: i
    for i, name in enumerate(
        ("r0", "r1", "share0", "share1", "slot0", "slot1", "p00", "p01", "p10", "p11")
    )
}


SMEM = pl.BlockSpec(memory_space=pltpu.SMEM)


def dot_nn(a, b, **kw):
    return lax.dot_general(a, b, (((1,), (0,)), ((), ())), preferred_element_type=F32, **kw)


def dot_nt(a, b, **kw):
    return lax.dot_general(a, b, (((1,), (1,)), ((), ())), preferred_element_type=F32, **kw)


def dot_tn(a, b, **kw):
    return lax.dot_general(a, b, (((0,), (0,)), ((), ())), preferred_element_type=F32, **kw)


def thirds(values):
    out = []
    for _ in range(3):
        out.append(values.astype(BF16))
        values = values - out[-1].astype(F32)
    return out


def lanes(rows, width=128):
    return lax.broadcasted_iota(jnp.int32, (rows, width), 1)


def rms_scale(values):
    return lax.rsqrt(jnp.mean(values * values, axis=-1, keepdims=True) + EPSILON)


def row_vectors(small):
    pick = lax.broadcasted_iota(jnp.int32, (8, 128), 0) + GAIN0 == lanes(8)
    rows = dot_nt(pick.astype(BF16), small)
    return rows[0:1], rows[1:2], rows[2:3], rows[3:4]


def stat_columns(stat):
    return {name: stat[:, i : i + 1] for name, i in STAT.items()}


def slot_picks(stat, slots):
    place = lanes(stat["slot0"].shape[0], slots).astype(F32)
    first = (place == stat["slot0"]).astype(BF16)
    second = (place == stat["slot1"]).astype(BF16)
    return first, second


def const_weights(stat, experts):
    out = []
    for kind in (experts + 1, experts + 2, experts + 3):
        out.append(
            stat["share0"] * (stat["r0"] == kind).astype(F32)
            + stat["share1"] * (stat["r1"] == kind).astype(F32)
        )
    return out


def doc_index(lengths, places):
    place, end = lax.axis_index("expert"), 0
    doc = jnp.zeros_like(places)
    for j in range(lengths.shape[2]):
        end = end + lengths[0, place, j]
        doc = doc + (places >= end).astype(jnp.int32)
    return doc


def block_routes(perm, routes_all, layer, rows):
    mine = routes_all[perm[0, lax.axis_index("expert")]].astype(F32)
    routes = jnp.transpose(mine)[:rows].astype(jnp.int32)
    return routes[:, 2 * layer : 2 * layer + 1], routes[:, 2 * layer + 1 : 2 * layer + 2]


def padded(w_res, ref):
    count = w_res.shape[0]
    ref[...] = jnp.zeros(ref.shape, F32)
    ref[0:count, 0:count] = w_res[...]
    return ref[...]


def attend_part(stream, small, w_qkv_t, w_out, lengths, attn_in_ref, qkv_ref, probs_ref, attn_ref):
    rows, width = stream.shape
    gain, _, _, _ = row_vectors(small)
    attn_in_ref[...] = (stream * rms_scale(stream) * gain).astype(BF16)

    def project(i, carry):
        at = pl.multiple_of(i * width, width)
        qkv_ref[:, pl.ds(at, width)] = dot_nt(
            attn_in_ref[...], w_qkv_t[pl.ds(at, width), :]
        ).astype(BF16)
        return carry

    lax.fori_loop(0, 3, project, 0, unroll=True)
    head_dim = width // HEADS
    factor = 1.0 / head_dim**0.5
    allowed = jnp.logical_and(
        doc_index(lengths, lax.broadcasted_iota(jnp.int32, (rows, 1), 0))
        == doc_index(lengths, lax.broadcasted_iota(jnp.int32, (1, rows), 1)),
        lax.broadcasted_iota(jnp.int32, (rows, rows), 0)
        >= lax.broadcasted_iota(jnp.int32, (rows, rows), 1),
    )

    def heads(i, carry):
        at = pl.multiple_of(i * 2 * head_dim, 2 * head_dim)
        query = qkv_ref[:, pl.ds(at, 2 * head_dim)]
        key = qkv_ref[:, pl.ds(pl.multiple_of(at + width, 128), 2 * head_dim)]
        value = qkv_ref[:, pl.ds(pl.multiple_of(at + 2 * width, 128), 2 * head_dim)]
        second = lanes(rows, 2 * head_dim) >= head_dim
        mixed = []
        for sub in (0, 1):
            mine = second if sub else jnp.logical_not(second)
            scores = dot_nt(jnp.where(mine, query, jnp.zeros_like(query)), key) * factor
            scores = jnp.where(allowed, scores, MASKED)
            exponent = jnp.exp(scores - jnp.max(scores, axis=-1, keepdims=True))
            probs = exponent / jnp.sum(exponent, axis=-1, keepdims=True)
            probs_ref[2 * i + sub] = probs
            mixed.append(dot_nn(probs.astype(BF16), value))
        attn_ref[:, pl.ds(at, 2 * head_dim)] = jnp.where(second, mixed[1], mixed[0]).astype(BF16)
        return carry

    lax.fori_loop(0, HEADS // 2, heads, 0, unroll=True)
    return stream + dot_nn(attn_ref[...], w_out[...])


def route_part(mid, small, routes, prev_logits, w_res, experts):
    rows = mid.shape[0]
    _, gain, _, _ = row_vectors(small)
    hidden = (mid * rms_scale(mid) * gain).astype(BF16)
    lane = lanes(rows)
    raw = dot_nn(hidden, small)
    logits = jnp.where(lane < CONST0, raw, 0.0)
    if prev_logits is not None:
        logits = logits + dot_nn(prev_logits, w_res, precision=HIGH)
    r0, r1 = routes
    hot0, hot1 = (lane == r0).astype(F32), (lane == r1).astype(F32)
    c0 = jnp.sum(hot0 * logits, axis=-1, keepdims=True)
    c1 = jnp.sum(hot1 * logits, axis=-1, keepdims=True)
    peak = jnp.maximum(c0, c1)
    e0, e1 = jnp.exp(c0 - peak), jnp.exp(c1 - peak)
    total = e0 + e1
    share0, share1 = e0 / total, e1 / total
    probs = []
    for j in (0, 1):
        a = raw[:, CONST0 + 2 * j : CONST0 + 2 * j + 1]
        b = raw[:, CONST0 + 2 * j + 1 : CONST0 + 2 * j + 2]
        top = jnp.maximum(a, b)
        ea, eb = jnp.exp(a - top), jnp.exp(b - top)
        probs += [ea / (ea + eb), eb / (ea + eb)]
    earlier = lax.broadcasted_iota(jnp.int32, (rows, rows), 0) > lax.broadcasted_iota(
        jnp.int32, (rows, rows), 1
    )
    before = dot_nn(earlier.astype(BF16), (hot0 + hot1).astype(BF16))
    f0, f1 = r0.astype(F32), r1.astype(F32)
    slot0 = jnp.where(
        r0 < experts, f0 * CAP + jnp.sum(before * hot0, axis=-1, keepdims=True), -1.0
    )
    slot1 = jnp.where(
        r1 < experts, f1 * CAP + jnp.sum(before * hot1, axis=-1, keepdims=True), -1.0
    )
    stat = jnp.zeros((rows, 128), F32)
    for i, column in enumerate([f0, f1, share0, share1, slot0, slot1] + probs):
        stat = jnp.where(lane == i, column, stat)
    first, second = slot_picks({"slot0": slot0, "slot1": slot1}, experts * CAP)
    outgoing = dot_tn(first + second, hidden).astype(BF16)
    return logits, stat, outgoing


def combine_part(mid, small, stat, returned, experts):
    _, gain, vec0, vec1 = row_vectors(small)
    hidden_full = mid * rms_scale(mid) * gain
    first, second = slot_picks(stat, experts * CAP)
    pair0, pair1 = dot_nn(first, returned), dot_nn(second, returned)
    copy, const0, const1 = const_weights(stat, experts)
    local = copy + const0 * stat["p00"] + const1 * stat["p10"]
    moe = stat["share0"] * pair0 + stat["share1"] * pair1 + local * hidden_full
    moe = moe + (const0 * stat["p01"]) * vec0 + (const1 * stat["p11"]) * vec1
    return mid + moe, hidden_full, pair0, pair1


def share_backward(grad, small, stat, hidden_full, pair0, pair1, extra, experts):
    rows = grad.shape[0]
    _, _, vec0, vec1 = row_vectors(small)
    first, second = slot_picks(stat, experts * CAP)
    lane = lanes(rows).astype(F32)
    rowsum = functools.partial(jnp.sum, axis=-1, keepdims=True)
    dot_hidden = rowsum(grad * hidden_full)
    dot_vec = (rowsum(grad * vec0), rowsum(grad * vec1))
    _, const0, const1 = const_weights(stat, experts)
    probs = ((stat["p00"], stat["p01"]), (stat["p10"], stat["p11"]))
    value = [probs[j][0] * dot_hidden + probs[j][1] * dot_vec[j] for j in (0, 1)]
    shares = []
    for r, pair in ((stat["r0"], pair0), (stat["r1"], pair1)):
        shares.append(
            rowsum(grad * pair)
            + (r == experts + 1).astype(F32) * dot_hidden
            + (r == experts + 2).astype(F32) * value[0]
            + (r == experts + 3).astype(F32) * value[1]
        )
    inner = stat["share0"] * shares[0] + stat["share1"] * shares[1]
    g_small = (lane == stat["r0"]).astype(F32) * (stat["share0"] * (shares[0] - inner))
    g_small = g_small + (lane == stat["r1"]).astype(F32) * (stat["share1"] * (shares[1] - inner))
    if extra is not None:
        g_small = g_small + extra
    g_logits = g_small
    for j, weight in ((0, const0), (1, const1)):
        q = (weight * dot_hidden, weight * dot_vec[j])
        mean = probs[j][0] * q[0] + probs[j][1] * q[1]
        for c in (0, 1):
            g_small = jnp.where(lane == CONST0 + 2 * j + c, probs[j][c] * (q[c] - mean), g_small)
    sent0 = (jnp.where(stat["r0"] < experts, stat["share0"], 0.0) * grad).astype(BF16)
    sent1 = (jnp.where(stat["r1"] < experts, stat["share1"], 0.0) * grad).astype(BF16)
    outgoing = (dot_tn(first, sent0) + dot_tn(second, sent1)).astype(BF16)
    hidden = hidden_full.astype(BF16)
    projections = sum(dot_tn(part, hidden) for part in thirds(g_small)[::-1])
    vector0 = jnp.sum((const0 * stat["p01"]) * grad, axis=0, keepdims=True)
    vector1 = jnp.sum((const1 * stat["p11"]) * grad, axis=0, keepdims=True)
    return g_small, g_logits, outgoing, projections, vector0, vector1


def store_small(ref, projections, vector0, vector1):
    ref[0:16, :] = projections[0:16]
    ref[16:24, :] = jnp.zeros((8, ref.shape[1]), F32)
    ref[VECTOR0 : VECTOR0 + 1, :] = vector0
    ref[VECTOR0 + 1 : VECTOR0 + 2, :] = vector1


def first_kernel(experts, tokens, small, w_qkv_t, w_out, lengths, perm, routes_all,
                 attn_in, qkv, probs, attn, mid_ref, logits_ref, stat_ref, out_ref):
    mid = attend_part(tokens[...].astype(F32), small[...], w_qkv_t, w_out, lengths, attn_in, qkv, probs, attn)
    mid_ref[...] = mid
    routes = block_routes(perm, routes_all, 0, mid.shape[0])
    logits, stat, out = route_part(mid, small[...], routes, None, None, experts)
    logits_ref[...], stat_ref[...], out_ref[...] = logits, stat, out


def middle_kernel(experts, mid_in, small_in, stat_in, returned, small, w_qkv_t, w_out, lengths, perm, routes_all, logits_in, w_res,
                  stream_ref, attn_in, qkv, probs, attn, mid_ref, stat_ref, out_ref, res_ref):
    stream, _, _, _ = combine_part(mid_in[...], small_in[...], stat_columns(stat_in[...]), returned[...], experts)
    stream_ref[...] = stream
    mid = attend_part(stream, small[...], w_qkv_t, w_out, lengths, attn_in, qkv, probs, attn)
    mid_ref[...] = mid
    routes = block_routes(perm, routes_all, 1, mid.shape[0])
    _, stat, out = route_part(mid, small[...], routes, logits_in[...], padded(w_res, res_ref), experts)
    stat_ref[...], out_ref[...] = stat, out


def turn_kernel(experts, mid, small, stat_in, returned, cotangent, logits_in, w_res,
                output, g_small_ref, extra_ref, out_ref, small_grad, res_grad, res_ref):
    stat = stat_columns(stat_in[...])
    stream, hidden_full, pair0, pair1 = combine_part(mid[...], small[...], stat, returned[...], experts)
    output[...] = stream.astype(BF16)
    grad = cotangent[...].astype(F32)
    g_small, g_logits, out, projections, v0, v1 = share_backward(grad, small[...], stat, hidden_full, pair0, pair1, None, experts)
    g_small_ref[...] = g_small
    out_ref[...] = out
    store_small(small_grad, projections, v0, v1)
    res_grad[...] = dot_tn(logits_in[...], g_logits, precision=HIGH)
    extra_ref[...] = dot_nt(g_logits, padded(w_res, res_ref), precision=HIGH)


def layer_backward(experts, grad, back, g_small, stat, mid, small, stream, w_qkv_t, w_out, attn_in, qkv, probs, attn,
                   qkv_grad, out_grad, small_grad, g_qkv, g_attn):
    rows, width = mid.shape
    gain1, gain2, _, _ = row_vectors(small)
    first, second = slot_picks(stat, experts * CAP)
    copy, const0, const1 = const_weights(stat, experts)
    local = copy + const0 * stat["p00"] + const1 * stat["p10"]
    g_full = sum(dot_nt(part, small) for part in thirds(g_small)[::-1]) + dot_nn(first + second, back)
    g_full = g_full + grad * local
    s2 = rms_scale(mid)
    small_grad[GAIN0 + 1 : GAIN0 + 2, :] = jnp.sum(g_full * mid * s2, axis=0, keepdims=True)
    m = g_full * gain2
    g_mid = grad + s2 * m - mid * (s2 * s2 * s2 * jnp.mean(m * mid, axis=-1, keepdims=True))
    branch = g_mid.astype(BF16)
    out_grad[...] = dot_tn(attn[...], branch).astype(out_grad.dtype)
    g_attn[...] = dot_nt(branch, w_out[...]).astype(BF16)
    head_dim = width // HEADS
    factor = 1.0 / head_dim**0.5

    def heads(i, carry):
        at = pl.multiple_of(i * 2 * head_dim, 2 * head_dim)
        at_k = pl.multiple_of(at + width, 128)
        at_v = pl.multiple_of(at + 2 * width, 128)
        query = qkv[:, pl.ds(at, 2 * head_dim)]
        key = qkv[:, pl.ds(at_k, 2 * head_dim)]
        value = qkv[:, pl.ds(at_v, 2 * head_dim)]
        ga = g_attn[:, pl.ds(at, 2 * head_dim)]
        second_half = lanes(rows, 2 * head_dim) >= head_dim
        gq, gk, gv = [], [], []
        for sub in (0, 1):
            mine = second_half if sub else jnp.logical_not(second_half)
            p = probs[2 * i + sub]
            gp = dot_nt(jnp.where(mine, ga, jnp.zeros_like(ga)), value)
            gs = (p * (gp - jnp.sum(p * gp, axis=-1, keepdims=True))).astype(BF16)
            gq.append(dot_nn(gs, key))
            gk.append(dot_tn(gs, query))
            gv.append(dot_tn(p.astype(BF16), ga))
        g_qkv[:, pl.ds(at, 2 * head_dim)] = (jnp.where(second_half, gq[1], gq[0]) * factor).astype(BF16)
        g_qkv[:, pl.ds(at_k, 2 * head_dim)] = (jnp.where(second_half, gk[1], gk[0]) * factor).astype(BF16)
        g_qkv[:, pl.ds(at_v, 2 * head_dim)] = jnp.where(second_half, gv[1], gv[0]).astype(BF16)
        return carry

    lax.fori_loop(0, HEADS // 2, heads, 0, unroll=True)

    def weights(i, carry):
        at = pl.multiple_of(i * width, width)
        qkv_grad[pl.ds(at, width), :] = dot_tn(g_qkv[:, pl.ds(at, width)], attn_in[...]).astype(qkv_grad.dtype)
        return carry + dot_nn(g_qkv[:, pl.ds(at, width)], w_qkv_t[pl.ds(at, width), :])

    g_in = lax.fori_loop(0, 3, weights, jnp.zeros((rows, width), F32))
    s1 = rms_scale(stream)
    small_grad[GAIN0 : GAIN0 + 1, :] = jnp.sum(g_in * stream * s1, axis=0, keepdims=True)
    n = g_in * gain1
    return g_mid + s1 * n - stream * (s1 * s1 * s1 * jnp.mean(n * stream, axis=-1, keepdims=True))


def between_kernel(experts, cotangent, back, g_small, stat_in, mid, small, stream, w_qkv_t, w_out, attn_in, qkv, probs, attn, small_grad_in,
                   mid0, small0, stat0_in, returned0, extra,
                   qkv_grad, out_grad, small_grad, grad_ref, g_small0_ref, out_ref, small_grad0, g_qkv, g_attn):
    small_grad[...] = small_grad_in[...]
    grad = layer_backward(experts, cotangent[...].astype(F32), back[...], g_small[...], stat_columns(stat_in[...]), mid[...],
                          small[...], stream[...], w_qkv_t, w_out, attn_in, qkv, probs, attn, qkv_grad, out_grad, small_grad, g_qkv, g_attn)
    grad_ref[...] = grad
    stat0 = stat_columns(stat0_in[...])
    _, hidden_full, pair0, pair1 = combine_part(mid0[...], small0[...], stat0, returned0[...], experts)
    g_small0, _, out, projections, v0, v1 = share_backward(grad, small0[...], stat0, hidden_full, pair0, pair1, extra[...], experts)
    g_small0_ref[...] = g_small0
    out_ref[...] = out
    store_small(small_grad0, projections, v0, v1)


def last_kernel(experts, grad_in, back, g_small, stat_in, mid, small, tokens, w_qkv_t, w_out, attn_in, qkv, probs, attn, small_grad_in,
                qkv_grad, out_grad, small_grad, grad_ref, g_qkv, g_attn):
    small_grad[...] = small_grad_in[...]
    grad_ref[...] = layer_backward(experts, grad_in[...], back[...], g_small[...], stat_columns(stat_in[...]), mid[...], small[...],
                                   tokens[...].astype(F32), w_qkv_t, w_out, attn_in, qkv, probs, attn, qkv_grad, out_grad, small_grad,
                                   g_qkv, g_attn)


def local_call(kernel, experts, args, outs, scratch=(), scalars=()):
    return pl.pallas_call(
        functools.partial(kernel, experts),
        out_shape=[jax.ShapeDtypeStruct(shape, dtype) for shape, dtype in outs],
        in_specs=[SMEM if i in scalars else VMEM for i in range(len(args))],
        out_specs=[VMEM] * len(outs),
        scratch_shapes=[pltpu.VMEM(shape, dtype) for shape, dtype in scratch],
        compiler_params=pltpu.CompilerParams(vmem_limit_bytes=60 * 2**20),
        cost_estimate=pl.CostEstimate(flops=10**10, bytes_accessed=6 * 10**7, transcendentals=0),
    )(*args)


class Place:
    def __init__(self, spread):
        self.spread = spread
        self.d, self.e = lax.axis_index("dp"), lax.axis_index("expert")
        self.t, self.f = self.d // spread, lax.rem(self.d, spread)
        self.y, self.c = self.e // 2, lax.rem(self.e, 2)
        self.above, self.below = self.t < LINE - 1, self.t > 0
        self.inside = jnp.logical_and(self.above, self.below)
        self.up = jnp.where(self.t == 1, 1, 0)
        self.ahead = 2 * self.up - 1
        self.sibling = (self.d, self.e + 1 - 2 * self.c)
        self.across = (self.d, lax.rem(self.e + 2, 4))
        self.corner = (self.d, 3 - self.e)
        self.beside = (self.t * spread + 1 - self.f, self.e)
        self.mates = [(self.d, self.e), self.sibling, self.across, self.corner]

    def block(self, i):
        return pick(i, [e for _, e in self.mates])

    def on_line(self, up):
        return (self.d + self.spread * (2 * up - 1), self.e)


def pick(index, values):
    out = values[-1]
    for n in range(len(values) - 2, -1, -1):
        out = jnp.where(index == n, values[n], out)
    return out


def greet(always, place, meanwhile=lambda: None):
    barrier = pltpu.get_barrier_semaphore()
    for device in always:
        pl.semaphore_signal(barrier, inc=1, device_id=device, device_id_type=MESH)
    for up, there in ((1, place.above), (0, place.below)):

        @pl.when(there)
        def _(up=up):
            pl.semaphore_signal(barrier, inc=1, device_id=place.on_line(up), device_id_type=MESH)

    meanwhile()
    ends = place.above.astype(jnp.int32) + place.below.astype(jnp.int32)
    pl.semaphore_wait(barrier, len(always) + ends)


def remote(src, dst, send, recv, device):
    return pltpu.make_async_remote_copy(
        src_ref=src, dst_ref=dst, send_sem=send, recv_sem=recv, device_id=device, device_id_type=MESH)


def dma(*shape):
    return pltpu.SemaphoreType.DMA(shape)


def along(place, body, start=0):
    if start == 0:
        body(place.t)

    def step(k, carry):
        for t in (place.t + k, place.t - k):

            @pl.when(jnp.logical_and(t >= 0, t < LINE))
            def _(t=t):
                body(t)

        return carry

    lax.fori_loop(1, LINE, step, 0)


class Rider:
    partners = ()

    def begin(self):
        pass

    def ready(self):
        pass

    def after_first(self):
        pass

    def in_line(self):
        pass

    def after_relay(self):
        pass

    def finish(self):
        pass


class Line:
    def __init__(self, place, x, part, stage, arrived, final, returned, sems):
        self.p = place
        self.x, self.part, self.stage, self.arrived = x, part, stage, arrived
        self.final, self.returned = final, returned
        (self.out_send, self.x_recv, self.x_send, self.sum_send, self.sum_recv, self.ret_send, self.ret_recv) = sems

    @staticmethod
    def scratch(local, width):
        shape = (local, 4, CAP, width)
        return [
            pltpu.VMEM((local, LINE, 4, CAP, width), BF16),
            pltpu.VMEM((LINE,) + shape, F32),
            pltpu.VMEM((LINE,) + shape, BF16),
            pltpu.VMEM((2, LINE) + shape, BF16),
            pltpu.VMEM((4, local, CAP, width), BF16),
            dma(4), dma(LINE, 4), dma(2, LINE, 4), dma(LINE, 4), dma(2, LINE, 4), dma(4), dma(4),
        ]

    def slot_copy(self, out, i):
        to, p = self.p.mates[i], self.p
        return remote(out.at[to[1]], self.x.at[:, p.t, p.e], self.out_send.at[i], self.x_recv.at[p.t, p.e], to)

    def x_copy(self, up, s, b):
        at = self.x.at[:, s, b]
        return remote(at, at, self.x_send.at[up, s, b], self.x_recv.at[s, b], self.p.on_line(up))

    def sum_copy(self, up, s, b):
        return remote(self.stage.at[s, :, b], self.arrived.at[up, s, :, b], self.sum_send.at[s, b],
                      self.sum_recv.at[up, s, b], self.p.on_line(up))

    def ret_copy(self, i, to_mate=True):
        to = self.p.block(i)
        row = self.p.e if to_mate else to
        return remote(self.final.at[to], self.returned.at[row], self.ret_send.at[i], self.ret_recv.at[row], (self.p.d, to))

    def send_sum(self, up, s, b, total):
        self.stage[s, :, b] = total.astype(BF16)
        self.sum_copy(up, s, b).start()

    def relay(self, n):
        p = self.p
        kind = pick(n, (0, 0, 1, 1, 2, 1, 2, 1, 2, 0, 2, 0))
        b = p.block(pick(n, (0, 1, 0, 1, 0, 2, 1, 3, 2, 2, 3, 3)))
        s = p.t + p.ahead * pick(kind, (1, 2, -1))
        way = jnp.where(kind == 2, 1 - p.up, p.up)

        @pl.when(p.inside)
        def _():
            self.sum_copy(way, s, b).wait_recv()
            self.send_sum(way, s, b, self.part[s, :, b] + self.arrived[way, s, :, b].astype(F32))

    def run(self, out, compute, kept, pieces, rider):
        p = self.p
        t, e = p.t, p.e
        blocks = [b for _, b in p.mates]
        greet(p.mates[1:] + list(rider.partners), p)
        for i in (2, 3, 1):
            self.slot_copy(out, i).start()
        self.x[:, t, e] = out[e]
        rider.begin()
        for i in range(4):
            if i:
                self.x_copy(0, t, blocks[i]).wait_recv()
            for up, there in ((0, p.below), (1, p.above)):

                @pl.when(there)
                def _(up=up, i=i):
                    self.x_copy(up, t, blocks[i]).start()

        rider.ready()

        def step(n, carry):
            k = jnp.where(n < 2, 1, jnp.where(jnp.logical_or(n == 2, n == 5), 2, 3))
            half = jnp.where(jnp.logical_or(n == 1, n >= 4), 1, 0)
            pair = p.y + half - 2 * p.y * half
            first = jnp.where(half == 0, blocks[0], blocks[2])
            second = jnp.where(half == 0, blocks[1], blocks[3])
            for b in (first, second):
                for up, there, onward, before_end in ((0, t + k < LINE, p.below, t == 1), (1, t - k >= 0, p.above, t == LINE - 2)):
                    s = t - k if up else t + k
                    put_off = jnp.logical_and(before_end, n == 1)

                    @pl.when(there)
                    def _(up=up, onward=onward, s=s, b=b, put_off=put_off):
                        self.x_copy(up, s, b).wait_recv()

                        @pl.when(jnp.logical_and(onward, jnp.logical_not(put_off)))
                        def _():
                            self.x_copy(up, s, b).start()

            for up, before_end in ((0, t == 1), (1, t == LINE - 2)):

                @pl.when(jnp.logical_and(before_end, n == 5))
                def _(up=up):
                    for b in (first, second):
                        self.x_copy(up, t - 1 if up else t + 1, b).start()

            @pl.when(jnp.logical_not(p.inside))
            def _():
                s = jnp.where(t == 0, k, LINE - 1 - k)
                compute(s, 2 * pair, 2)

                @pl.when(half == 1)
                def _():
                    kept(s)

            for up, starts, s in ((1, t == 0, k), (0, t == LINE - 1, LINE - 1 - k)):

                @pl.when(starts)
                def _(up=up, s=s):
                    for b in (first, second):
                        self.send_sum(up, s, b, self.part[s, :, b])

            rest = jnp.logical_and(p.inside, jnp.logical_or(n == 5, jnp.logical_and(n >= 1, n <= 2)))

            @pl.when(jnp.logical_or(n == 0, rest))
            def _():
                s = t + p.ahead * jnp.where(n == 0, 0, jnp.where(n == 1, 1, jnp.where(n == 2, -1, 2)))
                compute(s, 0, 4)
                kept(s)

            @pl.when(n == 0)
            def _():
                rider.after_first()

            @pl.when(n == 3)
            def _():
                rider.in_line()

            return carry

        lax.fori_loop(0, 6, step, 0)

        def passing(n, carry):
            self.relay(n)
            pieces(n)
            return carry

        lax.fori_loop(0, 12, passing, 0)
        rider.after_relay()

        def end(i, carry):
            b = p.block(i)
            for up, there in ((1, p.below), (0, p.above)):

                @pl.when(there)
                def _(up=up):
                    self.sum_copy(up, t, b).wait_recv()
                    self.part[t, :, b] = self.part[t, :, b] + self.arrived[up, t, :, b].astype(F32)

            self.final[b] = self.part[t, :, b].astype(BF16)

            @pl.when(i > 0)
            def _():
                self.ret_copy(i).start()

            return carry

        lax.fori_loop(0, 4, end, 0)
        self.returned[e] = self.final[e]

        def sent(n, carry):
            s, b = n // 4, lax.rem(n, 4)
            for up, mine in ((0, jnp.logical_and(p.below, s >= t)), (1, jnp.logical_and(p.above, s <= t))):

                @pl.when(mine)
                def _(up=up):
                    self.x_copy(up, s, b).wait_send()

            @pl.when(s != t)
            def _():
                self.sum_copy(0, s, b).wait_send()

            return carry

        for i in (1, 2, 3):
            self.slot_copy(out, i).wait_send()
        lax.fori_loop(0, 4 * LINE, sent, 0)
        rider.finish()
        for i in (1, 2, 3):
            self.ret_copy(i).wait_send()
            self.ret_copy(i, False).wait_recv()


def split(refs, *counts):
    out, at = [], 0
    for count in counts:
        out.append(refs[at : at + count])
        at += count
    return out + [refs[at:]]


def expert_forward_kernel(spread, parts, late, ride, out, *refs):
    weights_in, given, outs, late_out, whole, scratch, line_refs, sems, ride_refs = split(
        refs, 3 * parts, 8 if ride else 0, 4, late, 5 if ride else 0, 3 * parts, 5, 7)
    (g_all, u_all, keep_sem, load_sem, late_sem), ride_refs = ride_refs[:5], ride_refs[5:]
    returned, x_keep, g_keep, u_keep = outs
    gate, up, down = scratch[:parts], scratch[parts : 2 * parts], scratch[2 * parts :]
    x, part, stage, arrived, final = line_refs
    local, _, _, _, width = x.shape
    p = Place(spread)
    line = Line(p, x, part, stage, arrived, final, returned, sems)
    rider = WeightRider(p, given, whole, ride_refs) if ride else Rider()

    def load(i):
        given = weights_in[i].shape[0]
        return pltpu.make_async_copy(weights_in[i], scratch[i].at[0:given], load_sem.at[i])

    for i in range(3 * parts):
        load(i).start()

    def late_copy():
        return remote(weights_in[-2].at[1:local], scratch[-1].at[1:local], late_sem.at[0], late_sem.at[1], p.beside)

    def late_store():
        return pltpu.make_async_copy(scratch[-1], late_out[0], late_sem.at[2])

    def keep_x(s):
        return pltpu.make_async_copy(x.at[:, s], x_keep.at[:, s], keep_sem.at[0, s])

    def keep_g(s):
        return pltpu.make_async_copy(g_all.at[s], g_keep.at[s], keep_sem.at[1, s])

    def keep_u(s):
        return pltpu.make_async_copy(u_all.at[s], u_keep.at[s], keep_sem.at[2, s])

    def kept(s):
        keep_x(s).start()
        keep_g(s).start()
        keep_u(s).start()

    def compute(s, first, count):
        rows = count * CAP
        at = pl.multiple_of(first * CAP, CAP)

        def one(l, carry):
            rows_in = x[l, s, pl.ds(first, count)].reshape(rows, width)
            total = jnp.zeros((rows, width), F32)
            for q in range(parts):
                cols = gate[q].shape[2]
                here = slice(q * cols, (q + 1) * cols)
                g = dot_nn(rows_in, gate[q][l])
                u = dot_nn(rows_in, up[q][l])
                g_all[s, l, pl.ds(at, rows), here] = g
                u_all[s, l, pl.ds(at, rows), here] = u
                act = (g * jax.nn.sigmoid(g) * u).astype(BF16)
                total = total + dot_nn(act, down[q][l])
            part[s, l, pl.ds(first, count)] = total.reshape(count, CAP, width)
            return carry

        lax.fori_loop(0, local, one, 0)

    class Loaded(Rider):
        partners = [p.beside] if late else []
        after_first, in_line, after_relay = rider.after_first, rider.in_line, rider.after_relay

        def begin(self):
            if late:
                late_copy().start()
            rider.begin()

        def ready(self):
            for i in range(3 * parts):
                load(i).wait()
            if late:
                late_copy().wait_recv()
                late_store().start()

        def finish(self):
            rider.finish()
            if late:
                late_copy().wait_send()
                late_store().wait()

    line.run(out, compute, kept, lambda n: None, Loaded())
    for s in range(LINE):
        keep_x(s).wait()
        keep_g(s).wait()
        keep_u(s).wait()


def expert_backward_kernel(spread, parts, exchange, ride, out, *refs):
    loads_in, given, outs, came, ride_outs, loads, line_refs, sems, rest = split(
        refs, 3 + 3 * parts, 4 if ride else 0, 1 + 3 * parts - exchange, exchange, 3 if ride else 0, 3 + 3 * parts, 5, 7)
    (act_all, gg_all, gu_all), grads, (load_sem, grad_sem, w_send, w_recv), ride_refs = split(rest, 3, 3 * parts, 4)
    returned, grads_out = outs[0], list(outs[1:])
    if exchange:
        grads_out.insert(1, None)
    x_in, g_all, u_all = loads[:3]
    gate, up, down = loads[3 : 3 + parts], loads[3 + parts : 3 + 2 * parts], loads[3 + 2 * parts :]
    x, part, stage, arrived, final = line_refs
    local, _, _, _, width = x.shape
    p = Place(spread)
    line = Line(p, x, part, stage, arrived, final, returned, sems)
    rider = GradientRider(p, given, ride_outs, ride_refs) if ride else Rider()

    def load(i):
        return pltpu.make_async_copy(loads_in[i], loads[i], load_sem.at[i])

    def store(i, l):
        return pltpu.make_async_copy(grads[i].at[l], grads_out[i].at[l], grad_sem.at[i, l])

    for i in range(3 + 3 * parts):
        load(i).start()

    def compute(s, first, count):
        rows = count * CAP
        at = pl.multiple_of(first * CAP, CAP)
        into = pl.ds(pl.multiple_of((4 * s + first) * CAP, CAP), rows)

        def one(l, carry):
            rows_in = x[l, s, pl.ds(first, count)].reshape(rows, width)
            total = jnp.zeros((rows, width), F32)
            for q in range(parts):
                cols = gate[q].shape[2]
                here = slice(q * cols, (q + 1) * cols)
                g, u = g_all[s, l, pl.ds(at, rows), here], u_all[s, l, pl.ds(at, rows), here]
                g_act = dot_nt(rows_in, down[q][l])
                sigma = jax.nn.sigmoid(g)
                swish = g * sigma
                gg = (g_act * u * sigma * (1.0 + g * (1.0 - sigma))).astype(BF16)
                gu = (g_act * swish).astype(BF16)
                act_all[l, into, here] = (swish * u).astype(BF16)
                gg_all[l, into, here] = gg
                gu_all[l, into, here] = gu
                total = total + dot_nt(gg, gate[q][l]) + dot_nt(gu, up[q][l])
            part[s, l, pl.ds(first, count)] = total.reshape(count, CAP, width)
            return carry

        lax.fori_loop(0, local, one, 0)

    def weights(kind, l):
        x_rows, g_rows = (a[l].reshape(LINE * 4 * CAP, width) for a in (x_in, x))
        value = dot_tn(act_all[l], g_rows) if kind == 2 else dot_tn(x_rows, (gg_all, gu_all)[kind][l])
        for q in range(parts):
            i = kind * parts + q
            cols = gate[q].shape[2]
            here = slice(q * cols, (q + 1) * cols)
            grads[i][l] = (value[here] if kind == 2 else value[:, here]).astype(grads[i].dtype)
            if grads_out[i] is not None:
                store(i, l).start()

    def pieces(n):
        for kind in range(3):
            at = n - 1 - 2 * local * kind

            @pl.when(jnp.logical_and(lax.rem(n, 2) == 1, jnp.logical_and(at >= 0, at < 2 * local)))
            def _(kind=kind, at=at):
                weights(kind, at // 2)

        @pl.when(n == 2 * local - 1)
        def _():
            for copy in sent_gate():
                copy.start()

    def sent_gate():
        return [remote(grads[1], came[0], w_send.at[0], w_recv.at[0], p.beside)] if exchange else []

    class Loaded(Rider):
        partners = [p.beside] if exchange else []
        after_first, in_line, after_relay, finish = (
            rider.after_first, rider.in_line, rider.after_relay, rider.finish)

        def begin(self):
            rider.begin()

        def ready(self):
            for i in range(3 + 3 * parts):
                load(i).wait()

    line.run(out, compute, lambda s: None, pieces, Loaded())
    for copy in sent_gate():
        copy.wait()
    for i in range(3 * parts):
        for l in range(local if grads_out[i] is not None else 0):
            store(i, l).wait()


def remote_params(call_id):
    return pltpu.CompilerParams(collective_id=call_id, has_side_effects=True, vmem_limit_bytes=61 * 2**20)


def struct(shape, dtype):
    return jax.ShapeDtypeStruct(tuple(shape), dtype)


def expert_forward(spread, call_id, out, weights, late=False, ride=None):
    parts = len(weights) // 3
    _, local, cap, width = out.shape
    columns = sum(w.shape[2] for w in weights[:parts])
    kept = (LINE, local, 4 * cap, columns)
    outs = [struct(out.shape, BF16), struct((local, LINE, 4, cap, width), BF16), struct(kept, F32), struct(kept, F32)]
    outs += [struct(weights[-2].shape, BF16)] * late
    scratch = [pltpu.VMEM((local,) + w.shape[1:], BF16) for w in weights] + Line.scratch(local, width)
    scratch += [pltpu.VMEM(kept, F32), pltpu.VMEM(kept, F32), dma(3, LINE), dma(3 * parts), dma(3)]
    more = ride or ()
    count = LINE * spread
    if ride:
        outs += [struct((count * s.shape[0], s.shape[1]), BF16) for s in ride[3:6]]
        outs += [struct(w.shape, BF16) for w in ride[6:]]
        scratch += WeightRider.scratch(count)
    return pl.pallas_call(
        functools.partial(expert_forward_kernel, spread, parts, int(late), ride is not None),
        out_shape=outs,
        in_specs=[VMEM] + [ANY] * (len(weights) - 1) + [VMEM if late else ANY] + [ANY] * len(more),
        out_specs=[VMEM] + [ANY] * (len(outs) - 1),
        scratch_shapes=scratch,
        compiler_params=remote_params(call_id),
        cost_estimate=pl.CostEstimate(flops=2 * 10**10, bytes_accessed=2 * 10**8, transcendentals=0),
    )(out, *weights, *more)


def expert_backward(spread, call_id, out, kept, weights, exchange=False, ride=None):
    parts = len(weights) // 3
    _, local, cap, width = out.shape
    columns = sum(w.shape[2] for w in weights[:parts])
    loads = list(kept) + list(weights)
    grads = [(w.shape, F32 if i % parts == 0 else BF16) for i, w in enumerate(weights)]
    wide = pltpu.VMEM((local, LINE * 4 * cap, columns), BF16)
    outs = [struct(out.shape, BF16)] + [struct(*g) for i, g in enumerate(grads) if not exchange or i != 1]
    if exchange:
        outs.append(struct(*grads[1]))
    specs = [VMEM] + [ANY] * len(grads)
    scratch = [pltpu.VMEM(a.shape, a.dtype) for a in loads] + Line.scratch(local, width)
    scratch += [wide] * 3 + [pltpu.VMEM(*g) for g in grads] + [dma(len(loads)), dma(len(grads), local), dma(1), dma(1)]
    more = ride or ()
    if ride:
        depths = [g.shape[0] // (LINE * spread) for g in ride[:2]]
        outs.append(struct((LINE, spread, sum(depths) // 2, width // 2), F32))
        outs += [struct(g.shape, BF16) for g in ride[2:]]
        specs += [VMEM, ANY, ANY]
        scratch += GradientRider.scratch(spread, depths, width)
    return pl.pallas_call(
        functools.partial(expert_backward_kernel, spread, parts, int(exchange), ride is not None),
        out_shape=outs,
        in_specs=[VMEM] + [ANY] * (len(loads) + len(more)),
        out_specs=specs,
        scratch_shapes=scratch,
        compiler_params=remote_params(call_id),
        cost_estimate=pl.CostEstimate(flops=4 * 10**10, bytes_accessed=2 * 10**8, transcendentals=0),
    )(out, *loads, *more)


def from_partner(array, shift, spread, groups):
    pairs = [
        (t * spread + (f + shift) % spread, t * spread + f) for t in range(groups) for f in range(spread)
    ]
    return lax.ppermute(array, "dp", pairs)


def to_partner(array, shift, spread, groups):
    pairs = [
        (t * spread + f, t * spread + (f + shift) % spread) for t in range(groups) for f in range(spread)
    ]
    return lax.ppermute(array, "dp", pairs)


def pair_weights(shard, axis, spread):
    parts = [shard] + [from_partner(shard, i, spread, LINE) for i in range(1, spread)]
    if shard.shape[axis] % 128:
        return [jnp.concatenate(parts, axis=axis)]
    return parts


def pair_sum(parts, axis, spread):
    if len(parts) == 1 and spread > 1:
        parts = jnp.split(parts[0], spread, axis=axis)
    total = parts[0]
    for i in range(1, spread):
        total = total + to_partner(parts[i].astype(BF16), i, spread, LINE).astype(F32)
    return total


class LineGather:
    def __init__(self, place, pairs, shards, quarters, sems):
        self.p, self.shards, self.quarters = place, shards, quarters
        self.send, self.recv, self.x_send, self.x_recv = sems
        self.columns = [place.f, 1 - place.f] if pairs else [0]

    @staticmethod
    def shapes(shards, columns):
        (a, wide), (b, _), (c, narrow) = shards
        return [(LINE, columns, a // 2, wide // 2), (LINE, columns, b // 2, wide // 2), (LINE, columns, c, narrow)]

    @staticmethod
    def scratch(columns):
        return [dma(2, LINE, columns, 3), dma(LINE, columns, 3), dma(3), dma(3)]

    def copy(self, kind, up, t, f):
        at = self.quarters[kind].at[t, f]
        return remote(at, at, self.send.at[up, t, f, kind], self.recv.at[t, f, kind], self.p.on_line(up))

    def x_copy(self, kind, f):
        at = self.quarters[kind].at[self.p.t, f]
        return remote(at, at, self.x_send.at[kind], self.x_recv.at[kind], self.p.beside)

    def both_ways(self, f):
        p = self.p
        for up, there in ((0, p.below), (1, p.above)):

            @pl.when(there)
            def _(up=up):
                for kind in range(3):
                    self.copy(kind, up, p.t, f).start()

    def begin(self):
        p, f = self.p, self.columns[0]
        for kind in (0, 1):
            half, wide = self.quarters[kind].shape[2:]
            self.quarters[kind][p.t, f] = self.shards[kind][
                pl.ds(pl.multiple_of(p.y * half, 16), half), pl.ds(pl.multiple_of(p.c * wide, 128), wide)]
        self.quarters[2][p.t, f] = self.shards[2][...]
        for kind in range(3 if len(self.columns) == 2 else 0):
            self.x_copy(kind, f).start()
        self.both_ways(f)

    def beside(self, then):
        for f in self.columns[1:]:
            for kind in range(3):
                self.x_copy(kind, f).wait_recv()
            self.both_ways(f)
            then(self.p.t, f)

    def step(self, k, then):
        p = self.p
        for f in self.columns:
            for up, there, onward in ((0, p.t + k < LINE, p.below), (1, p.t - k >= 0, p.above)):
                t = p.t - k if up else p.t + k

                @pl.when(there)
                def _(up=up, onward=onward, t=t, f=f):
                    for kind in range(3):
                        self.copy(kind, up, t, f).wait_recv()

                    @pl.when(onward)
                    def _():
                        for kind in range(3):
                            self.copy(kind, up, t, f).start()

                    then(t, f)

    def finish(self):
        p = self.p

        def line(t, carry):
            for up, mine in ((0, jnp.logical_and(p.below, t >= p.t)), (1, jnp.logical_and(p.above, t <= p.t))):

                @pl.when(mine)
                def _(up=up):
                    for f in self.columns:
                        for kind in range(3):
                            self.copy(kind, up, t, f).wait_send()

            return carry

        lax.fori_loop(0, LINE, line, 0)
        for f in self.columns[1:]:
            for kind in range(3):
                self.x_copy(kind, 1 - f).wait_send()


class Spread:
    def __init__(self, place, quarters, shards, whole, sems):
        self.p, self.quarters, self.shards, self.whole = place, quarters, shards, whole
        self.y_send, self.y_recv, self.c_send, self.c_recv, self.l_sem, self.s_sem = sems

    @staticmethod
    def scratch(count):
        return [dma(count, 2), dma(count, 2), dma(count, 2, 2), dma(count, 2, 2), dma(count, 3), dma(3)]

    def region(self, kind, s, y, c):
        depth = self.shards[kind].shape[0]
        if kind == 2:
            return self.whole[2].at[pl.ds(pl.multiple_of(s * depth, 16), depth)]
        half, wide = depth // 2, self.shards[kind].shape[1] // 2
        return self.whole[kind].at[
            pl.ds(pl.multiple_of(s * depth + y * half, 16), half), pl.ds(pl.multiple_of(c * wide, 128), wide)]

    def mine(self, kind, s):
        return self.region(kind, s, self.p.y, self.p.c)

    def y_copy(self, kind, src, s):
        return remote(src, self.mine(kind, s), self.y_send.at[s, kind], self.y_recv.at[s, kind], self.p.across)

    def y_came(self, kind, s):
        at = self.region(kind, s, 1 - self.p.y, self.p.c)
        return remote(at, at, self.y_send.at[s, kind], self.y_recv.at[s, kind], self.p.across)

    def c_copy(self, kind, src, s, y):
        return remote(src, self.region(kind, s, y, self.p.c), self.c_send.at[s, y, kind], self.c_recv.at[s, y, kind],
                      self.p.sibling)

    def c_came(self, kind, s, y):
        at = self.region(kind, s, y, 1 - self.p.c)
        return remote(at, at, self.c_send.at[s, y, kind], self.c_recv.at[s, y, kind], self.p.sibling)

    def local(self, kind, src, s):
        return pltpu.make_async_copy(src, self.mine(kind, s), self.l_sem.at[s, kind])

    def shard(self, kind):
        depth = self.shards[kind].shape[0]
        at = self.whole[kind].at[pl.ds(pl.multiple_of(self.p.d * depth, 16), depth)]
        return pltpu.make_async_copy(self.shards[kind], at, self.s_sem.at[kind])

    def own_shard(self):
        for kind in range(3):
            self.shard(kind).start()

    def push(self, s, sources, here=True):
        if here:
            for kind in range(3):
                self.local(kind, sources[kind], s).start()
        for kind in (0, 1):
            self.y_copy(kind, sources[kind], s).start()
            self.c_copy(kind, sources[kind], s, self.p.y).start()

    def across(self, s):
        for kind in (0, 1):
            self.y_came(kind, s).wait_recv()
            self.c_copy(kind, self.region(kind, s, 1 - self.p.y, self.p.c), s, 1 - self.p.y).start()

    def finish_shard(self, s, here=True):
        @pl.when(s != self.p.d)
        def _():
            for kind in range(3 if here else 0):
                self.local(kind, self.mine(kind, s), s).wait()
            for kind in (0, 1):
                self.y_came(kind, s).wait_send()
                for y in (0, 1):
                    self.c_came(kind, s, y).wait_send()
                    self.c_came(kind, s, y).wait_recv()

    def finish_own(self):
        for kind in range(3):
            self.shard(kind).wait()


class WeightRider:
    def __init__(self, place, given, whole, sems):
        self.p, self.quarters, self.own, self.other = place, given[:3], given[6:], whole[3:]
        self.w_send, self.w_recv, self.x_send, self.x_recv, *more = sems
        self.spread = Spread(place, self.quarters, given[3:6], whole[:3], more)

    @staticmethod
    def scratch(count):
        return [dma(2), dma(2), dma(LINE, 3), dma(LINE, 3)] + Spread.scratch(count)

    def place_of(self, t):
        return t * self.p.spread + self.p.f

    def beside_of(self, t):
        return t * self.p.spread + 1 - self.p.f

    def x_copy(self, kind, t, s):
        return remote(self.quarters[kind].at[t, 0], self.spread.mine(kind, s), self.x_send.at[t, kind],
                      self.x_recv.at[t, kind], self.p.beside)

    def weight(self, i):
        return remote(self.own[i], self.other[i], self.w_send.at[i], self.w_recv.at[i], self.p.beside)

    def begin(self):
        self.spread.own_shard()

        def body(t):
            for kind in range(3):
                self.x_copy(kind, t, self.place_of(t)).start()

            @pl.when(t != self.p.t)
            def _():
                self.spread.push(self.place_of(t), [q.at[t, 0] for q in self.quarters])

        along(self.p, body)
        for i in range(2):
            self.weight(i).start()

    def after_first(self):
        pass

    def in_line(self):
        def body(t):
            s = self.beside_of(t)
            for kind in range(3):
                self.x_copy(kind, t, s).wait_recv()
            self.spread.push(s, [self.spread.mine(kind, s) for kind in range(3)], here=False)

        along(self.p, body)

    def after_relay(self):
        along(self.p, lambda t: self.spread.across(self.place_of(t)), start=1)
        along(self.p, lambda t: self.spread.across(self.beside_of(t)))

    def finish(self):
        self.spread.finish_own()
        for i in range(2):
            self.weight(i).wait()

        def line(t, carry):
            for kind in range(3):
                self.x_copy(kind, t, self.place_of(t)).wait_send()
            self.spread.finish_shard(self.place_of(t))
            self.spread.finish_shard(self.beside_of(t), here=False)
            return carry

        lax.fori_loop(0, LINE, line, 0)


def pack_small(l, router, const, gains, vectors, rows, small):
    rows[...] = jnp.zeros(rows.shape, F32)
    for r in range(router.shape[0]):
        rows[r : r + 1, :] = router[r, l : l + 1, :]
    for j in (0, 1):
        rows[CONST0 + 2 * j : CONST0 + 2 * j + 2, :] = const[l, j]
    rows[GAIN0 : GAIN0 + 2, :] = gains[l]
    rows[VECTOR0 : VECTOR0 + 2, :] = vectors[l]
    place = lax.broadcasted_iota(jnp.int32, (rows.shape[0], 128), 0) == lanes(rows.shape[0])
    small[l] = dot_tn(rows[...].astype(BF16), place.astype(BF16)).astype(BF16)


def dense_gather_kernel(spread, qkv_wide, out_wide, router, const, gains, vectors, routes_in, *refs):
    p = Place(spread)
    wide, whole, quarters1, (routes_all,), own, firsts, partner, shards1_out, quarters0, loaded, rounded, shards, (rows, routes), rest = split(
        refs, 3, 3, 3, 1, 6, 2, 2, 3, 3, 3, 3, 3, 2)
    qkv, out, small = shards
    sems0, sems1, (r_send, r_recv, w_send, w_recv, load_sem, own_sem, first_sem, shard_sem), spread_sems = split(rest, 4, 4, 8)
    shards0, shards1 = ([ref.at[l] for ref in (qkv, out, small)] for l in (0, 1))
    line0 = LineGather(p, True, shards0, quarters0, sems0)
    line1 = LineGather(p, False, shards1, quarters1, sems1)
    spreading = Spread(p, quarters0, shards0, whole, spread_sems)

    def load(l, kind):
        return pltpu.make_async_copy(wide[kind].at[l], loaded[kind].at[l], load_sem.at[l, kind])

    def store(l, kind):
        return pltpu.make_async_copy(rounded[kind].at[l], own[3 * l + kind], own_sem.at[l, kind])

    def first(l):
        return pltpu.make_async_copy(rounded[2].at[l, 0:1], firsts[l], first_sem.at[l])

    def weight(kind):
        return remote(rounded[kind].at[0], partner[kind], w_send.at[kind], w_recv.at[kind], p.beside)

    def round_weights(l, kind):
        load(l, kind).wait()

        def one(i, carry):
            rounded[kind][l, i] = loaded[kind][l, i].astype(BF16)
            return carry

        lax.fori_loop(0, rounded[kind].shape[1], one, 0)
        store(l, kind).start()
        if kind == 2:
            first(l).start()

    def shard1(kind):
        return pltpu.make_async_copy(shards[kind].at[1], shards1_out[kind], shard_sem.at[kind])

    for l in (0, 1):
        for kind in range(3):
            load(l, kind).start()
    def round_shards():
        for l in (0, 1):
            qkv[l], out[l] = qkv_wide[l].astype(BF16), out_wide[l].astype(BF16)
            pack_small(l, router, const, gains, vectors, rows, small)
        for kind in range(3):
            shard1(kind).start()
        routes[...] = jnp.zeros(routes.shape, jnp.int32)
        for l in (0, 1):
            routes[2 * l : 2 * l + 2, 0 : routes_in.shape[2]] = routes_in[l]

    greet(p.mates[1:] + [p.beside], p, round_shards)

    def route_copy(i, row):
        return remote(routes, routes_all.at[row], r_send.at[i], r_recv.at[row], p.mates[i])

    def push(t, f):
        spreading.push(t * spread + f, [q.at[t, f] for q in quarters0])

    line0.begin()
    for kind in (0, 1):
        round_weights(0, kind)
        weight(kind).start()
    routes_all[p.e] = routes[...]
    for i in (1, 2, 3):
        route_copy(i, p.e).start()
    spreading.own_shard()
    line0.beside(push)
    line1.begin()
    lax.fori_loop(1, LINE, lambda k, carry: (line0.step(k, push), carry)[1], 0)
    round_weights(0, 2)
    lax.fori_loop(1, LINE, lambda k, carry: (line1.step(k, lambda t, f: None), carry)[1], 0)
    for kind in range(3):
        round_weights(1, kind)
    along(p, lambda t: spreading.across(t * spread + p.f), start=1)
    along(p, lambda t: spreading.across(t * spread + 1 - p.f))
    spreading.finish_own()
    lax.fori_loop(0, LINE * spread, lambda s, carry: (spreading.finish_shard(s), carry)[1], 0)
    line0.finish()
    line1.finish()
    for l in (0, 1):
        for kind in range(3):
            store(l, kind).wait()
        first(l).wait()
    for kind in (0, 1):
        weight(kind).wait()
    for kind in range(3):
        shard1(kind).wait()
    for i in (1, 2, 3):
        route_copy(i, p.e).wait_send()
        route_copy(i, p.mates[i][1]).wait_recv()


def dense_gather(spread, call_id, arrays, routes, wide):
    count = spread * LINE
    layers, depth = arrays[1].shape[:2]
    shards = [arrays[0].shape[1:], arrays[1].shape[1:], (depth, 128)]
    pairs, single = LineGather.shapes(shards, 2), LineGather.shapes(shards, 1)
    outs = [struct((count * rows, width), BF16) for rows, width in shards]
    packed = (8, -(-routes.shape[2] // 128) * 128)
    outs += [struct(q, BF16) for q in single] + [struct((4,) + packed, jnp.int32)]
    outs += [struct(w.shape[1:], BF16) for w in wide] * 2 + [struct((1,) + wide[2].shape[2:], BF16)] * 2
    outs += [struct(w.shape[1:], BF16) for w in wide[:2]] + [struct(s, BF16) for s in shards]
    scratch = [pltpu.VMEM(q, BF16) for q in pairs] + [pltpu.VMEM(w.shape, F32) for w in wide]
    scratch += [pltpu.VMEM(w.shape, BF16) for w in wide] + [pltpu.VMEM((layers,) + s, BF16) for s in shards]
    scratch += [pltpu.VMEM((32, depth), F32), pltpu.VMEM(packed, jnp.int32)] + LineGather.scratch(2) + LineGather.scratch(1)
    scratch += [dma(4), dma(4), dma(2), dma(2), dma(2, 3), dma(2, 3), dma(2), dma(3)]
    return pl.pallas_call(
        functools.partial(dense_gather_kernel, spread),
        out_shape=outs,
        in_specs=[VMEM] * (len(arrays) + 1) + [ANY] * 3,
        out_specs=[ANY] * 3 + [VMEM] * 4 + [ANY] * 13,
        scratch_shapes=scratch + Spread.scratch(count),
        compiler_params=remote_params(call_id),
        cost_estimate=pl.CostEstimate(flops=10**10, bytes_accessed=10**8, transcendentals=0),
    )(*arrays, routes, *wide)


class Halve:
    def __init__(self, place, grads, quarter, scratch):
        self.p, self.grads, self.quarter = place, grads, quarter
        (self.mine, self.core, self.stage, self.came, self.l_sem, self.a_send, self.a_recv, self.y_send,
         self.y_recv) = scratch
        self.depths = [g.shape[0] // (LINE * place.spread) for g in grads]
        self.wide = grads[0].shape[1] // 2

    @staticmethod
    def scratch(spread, depths, width):
        count, rows, wide = LINE * spread, sum(depths) // 2, width // 2
        half = pltpu.VMEM((LINE, spread, rows, wide), BF16)
        everything = pltpu.VMEM((count * sum(depths), wide), BF16)
        return [everything, everything, half, half, dma(2), dma(2), dma(2), dma(LINE), dma(LINE)]

    def rows_of(self, kind):
        first = 0 if kind == 0 else self.grads[0].shape[0]
        return slice(first, first + self.grads[kind].shape[0])

    def lanes(self, c):
        return pl.ds(pl.multiple_of(c * self.wide, 128), self.wide)

    def local(self, kind):
        return pltpu.make_async_copy(
            self.grads[kind].at[:, self.lanes(self.p.c)], self.mine.at[self.rows_of(kind)], self.l_sem.at[kind])

    def a_copy(self, kind):
        return remote(self.grads[kind].at[:, self.lanes(1 - self.p.c)], self.core.at[self.rows_of(kind)],
                      self.a_send.at[kind], self.a_recv.at[kind], self.p.sibling)

    def y_copy(self, t):
        return remote(self.stage.at[t], self.came.at[t], self.y_send.at[t], self.y_recv.at[t], self.p.across)

    def pieces(self, t, f, y):
        s, row = t * self.p.spread + f, 0
        for kind, depth in enumerate(self.depths):
            at = self.rows_of(kind).start + s * depth + y * (depth // 2)
            here = pl.ds(pl.multiple_of(at, 16), depth // 2)
            yield slice(row, row + depth // 2), self.mine[here, :].astype(F32) + self.core[here, :].astype(F32)
            row += depth // 2

    def order(self, i):
        t = self.p.t
        down = LINE - 1 - i - jnp.where(LINE - 1 - i <= t, 1, 0)
        up = i + jnp.where(i >= t, 1, 0)
        return jnp.where(i == LINE - 1, t, jnp.where(t >= LINE // 2, up, down))

    def begin(self):
        for kind in (0, 1):
            self.a_copy(kind).start()
            self.local(kind).start()

    def after_first(self):
        for kind in (0, 1):
            self.a_copy(kind).wait_recv()
            self.local(kind).wait()

        def body(i, carry):
            t = self.order(i)
            for f in range(self.p.spread):
                for where, value in self.pieces(t, f, 1 - self.p.y):
                    self.stage[t, f, where] = value.astype(BF16)
            self.y_copy(t).start()
            return carry

        lax.fori_loop(0, LINE, body, 0)

        def own(t, carry):
            for f in range(self.p.spread):
                for where, value in self.pieces(t, f, self.p.y):
                    self.quarter[t, f, where] = value
            return carry

        lax.fori_loop(0, LINE, own, 0)

    def add(self, t):
        self.y_copy(t).wait_recv()
        self.quarter[t] = self.quarter[t] + self.came[t].astype(F32)

    def after_relay(self):
        lax.fori_loop(0, LINE, lambda i, carry: (self.add(self.order(i)), carry)[1], 0)

    def finish(self):
        for kind in (0, 1):
            self.a_copy(kind).wait_send()
        lax.fori_loop(0, LINE, lambda t, carry: (self.y_copy(t).wait_send(), carry)[1], 0)


class GradientRider:
    def __init__(self, place, given, outs, scratch):
        self.halve = Halve(place, given[:2], outs[0], scratch[:9])
        self.own, self.other = given[2:], outs[1:]
        self.p = place
        self.w_send, self.w_recv = scratch[9:]

    @staticmethod
    def scratch(spread, depths, width):
        return Halve.scratch(spread, depths, width) + [dma(2), dma(2)]

    def weight(self, i):
        return remote(self.own[i], self.other[i], self.w_send.at[i], self.w_recv.at[i], self.p.beside)

    def begin(self):
        self.halve.begin()
        for i in range(2):
            self.weight(i).start()

    def after_first(self):
        self.halve.after_first()

    def in_line(self):
        pass

    def after_relay(self):
        self.halve.after_relay()

    def finish(self):
        self.halve.finish()
        for i in range(2):
            self.weight(i).wait()


class LineSum:
    def __init__(self, place, depths, quarter, sums, scratch):
        self.p, self.depths, self.quarter, self.sums = place, depths, quarter, sums
        (self.stage, self.came, self.stage_x, self.came_x, self.z_send, self.z_recv, self.x_send, self.x_recv,
         self.e_send, self.e_recv) = scratch
        self.wide = sums[0].shape[1] // 2

    @staticmethod
    def scratch(spread, depths, width):
        rows, wide = sum(depths) // 2, width // 2
        return [
            pltpu.VMEM((LINE, spread, rows, wide), BF16),
            pltpu.VMEM((2, LINE, spread, rows, wide), BF16),
            pltpu.VMEM((rows, wide), BF16),
            pltpu.VMEM((rows, wide), BF16),
            dma(LINE), dma(2, LINE), dma(1), dma(1), dma(3, 2), dma(3, 2),
        ]

    def lanes(self, c):
        return pl.ds(pl.multiple_of(c * self.wide, 128), self.wide)

    def z_copy(self, up, t):
        return remote(self.stage.at[t], self.came.at[up, t], self.z_send.at[t], self.z_recv.at[up, t], self.p.on_line(up))

    def x_copy(self):
        return remote(self.stage_x, self.came_x, self.x_send.at[0], self.x_recv.at[0], self.p.beside)

    def e_copy(self, i, kind, y, c):
        half = self.depths[kind] // 2
        at = self.sums[kind].at[pl.ds(pl.multiple_of(y * half, 8), half), self.lanes(c)]
        return remote(at, at, self.e_send.at[i, kind], self.e_recv.at[i, kind], self.p.across if i == 0 else self.p.sibling)

    def start(self, t):
        p = self.p
        for up, mine in ((1, jnp.logical_and(p.t == 0, t > 0)), (0, jnp.logical_and(p.t == LINE - 1, t < LINE - 1))):

            @pl.when(mine)
            def _(up=up):
                self.stage[t] = self.quarter[t].astype(BF16)
                self.z_copy(up, t).start()

    def relay(self, kind):
        p = self.p

        @pl.when(p.inside)
        def _():
            t = {"near": p.t + p.ahead, "far": p.t + 2 * p.ahead, "back": p.t - p.ahead}[kind]
            way = 1 - p.up if kind == "back" else p.up
            self.z_copy(way, t).wait_recv()
            self.stage[t] = (self.quarter[t] + self.came[way, t].astype(F32)).astype(BF16)
            self.z_copy(way, t).start()

    def after_z(self):
        p = self.p

        for up, there in ((1, p.below), (0, p.above)):

            @pl.when(there)
            def _(up=up):
                self.z_copy(up, p.t).wait_recv()
                self.quarter[p.t] = self.quarter[p.t] + self.came[up, p.t].astype(F32)

        self.stage_x[...] = self.quarter[p.t, 1 - p.f].astype(BF16)
        self.x_copy().start()

    def after_x(self):
        p = self.p
        self.x_copy().wait_recv()
        row = 0
        for kind, depth in enumerate(self.depths):
            half = depth // 2
            value = self.quarter[p.t, p.f, row : row + half] + self.came_x[row : row + half].astype(F32)
            self.sums[kind][pl.ds(pl.multiple_of(p.y * half, 8), half), self.lanes(p.c)] = value
            row += half
        for i in (0, 1):
            for kind in (0, 1):
                self.e_copy(i, kind, p.y, p.c).start()

    def finish(self):
        p = self.p
        for kind in (0, 1):
            self.e_copy(0, kind, 1 - p.y, p.c).wait_recv()
            self.e_copy(2, kind, 1 - p.y, p.c).start()
        for kind in (0, 1):
            self.e_copy(0, kind, p.y, p.c).wait_send()
            self.e_copy(1, kind, p.y, p.c).wait_send()
            self.e_copy(1, kind, p.y, 1 - p.c).wait_recv()
            self.e_copy(2, kind, 1 - p.y, p.c).wait_send()
            self.e_copy(2, kind, 1 - p.y, 1 - p.c).wait_recv()
        self.x_copy().wait_send()

        def body(t, carry):
            @pl.when(t != p.t)
            def _():
                self.z_copy(0, t).wait_send()

            return carry

        lax.fori_loop(0, LINE, body, 0)


class SmallSum:
    def __init__(self, place, grads, total, scratch):
        self.p, self.grads, self.total = place, grads, total
        self.stage, self.came, self.send, self.recv = scratch
        p = place
        near = (p.d + p.spread - 2 * p.spread * lax.rem(p.t, 2), p.e)
        self.far = (lax.rem(p.d + 2 * p.spread, LINE * p.spread), p.e)
        self.partners = [p.sibling, p.across, near, self.far, p.beside]

    @staticmethod
    def scratch(rows, width):
        half = pltpu.VMEM((5, rows, width // 2), F32)
        return [half, half, dma(6), dma(6)]

    def lanes(self, c):
        wide = self.grads.shape[1] // 2
        return pl.ds(pl.multiple_of(c * wide, 128), wide)

    def copy(self, i):
        src = self.grads.at[:, self.lanes(1 - self.p.c)] if i == 0 else self.stage.at[i]
        return remote(src, self.came.at[i], self.send.at[i], self.recv.at[i], self.partners[i])

    def last(self, c):
        at = self.total.at[:, self.lanes(c)]
        return remote(at, at, self.send.at[5], self.recv.at[5], self.p.sibling)

    def step(self, i):
        if i == 0:
            self.copy(0).start()
            return
        self.copy(i - 1).wait_recv()
        mine = self.grads[:, self.lanes(self.p.c)] if i == 1 else self.stage[i - 1]
        value = mine + self.came[i - 1]
        if i < 5:
            self.stage[i] = value
            self.copy(i).start()
        else:
            self.total[:, self.lanes(self.p.c)] = value
            self.last(self.p.c).start()

    def finish(self):
        for i in range(5):
            self.copy(i).wait_send()
        self.last(self.p.c).wait_send()
        self.last(1 - self.p.c).wait_recv()


def dense_reduce_kernel(spread, depths, small0, small1, res, qkv0, out0, quarter1, up0, down0, small_sum, *refs):
    p = Place(spread)
    sums, came, (small, mine0, mine1), (w_send, w_recv), halve_refs, line0, line1, small_refs = split(refs, 2, 2, 3, 2, 9, 10, 10)
    sums0, sums1 = ([ref.at[l] for ref in sums] for l in (0, 1))
    halve = Halve(p, (qkv0, out0), mine0, halve_refs)
    sum0 = LineSum(p, depths, mine0, sums0, line0)
    sum1 = LineSum(p, depths, mine1, sums1, line1)
    little = SmallSum(p, small, small_sum, small_refs)
    pieces = ((up0, came[0]), (down0.at[0], came[1].at[0]), (down0.at[1], came[1].at[1]))
    weights = [remote(mine, other, w_send.at[i], w_recv.at[i], p.beside) for i, (mine, other) in enumerate(pieces)]
    greet([p.sibling, p.across, p.beside, little.far], p)
    halve.begin()
    weights[0].start()
    rows = small0.shape[0]
    small[0:rows, :] = small0[...]
    small[rows : 2 * rows, :] = small1[...]
    small[2 * rows :, :] = jnp.zeros((16, small.shape[1]), F32)
    small[2 * rows :, 0:128] = res[0:16, :]
    little.step(0)
    mine1[...] = quarter1[...]
    for i in range(LINE):
        sum1.start(halve.order(i))
    little.step(1)
    halve.after_first()
    little.step(2)

    def arrive(i):
        halve.add(halve.order(i))
        sum0.start(halve.order(i))

    sum1.relay("far")
    sum1.relay("near")
    arrive(0)
    little.step(3)
    sum1.relay("back")
    arrive(1)
    sum0.relay("far")
    sum1.after_z()
    weights[1].start()
    arrive(2)
    sum0.relay("near")
    sum1.after_x()
    sum0.relay("back")
    arrive(3)
    little.step(4)
    sum0.after_z()
    weights[2].start()
    little.step(5)
    sum0.after_x()
    sum1.finish()
    halve.finish()
    little.finish()
    sum0.finish()
    for copy in weights:
        copy.wait()


def dense_reduce(spread, call_id, smalls, grads0, quarter1, weights0):
    count = LINE * spread
    depths = [g.shape[0] // count for g in grads0]
    width = grads0[0].shape[1]
    small = (2 * smalls[0].shape[0] + 16, width)
    line = LineSum.scratch(spread, depths, width)
    mine = pltpu.VMEM(quarter1.shape, F32)
    scratch = [pltpu.VMEM(small, F32), mine, mine, dma(3), dma(3)] + Halve.scratch(spread, depths, width) + line + line
    return pl.pallas_call(
        functools.partial(dense_reduce_kernel, spread, depths),
        out_shape=[struct(small, F32)] + [struct((2, depth, width), F32) for depth in depths]
        + [struct(w.shape, BF16) for w in weights0],
        in_specs=[VMEM] * 3 + [ANY, ANY, VMEM, ANY, ANY],
        out_specs=[VMEM] * 3 + [ANY] * 2,
        scratch_shapes=scratch + SmallSum.scratch(*small),
        compiler_params=remote_params(call_id),
        cost_estimate=pl.CostEstimate(flops=2 * 10**10, bytes_accessed=2 * 10**8, transcendentals=0),
    )(*smalls, *grads0, quarter1, *weights0)


def stack_kernel(small, qkv, out, *refs):
    parts, (qkv_out, out_out, *stacked), (router, const, gains, vectors, residual) = split(refs, 12, 5)
    qkv_out[...], out_out[...] = qkv[...], out[...]
    for kind, ref in enumerate(stacked):
        for l in (0, 1):
            mine, came = parts[4 * kind + 2 * l], parts[4 * kind + 2 * l + 1]
            ref[l] = mine[...] + came[...].astype(F32)

    @pl.when(jnp.logical_and(pl.program_id(0) == 0, pl.program_id(1) == 0))
    def _():
        depth, width = gains.shape[2], small.shape[1]
        here = lanes(depth, width) == lax.axis_index("dp") * depth + lax.broadcasted_iota(jnp.int32, (depth, width), 0)
        rows = dot_nt(small[...], here.astype(F32), precision=HIGH)
        for l in (0, 1):
            first = 24 * l
            for r in range(CONST0):
                router[r, l : l + 1, :] = rows[first + r : first + r + 1]
            for j in (0, 1):
                at = first + CONST0 + 2 * j
                const[l, j] = rows[at : at + 2]
            gains[l] = rows[first + GAIN0 : first + GAIN0 + 2]
            vectors[l] = rows[first + VECTOR0 : first + VECTOR0 + 2]
        residual[...] = small[48 : 48 + CONST0, 0:CONST0]


def stack_results(small, qkv, out, parts, depth):
    flat = [part for kind in parts for layer in kind for part in layer]
    local, steps = flat[0].shape[0], 2

    def rows_of(shape, lead=None):
        rows, wide = shape[-2] // steps, shape[-1]
        if lead:
            return pl.BlockSpec((lead, 1, rows, wide), lambda l, n: (0, l, n, 0))
        return pl.BlockSpec((1, rows, wide), lambda l, n: (l, n, 0))

    def whole(shape):
        return pl.BlockSpec(shape, lambda l, n: (0,) * len(shape))

    stacked = [(2,) + kind[0][0].shape for kind in parts]
    little = [(CONST0, 2, depth), (2, 2, 2, depth), (2, 2, depth), (2, 2, depth), (CONST0, CONST0)]
    return pl.pallas_call(
        stack_kernel,
        out_shape=[struct(a.shape, F32) for a in (qkv, out)] + [struct(s, F32) for s in stacked + little],
        grid=(local, steps),
        in_specs=[whole(small.shape)] + [rows_of(a.shape) for a in (qkv, out, *flat)],
        out_specs=[rows_of(a.shape) for a in (qkv, out)] + [rows_of(s, 2) for s in stacked] + [whole(s) for s in little],
        compiler_params=pltpu.CompilerParams(vmem_limit_bytes=60 * 2**20),
        cost_estimate=pl.CostEstimate(flops=10**7, bytes_accessed=3 * 10**7, transcendentals=0),
    )(small, qkv, out, *flat)


def per_device(
    tokens, seq_lengths, block_perm, routes, norm_gains, w_qkv, w_out, w_router, w_residual, w_const, v_const,
    w_gate, w_up, w_down, cotangent,
):
    rows, width = tokens.shape
    owners = lax.axis_size("expert")
    shards = lax.axis_size("dp")
    spread = shards // LINE
    local = w_gate.shape[1]
    experts = local * owners
    layers = routes.shape[0]
    slots = experts * CAP

    depth = w_out.shape[1]
    qkv_t = jnp.swapaxes(w_qkv, 1, 2)
    in_kernels = spread == 2 and owners == 4 and layers == local == 2 and qkv_t.shape[1] % 32 == 0 and depth % 32 == 0
    if in_kernels:
        arrays = (qkv_t, w_out, jnp.transpose(w_router, (2, 0, 1)), jnp.swapaxes(w_const, 2, 3), norm_gains, v_const)
        *gathered, routes_all, g0, u0, d0, g1, u1, d1, first0, first1, gate, up, qkv1_own, out1_own, small1_own = dense_gather(
            spread, 4, arrays, jnp.swapaxes(routes, 1, 2), (w_gate, w_up, w_down))
        weights = [[g0, gate, u0, up, d0, from_partner(first0, 1, spread, LINE)]]
        dense = [(gathered[2], gathered[0], gathered[1])]
    else:
        weights = []
        for l in range(layers):
            own = [(w_gate[l].astype(BF16), 2), (w_up[l].astype(BF16), 2), (w_down[l].astype(BF16), 1)]
            weights.append([part for w, axis in own for part in pair_weights(w, axis, spread)])
        small = jnp.concatenate(
            [
                w_router, w_const[:, 0], w_const[:, 1], jnp.swapaxes(norm_gains, 1, 2), jnp.swapaxes(v_const, 1, 2),
                jnp.zeros((layers, depth, 108), F32),
            ],
            axis=2,
        ).astype(BF16)
        packed_routes = jnp.zeros((8, -(-rows // 128) * 128), jnp.int32).at[: 2 * layers, :rows].set(
            jnp.swapaxes(routes, 1, 2).reshape(2 * layers, rows))
        routes_all = lax.all_gather(packed_routes, "expert", axis=0)
        qkv_all = lax.all_gather(qkv_t.astype(BF16), "dp", axis=1, tiled=True)
        out_all = lax.all_gather(w_out.astype(BF16), "dp", axis=1, tiled=True)
        small_all = lax.all_gather(small, "dp", axis=1, tiled=True)
        dense = [(small_all[l], qkv_all[l], out_all[l]) for l in range(layers)]

    cols = ((rows, width), F32)
    attention = [((rows, width), BF16), ((rows, 3 * width), BF16), ((HEADS, rows, rows), F32), ((rows, width), BF16)]
    residual = ((128, 128), F32)
    per_token, sent = ((rows, 128), F32), ((slots, width), BF16)

    def group(array):
        return array.reshape(owners, local, CAP, width)

    attn_in0, qkv0, probs0, attn0, mid0, logits0, stat0, out = local_call(
        first_kernel, experts, (tokens, *dense[0], seq_lengths, block_perm, routes_all),
        attention + [cols, per_token, per_token, sent], scalars=(4, 5))
    ride = (*gathered[3:], qkv1_own, out1_own, small1_own, g1, u1) if in_kernels else None
    ret0, *kept0 = expert_forward(spread, 0, group(out), weights[0], in_kernels, ride)
    if in_kernels:
        kept0, weights[0][5], (qkv_all, out_all, small_all), (gate, up) = kept0[:3], kept0[3], kept0[4:7], kept0[7:]
        dense.append((small_all, qkv_all, out_all))
        first1, ret0 = lax.optimization_barrier((first1, ret0))
        weights.append([g1, gate, u1, up, d1, from_partner(first1, 1, spread, LINE)])
    ret0 = ret0.reshape(slots, width)
    stream1, attn_in1, qkv1, probs1, attn1, mid1, stat1, out = local_call(
        middle_kernel, experts,
        (mid0, dense[0][0], stat0, ret0, *dense[1], seq_lengths, block_perm, routes_all, logits0, w_residual),
        [cols] + attention + [cols, per_token, sent], [residual], scalars=(7, 8))
    ret1, *kept1 = expert_forward(spread, 1, group(out), weights[1], in_kernels)
    if in_kernels:
        weights[1][5] = kept1.pop()
    ret1 = ret1.reshape(slots, width)

    small_grads = ((24, width), F32)
    output, g_small1, extra, out, small_grad1, res_grad = local_call(
        turn_kernel, experts, (mid1, dense[1][0], stat1, ret1, cotangent, logits0, w_residual),
        [((rows, width), BF16), per_token, per_token, sent, small_grads, residual], [residual])
    back, *expert_grads1 = expert_backward(spread, 2, group(out), kept1, weights[1], in_kernels)
    ride = None
    grad_type = BF16 if in_kernels else F32
    dense_grads = [((3 * width, width), grad_type), ((width, width), grad_type), small_grads]
    attention_scratch = [((rows, 3 * width), BF16), ((rows, width), BF16)]
    qkv_grad1, out_grad1, small_grad1, grad, g_small0, out, small_grad0 = local_call(
        between_kernel, experts,
        (cotangent, back.reshape(slots, width), g_small1, stat1, mid1, dense[1][0], stream1, dense[1][1], dense[1][2],
         attn_in1, qkv1, probs1, attn1, small_grad1, mid0, dense[0][0], stat0, ret0, extra),
        dense_grads + [cols, per_token, sent, small_grads], attention_scratch)
    if in_kernels:
        gate1, up1, up1_sent, down1, down1_sent, gate1_came = expert_grads1
        ride = (qkv_grad1, out_grad1, up1_sent, down1_sent)
    back, *expert_grads0 = expert_backward(spread, 3, group(out), kept0, weights[0], in_kernels, ride)
    qkv_grad0, out_grad0, small_grad0, tokens_grad = local_call(
        last_kernel, experts,
        (grad, back.reshape(slots, width), g_small0, stat0, mid0, dense[0][0], tokens, dense[0][1], dense[0][2],
         attn_in0, qkv0, probs0, attn0, small_grad0),
        dense_grads + [cols], attention_scratch)

    if in_kernels:
        gate0, up0, up0_sent, down0, down0_sent, gate0_came, quarter1, up1_came, down1_came = expert_grads0
        packed, qkv_grad, out_grad, up0_came, down0_came = dense_reduce(
            spread, 5, (small_grad0, small_grad1, res_grad), (qkv_grad0, out_grad0), quarter1, (up0_sent, down0_sent))
        pairs = (
            ((gate0, gate0_came), (gate1, gate1_came)), ((up0, up0_came), (up1, up1_came)),
            ((down0, down0_came), (down1, down1_came)))
        qkv_grad, out_grad, gate_grad, up_grad, down_grad, router_grad, const_grad, gains_grad, vector_grad, residual_grad = (
            stack_results(packed, qkv_grad, out_grad, pairs, depth))
        router_grad = jnp.transpose(router_grad, (1, 2, 0))
        const_grad = jnp.swapaxes(const_grad, 2, 3)
    else:
        gate_grad, up_grad, down_grad = (
            jnp.stack([
                pair_sum(grads[at * len(grads) // 3 : (at + 1) * len(grads) // 3], axis, spread)
                for grads in (expert_grads0, expert_grads1)])
            for axis, at in ((2, 0), (2, 1), (1, 2)))
        packed = jnp.concatenate([small_grad0, small_grad1, jnp.pad(res_grad[:16], ((0, 0), (0, width - 128)))])
        packed = lax.psum(packed, ("dp", "expert"))
        qkv_grad, out_grad = (
            lax.psum(lax.psum_scatter(jnp.stack(pair), "dp", scatter_dimension=1, tiled=True), "expert")
            for pair in ((qkv_grad0, qkv_grad1), (out_grad0, out_grad1)))
        mine = lax.dynamic_slice_in_dim(packed, lax.axis_index("dp") * depth, depth, axis=1)
        mine = jnp.stack([mine[:24], mine[24:48]])
        router_grad = jnp.swapaxes(mine[:, :CONST0], 1, 2)
        const_grad = jnp.swapaxes(mine[:, CONST0:GAIN0].reshape(layers, 2, 2, depth), 2, 3)
        residual_grad = packed[48 : 48 + CONST0, :CONST0]
        gains_grad, vector_grad = mine[:, GAIN0 : GAIN0 + 2], mine[:, VECTOR0 : VECTOR0 + 2]
    return (
        output, tokens_grad, gains_grad, jnp.swapaxes(qkv_grad, 1, 2), out_grad, router_grad,
        residual_grad, const_grad, vector_grad, gate_grad, up_grad, down_grad,
    )


def solution(mesh):
    in_specs = (
        P(("dp", "expert"), None), P("dp", None, None), P("dp", None), P(None, ("dp", "expert"), None),
        P(None, None, "dp"), P(None, None, "dp"), P(None, "dp", None), P(None, "dp", None), P(),
        P(None, None, "dp", None), P(None, None, "dp"), P(None, "expert", None, "dp"), P(None, "expert", None, "dp"),
        P(None, "expert", "dp", None), P(("dp", "expert"), None),
    )
    out_specs = (
        P(("dp", "expert"), None), P(("dp", "expert"), None), P(None, None, "dp"), P(None, None, "dp"),
        P(None, "dp", None), P(None, "dp", None), P(), P(None, None, "dp", None), P(None, None, "dp"),
        P(None, "expert", None, "dp"), P(None, "expert", None, "dp"), P(None, "expert", "dp", None),
    )
    return jax.shard_map(per_device, mesh=mesh, in_specs=in_specs, out_specs=out_specs, check_vma=False)
```

```python
import functools

import jax
import jax.numpy as jnp
from jax import lax
from jax.experimental import pallas as pl
from jax.experimental.pallas import tpu as pltpu
from jax.sharding import PartitionSpec as P

HEADS = 12
CAP = 48
LINE = 4
EPSILON = 1e-05
MASKED = -1e30
HIGH = lax.Precision.HIGHEST
F32 = jnp.float32
BF16 = jnp.bfloat16
MESH = pl.DeviceIdType.MESH
VMEM = pl.BlockSpec(memory_space=pltpu.VMEM)
ANY = pl.BlockSpec(memory_space=pl.ANY)

CONST0, GAIN0, VECTOR0 = 12, 16, 18
STAT = {
    name: i
    for i, name in enumerate(
        ("r0", "r1", "share0", "share1", "slot0", "slot1", "p00", "p01", "p10", "p11")
    )
}


SMEM = pl.BlockSpec(memory_space=pltpu.SMEM)


def dot_nn(a, b, **kw):
    return lax.dot_general(a, b, (((1,), (0,)), ((), ())), preferred_element_type=F32, **kw)


def dot_nt(a, b, **kw):
    return lax.dot_general(a, b, (((1,), (1,)), ((), ())), preferred_element_type=F32, **kw)


def dot_tn(a, b, **kw):
    return lax.dot_general(a, b, (((0,), (0,)), ((), ())), preferred_element_type=F32, **kw)


def thirds(values):
    out = []
    for _ in range(3):
        out.append(values.astype(BF16))
        values = values - out[-1].astype(F32)
    return out


def lanes(rows, width=128):
    return lax.broadcasted_iota(jnp.int32, (rows, width), 1)


def rms_scale(values):
    return lax.rsqrt(jnp.mean(values * values, axis=-1, keepdims=True) + EPSILON)


def row_vectors(small):
    pick = lax.broadcasted_iota(jnp.int32, (8, 128), 0) + GAIN0 == lanes(8)
    rows = dot_nt(pick.astype(BF16), small)
    return rows[0:1], rows[1:2], rows[2:3], rows[3:4]


def stat_columns(stat):
    return {name: stat[:, i : i + 1] for name, i in STAT.items()}


def slot_picks(stat, slots):
    place = lanes(stat["slot0"].shape[0], slots).astype(F32)
    first = (place == stat["slot0"]).astype(BF16)
    second = (place == stat["slot1"]).astype(BF16)
    return first, second


def const_weights(stat, experts):
    out = []
    for kind in (experts + 1, experts + 2, experts + 3):
        out.append(
            stat["share0"] * (stat["r0"] == kind).astype(F32)
            + stat["share1"] * (stat["r1"] == kind).astype(F32)
        )
    return out


def doc_index(lengths, places):
    place, end = lax.axis_index("expert"), 0
    doc = jnp.zeros_like(places)
    for j in range(lengths.shape[2]):
        end = end + lengths[0, place, j]
        doc = doc + (places >= end).astype(jnp.int32)
    return doc


def block_routes(perm, routes_all, layer, rows):
    mine = routes_all[perm[0, lax.axis_index("expert")]].astype(F32)
    routes = jnp.transpose(mine)[:rows].astype(jnp.int32)
    return routes[:, 2 * layer : 2 * layer + 1], routes[:, 2 * layer + 1 : 2 * layer + 2]


def padded(w_res, ref):
    count = w_res.shape[0]
    ref[...] = jnp.zeros(ref.shape, F32)
    ref[0:count, 0:count] = w_res[...]
    return ref[...]


def attend_part(stream, small, w_qkv_t, w_out, lengths, attn_in_ref, qkv_ref, probs_ref, attn_ref):
    rows, width = stream.shape
    gain, _, _, _ = row_vectors(small)
    attn_in_ref[...] = (stream * rms_scale(stream) * gain).astype(BF16)

    def project(i, carry):
        at = pl.multiple_of(i * width, width)
        qkv_ref[:, pl.ds(at, width)] = dot_nt(
            attn_in_ref[...], w_qkv_t[pl.ds(at, width), :]
        ).astype(BF16)
        return carry

    lax.fori_loop(0, 3, project, 0, unroll=True)
    head_dim = width // HEADS
    factor = 1.0 / head_dim**0.5
    allowed = jnp.logical_and(
        doc_index(lengths, lax.broadcasted_iota(jnp.int32, (rows, 1), 0))
        == doc_index(lengths, lax.broadcasted_iota(jnp.int32, (1, rows), 1)),
        lax.broadcasted_iota(jnp.int32, (rows, rows), 0)
        >= lax.broadcasted_iota(jnp.int32, (rows, rows), 1),
    )

    def heads(i, carry):
        at = pl.multiple_of(i * 2 * head_dim, 2 * head_dim)
        query = qkv_ref[:, pl.ds(at, 2 * head_dim)]
        key = qkv_ref[:, pl.ds(pl.multiple_of(at + width, 128), 2 * head_dim)]
        value = qkv_ref[:, pl.ds(pl.multiple_of(at + 2 * width, 128), 2 * head_dim)]
        second = lanes(rows, 2 * head_dim) >= head_dim
        mixed = []
        for sub in (0, 1):
            mine = second if sub else jnp.logical_not(second)
            scores = dot_nt(jnp.where(mine, query, jnp.zeros_like(query)), key) * factor
            scores = jnp.where(allowed, scores, MASKED)
            exponent = jnp.exp(scores - jnp.max(scores, axis=-1, keepdims=True))
            probs = exponent / jnp.sum(exponent, axis=-1, keepdims=True)
            probs_ref[2 * i + sub] = probs
            mixed.append(dot_nn(probs.astype(BF16), value))
        attn_ref[:, pl.ds(at, 2 * head_dim)] = jnp.where(second, mixed[1], mixed[0]).astype(BF16)
        return carry

    lax.fori_loop(0, HEADS // 2, heads, 0, unroll=True)
    return stream + dot_nn(attn_ref[...], w_out[...])


def route_part(mid, small, routes, prev_logits, w_res, experts):
    rows = mid.shape[0]
    _, gain, _, _ = row_vectors(small)
    hidden = (mid * rms_scale(mid) * gain).astype(BF16)
    lane = lanes(rows)
    raw = dot_nn(hidden, small)
    logits = jnp.where(lane < CONST0, raw, 0.0)
    if prev_logits is not None:
        logits = logits + dot_nn(prev_logits, w_res, precision=HIGH)
    r0, r1 = routes
    hot0, hot1 = (lane == r0).astype(F32), (lane == r1).astype(F32)
    c0 = jnp.sum(hot0 * logits, axis=-1, keepdims=True)
    c1 = jnp.sum(hot1 * logits, axis=-1, keepdims=True)
    peak = jnp.maximum(c0, c1)
    e0, e1 = jnp.exp(c0 - peak), jnp.exp(c1 - peak)
    total = e0 + e1
    share0, share1 = e0 / total, e1 / total
    probs = []
    for j in (0, 1):
        a = raw[:, CONST0 + 2 * j : CONST0 + 2 * j + 1]
        b = raw[:, CONST0 + 2 * j + 1 : CONST0 + 2 * j + 2]
        top = jnp.maximum(a, b)
        ea, eb = jnp.exp(a - top), jnp.exp(b - top)
        probs += [ea / (ea + eb), eb / (ea + eb)]
    earlier = lax.broadcasted_iota(jnp.int32, (rows, rows), 0) > lax.broadcasted_iota(
        jnp.int32, (rows, rows), 1
    )
    before = dot_nn(earlier.astype(BF16), (hot0 + hot1).astype(BF16))
    f0, f1 = r0.astype(F32), r1.astype(F32)
    slot0 = jnp.where(
        r0 < experts, f0 * CAP + jnp.sum(before * hot0, axis=-1, keepdims=True), -1.0
    )
    slot1 = jnp.where(
        r1 < experts, f1 * CAP + jnp.sum(before * hot1, axis=-1, keepdims=True), -1.0
    )
    stat = jnp.zeros((rows, 128), F32)
    for i, column in enumerate([f0, f1, share0, share1, slot0, slot1] + probs):
        stat = jnp.where(lane == i, column, stat)
    first, second = slot_picks({"slot0": slot0, "slot1": slot1}, experts * CAP)
    outgoing = dot_tn(first + second, hidden).astype(BF16)
    return logits, stat, outgoing


def combine_part(mid, small, stat, returned, experts):
    _, gain, vec0, vec1 = row_vectors(small)
    hidden_full = mid * rms_scale(mid) * gain
    first, second = slot_picks(stat, experts * CAP)
    pair0, pair1 = dot_nn(first, returned), dot_nn(second, returned)
    copy, const0, const1 = const_weights(stat, experts)
    local = copy + const0 * stat["p00"] + const1 * stat["p10"]
    moe = stat["share0"] * pair0 + stat["share1"] * pair1 + local * hidden_full
    moe = moe + (const0 * stat["p01"]) * vec0 + (const1 * stat["p11"]) * vec1
    return mid + moe, hidden_full, pair0, pair1


def share_backward(grad, small, stat, hidden_full, pair0, pair1, extra, experts):
    rows = grad.shape[0]
    _, _, vec0, vec1 = row_vectors(small)
    first, second = slot_picks(stat, experts * CAP)
    lane = lanes(rows).astype(F32)
    rowsum = functools.partial(jnp.sum, axis=-1, keepdims=True)
    dot_hidden = rowsum(grad * hidden_full)
    dot_vec = (rowsum(grad * vec0), rowsum(grad * vec1))
    _, const0, const1 = const_weights(stat, experts)
    probs = ((stat["p00"], stat["p01"]), (stat["p10"], stat["p11"]))
    value = [probs[j][0] * dot_hidden + probs[j][1] * dot_vec[j] for j in (0, 1)]
    shares = []
    for r, pair in ((stat["r0"], pair0), (stat["r1"], pair1)):
        shares.append(
            rowsum(grad * pair)
            + (r == experts + 1).astype(F32) * dot_hidden
            + (r == experts + 2).astype(F32) * value[0]
            + (r == experts + 3).astype(F32) * value[1]
        )
    inner = stat["share0"] * shares[0] + stat["share1"] * shares[1]
    g_small = (lane == stat["r0"]).astype(F32) * (stat["share0"] * (shares[0] - inner))
    g_small = g_small + (lane == stat["r1"]).astype(F32) * (stat["share1"] * (shares[1] - inner))
    if extra is not None:
        g_small = g_small + extra
    g_logits = g_small
    for j, weight in ((0, const0), (1, const1)):
        q = (weight * dot_hidden, weight * dot_vec[j])
        mean = probs[j][0] * q[0] + probs[j][1] * q[1]
        for c in (0, 1):
            g_small = jnp.where(lane == CONST0 + 2 * j + c, probs[j][c] * (q[c] - mean), g_small)
    sent0 = (jnp.where(stat["r0"] < experts, stat["share0"], 0.0) * grad).astype(BF16)
    sent1 = (jnp.where(stat["r1"] < experts, stat["share1"], 0.0) * grad).astype(BF16)
    outgoing = (dot_tn(first, sent0) + dot_tn(second, sent1)).astype(BF16)
    hidden = hidden_full.astype(BF16)
    projections = sum(dot_tn(part, hidden) for part in thirds(g_small)[::-1])
    vector0 = jnp.sum((const0 * stat["p01"]) * grad, axis=0, keepdims=True)
    vector1 = jnp.sum((const1 * stat["p11"]) * grad, axis=0, keepdims=True)
    return g_small, g_logits, outgoing, projections, vector0, vector1


def store_small(ref, projections, vector0, vector1):
    ref[0:16, :] = projections[0:16]
    ref[16:24, :] = jnp.zeros((8, ref.shape[1]), F32)
    ref[VECTOR0 : VECTOR0 + 1, :] = vector0
    ref[VECTOR0 + 1 : VECTOR0 + 2, :] = vector1


def first_kernel(experts, tokens, small, w_qkv_t, w_out, lengths, perm, routes_all,
                 attn_in, qkv, probs, attn, mid_ref, logits_ref, stat_ref, out_ref):
    mid = attend_part(tokens[...].astype(F32), small[...], w_qkv_t, w_out, lengths, attn_in, qkv, probs, attn)
    mid_ref[...] = mid
    routes = block_routes(perm, routes_all, 0, mid.shape[0])
    logits, stat, out = route_part(mid, small[...], routes, None, None, experts)
    logits_ref[...], stat_ref[...], out_ref[...] = logits, stat, out


def middle_kernel(experts, mid_in, small_in, stat_in, returned, small, w_qkv_t, w_out, lengths, perm, routes_all, logits_in, w_res,
                  stream_ref, attn_in, qkv, probs, attn, mid_ref, stat_ref, out_ref, res_ref):
    stream, _, _, _ = combine_part(mid_in[...], small_in[...], stat_columns(stat_in[...]), returned[...], experts)
    stream_ref[...] = stream
    mid = attend_part(stream, small[...], w_qkv_t, w_out, lengths, attn_in, qkv, probs, attn)
    mid_ref[...] = mid
    routes = block_routes(perm, routes_all, 1, mid.shape[0])
    _, stat, out = route_part(mid, small[...], routes, logits_in[...], padded(w_res, res_ref), experts)
    stat_ref[...], out_ref[...] = stat, out


def turn_kernel(experts, mid, small, stat_in, returned, cotangent, logits_in, w_res,
                output, g_small_ref, extra_ref, out_ref, small_grad, res_grad, res_ref):
    stat = stat_columns(stat_in[...])
    stream, hidden_full, pair0, pair1 = combine_part(mid[...], small[...], stat, returned[...], experts)
    output[...] = stream.astype(BF16)
    grad = cotangent[...].astype(F32)
    g_small, g_logits, out, projections, v0, v1 = share_backward(grad, small[...], stat, hidden_full, pair0, pair1, None, experts)
    g_small_ref[...] = g_small
    out_ref[...] = out
    store_small(small_grad, projections, v0, v1)
    res_grad[...] = dot_tn(logits_in[...], g_logits, precision=HIGH)
    extra_ref[...] = dot_nt(g_logits, padded(w_res, res_ref), precision=HIGH)


def layer_backward(experts, grad, back, g_small, stat, mid, small, stream, w_qkv_t, w_out, attn_in, qkv, probs, attn,
                   qkv_grad, out_grad, small_grad, g_qkv, g_attn):
    rows, width = mid.shape
    gain1, gain2, _, _ = row_vectors(small)
    first, second = slot_picks(stat, experts * CAP)
    copy, const0, const1 = const_weights(stat, experts)
    local = copy + const0 * stat["p00"] + const1 * stat["p10"]
    g_full = sum(dot_nt(part, small) for part in thirds(g_small)[::-1]) + dot_nn(first + second, back)
    g_full = g_full + grad * local
    s2 = rms_scale(mid)
    small_grad[GAIN0 + 1 : GAIN0 + 2, :] = jnp.sum(g_full * mid * s2, axis=0, keepdims=True)
    m = g_full * gain2
    g_mid = grad + s2 * m - mid * (s2 * s2 * s2 * jnp.mean(m * mid, axis=-1, keepdims=True))
    branch = g_mid.astype(BF16)
    out_grad[...] = dot_tn(attn[...], branch).astype(out_grad.dtype)
    g_attn[...] = dot_nt(branch, w_out[...]).astype(BF16)
    head_dim = width // HEADS
    factor = 1.0 / head_dim**0.5

    def heads(i, carry):
        at = pl.multiple_of(i * 2 * head_dim, 2 * head_dim)
        at_k = pl.multiple_of(at + width, 128)
        at_v = pl.multiple_of(at + 2 * width, 128)
        query = qkv[:, pl.ds(at, 2 * head_dim)]
        key = qkv[:, pl.ds(at_k, 2 * head_dim)]
        value = qkv[:, pl.ds(at_v, 2 * head_dim)]
        ga = g_attn[:, pl.ds(at, 2 * head_dim)]
        second_half = lanes(rows, 2 * head_dim) >= head_dim
        gq, gk, gv = [], [], []
        for sub in (0, 1):
            mine = second_half if sub else jnp.logical_not(second_half)
            p = probs[2 * i + sub]
            gp = dot_nt(jnp.where(mine, ga, jnp.zeros_like(ga)), value)
            gs = (p * (gp - jnp.sum(p * gp, axis=-1, keepdims=True))).astype(BF16)
            gq.append(dot_nn(gs, key))
            gk.append(dot_tn(gs, query))
            gv.append(dot_tn(p.astype(BF16), ga))
        g_qkv[:, pl.ds(at, 2 * head_dim)] = (jnp.where(second_half, gq[1], gq[0]) * factor).astype(BF16)
        g_qkv[:, pl.ds(at_k, 2 * head_dim)] = (jnp.where(second_half, gk[1], gk[0]) * factor).astype(BF16)
        g_qkv[:, pl.ds(at_v, 2 * head_dim)] = jnp.where(second_half, gv[1], gv[0]).astype(BF16)
        return carry

    lax.fori_loop(0, HEADS // 2, heads, 0, unroll=True)

    def weights(i, carry):
        at = pl.multiple_of(i * width, width)
        qkv_grad[pl.ds(at, width), :] = dot_tn(g_qkv[:, pl.ds(at, width)], attn_in[...]).astype(qkv_grad.dtype)
        return carry + dot_nn(g_qkv[:, pl.ds(at, width)], w_qkv_t[pl.ds(at, width), :])

    g_in = lax.fori_loop(0, 3, weights, jnp.zeros((rows, width), F32))
    s1 = rms_scale(stream)
    small_grad[GAIN0 : GAIN0 + 1, :] = jnp.sum(g_in * stream * s1, axis=0, keepdims=True)
    n = g_in * gain1
    return g_mid + s1 * n - stream * (s1 * s1 * s1 * jnp.mean(n * stream, axis=-1, keepdims=True))


def between_kernel(experts, cotangent, back, g_small, stat_in, mid, small, stream, w_qkv_t, w_out, attn_in, qkv, probs, attn, small_grad_in,
                   mid0, small0, stat0_in, returned0, extra,
                   qkv_grad, out_grad, small_grad, grad_ref, g_small0_ref, out_ref, small_grad0, g_qkv, g_attn):
    small_grad[...] = small_grad_in[...]
    grad = layer_backward(experts, cotangent[...].astype(F32), back[...], g_small[...], stat_columns(stat_in[...]), mid[...],
                          small[...], stream[...], w_qkv_t, w_out, attn_in, qkv, probs, attn, qkv_grad, out_grad, small_grad, g_qkv, g_attn)
    grad_ref[...] = grad
    stat0 = stat_columns(stat0_in[...])
    _, hidden_full, pair0, pair1 = combine_part(mid0[...], small0[...], stat0, returned0[...], experts)
    g_small0, _, out, projections, v0, v1 = share_backward(grad, small0[...], stat0, hidden_full, pair0, pair1, extra[...], experts)
    g_small0_ref[...] = g_small0
    out_ref[...] = out
    store_small(small_grad0, projections, v0, v1)


def last_kernel(experts, grad_in, back, g_small, stat_in, mid, small, tokens, w_qkv_t, w_out, attn_in, qkv, probs, attn, small_grad_in,
                qkv_grad, out_grad, small_grad, grad_ref, g_qkv, g_attn):
    small_grad[...] = small_grad_in[...]
    grad_ref[...] = layer_backward(experts, grad_in[...], back[...], g_small[...], stat_columns(stat_in[...]), mid[...], small[...],
                                   tokens[...].astype(F32), w_qkv_t, w_out, attn_in, qkv, probs, attn, qkv_grad, out_grad, small_grad,
                                   g_qkv, g_attn)


def local_call(kernel, experts, args, outs, scratch=(), scalars=()):
    return pl.pallas_call(
        functools.partial(kernel, experts),
        out_shape=[jax.ShapeDtypeStruct(shape, dtype) for shape, dtype in outs],
        in_specs=[SMEM if i in scalars else VMEM for i in range(len(args))],
        out_specs=[VMEM] * len(outs),
        scratch_shapes=[pltpu.VMEM(shape, dtype) for shape, dtype in scratch],
        compiler_params=pltpu.CompilerParams(vmem_limit_bytes=60 * 2**20),
        cost_estimate=pl.CostEstimate(flops=10**10, bytes_accessed=6 * 10**7, transcendentals=0),
    )(*args)


class Place:
    def __init__(self, spread):
        self.spread = spread
        self.d, self.e = lax.axis_index("dp"), lax.axis_index("expert")
        self.t, self.f = self.d // spread, lax.rem(self.d, spread)
        self.y, self.c = self.e // 2, lax.rem(self.e, 2)
        self.above, self.below = self.t < LINE - 1, self.t > 0
        self.inside = jnp.logical_and(self.above, self.below)
        self.up = jnp.where(self.t == 1, 1, 0)
        self.ahead = 2 * self.up - 1
        self.sibling = (self.d, self.e + 1 - 2 * self.c)
        self.across = (self.d, lax.rem(self.e + 2, 4))
        self.corner = (self.d, 3 - self.e)
        self.beside = (self.t * spread + 1 - self.f, self.e)
        self.mates = [(self.d, self.e), self.sibling, self.across, self.corner]

    def block(self, i):
        return pick(i, [e for _, e in self.mates])

    def on_line(self, up):
        return (self.d + self.spread * (2 * up - 1), self.e)


def pick(index, values):
    out = values[-1]
    for n in range(len(values) - 2, -1, -1):
        out = jnp.where(index == n, values[n], out)
    return out


def greet(always, place, meanwhile=lambda: None):
    barrier = pltpu.get_barrier_semaphore()
    for device in always:
        pl.semaphore_signal(barrier, inc=1, device_id=device, device_id_type=MESH)
    for up, there in ((1, place.above), (0, place.below)):

        @pl.when(there)
        def _(up=up):
            pl.semaphore_signal(barrier, inc=1, device_id=place.on_line(up), device_id_type=MESH)

    meanwhile()
    ends = place.above.astype(jnp.int32) + place.below.astype(jnp.int32)
    pl.semaphore_wait(barrier, len(always) + ends)


def remote(src, dst, send, recv, device):
    return pltpu.make_async_remote_copy(
        src_ref=src, dst_ref=dst, send_sem=send, recv_sem=recv, device_id=device, device_id_type=MESH)


def dma(*shape):
    return pltpu.SemaphoreType.DMA(shape)


def along(place, body, start=0):
    if start == 0:
        body(place.t)

    def step(k, carry):
        for t in (place.t + k, place.t - k):

            @pl.when(jnp.logical_and(t >= 0, t < LINE))
            def _(t=t):
                body(t)

        return carry

    lax.fori_loop(1, LINE, step, 0)


class Rider:
    partners = ()

    def begin(self):
        pass

    def ready(self):
        pass

    def after_first(self):
        pass

    def in_line(self):
        pass

    def after_relay(self):
        pass

    def finish(self):
        pass


class Line:
    def __init__(self, place, x, part, stage, arrived, final, returned, sems):
        self.p = place
        self.x, self.part, self.stage, self.arrived = x, part, stage, arrived
        self.final, self.returned = final, returned
        (self.out_send, self.x_recv, self.x_send, self.sum_send, self.sum_recv, self.ret_send, self.ret_recv) = sems

    @staticmethod
    def scratch(local, width):
        shape = (local, 4, CAP, width)
        return [
            pltpu.VMEM((local, LINE, 4, CAP, width), BF16),
            pltpu.VMEM((LINE,) + shape, F32),
            pltpu.VMEM((LINE,) + shape, BF16),
            pltpu.VMEM((2, LINE) + shape, BF16),
            pltpu.VMEM((4, local, CAP, width), BF16),
            dma(4), dma(LINE, 4), dma(2, LINE, 4), dma(LINE, 4), dma(2, LINE, 4), dma(4), dma(4),
        ]

    def slot_copy(self, out, i):
        to, p = self.p.mates[i], self.p
        return remote(out.at[to[1]], self.x.at[:, p.t, p.e], self.out_send.at[i], self.x_recv.at[p.t, p.e], to)

    def x_copy(self, up, s, b):
        at = self.x.at[:, s, b]
        return remote(at, at, self.x_send.at[up, s, b], self.x_recv.at[s, b], self.p.on_line(up))

    def sum_copy(self, up, s, b):
        return remote(self.stage.at[s, :, b], self.arrived.at[up, s, :, b], self.sum_send.at[s, b],
                      self.sum_recv.at[up, s, b], self.p.on_line(up))

    def ret_copy(self, i, to_mate=True):
        to = self.p.block(i)
        row = self.p.e if to_mate else to
        return remote(self.final.at[to], self.returned.at[row], self.ret_send.at[i], self.ret_recv.at[row], (self.p.d, to))

    def send_sum(self, up, s, b, total):
        self.stage[s, :, b] = total.astype(BF16)
        self.sum_copy(up, s, b).start()

    def relay(self, n):
        p = self.p
        kind = pick(n, (0, 0, 1, 1, 2, 1, 2, 1, 2, 0, 2, 0))
        b = p.block(pick(n, (0, 1, 0, 1, 0, 2, 1, 3, 2, 2, 3, 3)))
        s = p.t + p.ahead * pick(kind, (1, 2, -1))
        way = jnp.where(kind == 2, 1 - p.up, p.up)

        @pl.when(p.inside)
        def _():
            self.sum_copy(way, s, b).wait_recv()
            self.send_sum(way, s, b, self.part[s, :, b] + self.arrived[way, s, :, b].astype(F32))

    def run(self, out, compute, kept, pieces, rider):
        p = self.p
        t, e = p.t, p.e
        blocks = [b for _, b in p.mates]
        greet(p.mates[1:] + list(rider.partners), p)
        for i in (2, 3, 1):
            self.slot_copy(out, i).start()
        self.x[:, t, e] = out[e]
        rider.begin()
        for i in range(4):
            if i:
                self.x_copy(0, t, blocks[i]).wait_recv()
            for up, there in ((0, p.below), (1, p.above)):

                @pl.when(there)
                def _(up=up, i=i):
                    self.x_copy(up, t, blocks[i]).start()

        rider.ready()

        def step(n, carry):
            k = jnp.where(n < 2, 1, jnp.where(jnp.logical_or(n == 2, n == 5), 2, 3))
            half = jnp.where(jnp.logical_or(n == 1, n >= 4), 1, 0)
            pair = p.y + half - 2 * p.y * half
            first = jnp.where(half == 0, blocks[0], blocks[2])
            second = jnp.where(half == 0, blocks[1], blocks[3])
            for b in (first, second):
                for up, there, onward, before_end in ((0, t + k < LINE, p.below, t == 1), (1, t - k >= 0, p.above, t == LINE - 2)):
                    s = t - k if up else t + k
                    put_off = jnp.logical_and(before_end, n == 1)

                    @pl.when(there)
                    def _(up=up, onward=onward, s=s, b=b, put_off=put_off):
                        self.x_copy(up, s, b).wait_recv()

                        @pl.when(jnp.logical_and(onward, jnp.logical_not(put_off)))
                        def _():
                            self.x_copy(up, s, b).start()

            for up, before_end in ((0, t == 1), (1, t == LINE - 2)):

                @pl.when(jnp.logical_and(before_end, n == 5))
                def _(up=up):
                    for b in (first, second):
                        self.x_copy(up, t - 1 if up else t + 1, b).start()

            @pl.when(jnp.logical_not(p.inside))
            def _():
                s = jnp.where(t == 0, k, LINE - 1 - k)
                compute(s, 2 * pair, 2)

                @pl.when(half == 1)
                def _():
                    kept(s)

            for up, starts, s in ((1, t == 0, k), (0, t == LINE - 1, LINE - 1 - k)):

                @pl.when(starts)
                def _(up=up, s=s):
                    for b in (first, second):
                        self.send_sum(up, s, b, self.part[s, :, b])

            rest = jnp.logical_and(p.inside, jnp.logical_or(n == 5, jnp.logical_and(n >= 1, n <= 2)))

            @pl.when(jnp.logical_or(n == 0, rest))
            def _():
                s = t + p.ahead * jnp.where(n == 0, 0, jnp.where(n == 1, 1, jnp.where(n == 2, -1, 2)))
                compute(s, 0, 4)
                kept(s)

            @pl.when(n == 0)
            def _():
                rider.after_first()

            @pl.when(n == 3)
            def _():
                rider.in_line()

            return carry

        lax.fori_loop(0, 6, step, 0)

        def passing(n, carry):
            self.relay(n)
            pieces(n)
            return carry

        lax.fori_loop(0, 12, passing, 0)
        rider.after_relay()

        def end(i, carry):
            b = p.block(i)
            for up, there in ((1, p.below), (0, p.above)):

                @pl.when(there)
                def _(up=up):
                    self.sum_copy(up, t, b).wait_recv()
                    self.part[t, :, b] = self.part[t, :, b] + self.arrived[up, t, :, b].astype(F32)

            self.final[b] = self.part[t, :, b].astype(BF16)

            @pl.when(i > 0)
            def _():
                self.ret_copy(i).start()

            return carry

        lax.fori_loop(0, 4, end, 0)
        self.returned[e] = self.final[e]

        def sent(n, carry):
            s, b = n // 4, lax.rem(n, 4)
            for up, mine in ((0, jnp.logical_and(p.below, s >= t)), (1, jnp.logical_and(p.above, s <= t))):

                @pl.when(mine)
                def _(up=up):
                    self.x_copy(up, s, b).wait_send()

            @pl.when(s != t)
            def _():
                self.sum_copy(0, s, b).wait_send()

            return carry

        for i in (1, 2, 3):
            self.slot_copy(out, i).wait_send()
        lax.fori_loop(0, 4 * LINE, sent, 0)
        rider.finish()
        for i in (1, 2, 3):
            self.ret_copy(i).wait_send()
            self.ret_copy(i, False).wait_recv()


def split(refs, *counts):
    out, at = [], 0
    for count in counts:
        out.append(refs[at : at + count])
        at += count
    return out + [refs[at:]]


def expert_forward_kernel(spread, parts, late, ride, out, *refs):
    weights_in, given, outs, late_out, whole, scratch, line_refs, sems, ride_refs = split(
        refs, 3 * parts, 8 if ride else 0, 4, late, 5 if ride else 0, 3 * parts, 5, 7)
    (g_all, u_all, keep_sem, load_sem, late_sem), ride_refs = ride_refs[:5], ride_refs[5:]
    returned, x_keep, g_keep, u_keep = outs
    gate, up, down = scratch[:parts], scratch[parts : 2 * parts], scratch[2 * parts :]
    x, part, stage, arrived, final = line_refs
    local, _, _, _, width = x.shape
    p = Place(spread)
    line = Line(p, x, part, stage, arrived, final, returned, sems)
    rider = WeightRider(p, given, whole, ride_refs) if ride else Rider()

    def load(i):
        given = weights_in[i].shape[0]
        return pltpu.make_async_copy(weights_in[i], scratch[i].at[0:given], load_sem.at[i])

    for i in range(3 * parts):
        load(i).start()

    def late_copy():
        return remote(weights_in[-2].at[1:local], scratch[-1].at[1:local], late_sem.at[0], late_sem.at[1], p.beside)

    def late_store():
        return pltpu.make_async_copy(scratch[-1], late_out[0], late_sem.at[2])

    def keep_x(s):
        return pltpu.make_async_copy(x.at[:, s], x_keep.at[:, s], keep_sem.at[0, s])

    def keep_g(s):
        return pltpu.make_async_copy(g_all.at[s], g_keep.at[s], keep_sem.at[1, s])

    def keep_u(s):
        return pltpu.make_async_copy(u_all.at[s], u_keep.at[s], keep_sem.at[2, s])

    def kept(s):
        keep_x(s).start()
        keep_g(s).start()
        keep_u(s).start()

    def compute(s, first, count):
        rows = count * CAP
        at = pl.multiple_of(first * CAP, CAP)

        def one(l, carry):
            rows_in = x[l, s, pl.ds(first, count)].reshape(rows, width)
            total = jnp.zeros((rows, width), F32)
            for q in range(parts):
                cols = gate[q].shape[2]
                here = slice(q * cols, (q + 1) * cols)
                g = dot_nn(rows_in, gate[q][l])
                u = dot_nn(rows_in, up[q][l])
                g_all[s, l, pl.ds(at, rows), here] = g
                u_all[s, l, pl.ds(at, rows), here] = u
                act = (g * jax.nn.sigmoid(g) * u).astype(BF16)
                total = total + dot_nn(act, down[q][l])
            part[s, l, pl.ds(first, count)] = total.reshape(count, CAP, width)
            return carry

        lax.fori_loop(0, local, one, 0)

    class Loaded(Rider):
        partners = [p.beside] if late else []
        after_first, in_line, after_relay = rider.after_first, rider.in_line, rider.after_relay

        def begin(self):
            if late:
                late_copy().start()
            rider.begin()

        def ready(self):
            for i in range(3 * parts):
                load(i).wait()
            if late:
                late_copy().wait_recv()
                late_store().start()

        def finish(self):
            rider.finish()
            if late:
                late_copy().wait_send()
                late_store().wait()

    line.run(out, compute, kept, lambda n: None, Loaded())
    for s in range(LINE):
        keep_x(s).wait()
        keep_g(s).wait()
        keep_u(s).wait()


def expert_backward_kernel(spread, parts, exchange, ride, out, *refs):
    loads_in, given, outs, came, ride_outs, loads, line_refs, sems, rest = split(
        refs, 3 + 3 * parts, 4 if ride else 0, 1 + 3 * parts - exchange, exchange, 3 if ride else 0, 3 + 3 * parts, 5, 7)
    (act_all, gg_all, gu_all), grads, (load_sem, grad_sem, w_send, w_recv), ride_refs = split(rest, 3, 3 * parts, 4)
    returned, grads_out = outs[0], list(outs[1:])
    if exchange:
        grads_out.insert(1, None)
    x_in, g_all, u_all = loads[:3]
    gate, up, down = loads[3 : 3 + parts], loads[3 + parts : 3 + 2 * parts], loads[3 + 2 * parts :]
    x, part, stage, arrived, final = line_refs
    local, _, _, _, width = x.shape
    p = Place(spread)
    line = Line(p, x, part, stage, arrived, final, returned, sems)
    rider = GradientRider(p, given, ride_outs, ride_refs) if ride else Rider()

    def load(i):
        return pltpu.make_async_copy(loads_in[i], loads[i], load_sem.at[i])

    def store(i, l):
        return pltpu.make_async_copy(grads[i].at[l], grads_out[i].at[l], grad_sem.at[i, l])

    for i in range(3 + 3 * parts):
        load(i).start()

    def compute(s, first, count):
        rows = count * CAP
        at = pl.multiple_of(first * CAP, CAP)
        into = pl.ds(pl.multiple_of((4 * s + first) * CAP, CAP), rows)

        def one(l, carry):
            rows_in = x[l, s, pl.ds(first, count)].reshape(rows, width)
            total = jnp.zeros((rows, width), F32)
            for q in range(parts):
                cols = gate[q].shape[2]
                here = slice(q * cols, (q + 1) * cols)
                g, u = g_all[s, l, pl.ds(at, rows), here], u_all[s, l, pl.ds(at, rows), here]
                g_act = dot_nt(rows_in, down[q][l])
                sigma = jax.nn.sigmoid(g)
                swish = g * sigma
                gg = (g_act * u * sigma * (1.0 + g * (1.0 - sigma))).astype(BF16)
                gu = (g_act * swish).astype(BF16)
                act_all[l, into, here] = (swish * u).astype(BF16)
                gg_all[l, into, here] = gg
                gu_all[l, into, here] = gu
                total = total + dot_nt(gg, gate[q][l]) + dot_nt(gu, up[q][l])
            part[s, l, pl.ds(first, count)] = total.reshape(count, CAP, width)
            return carry

        lax.fori_loop(0, local, one, 0)

    def weights(kind, l):
        x_rows, g_rows = (a[l].reshape(LINE * 4 * CAP, width) for a in (x_in, x))
        value = dot_tn(act_all[l], g_rows) if kind == 2 else dot_tn(x_rows, (gg_all, gu_all)[kind][l])
        for q in range(parts):
            i = kind * parts + q
            cols = gate[q].shape[2]
            here = slice(q * cols, (q + 1) * cols)
            grads[i][l] = (value[here] if kind == 2 else value[:, here]).astype(grads[i].dtype)
            if grads_out[i] is not None:
                store(i, l).start()

    def pieces(n):
        for kind in range(3):
            at = n - 1 - 2 * local * kind

            @pl.when(jnp.logical_and(lax.rem(n, 2) == 1, jnp.logical_and(at >= 0, at < 2 * local)))
            def _(kind=kind, at=at):
                weights(kind, at // 2)

        @pl.when(n == 2 * local - 1)
        def _():
            for copy in sent_gate():
                copy.start()

    def sent_gate():
        return [remote(grads[1], came[0], w_send.at[0], w_recv.at[0], p.beside)] if exchange else []

    class Loaded(Rider):
        partners = [p.beside] if exchange else []
        after_first, in_line, after_relay, finish = (
            rider.after_first, rider.in_line, rider.after_relay, rider.finish)

        def begin(self):
            rider.begin()

        def ready(self):
            for i in range(3 + 3 * parts):
                load(i).wait()

    line.run(out, compute, lambda s: None, pieces, Loaded())
    for copy in sent_gate():
        copy.wait()
    for i in range(3 * parts):
        for l in range(local if grads_out[i] is not None else 0):
            store(i, l).wait()


def remote_params(call_id):
    return pltpu.CompilerParams(collective_id=call_id, has_side_effects=True, vmem_limit_bytes=61 * 2**20)


def struct(shape, dtype):
    return jax.ShapeDtypeStruct(tuple(shape), dtype)


def expert_forward(spread, call_id, out, weights, late=False, ride=None):
    parts = len(weights) // 3
    _, local, cap, width = out.shape
    columns = sum(w.shape[2] for w in weights[:parts])
    kept = (LINE, local, 4 * cap, columns)
    outs = [struct(out.shape, BF16), struct((local, LINE, 4, cap, width), BF16), struct(kept, F32), struct(kept, F32)]
    outs += [struct(weights[-2].shape, BF16)] * late
    scratch = [pltpu.VMEM((local,) + w.shape[1:], BF16) for w in weights] + Line.scratch(local, width)
    scratch += [pltpu.VMEM(kept, F32), pltpu.VMEM(kept, F32), dma(3, LINE), dma(3 * parts), dma(3)]
    more = ride or ()
    count = LINE * spread
    if ride:
        outs += [struct((count * s.shape[0], s.shape[1]), BF16) for s in ride[3:6]]
        outs += [struct(w.shape, BF16) for w in ride[6:]]
        scratch += WeightRider.scratch(count)
    return pl.pallas_call(
        functools.partial(expert_forward_kernel, spread, parts, int(late), ride is not None),
        out_shape=outs,
        in_specs=[VMEM] + [ANY] * (len(weights) - 1) + [VMEM if late else ANY] + [ANY] * len(more),
        out_specs=[VMEM] + [ANY] * (len(outs) - 1),
        scratch_shapes=scratch,
        compiler_params=remote_params(call_id),
        cost_estimate=pl.CostEstimate(flops=2 * 10**10, bytes_accessed=2 * 10**8, transcendentals=0),
    )(out, *weights, *more)


def expert_backward(spread, call_id, out, kept, weights, exchange=False, ride=None):
    parts = len(weights) // 3
    _, local, cap, width = out.shape
    columns = sum(w.shape[2] for w in weights[:parts])
    loads = list(kept) + list(weights)
    grads = [(w.shape, F32 if i % parts == 0 else BF16) for i, w in enumerate(weights)]
    wide = pltpu.VMEM((local, LINE * 4 * cap, columns), BF16)
    outs = [struct(out.shape, BF16)] + [struct(*g) for i, g in enumerate(grads) if not exchange or i != 1]
    if exchange:
        outs.append(struct(*grads[1]))
    specs = [VMEM] + [ANY] * len(grads)
    scratch = [pltpu.VMEM(a.shape, a.dtype) for a in loads] + Line.scratch(local, width)
    scratch += [wide] * 3 + [pltpu.VMEM(*g) for g in grads] + [dma(len(loads)), dma(len(grads), local), dma(1), dma(1)]
    more = ride or ()
    if ride:
        depths = [g.shape[0] // (LINE * spread) for g in ride[:2]]
        outs.append(struct((LINE, spread, sum(depths) // 2, width // 2), F32))
        outs += [struct(g.shape, BF16) for g in ride[2:]]
        specs += [VMEM, ANY, ANY]
        scratch += GradientRider.scratch(spread, depths, width)
    return pl.pallas_call(
        functools.partial(expert_backward_kernel, spread, parts, int(exchange), ride is not None),
        out_shape=outs,
        in_specs=[VMEM] + [ANY] * (len(loads) + len(more)),
        out_specs=specs,
        scratch_shapes=scratch,
        compiler_params=remote_params(call_id),
        cost_estimate=pl.CostEstimate(flops=4 * 10**10, bytes_accessed=2 * 10**8, transcendentals=0),
    )(out, *loads, *more)


def from_partner(array, shift, spread, groups):
    pairs = [
        (t * spread + (f + shift) % spread, t * spread + f) for t in range(groups) for f in range(spread)
    ]
    return lax.ppermute(array, "dp", pairs)


def to_partner(array, shift, spread, groups):
    pairs = [
        (t * spread + f, t * spread + (f + shift) % spread) for t in range(groups) for f in range(spread)
    ]
    return lax.ppermute(array, "dp", pairs)


def pair_weights(shard, axis, spread):
    parts = [shard] + [from_partner(shard, i, spread, LINE) for i in range(1, spread)]
    if shard.shape[axis] % 128:
        return [jnp.concatenate(parts, axis=axis)]
    return parts


def pair_sum(parts, axis, spread):
    if len(parts) == 1 and spread > 1:
        parts = jnp.split(parts[0], spread, axis=axis)
    total = parts[0]
    for i in range(1, spread):
        total = total + to_partner(parts[i].astype(BF16), i, spread, LINE).astype(F32)
    return total


class LineGather:
    def __init__(self, place, pairs, shards, quarters, sems):
        self.p, self.shards, self.quarters = place, shards, quarters
        self.send, self.recv, self.x_send, self.x_recv = sems
        self.columns = [place.f, 1 - place.f] if pairs else [0]

    @staticmethod
    def shapes(shards, columns):
        (a, wide), (b, _), (c, narrow) = shards
        return [(LINE, columns, a // 2, wide // 2), (LINE, columns, b // 2, wide // 2), (LINE, columns, c, narrow)]

    @staticmethod
    def scratch(columns):
        return [dma(2, LINE, columns, 3), dma(LINE, columns, 3), dma(3), dma(3)]

    def copy(self, kind, up, t, f):
        at = self.quarters[kind].at[t, f]
        return remote(at, at, self.send.at[up, t, f, kind], self.recv.at[t, f, kind], self.p.on_line(up))

    def x_copy(self, kind, f):
        at = self.quarters[kind].at[self.p.t, f]
        return remote(at, at, self.x_send.at[kind], self.x_recv.at[kind], self.p.beside)

    def both_ways(self, f):
        p = self.p
        for up, there in ((0, p.below), (1, p.above)):

            @pl.when(there)
            def _(up=up):
                for kind in range(3):
                    self.copy(kind, up, p.t, f).start()

    def begin(self):
        p, f = self.p, self.columns[0]
        for kind in (0, 1):
            half, wide = self.quarters[kind].shape[2:]
            self.quarters[kind][p.t, f] = self.shards[kind][
                pl.ds(pl.multiple_of(p.y * half, 16), half), pl.ds(pl.multiple_of(p.c * wide, 128), wide)]
        self.quarters[2][p.t, f] = self.shards[2][...]
        for kind in range(3 if len(self.columns) == 2 else 0):
            self.x_copy(kind, f).start()
        self.both_ways(f)

    def beside(self, then):
        for f in self.columns[1:]:
            for kind in range(3):
                self.x_copy(kind, f).wait_recv()
            self.both_ways(f)
            then(self.p.t, f)

    def step(self, k, then):
        p = self.p
        for f in self.columns:
            for up, there, onward in ((0, p.t + k < LINE, p.below), (1, p.t - k >= 0, p.above)):
                t = p.t - k if up else p.t + k

                @pl.when(there)
                def _(up=up, onward=onward, t=t, f=f):
                    for kind in range(3):
                        self.copy(kind, up, t, f).wait_recv()

                    @pl.when(onward)
                    def _():
                        for kind in range(3):
                            self.copy(kind, up, t, f).start()

                    then(t, f)

    def finish(self):
        p = self.p

        def line(t, carry):
            for up, mine in ((0, jnp.logical_and(p.below, t >= p.t)), (1, jnp.logical_and(p.above, t <= p.t))):

                @pl.when(mine)
                def _(up=up):
                    for f in self.columns:
                        for kind in range(3):
                            self.copy(kind, up, t, f).wait_send()

            return carry

        lax.fori_loop(0, LINE, line, 0)
        for f in self.columns[1:]:
            for kind in range(3):
                self.x_copy(kind, 1 - f).wait_send()


class Spread:
    def __init__(self, place, quarters, shards, whole, sems):
        self.p, self.quarters, self.shards, self.whole = place, quarters, shards, whole
        self.y_send, self.y_recv, self.c_send, self.c_recv, self.l_sem, self.s_sem = sems

    @staticmethod
    def scratch(count):
        return [dma(count, 2), dma(count, 2), dma(count, 2, 2), dma(count, 2, 2), dma(count, 3), dma(3)]

    def region(self, kind, s, y, c):
        depth = self.shards[kind].shape[0]
        if kind == 2:
            return self.whole[2].at[pl.ds(pl.multiple_of(s * depth, 16), depth)]
        half, wide = depth // 2, self.shards[kind].shape[1] // 2
        return self.whole[kind].at[
            pl.ds(pl.multiple_of(s * depth + y * half, 16), half), pl.ds(pl.multiple_of(c * wide, 128), wide)]

    def mine(self, kind, s):
        return self.region(kind, s, self.p.y, self.p.c)

    def y_copy(self, kind, src, s):
        return remote(src, self.mine(kind, s), self.y_send.at[s, kind], self.y_recv.at[s, kind], self.p.across)

    def y_came(self, kind, s):
        at = self.region(kind, s, 1 - self.p.y, self.p.c)
        return remote(at, at, self.y_send.at[s, kind], self.y_recv.at[s, kind], self.p.across)

    def c_copy(self, kind, src, s, y):
        return remote(src, self.region(kind, s, y, self.p.c), self.c_send.at[s, y, kind], self.c_recv.at[s, y, kind],
                      self.p.sibling)

    def c_came(self, kind, s, y):
        at = self.region(kind, s, y, 1 - self.p.c)
        return remote(at, at, self.c_send.at[s, y, kind], self.c_recv.at[s, y, kind], self.p.sibling)

    def local(self, kind, src, s):
        return pltpu.make_async_copy(src, self.mine(kind, s), self.l_sem.at[s, kind])

    def shard(self, kind):
        depth = self.shards[kind].shape[0]
        at = self.whole[kind].at[pl.ds(pl.multiple_of(self.p.d * depth, 16), depth)]
        return pltpu.make_async_copy(self.shards[kind], at, self.s_sem.at[kind])

    def own_shard(self):
        for kind in range(3):
            self.shard(kind).start()

    def push(self, s, sources, here=True):
        if here:
            for kind in range(3):
                self.local(kind, sources[kind], s).start()
        for kind in (0, 1):
            self.y_copy(kind, sources[kind], s).start()
            self.c_copy(kind, sources[kind], s, self.p.y).start()

    def across(self, s):
        for kind in (0, 1):
            self.y_came(kind, s).wait_recv()
            self.c_copy(kind, self.region(kind, s, 1 - self.p.y, self.p.c), s, 1 - self.p.y).start()

    def finish_shard(self, s, here=True):
        @pl.when(s != self.p.d)
        def _():
            for kind in range(3 if here else 0):
                self.local(kind, self.mine(kind, s), s).wait()
            for kind in (0, 1):
                self.y_came(kind, s).wait_send()
                for y in (0, 1):
                    self.c_came(kind, s, y).wait_send()
                    self.c_came(kind, s, y).wait_recv()

    def finish_own(self):
        for kind in range(3):
            self.shard(kind).wait()


class WeightRider:
    def __init__(self, place, given, whole, sems):
        self.p, self.quarters, self.own, self.other = place, given[:3], given[6:], whole[3:]
        self.w_send, self.w_recv, self.x_send, self.x_recv, *more = sems
        self.spread = Spread(place, self.quarters, given[3:6], whole[:3], more)

    @staticmethod
    def scratch(count):
        return [dma(2), dma(2), dma(LINE, 3), dma(LINE, 3)] + Spread.scratch(count)

    def place_of(self, t):
        return t * self.p.spread + self.p.f

    def beside_of(self, t):
        return t * self.p.spread + 1 - self.p.f

    def x_copy(self, kind, t, s):
        return remote(self.quarters[kind].at[t, 0], self.spread.mine(kind, s), self.x_send.at[t, kind],
                      self.x_recv.at[t, kind], self.p.beside)

    def weight(self, i):
        return remote(self.own[i], self.other[i], self.w_send.at[i], self.w_recv.at[i], self.p.beside)

    def begin(self):
        self.spread.own_shard()

        def body(t):
            for kind in range(3):
                self.x_copy(kind, t, self.place_of(t)).start()

            @pl.when(t != self.p.t)
            def _():
                self.spread.push(self.place_of(t), [q.at[t, 0] for q in self.quarters])

        along(self.p, body)
        for i in range(2):
            self.weight(i).start()

    def after_first(self):
        pass

    def in_line(self):
        def body(t):
            s = self.beside_of(t)
            for kind in range(3):
                self.x_copy(kind, t, s).wait_recv()
            self.spread.push(s, [self.spread.mine(kind, s) for kind in range(3)], here=False)

        along(self.p, body)

    def after_relay(self):
        along(self.p, lambda t: self.spread.across(self.place_of(t)), start=1)
        along(self.p, lambda t: self.spread.across(self.beside_of(t)))

    def finish(self):
        self.spread.finish_own()
        for i in range(2):
            self.weight(i).wait()

        def line(t, carry):
            for kind in range(3):
                self.x_copy(kind, t, self.place_of(t)).wait_send()
            self.spread.finish_shard(self.place_of(t))
            self.spread.finish_shard(self.beside_of(t), here=False)
            return carry

        lax.fori_loop(0, LINE, line, 0)


def pack_small(l, router, const, gains, vectors, rows, small):
    rows[...] = jnp.zeros(rows.shape, F32)
    for r in range(router.shape[0]):
        rows[r : r + 1, :] = router[r, l : l + 1, :]
    for j in (0, 1):
        rows[CONST0 + 2 * j : CONST0 + 2 * j + 2, :] = const[l, j]
    rows[GAIN0 : GAIN0 + 2, :] = gains[l]
    rows[VECTOR0 : VECTOR0 + 2, :] = vectors[l]
    place = lax.broadcasted_iota(jnp.int32, (rows.shape[0], 128), 0) == lanes(rows.shape[0])
    small[l] = dot_tn(rows[...].astype(BF16), place.astype(BF16)).astype(BF16)


def dense_gather_kernel(spread, qkv_wide, out_wide, router, const, gains, vectors, routes_in, *refs):
    p = Place(spread)
    wide, whole, quarters1, (routes_all,), own, firsts, partner, shards1_out, quarters0, loaded, rounded, shards, (rows, routes), rest = split(
        refs, 3, 3, 3, 1, 6, 2, 2, 3, 3, 3, 3, 3, 2)
    qkv, out, small = shards
    sems0, sems1, (r_send, r_recv, w_send, w_recv, load_sem, own_sem, first_sem, shard_sem), spread_sems = split(rest, 4, 4, 8)
    shards0, shards1 = ([ref.at[l] for ref in (qkv, out, small)] for l in (0, 1))
    line0 = LineGather(p, True, shards0, quarters0, sems0)
    line1 = LineGather(p, False, shards1, quarters1, sems1)
    spreading = Spread(p, quarters0, shards0, whole, spread_sems)

    def load(l, kind):
        return pltpu.make_async_copy(wide[kind].at[l], loaded[kind].at[l], load_sem.at[l, kind])

    def store(l, kind):
        return pltpu.make_async_copy(rounded[kind].at[l], own[3 * l + kind], own_sem.at[l, kind])

    def first(l):
        return pltpu.make_async_copy(rounded[2].at[l, 0:1], firsts[l], first_sem.at[l])

    def weight(kind):
        return remote(rounded[kind].at[0], partner[kind], w_send.at[kind], w_recv.at[kind], p.beside)

    def round_weights(l, kind):
        load(l, kind).wait()

        def one(i, carry):
            rounded[kind][l, i] = loaded[kind][l, i].astype(BF16)
            return carry

        lax.fori_loop(0, rounded[kind].shape[1], one, 0)
        store(l, kind).start()
        if kind == 2:
            first(l).start()

    def shard1(kind):
        return pltpu.make_async_copy(shards[kind].at[1], shards1_out[kind], shard_sem.at[kind])

    for l in (0, 1):
        for kind in range(3):
            load(l, kind).start()
    def round_shards():
        for l in (0, 1):
            qkv[l], out[l] = qkv_wide[l].astype(BF16), out_wide[l].astype(BF16)
            pack_small(l, router, const, gains, vectors, rows, small)
        for kind in range(3):
            shard1(kind).start()
        routes[...] = jnp.zeros(routes.shape, jnp.int32)
        for l in (0, 1):
            routes[2 * l : 2 * l + 2, 0 : routes_in.shape[2]] = routes_in[l]

    greet(p.mates[1:] + [p.beside], p, round_shards)

    def route_copy(i, row):
        return remote(routes, routes_all.at[row], r_send.at[i], r_recv.at[row], p.mates[i])

    def push(t, f):
        spreading.push(t * spread + f, [q.at[t, f] for q in quarters0])

    line0.begin()
    for kind in (0, 1):
        round_weights(0, kind)
        weight(kind).start()
    routes_all[p.e] = routes[...]
    for i in (1, 2, 3):
        route_copy(i, p.e).start()
    spreading.own_shard()
    line0.beside(push)
    line1.begin()
    lax.fori_loop(1, LINE, lambda k, carry: (line0.step(k, push), carry)[1], 0)
    round_weights(0, 2)
    lax.fori_loop(1, LINE, lambda k, carry: (line1.step(k, lambda t, f: None), carry)[1], 0)
    for kind in range(3):
        round_weights(1, kind)
    along(p, lambda t: spreading.across(t * spread + p.f), start=1)
    along(p, lambda t: spreading.across(t * spread + 1 - p.f))
    spreading.finish_own()
    lax.fori_loop(0, LINE * spread, lambda s, carry: (spreading.finish_shard(s), carry)[1], 0)
    line0.finish()
    line1.finish()
    for l in (0, 1):
        for kind in range(3):
            store(l, kind).wait()
        first(l).wait()
    for kind in (0, 1):
        weight(kind).wait()
    for kind in range(3):
        shard1(kind).wait()
    for i in (1, 2, 3):
        route_copy(i, p.e).wait_send()
        route_copy(i, p.mates[i][1]).wait_recv()


def dense_gather(spread, call_id, arrays, routes, wide):
    count = spread * LINE
    layers, depth = arrays[1].shape[:2]
    shards = [arrays[0].shape[1:], arrays[1].shape[1:], (depth, 128)]
    pairs, single = LineGather.shapes(shards, 2), LineGather.shapes(shards, 1)
    outs = [struct((count * rows, width), BF16) for rows, width in shards]
    packed = (8, -(-routes.shape[2] // 128) * 128)
    outs += [struct(q, BF16) for q in single] + [struct((4,) + packed, jnp.int32)]
    outs += [struct(w.shape[1:], BF16) for w in wide] * 2 + [struct((1,) + wide[2].shape[2:], BF16)] * 2
    outs += [struct(w.shape[1:], BF16) for w in wide[:2]] + [struct(s, BF16) for s in shards]
    scratch = [pltpu.VMEM(q, BF16) for q in pairs] + [pltpu.VMEM(w.shape, F32) for w in wide]
    scratch += [pltpu.VMEM(w.shape, BF16) for w in wide] + [pltpu.VMEM((layers,) + s, BF16) for s in shards]
    scratch += [pltpu.VMEM((32, depth), F32), pltpu.VMEM(packed, jnp.int32)] + LineGather.scratch(2) + LineGather.scratch(1)
    scratch += [dma(4), dma(4), dma(2), dma(2), dma(2, 3), dma(2, 3), dma(2), dma(3)]
    return pl.pallas_call(
        functools.partial(dense_gather_kernel, spread),
        out_shape=outs,
        in_specs=[VMEM] * (len(arrays) + 1) + [ANY] * 3,
        out_specs=[ANY] * 3 + [VMEM] * 4 + [ANY] * 13,
        scratch_shapes=scratch + Spread.scratch(count),
        compiler_params=remote_params(call_id),
        cost_estimate=pl.CostEstimate(flops=10**10, bytes_accessed=10**8, transcendentals=0),
    )(*arrays, routes, *wide)


class Halve:
    def __init__(self, place, grads, quarter, scratch):
        self.p, self.grads, self.quarter = place, grads, quarter
        (self.mine, self.core, self.stage, self.came, self.l_sem, self.a_send, self.a_recv, self.y_send,
         self.y_recv) = scratch
        self.depths = [g.shape[0] // (LINE * place.spread) for g in grads]
        self.wide = grads[0].shape[1] // 2

    @staticmethod
    def scratch(spread, depths, width):
        count, rows, wide = LINE * spread, sum(depths) // 2, width // 2
        half = pltpu.VMEM((LINE, spread, rows, wide), BF16)
        everything = pltpu.VMEM((count * sum(depths), wide), BF16)
        return [everything, everything, half, half, dma(2), dma(2), dma(2), dma(LINE), dma(LINE)]

    def rows_of(self, kind):
        first = 0 if kind == 0 else self.grads[0].shape[0]
        return slice(first, first + self.grads[kind].shape[0])

    def lanes(self, c):
        return pl.ds(pl.multiple_of(c * self.wide, 128), self.wide)

    def local(self, kind):
        return pltpu.make_async_copy(
            self.grads[kind].at[:, self.lanes(self.p.c)], self.mine.at[self.rows_of(kind)], self.l_sem.at[kind])

    def a_copy(self, kind):
        return remote(self.grads[kind].at[:, self.lanes(1 - self.p.c)], self.core.at[self.rows_of(kind)],
                      self.a_send.at[kind], self.a_recv.at[kind], self.p.sibling)

    def y_copy(self, t):
        return remote(self.stage.at[t], self.came.at[t], self.y_send.at[t], self.y_recv.at[t], self.p.across)

    def pieces(self, t, f, y):
        s, row = t * self.p.spread + f, 0
        for kind, depth in enumerate(self.depths):
            at = self.rows_of(kind).start + s * depth + y * (depth // 2)
            here = pl.ds(pl.multiple_of(at, 16), depth // 2)
            yield slice(row, row + depth // 2), self.mine[here, :].astype(F32) + self.core[here, :].astype(F32)
            row += depth // 2

    def order(self, i):
        t = self.p.t
        down = LINE - 1 - i - jnp.where(LINE - 1 - i <= t, 1, 0)
        up = i + jnp.where(i >= t, 1, 0)
        return jnp.where(i == LINE - 1, t, jnp.where(t >= LINE // 2, up, down))

    def begin(self):
        for kind in (0, 1):
            self.a_copy(kind).start()
            self.local(kind).start()

    def after_first(self):
        for kind in (0, 1):
            self.a_copy(kind).wait_recv()
            self.local(kind).wait()

        def body(i, carry):
            t = self.order(i)
            for f in range(self.p.spread):
                for where, value in self.pieces(t, f, 1 - self.p.y):
                    self.stage[t, f, where] = value.astype(BF16)
            self.y_copy(t).start()
            return carry

        lax.fori_loop(0, LINE, body, 0)

        def own(t, carry):
            for f in range(self.p.spread):
                for where, value in self.pieces(t, f, self.p.y):
                    self.quarter[t, f, where] = value
            return carry

        lax.fori_loop(0, LINE, own, 0)

    def add(self, t):
        self.y_copy(t).wait_recv()
        self.quarter[t] = self.quarter[t] + self.came[t].astype(F32)

    def after_relay(self):
        lax.fori_loop(0, LINE, lambda i, carry: (self.add(self.order(i)), carry)[1], 0)

    def finish(self):
        for kind in (0, 1):
            self.a_copy(kind).wait_send()
        lax.fori_loop(0, LINE, lambda t, carry: (self.y_copy(t).wait_send(), carry)[1], 0)


class GradientRider:
    def __init__(self, place, given, outs, scratch):
        self.halve = Halve(place, given[:2], outs[0], scratch[:9])
        self.own, self.other = given[2:], outs[1:]
        self.p = place
        self.w_send, self.w_recv = scratch[9:]

    @staticmethod
    def scratch(spread, depths, width):
        return Halve.scratch(spread, depths, width) + [dma(2), dma(2)]

    def weight(self, i):
        return remote(self.own[i], self.other[i], self.w_send.at[i], self.w_recv.at[i], self.p.beside)

    def begin(self):
        self.halve.begin()
        for i in range(2):
            self.weight(i).start()

    def after_first(self):
        self.halve.after_first()

    def in_line(self):
        pass

    def after_relay(self):
        self.halve.after_relay()

    def finish(self):
        self.halve.finish()
        for i in range(2):
            self.weight(i).wait()


class LineSum:
    def __init__(self, place, depths, quarter, sums, scratch):
        self.p, self.depths, self.quarter, self.sums = place, depths, quarter, sums
        (self.stage, self.came, self.stage_x, self.came_x, self.z_send, self.z_recv, self.x_send, self.x_recv,
         self.e_send, self.e_recv) = scratch
        self.wide = sums[0].shape[1] // 2

    @staticmethod
    def scratch(spread, depths, width):
        rows, wide = sum(depths) // 2, width // 2
        return [
            pltpu.VMEM((LINE, spread, rows, wide), BF16),
            pltpu.VMEM((2, LINE, spread, rows, wide), BF16),
            pltpu.VMEM((rows, wide), BF16),
            pltpu.VMEM((rows, wide), BF16),
            dma(LINE), dma(2, LINE), dma(1), dma(1), dma(3, 2), dma(3, 2),
        ]

    def lanes(self, c):
        return pl.ds(pl.multiple_of(c * self.wide, 128), self.wide)

    def z_copy(self, up, t):
        return remote(self.stage.at[t], self.came.at[up, t], self.z_send.at[t], self.z_recv.at[up, t], self.p.on_line(up))

    def x_copy(self):
        return remote(self.stage_x, self.came_x, self.x_send.at[0], self.x_recv.at[0], self.p.beside)

    def e_copy(self, i, kind, y, c):
        half = self.depths[kind] // 2
        at = self.sums[kind].at[pl.ds(pl.multiple_of(y * half, 8), half), self.lanes(c)]
        return remote(at, at, self.e_send.at[i, kind], self.e_recv.at[i, kind], self.p.across if i == 0 else self.p.sibling)

    def start(self, t):
        p = self.p
        for up, mine in ((1, jnp.logical_and(p.t == 0, t > 0)), (0, jnp.logical_and(p.t == LINE - 1, t < LINE - 1))):

            @pl.when(mine)
            def _(up=up):
                self.stage[t] = self.quarter[t].astype(BF16)
                self.z_copy(up, t).start()

    def relay(self, kind):
        p = self.p

        @pl.when(p.inside)
        def _():
            t = {"near": p.t + p.ahead, "far": p.t + 2 * p.ahead, "back": p.t - p.ahead}[kind]
            way = 1 - p.up if kind == "back" else p.up
            self.z_copy(way, t).wait_recv()
            self.stage[t] = (self.quarter[t] + self.came[way, t].astype(F32)).astype(BF16)
            self.z_copy(way, t).start()

    def after_z(self):
        p = self.p

        for up, there in ((1, p.below), (0, p.above)):

            @pl.when(there)
            def _(up=up):
                self.z_copy(up, p.t).wait_recv()
                self.quarter[p.t] = self.quarter[p.t] + self.came[up, p.t].astype(F32)

        self.stage_x[...] = self.quarter[p.t, 1 - p.f].astype(BF16)
        self.x_copy().start()

    def after_x(self):
        p = self.p
        self.x_copy().wait_recv()
        row = 0
        for kind, depth in enumerate(self.depths):
            half = depth // 2
            value = self.quarter[p.t, p.f, row : row + half] + self.came_x[row : row + half].astype(F32)
            self.sums[kind][pl.ds(pl.multiple_of(p.y * half, 8), half), self.lanes(p.c)] = value
            row += half
        for i in (0, 1):
            for kind in (0, 1):
                self.e_copy(i, kind, p.y, p.c).start()

    def finish(self):
        p = self.p
        for kind in (0, 1):
            self.e_copy(0, kind, 1 - p.y, p.c).wait_recv()
            self.e_copy(2, kind, 1 - p.y, p.c).start()
        for kind in (0, 1):
            self.e_copy(0, kind, p.y, p.c).wait_send()
            self.e_copy(1, kind, p.y, p.c).wait_send()
            self.e_copy(1, kind, p.y, 1 - p.c).wait_recv()
            self.e_copy(2, kind, 1 - p.y, p.c).wait_send()
            self.e_copy(2, kind, 1 - p.y, 1 - p.c).wait_recv()
        self.x_copy().wait_send()

        def body(t, carry):
            @pl.when(t != p.t)
            def _():
                self.z_copy(0, t).wait_send()

            return carry

        lax.fori_loop(0, LINE, body, 0)


class SmallSum:
    def __init__(self, place, grads, total, scratch):
        self.p, self.grads, self.total = place, grads, total
        self.stage, self.came, self.send, self.recv = scratch
        p = place
        near = (p.d + p.spread - 2 * p.spread * lax.rem(p.t, 2), p.e)
        self.far = (lax.rem(p.d + 2 * p.spread, LINE * p.spread), p.e)
        self.partners = [p.sibling, p.across, near, self.far, p.beside]

    @staticmethod
    def scratch(rows, width):
        half = pltpu.VMEM((5, rows, width // 2), F32)
        return [half, half, dma(6), dma(6)]

    def lanes(self, c):
        wide = self.grads.shape[1] // 2
        return pl.ds(pl.multiple_of(c * wide, 128), wide)

    def copy(self, i):
        src = self.grads.at[:, self.lanes(1 - self.p.c)] if i == 0 else self.stage.at[i]
        return remote(src, self.came.at[i], self.send.at[i], self.recv.at[i], self.partners[i])

    def last(self, c):
        at = self.total.at[:, self.lanes(c)]
        return remote(at, at, self.send.at[5], self.recv.at[5], self.p.sibling)

    def step(self, i):
        if i == 0:
            self.copy(0).start()
            return
        self.copy(i - 1).wait_recv()
        mine = self.grads[:, self.lanes(self.p.c)] if i == 1 else self.stage[i - 1]
        value = mine + self.came[i - 1]
        if i < 5:
            self.stage[i] = value
            self.copy(i).start()
        else:
            self.total[:, self.lanes(self.p.c)] = value
            self.last(self.p.c).start()

    def finish(self):
        for i in range(5):
            self.copy(i).wait_send()
        self.last(self.p.c).wait_send()
        self.last(1 - self.p.c).wait_recv()


def dense_reduce_kernel(spread, depths, small0, small1, res, qkv0, out0, quarter1, up0, down0, small_sum, *refs):
    p = Place(spread)
    sums, came, (small, mine0, mine1), (w_send, w_recv), halve_refs, line0, line1, small_refs = split(refs, 2, 2, 3, 2, 9, 10, 10)
    sums0, sums1 = ([ref.at[l] for ref in sums] for l in (0, 1))
    halve = Halve(p, (qkv0, out0), mine0, halve_refs)
    sum0 = LineSum(p, depths, mine0, sums0, line0)
    sum1 = LineSum(p, depths, mine1, sums1, line1)
    little = SmallSum(p, small, small_sum, small_refs)
    pieces = ((up0, came[0]), (down0.at[0], came[1].at[0]), (down0.at[1], came[1].at[1]))
    weights = [remote(mine, other, w_send.at[i], w_recv.at[i], p.beside) for i, (mine, other) in enumerate(pieces)]
    greet([p.sibling, p.across, p.beside, little.far], p)
    halve.begin()
    weights[0].start()
    rows = small0.shape[0]
    small[0:rows, :] = small0[...]
    small[rows : 2 * rows, :] = small1[...]
    small[2 * rows :, :] = jnp.zeros((16, small.shape[1]), F32)
    small[2 * rows :, 0:128] = res[0:16, :]
    little.step(0)
    mine1[...] = quarter1[...]
    for i in range(LINE):
        sum1.start(halve.order(i))
    little.step(1)
    halve.after_first()
    little.step(2)

    def arrive(i):
        halve.add(halve.order(i))
        sum0.start(halve.order(i))

    sum1.relay("far")
    sum1.relay("near")
    arrive(0)
    little.step(3)
    sum1.relay("back")
    arrive(1)
    sum0.relay("far")
    sum1.after_z()
    weights[1].start()
    arrive(2)
    sum0.relay("near")
    sum1.after_x()
    sum0.relay("back")
    arrive(3)
    little.step(4)
    sum0.after_z()
    weights[2].start()
    little.step(5)
    sum0.after_x()
    sum1.finish()
    halve.finish()
    little.finish()
    sum0.finish()
    for copy in weights:
        copy.wait()


def dense_reduce(spread, call_id, smalls, grads0, quarter1, weights0):
    count = LINE * spread
    depths = [g.shape[0] // count for g in grads0]
    width = grads0[0].shape[1]
    small = (2 * smalls[0].shape[0] + 16, width)
    line = LineSum.scratch(spread, depths, width)
    mine = pltpu.VMEM(quarter1.shape, F32)
    scratch = [pltpu.VMEM(small, F32), mine, mine, dma(3), dma(3)] + Halve.scratch(spread, depths, width) + line + line
    return pl.pallas_call(
        functools.partial(dense_reduce_kernel, spread, depths),
        out_shape=[struct(small, F32)] + [struct((2, depth, width), F32) for depth in depths]
        + [struct(w.shape, BF16) for w in weights0],
        in_specs=[VMEM] * 3 + [ANY, ANY, VMEM, ANY, ANY],
        out_specs=[VMEM] * 3 + [ANY] * 2,
        scratch_shapes=scratch + SmallSum.scratch(*small),
        compiler_params=remote_params(call_id),
        cost_estimate=pl.CostEstimate(flops=2 * 10**10, bytes_accessed=2 * 10**8, transcendentals=0),
    )(*smalls, *grads0, quarter1, *weights0)


def stack_kernel(small, qkv, out, *refs):
    parts, (qkv_out, out_out, *stacked), (router, const, gains, vectors, residual) = split(refs, 12, 5)
    qkv_out[...], out_out[...] = qkv[...], out[...]
    for kind, ref in enumerate(stacked):
        for l in (0, 1):
            mine, came = parts[4 * kind + 2 * l], parts[4 * kind + 2 * l + 1]
            ref[l] = mine[...] + came[...].astype(F32)

    @pl.when(jnp.logical_and(pl.program_id(0) == 0, pl.program_id(1) == 0))
    def _():
        depth, width = gains.shape[2], small.shape[1]
        here = lanes(depth, width) == lax.axis_index("dp") * depth + lax.broadcasted_iota(jnp.int32, (depth, width), 0)
        rows = dot_nt(small[...], here.astype(F32), precision=HIGH)
        for l in (0, 1):
            first = 24 * l
            for r in range(CONST0):
                router[r, l : l + 1, :] = rows[first + r : first + r + 1]
            for j in (0, 1):
                at = first + CONST0 + 2 * j
                const[l, j] = rows[at : at + 2]
            gains[l] = rows[first + GAIN0 : first + GAIN0 + 2]
            vectors[l] = rows[first + VECTOR0 : first + VECTOR0 + 2]
        residual[...] = small[48 : 48 + CONST0, 0:CONST0]


def stack_results(small, qkv, out, parts, depth):
    flat = [part for kind in parts for layer in kind for part in layer]
    local, steps = flat[0].shape[0], 1

    def rows_of(shape, lead=None):
        rows, wide = shape[-2] // steps, shape[-1]
        if lead:
            return pl.BlockSpec((lead, 1, rows, wide), lambda l, n: (0, l, n, 0))
        return pl.BlockSpec((1, rows, wide), lambda l, n: (l, n, 0))

    def whole(shape):
        return pl.BlockSpec(shape, lambda l, n: (0,) * len(shape))

    stacked = [(2,) + kind[0][0].shape for kind in parts]
    little = [(CONST0, 2, depth), (2, 2, 2, depth), (2, 2, depth), (2, 2, depth), (CONST0, CONST0)]
    return pl.pallas_call(
        stack_kernel,
        out_shape=[struct(a.shape, F32) for a in (qkv, out)] + [struct(s, F32) for s in stacked + little],
        grid=(local, steps),
        in_specs=[whole(small.shape)] + [rows_of(a.shape) for a in (qkv, out, *flat)],
        out_specs=[rows_of(a.shape) for a in (qkv, out)] + [rows_of(s, 2) for s in stacked] + [whole(s) for s in little],
        compiler_params=pltpu.CompilerParams(vmem_limit_bytes=60 * 2**20),
        cost_estimate=pl.CostEstimate(flops=10**7, bytes_accessed=3 * 10**7, transcendentals=0),
    )(small, qkv, out, *flat)


def per_device(
    tokens, seq_lengths, block_perm, routes, norm_gains, w_qkv, w_out, w_router, w_residual, w_const, v_const,
    w_gate, w_up, w_down, cotangent,
):
    rows, width = tokens.shape
    owners = lax.axis_size("expert")
    shards = lax.axis_size("dp")
    spread = shards // LINE
    local = w_gate.shape[1]
    experts = local * owners
    layers = routes.shape[0]
    slots = experts * CAP

    depth = w_out.shape[1]
    qkv_t = jnp.swapaxes(w_qkv, 1, 2)
    in_kernels = spread == 2 and owners == 4 and layers == local == 2 and qkv_t.shape[1] % 32 == 0 and depth % 32 == 0
    if in_kernels:
        arrays = (qkv_t, w_out, jnp.transpose(w_router, (2, 0, 1)), jnp.swapaxes(w_const, 2, 3), norm_gains, v_const)
        *gathered, routes_all, g0, u0, d0, g1, u1, d1, first0, first1, gate, up, qkv1_own, out1_own, small1_own = dense_gather(
            spread, 4, arrays, jnp.swapaxes(routes, 1, 2), (w_gate, w_up, w_down))
        weights = [[g0, gate, u0, up, d0, from_partner(first0, 1, spread, LINE)]]
        dense = [(gathered[2], gathered[0], gathered[1])]
    else:
        weights = []
        for l in range(layers):
            own = [(w_gate[l].astype(BF16), 2), (w_up[l].astype(BF16), 2), (w_down[l].astype(BF16), 1)]
            weights.append([part for w, axis in own for part in pair_weights(w, axis, spread)])
        small = jnp.concatenate(
            [
                w_router, w_const[:, 0], w_const[:, 1], jnp.swapaxes(norm_gains, 1, 2), jnp.swapaxes(v_const, 1, 2),
                jnp.zeros((layers, depth, 108), F32),
            ],
            axis=2,
        ).astype(BF16)
        packed_routes = jnp.zeros((8, -(-rows // 128) * 128), jnp.int32).at[: 2 * layers, :rows].set(
            jnp.swapaxes(routes, 1, 2).reshape(2 * layers, rows))
        routes_all = lax.all_gather(packed_routes, "expert", axis=0)
        qkv_all = lax.all_gather(qkv_t.astype(BF16), "dp", axis=1, tiled=True)
        out_all = lax.all_gather(w_out.astype(BF16), "dp", axis=1, tiled=True)
        small_all = lax.all_gather(small, "dp", axis=1, tiled=True)
        dense = [(small_all[l], qkv_all[l], out_all[l]) for l in range(layers)]

    cols = ((rows, width), F32)
    attention = [((rows, width), BF16), ((rows, 3 * width), BF16), ((HEADS, rows, rows), F32), ((rows, width), BF16)]
    residual = ((128, 128), F32)
    per_token, sent = ((rows, 128), F32), ((slots, width), BF16)

    def group(array):
        return array.reshape(owners, local, CAP, width)

    attn_in0, qkv0, probs0, attn0, mid0, logits0, stat0, out = local_call(
        first_kernel, experts, (tokens, *dense[0], seq_lengths, block_perm, routes_all),
        attention + [cols, per_token, per_token, sent], scalars=(4, 5))
    ride = (*gathered[3:], qkv1_own, out1_own, small1_own, g1, u1) if in_kernels else None
    ret0, *kept0 = expert_forward(spread, 0, group(out), weights[0], in_kernels, ride)
    if in_kernels:
        kept0, weights[0][5], (qkv_all, out_all, small_all), (gate, up) = kept0[:3], kept0[3], kept0[4:7], kept0[7:]
        dense.append((small_all, qkv_all, out_all))
        first1, ret0 = lax.optimization_barrier((first1, ret0))
        weights.append([g1, gate, u1, up, d1, from_partner(first1, 1, spread, LINE)])
    ret0 = ret0.reshape(slots, width)
    stream1, attn_in1, qkv1, probs1, attn1, mid1, stat1, out = local_call(
        middle_kernel, experts,
        (mid0, dense[0][0], stat0, ret0, *dense[1], seq_lengths, block_perm, routes_all, logits0, w_residual),
        [cols] + attention + [cols, per_token, sent], [residual], scalars=(7, 8))
    ret1, *kept1 = expert_forward(spread, 1, group(out), weights[1], in_kernels)
    if in_kernels:
        weights[1][5] = kept1.pop()
    ret1 = ret1.reshape(slots, width)

    small_grads = ((24, width), F32)
    output, g_small1, extra, out, small_grad1, res_grad = local_call(
        turn_kernel, experts, (mid1, dense[1][0], stat1, ret1, cotangent, logits0, w_residual),
        [((rows, width), BF16), per_token, per_token, sent, small_grads, residual], [residual])
    back, *expert_grads1 = expert_backward(spread, 2, group(out), kept1, weights[1], in_kernels)
    ride = None
    grad_type = BF16 if in_kernels else F32
    dense_grads = [((3 * width, width), grad_type), ((width, width), grad_type), small_grads]
    attention_scratch = [((rows, 3 * width), BF16), ((rows, width), BF16)]
    qkv_grad1, out_grad1, small_grad1, grad, g_small0, out, small_grad0 = local_call(
        between_kernel, experts,
        (cotangent, back.reshape(slots, width), g_small1, stat1, mid1, dense[1][0], stream1, dense[1][1], dense[1][2],
         attn_in1, qkv1, probs1, attn1, small_grad1, mid0, dense[0][0], stat0, ret0, extra),
        dense_grads + [cols, per_token, sent, small_grads], attention_scratch)
    if in_kernels:
        gate1, up1, up1_sent, down1, down1_sent, gate1_came = expert_grads1
        ride = (qkv_grad1, out_grad1, up1_sent, down1_sent)
    back, *expert_grads0 = expert_backward(spread, 3, group(out), kept0, weights[0], in_kernels, ride)
    qkv_grad0, out_grad0, small_grad0, tokens_grad = local_call(
        last_kernel, experts,
        (grad, back.reshape(slots, width), g_small0, stat0, mid0, dense[0][0], tokens, dense[0][1], dense[0][2],
         attn_in0, qkv0, probs0, attn0, small_grad0),
        dense_grads + [cols], attention_scratch)

    if in_kernels:
        gate0, up0, up0_sent, down0, down0_sent, gate0_came, quarter1, up1_came, down1_came = expert_grads0
        packed, qkv_grad, out_grad, up0_came, down0_came = dense_reduce(
            spread, 5, (small_grad0, small_grad1, res_grad), (qkv_grad0, out_grad0), quarter1, (up0_sent, down0_sent))
        pairs = (
            ((gate0, gate0_came), (gate1, gate1_came)), ((up0, up0_came), (up1, up1_came)),
            ((down0, down0_came), (down1, down1_came)))
        qkv_grad, out_grad, gate_grad, up_grad, down_grad, router_grad, const_grad, gains_grad, vector_grad, residual_grad = (
            stack_results(packed, qkv_grad, out_grad, pairs, depth))
        router_grad = jnp.transpose(router_grad, (1, 2, 0))
        const_grad = jnp.swapaxes(const_grad, 2, 3)
    else:
        gate_grad, up_grad, down_grad = (
            jnp.stack([
                pair_sum(grads[at * len(grads) // 3 : (at + 1) * len(grads) // 3], axis, spread)
                for grads in (expert_grads0, expert_grads1)])
            for axis, at in ((2, 0), (2, 1), (1, 2)))
        packed = jnp.concatenate([small_grad0, small_grad1, jnp.pad(res_grad[:16], ((0, 0), (0, width - 128)))])
        packed = lax.psum(packed, ("dp", "expert"))
        qkv_grad, out_grad = (
            lax.psum(lax.psum_scatter(jnp.stack(pair), "dp", scatter_dimension=1, tiled=True), "expert")
            for pair in ((qkv_grad0, qkv_grad1), (out_grad0, out_grad1)))
        mine = lax.dynamic_slice_in_dim(packed, lax.axis_index("dp") * depth, depth, axis=1)
        mine = jnp.stack([mine[:24], mine[24:48]])
        router_grad = jnp.swapaxes(mine[:, :CONST0], 1, 2)
        const_grad = jnp.swapaxes(mine[:, CONST0:GAIN0].reshape(layers, 2, 2, depth), 2, 3)
        residual_grad = packed[48 : 48 + CONST0, :CONST0]
        gains_grad, vector_grad = mine[:, GAIN0 : GAIN0 + 2], mine[:, VECTOR0 : VECTOR0 + 2]
    return (
        output, tokens_grad, gains_grad, jnp.swapaxes(qkv_grad, 1, 2), out_grad, router_grad,
        residual_grad, const_grad, vector_grad, gate_grad, up_grad, down_grad,
    )


def solution(mesh):
    in_specs = (
        P(("dp", "expert"), None), P("dp", None, None), P("dp", None), P(None, ("dp", "expert"), None),
        P(None, None, "dp"), P(None, None, "dp"), P(None, "dp", None), P(None, "dp", None), P(),
        P(None, None, "dp", None), P(None, None, "dp"), P(None, "expert", None, "dp"), P(None, "expert", None, "dp"),
        P(None, "expert", "dp", None), P(("dp", "expert"), None),
    )
    out_specs = (
        P(("dp", "expert"), None), P(("dp", "expert"), None), P(None, None, "dp"), P(None, None, "dp"),
        P(None, "dp", None), P(None, "dp", None), P(), P(None, None, "dp", None), P(None, None, "dp"),
        P(None, "expert", None, "dp"), P(None, "expert", None, "dp"), P(None, "expert", "dp", None),
    )
    return jax.shard_map(per_device, mesh=mesh, in_specs=in_specs, out_specs=out_specs, check_vma=False)
```
